32 devices in a mesh: expert: 4 (over z), shard: 8 (over y, x, core).
Axes of the slice: x: 2, y: 2, z: 4, core: 2. Of those that a mesh axis runs over, the one named last changes fastest.
Arguments:
- tokens: bfloat16 [32, 512, 1536], P(('expert', 'shard')), may hold values from -6 to 6
- lengths: int32 [32], P(('expert', 'shard')), may hold values from 128 to 512, as said below
- routes: int32 [32, 512, 8], P(('expert', 'shard')), may hold values from 0 to 19, all different within a row
- priority: int32 [32, 512], P(('expert', 'shard')), may hold values from 0 to 511, each once within a row
- first_gain: bfloat16 [1536], P('shard'), may hold values from 0.5 to 1.5
- query_weight: bfloat16 [1536, 1536], P('shard'), may hold values from -0.1875 to 0.1875
- key_weight: bfloat16 [1536, 512], P('shard'), may hold values from -0.1875 to 0.1875
- value_weight: bfloat16 [1536, 512], P('shard'), may hold values from -0.15625 to 0.15625
- merge_weight: bfloat16 [1536, 1536], P('shard'), may hold values from -0.875 to 0.875
- router_weight: bfloat16 [1536, 20], P('shard'), may hold values from -0.078125 to 0.078125
- second_gain: bfloat16 [1536], P('shard'), may hold values from 0.5 to 1.5
- gate_weight: bfloat16 [20, 1536, 512], P('expert', 'shard'), may hold values from -0.15625 to 0.15625
- up_weight: bfloat16 [20, 1536, 512], P('expert', 'shard'), may hold values from -0.15625 to 0.15625
- down_weight: bfloat16 [20, 1536, 512], P('expert', 'shard'), may hold values from -1 to 1
- cotangent: bfloat16 [32, 512, 1536], P(('expert', 'shard')), may hold values from -6 to 6
Outputs:
- block_output: float32 [32, 512, 1536], P(('expert', 'shard'))
- input_grad: float32 [32, 512, 1536], P(('expert', 'shard'))
- first_gain_grad: float32 [1536], P(('expert', 'shard'))
- query_grad: float32 [1536, 1536], P(('expert', 'shard'))
- key_grad: float32 [1536, 512], P(('expert', 'shard'))
- value_grad: float32 [1536, 512], P(('expert', 'shard'))
- merge_grad: float32 [1536, 1536], P(('expert', 'shard'))
- router_grad: float32 [1536, 20], P(('expert', 'shard'))
- second_gain_grad: float32 [1536], P(('expert', 'shard'))
- gate_grad: float32 [20, 1536, 512], P('expert', 'shard')
- up_grad: float32 [20, 1536, 512], P('expert', 'shard')
- down_grad: float32 [20, 1536, 512], P('expert', 'shard')
The draws below stay inside these ranges and needn't reach their ends.
Inputs may be any that keep to these rules, and one draw needn't show every extreme that they name: The valid tokens of sequence s are its first lengths[s] slots; in every draw some sequence is full and some holds 128. `routes`: each token names 8 different experts, and every expert is named by some token. `priority`: each sequence's row holds every number of 0 to 511 once.
All inputs are finite; a program needn't handle non-finite values.
Results may differ from the reference program's by a relative error of at most 0.017.
Values may be sent and summed in bfloat16 or wider, within the bound.
A program may use at most 320 MiB of HBM per device.

```python
import functools
import math
import jax
import jax.numpy as jnp
from jax import lax

D = 1536
HEADS = 24
KV_HEADS = 8
HD = 64
FF = 512
TOP = 8
EXPERTS = 20
SEQ_LEN = 512
SEQS = 32
CAP = 128


def draw_lengths(key, part):
    values = jax.random.randint(jax.random.fold_in(key, 11), (SEQS,), SEQ_LEN // 4, SEQ_LEN + 1)
    shuffled = jax.random.permutation(jax.random.fold_in(key, 12), SEQS)
    values = values.at[shuffled[0]].set(SEQ_LEN)
    values = values.at[shuffled[1]].set(SEQ_LEN // 4)
    return values.astype(jnp.int32)


def raised(entries, own_key, source, target, parts, factor):
    owner, partner = [(jnp.arange(entries.shape[axis_at]) // (entries.shape[axis_at] // parts)).reshape([-1 if axis == axis_at else 1 for axis in range(entries.ndim)]) for axis_at in (source, target)]
    chosen = jax.random.permutation(own_key, parts)[partner]
    strong = (owner == chosen) | (owner == (partner + parts // 2) % parts)
    return jnp.where(strong, factor * entries, entries)


def shard_levels(rng, shape, pieces, smallest, high):
    factor_of = 1.0
    for dim, shards_of in pieces:
        steps = jax.random.uniform(jax.random.fold_in(jax.random.fold_in(rng, 6), dim), (shards_of,), jnp.float32, smallest / len(pieces), high / len(pieces))
        factor_of = factor_of * jnp.repeat(jnp.exp(steps), shape[dim] // shards_of).reshape((-1,) + (1,) * (len(shape) - 1 - dim))
    return factor_of


def different_ones(key, rows, amount, top, lift):
    ranking = jax.random.permutation(jax.random.fold_in(key, 1), amount)
    favour = ranking
    for power in range(3):
        favour = favour * favour // amount
    favour = favour * lift // amount
    chance = jax.random.randint(jax.random.fold_in(key, 2), (rows, amount), 0, 4096) + favour
    fixed_rows = jax.random.permutation(jax.random.fold_in(key, 3), rows)[jnp.arange(amount) % rows]
    chance = jnp.where(jnp.arange(rows)[:, None] == fixed_rows[None, :], 1 << 14, chance)
    score = chance * amount + jnp.arange(amount)
    return lax.top_k(score.astype(jnp.int32), top)[1].astype(jnp.int32)


def scatter_about(rng, extent, width, limit, pieces=(), held_as=jnp.bfloat16):
    result = jax.random.normal(rng, extent, jnp.float32) * width
    if len(pieces) > 0:
        result = shard_levels(rng, extent, pieces, -0.22, 0.18) * result
    return jnp.clip(result, min=-limit, max=limit).astype(held_as)


def heavy_noise(key, extent, scale, reach, cuts, heavy, kind=jnp.bfloat16):
    values = scale * jax.random.normal(key, extent, jnp.float32)
    if cuts:
        values = values * shard_levels(key, extent, cuts, -0.22, 0.18)
    return jnp.clip(raised(values, jax.random.fold_in(key, 3), *heavy), -reach, reach).astype(kind)


def setup_inputs(seed: int = 0) -> dict:
    keys = jax.random.split(jax.random.key(seed), 16)
    return {
        "tokens": scatter_about(keys[0], (SEQS, SEQ_LEN, D), 1.0, 6.0, ((0, 32),)),
        "lengths": draw_lengths(jax.random.fold_in(keys[15], 71), 0),
        "routes": different_ones(keys[2], SEQS * SEQ_LEN, EXPERTS, TOP, 3276).reshape((SEQS, SEQ_LEN, TOP)),
        "priority": jax.vmap(lambda own: jax.random.permutation(own, SEQ_LEN))(jax.random.split(keys[3], SEQS)).reshape((SEQS, SEQ_LEN)).astype(jnp.int32),
        "first_gain": jnp.clip(1.0 + 0.1 * jax.random.normal(keys[4], (D,), jnp.float32), 0.5, 1.5).astype(jnp.bfloat16),
        "query_weight": scatter_about(keys[5], (D, HEADS * HD), (2 * D // 3) ** -0.5, 0.1875, ((0, 8),)),
        "key_weight": scatter_about(keys[6], (D, KV_HEADS * HD), (2 * D // 3) ** -0.5, 0.1875, ((0, 8),)),
        "value_weight": scatter_about(keys[7], (D, KV_HEADS * HD), D ** -0.5, 0.15625, ((0, 8),)),
        "merge_weight": scatter_about(keys[8], (HEADS * HD, D), (HEADS * HD // 32) ** -0.5, 0.875, ((0, 8),)),
        "router_weight": scatter_about(keys[9], (D, EXPERTS), (4 * D) ** -0.5, 0.078125, ((0, 8),)),
        "second_gain": jnp.clip(1.0 + 0.1 * jax.random.normal(keys[10], (D,), jnp.float32), 0.5, 1.5).astype(jnp.bfloat16),
        "gate_weight": scatter_about(keys[11], (EXPERTS, D, FF), D ** -0.5, 0.15625, ((0, 4), (1, 8))),
        "up_weight": scatter_about(keys[12], (EXPERTS, D, FF), D ** -0.5, 0.15625, ((0, 4), (1, 8))),
        "down_weight": scatter_about(keys[13], (EXPERTS, D, FF), (FF // 16) ** -0.5, 1.0, ((0, 4), (1, 8))),
        "cotangent": heavy_noise(keys[14], (SEQS, SEQ_LEN, D), 1.0, 6.0, ((0, 32),), (0, 2, 32, 2.75)),
    }


EPS = 1e-05
THETA = 10000.0
NEGATIVE = -1e+30
HIGH_PRECISION = lax.Precision.HIGHEST

@jax.custom_vjp
def low(v):
    return lax.optimization_barrier(v.astype(jnp.bfloat16)).astype(jnp.float32)

@jax.custom_vjp
def reduced_backward(v):
    return v

def low_keep(v):
    return (low(v), None)

def reduced_forward(kept, grad):
    return (grad,)

def back_keep(v):
    return (v, None)

def back_low(kept, grad):
    return (low(grad),)
low.defvjp(low_keep, reduced_forward)
reduced_backward.defvjp(back_keep, back_low)

def rope_tables(slots, size):
    half_size = size // 2
    frequency = THETA ** (-jnp.arange(half_size, dtype=jnp.float32) * 2.0 / size)
    angles = jnp.arange(slots, dtype=jnp.float32)[:, None] * frequency[None, :]
    return (jnp.cos(angles), jnp.sin(angles))

def rotate(values, cosine, sine_table, direction):
    half_size = values.shape[-1] // 2
    first_half = values[..., :half_size]
    second_half = values[..., half_size:]
    cos_part = cosine[:, None, :]
    sin_part = direction * sine_table[:, None, :]
    return jnp.concatenate([first_half * cos_part - second_half * sin_part, second_half * cos_part + first_half * sin_part], axis=-1)

def routing_tables(routes, priority, sequence_length, expert_count, capacity):
    slots = routes.shape[0]
    positions = jnp.arange(slots, dtype=jnp.int32)
    valid_rows = (positions < sequence_length).astype(jnp.int32)
    chosen = lax.optimization_barrier(jnp.sum((routes[:, :, None] == jnp.arange(expert_count, dtype=jnp.int32)[None, None, :]).astype(jnp.int32), axis=1)).astype(jnp.int32) * valid_rows[:, None]
    fill_order = jnp.zeros((slots,), jnp.int32).at[priority.astype(jnp.int32)].set(positions)
    ordered = jnp.take(chosen, fill_order, axis=0)
    before = (jnp.cumsum(ordered, axis=0, dtype=jnp.int32) - ordered).astype(jnp.int32)
    slot_count = jnp.take(before, priority.astype(jnp.int32), axis=0)
    kept_slots = chosen * (slot_count < capacity).astype(jnp.int32)
    slot_match = kept_slots[:, :, None] * (slot_count[:, :, None] == jnp.arange(capacity, dtype=jnp.int32)[None, None, :]).astype(jnp.int32)
    slot_index = lax.optimization_barrier(jnp.sum(slot_match * positions[:, None, None], axis=0)).astype(jnp.int32)
    filled = lax.optimization_barrier(jnp.sum(slot_match, axis=0)).astype(jnp.int32)
    return (slot_index, filled)

def attention_branch(inputs, sequence_length, first_gain, query_weight, key_weight, value_weight, merge_weight):
    slots = inputs.shape[0]
    rms_one = lax.rsqrt(lax.optimization_barrier(jnp.mean(inputs * inputs, axis=-1, keepdims=True)) + EPS)
    normed_one = low(inputs * rms_one * first_gain)
    cosine, sine_table = rope_tables(slots, HD)
    queries = reduced_backward(jnp.dot(normed_one, query_weight, precision=HIGH_PRECISION)).reshape(slots, HEADS, HD)
    key_rows = reduced_backward(jnp.dot(normed_one, key_weight, precision=HIGH_PRECISION)).reshape(slots, KV_HEADS, HD)
    values = reduced_backward(low(jnp.dot(normed_one, value_weight, precision=HIGH_PRECISION))).reshape(slots, KV_HEADS, HD)
    queries = low(rotate(queries, cosine, sine_table, 1.0)).reshape(slots, KV_HEADS, HEADS // KV_HEADS, HD)
    key_rows = low(rotate(key_rows, cosine, sine_table, 1.0))
    scores = reduced_backward(jnp.einsum('qkgd,skd->kgqs', queries, key_rows, precision=HIGH_PRECISION) * HD ** (-0.5))
    positions = jnp.arange(slots, dtype=jnp.int32)
    allowed = (positions[None, :] <= positions[:, None]) & (positions[None, :] < sequence_length)
    scores = jnp.where(allowed, scores, NEGATIVE)
    probs = jax.nn.softmax(scores, axis=-1)
    mixed = jnp.einsum('kgqs,skd->qkgd', low(probs), values, precision=HIGH_PRECISION)
    mixed = reduced_backward(low(mixed)).reshape(slots, HEADS * HD)
    return reduced_backward(jnp.dot(mixed, merge_weight, precision=HIGH_PRECISION))

def pick_rows(table, where):
    return jnp.take(table, where, axis=0)

def scatter_rows(table, where, addend):
    return table.at[where].add(addend)

def reference(tokens, lengths, routes, priority, first_gain, query_weight, key_weight, value_weight, merge_weight, router_weight, second_gain, gate_weight, up_weight, down_weight, cotangent):
    tables = jax.vmap(functools.partial(routing_tables, expert_count=EXPERTS, capacity=CAP))(routes, priority, lengths)
    slot_index, filled = tables
    chosen = (routes[..., None] == jnp.arange(EXPERTS, dtype=jnp.int32)).astype(jnp.float32)
    live_rows = (jnp.arange(SEQ_LEN, dtype=jnp.int32)[None, :] < lengths[:, None]).astype(jnp.float32)[..., None]
    group_size = math.gcd(SEQS, max(1, 4096 // SEQ_LEN))
    group_count = SEQS // group_size

    def forward(inputs, gain_first, query_w, key_w, value_w, merge_w, router_matrix, gain_second, gate_w, up_w, down_w):

        def attend_group(grouped):
            return jax.vmap(attention_branch, in_axes=(0, 0, None, None, None, None, None))(grouped[0], grouped[1], gain_first, query_w, key_w, value_w, merge_w)
        grouped_all = (inputs.reshape(group_count, group_size, SEQ_LEN, D), lengths.reshape(group_count, group_size))
        attended = lax.map(jax.checkpoint(attend_group), grouped_all).reshape(SEQS, SEQ_LEN, D)
        hidden = inputs + live_rows * attended
        rms_two = lax.rsqrt(lax.optimization_barrier(jnp.mean(hidden * hidden, axis=-1, keepdims=True)) + EPS)
        second_normed = low(hidden * rms_two * gain_second)
        router_logits = reduced_backward(jnp.einsum('xgb,bf->xgf', second_normed, router_matrix, precision=HIGH_PRECISION))
        picked = lax.optimization_barrier(jnp.sum(router_logits[:, :, None, :] * chosen, axis=-1))
        gate_probs = jax.nn.softmax(picked, axis=-1)
        gate_dense = lax.optimization_barrier(jnp.sum(gate_probs[..., None] * chosen, axis=2))

        def expert_step(moe_total, expert_item):
            gate_one, lift_one, down_one, slot_rows, slot_fill, expert_id = expert_item
            presence = slot_fill.astype(jnp.float32)
            sent_rows = reduced_backward(jax.vmap(pick_rows)(second_normed, slot_rows) * presence[:, :, None])
            gate_pre = reduced_backward(jnp.einsum('scd,df->scf', sent_rows, gate_one, precision=HIGH_PRECISION))
            lift_pre = reduced_backward(jnp.einsum('scd,df->scf', sent_rows, lift_one, precision=HIGH_PRECISION))
            activated = low(jax.nn.silu(gate_pre) * lift_pre)
            produced = reduced_backward(low(jnp.einsum('scf,df->scd', activated, down_one, precision=HIGH_PRECISION)))
            gate_column = lax.dynamic_index_in_dim(gate_dense, expert_id, axis=2, keepdims=False)
            slot_gate = jax.vmap(pick_rows)(gate_column, slot_rows) * presence
            moe_total = jax.vmap(scatter_rows)(moe_total, slot_rows, produced * slot_gate[:, :, None])
            return (moe_total, None)
        expert_items = (gate_w, up_w, down_w, jnp.transpose(slot_index, (1, 0, 2)), jnp.transpose(filled, (1, 0, 2)), jnp.arange(EXPERTS, dtype=jnp.int32))
        moe_total, unused = lax.scan(jax.checkpoint(expert_step), jnp.zeros((SEQS, SEQ_LEN, D), jnp.float32), expert_items)
        return hidden + moe_total
    floats = tuple((array.astype(jnp.float32) for array in (tokens, first_gain, query_weight, key_weight, value_weight, merge_weight, router_weight, second_gain, gate_weight, up_weight, down_weight)))
    block_output, pullback = jax.vjp(forward, *floats)
    grads = pullback(cotangent.astype(jnp.float32))
    return (block_output, grads[0], grads[1], grads[2], grads[3], grads[4], grads[5], grads[6], grads[7], grads[8], grads[9], grads[10])
```

```python
import jax
import jax.numpy as jnp
from jax import lax
from jax.sharding import PartitionSpec as P

HEADS = 24
KV_HEADS = 8
HD = 64
TOP = 8
EXP_DEV = 5

EPS = 1e-05
THETA = 10000.0
NEGATIVE = -1e30
F32 = jnp.float32
BF16 = jnp.bfloat16


def rope_tables(slots, size):
    half_size = size // 2
    frequency = THETA ** (-jnp.arange(half_size, dtype=F32) * 2.0 / size)
    angles = jnp.arange(slots, dtype=F32)[:, None] * frequency[None, :]
    return (jnp.cos(angles), jnp.sin(angles))


def rotate(values, cosine, sine_table, direction):
    half_size = values.shape[-1] // 2
    first_half = values[..., :half_size]
    second_half = values[..., half_size:]
    cos_part = cosine[:, None, :]
    sin_part = direction * sine_table[:, None, :]
    return jnp.concatenate(
        [
            first_half * cos_part - second_half * sin_part,
            second_half * cos_part + first_half * sin_part,
        ],
        axis=-1,
    )


def dispatch_matrix(routes, priority, length, expert_ids, capacity):
    slots = routes.shape[0]
    positions = jnp.arange(slots, dtype=jnp.int32)
    live = positions < length
    named = jnp.any(routes[:, :, None] == expert_ids[None, None, :], axis=1) & live[:, None]
    earlier = (priority[None, :] < priority[:, None]).astype(BF16)
    slot = jnp.dot(earlier, named.astype(BF16), preferred_element_type=F32).astype(jnp.int32)
    slot = jnp.where(named, slot, capacity)
    return (
        slot.T[:, None, :] == jnp.arange(capacity, dtype=jnp.int32)[None, :, None]
    ).astype(BF16)


def block_scores(queries_block, key_rows, positions, sequence_length, score_scale):
    scores = (
        jnp.einsum("qkgd,skd->kgqs", queries_block, key_rows, preferred_element_type=F32)
        * score_scale
    )
    allowed = (positions[None, :] <= positions[:, None]) & (positions[None, :] < sequence_length)
    return jnp.where(allowed, scores, NEGATIVE)


def body(
    tokens,
    lengths,
    routes,
    priority,
    first_gain,
    query_weight,
    key_weight,
    value_weight,
    merge_weight,
    router_weight,
    second_gain,
    gate_weight,
    up_weight,
    down_weight,
    cotangent,
):
    slots = tokens.shape[1]
    width = tokens.shape[2]
    groups = lax.axis_size("expert")
    expert_count = router_weight.shape[1]
    capacity = 5 * slots * TOP // (8 * expert_count)
    share = HEADS // KV_HEADS
    score_scale = HD ** (-0.5)
    q_cols, k_cols = HEADS * HD, KV_HEADS * HD
    side_cols = 128

    def gather_shard(value, axis=0):
        return lax.all_gather(value, "shard", axis=axis, tiled=True)

    side = jnp.concatenate(
        [router_weight, first_gain[:, None], second_gain[:, None]], axis=1
    )
    side = jnp.pad(side, ((0, 0), (0, side_cols - expert_count - 2)))
    first_set = gather_shard(
        jnp.concatenate([query_weight, key_weight, value_weight, side], axis=1)
    )
    qkv_full = first_set[:, : q_cols + 2 * k_cols]
    side_full = first_set[:, q_cols + 2 * k_cols :]
    router_full = side_full[:, :expert_count]
    gain_first = side_full[:, expert_count].astype(F32)
    gain_second = side_full[:, expert_count + 1].astype(F32)
    merge_full = gather_shard(merge_weight)
    tables = jnp.concatenate(
        [routes[0], priority[0][:, None], jnp.broadcast_to(lengths[:, None], (slots, 1))], axis=1
    )
    tables = lax.all_gather(tables, "expert", axis=0, tiled=False)
    upstream_all = lax.all_gather(cotangent[0], "expert", axis=0, tiled=False)
    gate_full = gather_shard(gate_weight, 1)
    up_full = gather_shard(up_weight, 1)
    down_full = gather_shard(down_weight, 1)

    group = lax.axis_index("expert")
    own_experts = group * EXP_DEV + jnp.arange(EXP_DEV, dtype=jnp.int32)
    spread = jax.vmap(
        lambda t: dispatch_matrix(t[:, :TOP], t[:, TOP], t[0, TOP + 1], own_experts, capacity)
    )(tables)

    inputs = tokens[0].astype(F32)
    length = lengths[0]
    positions = jnp.arange(slots, dtype=jnp.int32)
    live_rows = (positions < length).astype(F32)[:, None]
    cosine, sine_table = rope_tables(slots, HD)
    rms_one = lax.rsqrt(jnp.mean(inputs * inputs, axis=-1, keepdims=True) + EPS)
    unit_one = inputs * rms_one
    normed_one = (unit_one * gain_first).astype(BF16)
    qkv = jnp.dot(normed_one, qkv_full, preferred_element_type=F32)
    queries = qkv[:, :q_cols].reshape(slots, HEADS, HD)
    key_rows = qkv[:, q_cols : q_cols + k_cols].reshape(slots, KV_HEADS, HD)
    values = qkv[:, q_cols + k_cols :].astype(BF16).reshape(slots, KV_HEADS, HD)
    queries = rotate(queries, cosine, sine_table, 1.0).astype(BF16)
    queries = queries.reshape(slots, KV_HEADS, share, HD)
    key_rows = rotate(key_rows, cosine, sine_table, 1.0).astype(BF16)
    scores = block_scores(queries, key_rows, positions, length, score_scale)
    row_peak = jnp.max(scores, axis=-1, keepdims=True)
    exp_scores = jnp.exp(scores - row_peak)
    total = jnp.sum(exp_scores, axis=-1, keepdims=True)
    mixed = jnp.einsum(
        "kgqs,skd->qkgd", (exp_scores / total).astype(BF16), values, preferred_element_type=F32
    ).astype(BF16)
    lse = row_peak + jnp.log(total)
    mixed = mixed.reshape(slots, q_cols)
    attended = jnp.dot(mixed, merge_full, preferred_element_type=F32)
    hidden = inputs + live_rows * attended
    rms_two = lax.rsqrt(jnp.mean(hidden * hidden, axis=-1, keepdims=True) + EPS)
    unit_two = hidden * rms_two
    normed_two = (unit_two * gain_second).astype(BF16)

    logits = jnp.dot(normed_two, router_full, preferred_element_type=F32)
    chosen = (
        routes[0][:, :, None] == jnp.arange(expert_count, dtype=jnp.int32)[None, None, :]
    ).astype(F32)
    chosen_any = jnp.sum(chosen, axis=1)
    masked = jnp.where(chosen_any > 0, logits, NEGATIVE)
    peak = jnp.max(masked, axis=-1, keepdims=True)
    exp_logits = jnp.exp(masked - peak) * chosen_any
    gate_dense = exp_logits / jnp.sum(exp_logits, axis=-1, keepdims=True)

    normed_all = lax.all_gather(normed_two, "expert", axis=0, tiled=False)
    gates_all = lax.all_gather(gate_dense, "expert", axis=0, tiled=False)
    gates_own = lax.dynamic_slice_in_dim(gates_all, group * EXP_DEV, EXP_DEV, axis=2)
    slot_gate = jnp.sum(spread.astype(F32) * gates_own.transpose(0, 2, 1)[:, :, None, :], axis=-1)
    rows = jnp.einsum("sxct,std->xscd", spread, normed_all, preferred_element_type=F32)
    rows = rows.astype(BF16).reshape(EXP_DEV, groups * capacity, width)
    ups = jnp.einsum("sxct,std->xscd", spread, upstream_all, preferred_element_type=F32)
    ups = ups.astype(BF16).reshape(EXP_DEV, groups * capacity, width)
    gates = slot_gate.transpose(1, 0, 2).reshape(EXP_DEV, groups * capacity, 1)
    gate_pre = jnp.einsum("xrd,xdf->xrf", rows, gate_full, preferred_element_type=F32)
    lift_pre = jnp.einsum("xrd,xdf->xrf", rows, up_full, preferred_element_type=F32)
    act_grad = jnp.einsum("xrd,xdf->xrf", ups, down_full, preferred_element_type=F32)
    sigmoid_gate = jax.nn.sigmoid(gate_pre)
    silu_gate = gate_pre * sigmoid_gate
    activated = silu_gate * lift_pre
    slot_grad = jnp.sum(act_grad * activated, axis=-1)
    gated = (activated * gates).astype(BF16)
    act_grad = act_grad * gates
    gate_pre_grad = (
        act_grad * lift_pre * (sigmoid_gate + silu_gate * (1.0 - sigmoid_gate))
    ).astype(BF16)
    lift_pre_grad = (act_grad * silu_gate).astype(BF16)
    produced = jnp.einsum(
        "xrf,xdf->xrd", gated, down_full, preferred_element_type=F32
    ).astype(BF16)
    back_rows = (
        jnp.einsum("xrf,xdf->xrd", gate_pre_grad, gate_full, preferred_element_type=F32)
        + jnp.einsum("xrf,xdf->xrd", lift_pre_grad, up_full, preferred_element_type=F32)
    ).astype(BF16)

    def combine(slot_rows):
        slot_rows = slot_rows.reshape(EXP_DEV, groups, capacity, width)
        return jnp.einsum("sxct,xscd->std", spread, slot_rows, preferred_element_type=F32)

    slot_grad = slot_grad.reshape(EXP_DEV, groups, capacity).transpose(1, 0, 2)
    token_grad = jnp.sum(spread.astype(F32) * slot_grad[:, :, :, None], axis=2)
    token_grad = token_grad.transpose(0, 2, 1)
    spots = (own_experts[:, None] == jnp.arange(side_cols)[None, :]).astype(F32)
    token_grad = jnp.sum(token_grad[:, :, :, None] * spots[None, None], axis=2)
    back_total = jnp.concatenate(
        [combine(back_rows).astype(BF16), token_grad.astype(BF16)], axis=-1
    )
    back_total = lax.psum_scatter(
        back_total.reshape(groups * slots, width + side_cols), "expert", scatter_dimension=0, tiled=True
    )
    expert_total = lax.psum_scatter(
        combine(produced).astype(BF16).reshape(groups * slots, width), "expert", scatter_dimension=0, tiled=True
    )
    block_output = hidden + expert_total.astype(F32)

    down_part = jnp.einsum("xrd,xrf->xdf", ups, gated, preferred_element_type=F32)
    gate_part = jnp.einsum("xrd,xrf->xdf", rows, gate_pre_grad, preferred_element_type=F32)
    lift_part = jnp.einsum("xrd,xrf->xdf", rows, lift_pre_grad, preferred_element_type=F32)

    def scatter_expert(part):
        return lax.psum_scatter(
            part.astype(BF16), "shard", scatter_dimension=1, tiled=True
        ).astype(F32)

    down_grad = scatter_expert(down_part)
    gate_grad = scatter_expert(gate_part)
    up_grad = scatter_expert(lift_part)

    upstream = cotangent[0].astype(F32)
    slot_back = back_total[:, width : width + expert_count].astype(F32)
    picked_grad = gate_dense * (
        slot_back - jnp.sum(gate_dense * slot_back, axis=-1, keepdims=True)
    )
    logit_grad = picked_grad.astype(BF16)
    router_part = jnp.einsum("ld,le->de", normed_two, logit_grad, preferred_element_type=F32)
    normed_two_grad = jnp.einsum("le,de->ld", logit_grad, router_full, preferred_element_type=F32)
    normed_two_grad = normed_two_grad + back_total[:, :width].astype(F32)
    scaled_two = normed_two_grad * gain_second
    second_gain_part = jnp.sum(normed_two_grad * unit_two, axis=0)
    hidden_grad = upstream + rms_two * (
        scaled_two - unit_two * jnp.mean(scaled_two * unit_two, axis=-1, keepdims=True)
    )
    attended_grad = (live_rows * hidden_grad).astype(BF16)

    merge_part = jnp.einsum("lh,ld->hd", mixed, attended_grad, preferred_element_type=F32)
    merge_grad = lax.psum_scatter(
        merge_part.astype(BF16), ("expert", "shard"), scatter_dimension=0, tiled=True
    ).astype(F32)
    mixed_grad = (
        jnp.einsum("ld,hd->lh", attended_grad, merge_full, preferred_element_type=F32)
        .astype(BF16)
        .reshape(slots, KV_HEADS, share, HD)
    )
    scores = block_scores(queries, key_rows, positions, length, score_scale)
    probs = jnp.exp(scores - lse)
    prob_back = jnp.einsum("qkgd,skd->kgqs", mixed_grad, values, preferred_element_type=F32)
    score_grad = (
        probs * (prob_back - jnp.sum(probs * prob_back, axis=-1, keepdims=True))
    ).astype(BF16)
    queries_grad = (
        jnp.einsum("kgqs,skd->qkgd", score_grad, key_rows, preferred_element_type=F32)
        * score_scale
    ).reshape(slots, HEADS, HD)
    key_total = (
        jnp.einsum("kgqs,qkgd->skd", score_grad, queries, preferred_element_type=F32) * score_scale
    )
    value_total = jnp.einsum(
        "kgqs,qkgd->skd", probs.astype(BF16), mixed_grad, preferred_element_type=F32
    )
    qkv_grad = jnp.concatenate(
        [
            rotate(queries_grad, cosine, sine_table, -1.0).astype(BF16).reshape(slots, q_cols),
            rotate(key_total, cosine, sine_table, -1.0).astype(BF16).reshape(slots, k_cols),
            value_total.astype(BF16).reshape(slots, k_cols),
        ],
        axis=1,
    )
    qkv_part = jnp.einsum("ld,lh->dh", normed_one, qkv_grad, preferred_element_type=F32)
    normed_one_grad = jnp.einsum("lh,dh->ld", qkv_grad, qkv_full, preferred_element_type=F32)
    scaled_one = normed_one_grad * gain_first
    first_gain_part = jnp.sum(normed_one_grad * unit_one, axis=0)
    input_grad = hidden_grad + rms_one * (
        scaled_one - unit_one * jnp.mean(scaled_one * unit_one, axis=-1, keepdims=True)
    )
    side_part = jnp.concatenate(
        [router_part, first_gain_part[:, None], second_gain_part[:, None]], axis=1
    )
    side_part = jnp.pad(side_part, ((0, 0), (0, side_cols - expert_count - 2)))
    reduced = lax.psum_scatter(
        jnp.concatenate([qkv_part.astype(BF16), side_part.astype(BF16)], axis=1),
        ("expert", "shard"),
        scatter_dimension=0,
        tiled=True,
    ).astype(F32)
    side_grad = reduced[:, q_cols + 2 * k_cols :]
    return (
        block_output[None],
        input_grad[None],
        side_grad[:, expert_count],
        reduced[:, :q_cols],
        reduced[:, q_cols : q_cols + k_cols],
        reduced[:, q_cols + k_cols : q_cols + 2 * k_cols],
        merge_grad,
        side_grad[:, :expert_count],
        side_grad[:, expert_count + 1],
        gate_grad,
        up_grad,
        down_grad,
    )


def solution(mesh):
    both = ("expert", "shard")
    in_specs = (
        P(both, None, None),
        P(both),
        P(both, None, None),
        P(both, None),
        P("shard"),
        P("shard", None),
        P("shard", None),
        P("shard", None),
        P("shard", None),
        P("shard", None),
        P("shard"),
        P("expert", "shard", None),
        P("expert", "shard", None),
        P("expert", "shard", None),
        P(both, None, None),
    )
    out_specs = (
        P(both, None, None),
        P(both, None, None),
        P(both),
        P(both, None),
        P(both, None),
        P(both, None),
        P(both, None),
        P(both, None),
        P(both),
        P("expert", "shard", None),
        P("expert", "shard", None),
        P("expert", "shard", None),
    )
    return jax.shard_map(body, mesh=mesh, in_specs=in_specs, out_specs=out_specs, check_vma=False)
```

```python
import jax
import jax.numpy as jnp
from jax import lax
from jax.sharding import PartitionSpec as P

HEADS = 24
KV_HEADS = 8
HD = 64
TOP = 8
EXP_DEV = 5

EPS = 1e-05
THETA = 10000.0
NEGATIVE = -1e30
AG_PARTS = 2
RS_PARTS = 2
F32 = jnp.float32
BF16 = jnp.bfloat16


def rope_tables(slots, size):
    half_size = size // 2
    frequency = THETA ** (-jnp.arange(half_size, dtype=F32) * 2.0 / size)
    angles = jnp.arange(slots, dtype=F32)[:, None] * frequency[None, :]
    return (jnp.cos(angles), jnp.sin(angles))


def rotate(values, cosine, sine_table, direction):
    half_size = values.shape[-1] // 2
    first_half = values[..., :half_size]
    second_half = values[..., half_size:]
    cos_part = cosine[:, None, :]
    sin_part = direction * sine_table[:, None, :]
    return jnp.concatenate(
        [
            first_half * cos_part - second_half * sin_part,
            second_half * cos_part + first_half * sin_part,
        ],
        axis=-1,
    )


def dispatch_matrix(routes, priority, length, expert_ids, capacity):
    slots = routes.shape[0]
    positions = jnp.arange(slots, dtype=jnp.int32)
    live = positions < length
    named = jnp.any(routes[:, :, None] == expert_ids[None, None, :], axis=1) & live[:, None]
    earlier = (priority[None, :] < priority[:, None]).astype(BF16)
    slot = jnp.dot(earlier, named.astype(BF16), preferred_element_type=F32).astype(jnp.int32)
    slot = jnp.where(named, slot, capacity)
    return (
        slot.T[:, None, :] == jnp.arange(capacity, dtype=jnp.int32)[None, :, None]
    ).astype(BF16)


def line_gather(block):
    count = lax.axis_size("expert")
    me = lax.axis_index("expert")
    up, down = [], []
    held_up = held_down = block
    for step in range(count - 1):
        held_up = lax.ppermute(
            held_up, "expert", [(i, i + 1) for i in range(step, count - 1)]
        )
        held_down = lax.ppermute(
            held_down, "expert", [(i + 1, i) for i in range(0, count - 1 - step)]
        )
        up.append(held_up)
        down.append(held_down)
    return [block] + [
        jnp.where(me > k, up[k], down[count - 2 - k]) for k in range(count - 1)
    ]


def line_scatter(parts):
    count = lax.axis_size("expert")
    total = parts[0].astype(F32)
    for step in range(count - 1):
        piece_up = parts[step + 1]
        piece_down = parts[count - 1 - step]
        if step:
            piece_up = piece_up.astype(F32) + held_up.astype(F32)
            piece_down = piece_down.astype(F32) + held_down.astype(F32)
        held_up = lax.ppermute(
            piece_up.astype(BF16), "expert", [(i, i + 1) for i in range(step + 1)]
        )
        held_down = lax.ppermute(
            piece_down.astype(BF16),
            "expert",
            [(i + 1, i) for i in range(count - 2 - step, count - 1)],
        )
    return total + held_up.astype(F32) + held_down.astype(F32)


def block_scores(queries_block, key_rows, positions, sequence_length, score_scale):
    scores = (
        jnp.einsum("qkgd,skd->kgqs", queries_block, key_rows, preferred_element_type=F32)
        * score_scale
    )
    allowed = (positions[None, :] <= positions[:, None]) & (positions[None, :] < sequence_length)
    return jnp.where(allowed, scores, NEGATIVE)


def body(
    tokens,
    lengths,
    routes,
    priority,
    first_gain,
    query_weight,
    key_weight,
    value_weight,
    merge_weight,
    router_weight,
    second_gain,
    gate_weight,
    up_weight,
    down_weight,
    cotangent,
):
    slots = tokens.shape[1]
    width = tokens.shape[2]
    groups = lax.axis_size("expert")
    expert_count = router_weight.shape[1]
    capacity = 5 * slots * TOP // (8 * expert_count)
    share = HEADS // KV_HEADS
    score_scale = HD ** (-0.5)
    q_cols, k_cols = HEADS * HD, KV_HEADS * HD
    side_cols = 128

    def gather_shard(value, axis=0):
        return lax.all_gather(value, "shard", axis=axis, tiled=True)

    def scatter_all(part):
        pieces = lax.axis_size("shard")
        columns = part.shape[-1]
        part = part.astype(BF16).reshape(groups, pieces, -1, columns).transpose(1, 0, 2, 3)
        part = lax.psum_scatter(
            part.reshape(-1, columns), "shard", scatter_dimension=0, tiled=True
        ).reshape(groups, -1, columns)
        me = lax.axis_index("expert")
        order = [
            lax.dynamic_index_in_dim(part, lax.rem(me - p + groups, groups), 0, keepdims=False)
            for p in range(groups)
        ]
        return line_scatter(order)

    side = jnp.concatenate(
        [router_weight, first_gain[:, None], second_gain[:, None]], axis=1
    )
    side = jnp.pad(side, ((0, 0), (0, side_cols - expert_count - 2)))
    first_set = gather_shard(
        jnp.concatenate([query_weight, key_weight, value_weight, side], axis=1)
    )
    qkv_full = first_set[:, : q_cols + 2 * k_cols]
    side_full = first_set[:, q_cols + 2 * k_cols :]
    router_full = side_full[:, :expert_count]
    gain_first = side_full[:, expert_count].astype(F32)
    gain_second = side_full[:, expert_count + 1].astype(F32)
    merge_full = gather_shard(merge_weight)
    tables = jnp.concatenate(
        [routes[0], priority[0][:, None], jnp.broadcast_to(lengths[:, None], (slots, 1))], axis=1
    )
    tables = jnp.stack(line_gather(tables))
    upstream_all = jnp.stack(line_gather(cotangent[0]))
    gate_full = gather_shard(gate_weight, 1)
    up_full = gather_shard(up_weight, 1)
    down_full = gather_shard(down_weight, 1)

    group = lax.axis_index("expert")
    own_experts = group * EXP_DEV + jnp.arange(EXP_DEV, dtype=jnp.int32)
    spread = jax.vmap(
        lambda t: dispatch_matrix(t[:, :TOP], t[:, TOP], t[0, TOP + 1], own_experts, capacity)
    )(tables)

    inputs = tokens[0].astype(F32)
    length = lengths[0]
    positions = jnp.arange(slots, dtype=jnp.int32)
    live_rows = (positions < length).astype(F32)[:, None]
    cosine, sine_table = rope_tables(slots, HD)
    rms_one = lax.rsqrt(jnp.mean(inputs * inputs, axis=-1, keepdims=True) + EPS)
    unit_one = inputs * rms_one
    normed_one = (unit_one * gain_first).astype(BF16)
    qkv = jnp.dot(normed_one, qkv_full, preferred_element_type=F32)
    queries = qkv[:, :q_cols].reshape(slots, HEADS, HD)
    key_rows = qkv[:, q_cols : q_cols + k_cols].reshape(slots, KV_HEADS, HD)
    values = qkv[:, q_cols + k_cols :].astype(BF16).reshape(slots, KV_HEADS, HD)
    queries = rotate(queries, cosine, sine_table, 1.0).astype(BF16)
    queries = queries.reshape(slots, KV_HEADS, share, HD)
    key_rows = rotate(key_rows, cosine, sine_table, 1.0).astype(BF16)
    scores = block_scores(queries, key_rows, positions, length, score_scale)
    row_peak = jnp.max(scores, axis=-1, keepdims=True)
    exp_scores = jnp.exp(scores - row_peak)
    total = jnp.sum(exp_scores, axis=-1, keepdims=True)
    mixed = jnp.einsum(
        "kgqs,skd->qkgd", (exp_scores / total).astype(BF16), values, preferred_element_type=F32
    ).astype(BF16)
    lse = row_peak + jnp.log(total)
    mixed = mixed.reshape(slots, q_cols)
    attended = jnp.dot(mixed, merge_full, preferred_element_type=F32)
    hidden = inputs + live_rows * attended
    rms_two = lax.rsqrt(jnp.mean(hidden * hidden, axis=-1, keepdims=True) + EPS)
    unit_two = hidden * rms_two
    normed_two = (unit_two * gain_second).astype(BF16)

    logits = jnp.dot(normed_two, router_full, preferred_element_type=F32)
    chosen = (
        routes[0][:, :, None] == jnp.arange(expert_count, dtype=jnp.int32)[None, None, :]
    ).astype(F32)
    chosen_any = jnp.sum(chosen, axis=1)
    masked = jnp.where(chosen_any > 0, logits, NEGATIVE)
    peak = jnp.max(masked, axis=-1, keepdims=True)
    exp_logits = jnp.exp(masked - peak) * chosen_any
    gate_dense = exp_logits / jnp.sum(exp_logits, axis=-1, keepdims=True)

    gates_side = jnp.pad(gate_dense, ((0, 0), (0, side_cols - expert_count)))
    gates_all = jnp.stack(line_gather(gates_side))
    gates_own = lax.dynamic_slice_in_dim(gates_all, group * EXP_DEV, EXP_DEV, axis=2)
    slot_gate = jnp.sum(spread.astype(F32) * gates_own.transpose(0, 2, 1)[:, :, None, :], axis=-1)
    gates = slot_gate.transpose(1, 0, 2).reshape(EXP_DEV, groups * capacity, 1)

    def dispatch(blocks):
        taken = jnp.einsum("sxct,std->xscd", spread, blocks, preferred_element_type=F32)
        return taken.astype(BF16).reshape(EXP_DEV, groups * capacity, blocks.shape[-1])

    ups = dispatch(upstream_all)
    act_grad = jnp.einsum("xrd,xdf->xrf", ups, down_full, preferred_element_type=F32)
    step = width // AG_PARTS
    rows, gate_pre, lift_pre = [], 0.0, 0.0
    for part in range(AG_PARTS):
        cut = slice(part * step, (part + 1) * step)
        piece = dispatch(jnp.stack(line_gather(normed_two[:, cut])))
        rows.append(piece)
        gate_pre = gate_pre + jnp.einsum(
            "xrd,xdf->xrf", piece, gate_full[:, cut], preferred_element_type=F32
        )
        lift_pre = lift_pre + jnp.einsum(
            "xrd,xdf->xrf", piece, up_full[:, cut], preferred_element_type=F32
        )
    sigmoid_gate = jax.nn.sigmoid(gate_pre)
    silu_gate = gate_pre * sigmoid_gate
    activated = silu_gate * lift_pre
    slot_grad = jnp.sum(act_grad * activated, axis=-1)
    gated = (activated * gates).astype(BF16)
    act_grad = act_grad * gates
    down_part = jnp.einsum("xrd,xrf->xdf", ups, gated, preferred_element_type=F32).astype(BF16)
    act_grad, gated, down_part = lax.optimization_barrier((act_grad, gated, down_part))
    gate_pre_grad = (
        act_grad * lift_pre * (sigmoid_gate + silu_gate * (1.0 - sigmoid_gate))
    ).astype(BF16)
    lift_pre_grad = (act_grad * silu_gate).astype(BF16)

    def combine(slot_rows):
        slot_rows = slot_rows.astype(BF16).reshape(EXP_DEV, groups, capacity, -1)
        return [
            jnp.einsum("xct,xcd->td", spread[p], slot_rows[:, p], preferred_element_type=F32)
            for p in range(groups)
        ]

    slot_grad = slot_grad.reshape(EXP_DEV, groups, capacity).transpose(1, 0, 2)
    token_grad = jnp.sum(spread.astype(F32) * slot_grad[:, :, :, None], axis=2)
    token_grad = token_grad.transpose(0, 2, 1)
    spots = (own_experts[:, None] == jnp.arange(side_cols)[None, :]).astype(F32)
    token_grad = jnp.sum(token_grad[:, :, :, None] * spots[None, None], axis=2)
    slot_back = line_scatter([token_grad[p] for p in range(groups)])[:, :expert_count]
    step = width // RS_PARTS
    back_total, expert_total = [], []
    for part in range(RS_PARTS):
        cut = slice(part * step, (part + 1) * step)
        back_rows = jnp.einsum(
            "xrf,xdf->xrd", gate_pre_grad, gate_full[:, cut], preferred_element_type=F32
        ) + jnp.einsum(
            "xrf,xdf->xrd", lift_pre_grad, up_full[:, cut], preferred_element_type=F32
        )
        back_total.append(line_scatter(combine(back_rows)))
    rows = jnp.concatenate(rows, axis=-1)
    gate_part = jnp.einsum(
        "xrd,xrf->xdf", rows, gate_pre_grad, preferred_element_type=F32
    ).astype(BF16)
    lift_part = jnp.einsum(
        "xrd,xrf->xdf", rows, lift_pre_grad, preferred_element_type=F32
    ).astype(BF16)
    produced = combine(jnp.einsum("xrf,xdf->xrd", gated, down_full, preferred_element_type=F32))
    produced = [part.astype(BF16) for part in produced]
    back_total, gate_part, lift_part, produced = lax.optimization_barrier(
        (back_total, gate_part, lift_part, produced)
    )
    back_total = jnp.concatenate(back_total, axis=1)
    block_output = hidden + line_scatter(produced)

    def scatter_expert(part):
        return lax.psum_scatter(
            part, "shard", scatter_dimension=1, tiled=True
        ).astype(F32)

    down_grad = scatter_expert(down_part)
    gate_grad = scatter_expert(gate_part)
    up_grad = scatter_expert(lift_part)

    upstream = cotangent[0].astype(F32)
    picked_grad = gate_dense * (
        slot_back - jnp.sum(gate_dense * slot_back, axis=-1, keepdims=True)
    )
    logit_grad = picked_grad.astype(BF16)
    router_part = jnp.einsum("ld,le->de", normed_two, logit_grad, preferred_element_type=F32)
    normed_two_grad = jnp.einsum("le,de->ld", logit_grad, router_full, preferred_element_type=F32)
    normed_two_grad = normed_two_grad + back_total
    scaled_two = normed_two_grad * gain_second
    second_gain_part = jnp.sum(normed_two_grad * unit_two, axis=0)
    hidden_grad = upstream + rms_two * (
        scaled_two - unit_two * jnp.mean(scaled_two * unit_two, axis=-1, keepdims=True)
    )
    attended_grad = (live_rows * hidden_grad).astype(BF16)

    merge_part = jnp.einsum("lh,ld->hd", mixed, attended_grad, preferred_element_type=F32)
    merge_grad = scatter_all(merge_part)
    mixed_grad = (
        jnp.einsum("ld,hd->lh", attended_grad, merge_full, preferred_element_type=F32)
        .astype(BF16)
        .reshape(slots, KV_HEADS, share, HD)
    )
    scores = block_scores(queries, key_rows, positions, length, score_scale)
    probs = jnp.exp(scores - lse)
    prob_back = jnp.einsum("qkgd,skd->kgqs", mixed_grad, values, preferred_element_type=F32)
    score_grad = (
        probs * (prob_back - jnp.sum(probs * prob_back, axis=-1, keepdims=True))
    ).astype(BF16)
    queries_grad = (
        jnp.einsum("kgqs,skd->qkgd", score_grad, key_rows, preferred_element_type=F32)
        * score_scale
    ).reshape(slots, HEADS, HD)
    key_total = (
        jnp.einsum("kgqs,qkgd->skd", score_grad, queries, preferred_element_type=F32) * score_scale
    )
    value_total = jnp.einsum(
        "kgqs,qkgd->skd", probs.astype(BF16), mixed_grad, preferred_element_type=F32
    )
    qkv_grad = jnp.concatenate(
        [
            rotate(queries_grad, cosine, sine_table, -1.0).astype(BF16).reshape(slots, q_cols),
            rotate(key_total, cosine, sine_table, -1.0).astype(BF16).reshape(slots, k_cols),
            value_total.astype(BF16).reshape(slots, k_cols),
        ],
        axis=1,
    )
    qkv_part = jnp.einsum("ld,lh->dh", normed_one, qkv_grad, preferred_element_type=F32)
    normed_one_grad = jnp.einsum("lh,dh->ld", qkv_grad, qkv_full, preferred_element_type=F32)
    scaled_one = normed_one_grad * gain_first
    first_gain_part = jnp.sum(normed_one_grad * unit_one, axis=0)
    input_grad = hidden_grad + rms_one * (
        scaled_one - unit_one * jnp.mean(scaled_one * unit_one, axis=-1, keepdims=True)
    )
    side_part = jnp.concatenate(
        [router_part, first_gain_part[:, None], second_gain_part[:, None]], axis=1
    )
    side_part = jnp.pad(side_part, ((0, 0), (0, side_cols - expert_count - 2)))
    reduced = scatter_all(jnp.concatenate([qkv_part, side_part], axis=1))
    side_grad = reduced[:, q_cols + 2 * k_cols :]
    return (
        block_output[None],
        input_grad[None],
        side_grad[:, expert_count],
        reduced[:, :q_cols],
        reduced[:, q_cols : q_cols + k_cols],
        reduced[:, q_cols + k_cols : q_cols + 2 * k_cols],
        merge_grad,
        side_grad[:, :expert_count],
        side_grad[:, expert_count + 1],
        gate_grad,
        up_grad,
        down_grad,
    )


def solution(mesh):
    both = ("expert", "shard")
    in_specs = (
        P(both, None, None),
        P(both),
        P(both, None, None),
        P(both, None),
        P("shard"),
        P("shard", None),
        P("shard", None),
        P("shard", None),
        P("shard", None),
        P("shard", None),
        P("shard"),
        P("expert", "shard", None),
        P("expert", "shard", None),
        P("expert", "shard", None),
        P(both, None, None),
    )
    out_specs = (
        P(both, None, None),
        P(both, None, None),
        P(both),
        P(both, None),
        P(both, None),
        P(both, None),
        P(both, None),
        P(both, None),
        P(both),
        P("expert", "shard", None),
        P("expert", "shard", None),
        P("expert", "shard", None),
    )
    return jax.shard_map(body, mesh=mesh, in_specs=in_specs, out_specs=out_specs, check_vma=False)
```

```python
import jax
import jax.numpy as jnp
from jax import lax
from jax.experimental import pallas as pl
from jax.experimental.pallas import tpu as pltpu
from jax.sharding import PartitionSpec as P

HEADS = 24
KV_HEADS = 8
HD = 64
TOP = 8
EXP_DEV = 5
SHARE = HEADS // KV_HEADS
Q_BLOCK = 128
VMEM_BYTES = 60 * 2**20

EPS = 1e-05
THETA = 10000.0
NEGATIVE = -1e30
AG_PARTS = 2
RS_PARTS = 2
F32 = jnp.float32
BF16 = jnp.bfloat16


def rope_tables(slots):
    frequency = THETA ** (-jnp.arange(HD // 2, dtype=F32) * 2.0 / HD)
    angles = jnp.arange(slots, dtype=F32)[:, None] * frequency[None, :]
    cosine, sine = jnp.cos(angles), jnp.sin(angles)
    return (
        jnp.concatenate([cosine] * 4, axis=1),
        jnp.concatenate([-sine, sine, -sine, sine], axis=1),
    )


def dispatch_matrix(routes, priority, length, expert_ids, capacity):
    slots = routes.shape[0]
    positions = jnp.arange(slots, dtype=jnp.int32)
    live = positions < length
    named = jnp.any(routes[:, :, None] == expert_ids[None, None, :], axis=1) & live[:, None]
    earlier = (priority[None, :] < priority[:, None]).astype(BF16)
    slot = jnp.dot(earlier, named.astype(BF16), preferred_element_type=F32).astype(jnp.int32)
    slot = jnp.where(named, slot, capacity)
    return (
        slot.T[:, None, :] == jnp.arange(capacity, dtype=jnp.int32)[None, :, None]
    ).astype(BF16)


def shift_perm(count, shift):
    return [(i, (i + shift) % count) for i in range(count)]


def direct_gather(block):
    count = lax.axis_size("expert")
    return [block] + [
        lax.ppermute(block, "expert", shift_perm(count, k)) for k in range(1, count)
    ]


def direct_scatter(parts):
    count = lax.axis_size("expert")
    total = parts[0].astype(F32)
    for k in range(1, count):
        total = total + lax.ppermute(parts[k], "expert", shift_perm(count, -k)).astype(F32)
    return total


def line_gather(block):
    return line_order(block, *line_hops(block))


def line_hops(block, first=0, last=None, held=None):
    count = lax.axis_size("expert")
    last = count - 1 if last is None else last
    held_up, held_down = (block, block) if held is None else held
    up, down = [], []
    for step in range(first, last):
        held_up = lax.ppermute(
            held_up, "expert", [(i, i + 1) for i in range(step, count - 1)]
        )
        held_down = lax.ppermute(
            held_down, "expert", [(i + 1, i) for i in range(0, count - 1 - step)]
        )
        up.append(held_up)
        down.append(held_down)
    return up, down


def line_order(block, up, down):
    count = lax.axis_size("expert")
    me = lax.axis_index("expert")
    return [block] + [
        jnp.where(me > k, up[k], down[count - 2 - k]) for k in range(count - 1)
    ]


def line_scatter(parts):
    held_up, held_down = scatter_hops(parts)
    return parts[0].astype(F32) + held_up.astype(F32) + held_down.astype(F32)


def scatter_hops(parts, first=0, last=None, held=None):
    count = lax.axis_size("expert")
    last = count - 1 if last is None else last
    held_up, held_down = (None, None) if held is None else held
    for step in range(first, last):
        piece_up = parts[step + 1]
        piece_down = parts[count - 1 - step]
        if step:
            piece_up = piece_up.astype(F32) + held_up.astype(F32)
            piece_down = piece_down.astype(F32) + held_down.astype(F32)
        held_up = lax.ppermute(
            piece_up.astype(BF16), "expert", [(i, i + 1) for i in range(step + 1)]
        )
        held_down = lax.ppermute(
            piece_down.astype(BF16),
            "expert",
            [(i + 1, i) for i in range(count - 2 - step, count - 1)],
        )
    return held_up, held_down


def turn(values, cosine, sine):
    first = lax.broadcasted_iota(jnp.int32, (1, 2 * HD), 1) % HD < HD // 2
    out = []
    for start in range(0, values.shape[1], 2 * HD):
        part = values[:, start : start + 2 * HD]
        other = jnp.where(
            first, pltpu.roll(part, 2 * HD - HD // 2, 1), pltpu.roll(part, HD // 2, 1)
        )
        out.append(part * cosine + other * sine)
    return out[0] if len(out) == 1 else jnp.concatenate(out, axis=1)


def last_keys(block, length):
    lane = lax.broadcasted_iota(jnp.int32, (1, SHARE * Q_BLOCK), 1)
    return jnp.minimum(block * Q_BLOCK + lane % Q_BLOCK, length - 1)


def head_block(values, pair_head, block):
    rows = slice(block * Q_BLOCK, (block + 1) * Q_BLOCK)
    heads = range(pair_head * SHARE, (pair_head + 1) * SHARE)
    return jnp.concatenate([values[rows, h * HD : (h + 1) * HD] for h in heads], axis=0)


def rows_of_heads(parts):
    tall = [
        part[:, g * Q_BLOCK : (g + 1) * Q_BLOCK] for part in parts for g in range(SHARE)
    ]
    return jnp.concatenate(tall, axis=0).T


def dot_last(a, b):
    return lax.dot_general(a, b, (((1,), (1,)), ((), ())), preferred_element_type=F32)


def attend_kernel(length_ref, qkv_ref, cos_ref, sin_ref, mixed_ref, low_ref, lse_ref):
    length = length_ref[0]
    slots = qkv_ref.shape[0]
    q_cols = 2 * SHARE * HD
    k_end = q_cols + 2 * HD
    cosine, sine = cos_ref[...], sin_ref[...]
    queries = (turn(qkv_ref[:, :q_cols], cosine, sine) * HD**-0.5).astype(BF16)
    keys = turn(qkv_ref[:, q_cols:k_end], cosine, sine).astype(BF16)
    values = qkv_ref[:, k_end:]
    low_ref[:, :q_cols] = queries
    low_ref[:, q_cols:k_end] = keys
    low_ref[:, k_end:] = values.astype(BF16)
    values_t = values.T.astype(BF16)
    blocks = slots // Q_BLOCK
    for block in range(blocks):
        span = (block + 1) * Q_BLOCK
        limit = last_keys(block, length)
        key_id = lax.broadcasted_iota(jnp.int32, (span, 1), 0)
        parts = []
        for head in range(2):
            scores = dot_last(
                keys[:span, head * HD : (head + 1) * HD], head_block(queries, head, block)
            )
            scores = jnp.where(key_id <= limit, scores, NEGATIVE)
            peak = jnp.max(scores, axis=0, keepdims=True)
            exp_scores = jnp.exp(scores - peak)
            total = jnp.sum(exp_scores, axis=0, keepdims=True)
            lse_ref[0, pl.ds(head * blocks + block, 1), :] = peak + jnp.log(total)
            part = jnp.dot(
                values_t[head * HD : (head + 1) * HD, :span],
                exp_scores.astype(BF16),
                preferred_element_type=F32,
            )
            parts.append(part / total)
        mixed_ref[block * Q_BLOCK : span, :] = rows_of_heads(parts).astype(BF16)


def attend_back_kernel(
    length_ref, low_ref, grad_ref, lse_ref, cos_ref, sin_ref, out_ref, dk_ref, dv_ref
):
    length = length_ref[0]
    slots = low_ref.shape[0]
    q_cols = 2 * SHARE * HD
    k_end = q_cols + 2 * HD
    cosine, sine = cos_ref[...], -sin_ref[...]
    queries = low_ref[:, :q_cols]
    keys = low_ref[:, q_cols:k_end]
    values = low_ref[:, k_end:]
    grad = grad_ref[...]
    keys_t = keys.astype(F32).T.astype(BF16)
    dk_ref[...] = jnp.zeros_like(dk_ref)
    dv_ref[...] = jnp.zeros_like(dv_ref)
    blocks = slots // Q_BLOCK
    for block in range(blocks):
        rows = slice(block * Q_BLOCK, (block + 1) * Q_BLOCK)
        span = (block + 1) * Q_BLOCK
        limit = last_keys(block, length)
        key_id = lax.broadcasted_iota(jnp.int32, (span, 1), 0)
        parts = []
        for head in range(2):
            cols = slice(head * HD, (head + 1) * HD)
            query = head_block(queries, head, block)
            out_grad = head_block(grad, head, block)
            scores = dot_last(keys[:span, cols], query)
            scores = jnp.where(key_id <= limit, scores, NEGATIVE)
            probs = jnp.exp(scores - lse_ref[0, pl.ds(head * blocks + block, 1), :])
            prob_back = dot_last(values[:span, cols], out_grad)
            mean = jnp.sum(probs * prob_back, axis=0, keepdims=True)
            score_grad = (probs * (prob_back - mean)).astype(BF16)
            dv_ref[head, :span, :] += jnp.dot(
                probs.astype(BF16), out_grad, preferred_element_type=F32
            )
            dk_ref[head, :span, :] += jnp.dot(score_grad, query, preferred_element_type=F32)
            parts.append(
                jnp.dot(keys_t[cols, :span], score_grad, preferred_element_type=F32)
                * HD**-0.5
            )
        out_ref[rows, :q_cols] = turn(rows_of_heads(parts), cosine[rows], sine[rows]).astype(
            BF16
        )
    key_grad = jnp.concatenate([dk_ref[0], dk_ref[1]], axis=1)
    out_ref[:, q_cols:k_end] = turn(key_grad, cosine, sine).astype(BF16)
    out_ref[:, k_end:] = jnp.concatenate([dv_ref[0], dv_ref[1]], axis=1).astype(BF16)


def column_block(slots, columns):
    return pl.BlockSpec((slots, columns), lambda p: (0, p))


def attention_specs(slots):
    pairs = KV_HEADS // 2
    q_cols, cols = 2 * SHARE * HD, 2 * (SHARE + 2) * HD
    blocks = slots // Q_BLOCK
    whole = pl.BlockSpec((slots, 2 * HD), lambda p: (0, 0))
    lse = pl.BlockSpec((1, 2 * blocks, SHARE * Q_BLOCK), lambda p: (p, 0, 0))
    scalar = pl.BlockSpec(memory_space=pltpu.SMEM)
    return pairs, q_cols, cols, blocks, whole, lse, scalar


def attend(length, qkv, cosine, sine):
    slots = qkv.shape[0]
    pairs, q_cols, cols, blocks, whole, lse, scalar = attention_specs(slots)
    return pl.pallas_call(
        attend_kernel,
        grid=(pairs,),
        in_specs=[scalar, column_block(slots, cols), whole, whole],
        out_specs=[column_block(slots, q_cols), column_block(slots, cols), lse],
        out_shape=[
            jax.ShapeDtypeStruct((slots, pairs * q_cols), BF16),
            jax.ShapeDtypeStruct((slots, pairs * cols), BF16),
            jax.ShapeDtypeStruct((pairs, 2 * blocks, SHARE * Q_BLOCK), F32),
        ],
        cost_estimate=pl.CostEstimate(
            flops=24 * HEADS * slots * slots * HD // 4, bytes_accessed=10**7, transcendentals=0
        ),
    )(length, qkv, cosine, sine)


def attend_back(length, low, grad, lse_rows, cosine, sine):
    slots = low.shape[0]
    pairs, q_cols, cols, blocks, whole, lse, scalar = attention_specs(slots)
    return pl.pallas_call(
        attend_back_kernel,
        grid=(pairs,),
        in_specs=[scalar, column_block(slots, cols), column_block(slots, q_cols), lse, whole, whole],
        out_specs=column_block(slots, cols),
        out_shape=jax.ShapeDtypeStruct((slots, pairs * cols), BF16),
        scratch_shapes=[pltpu.VMEM((2, slots, HD), F32), pltpu.VMEM((2, slots, HD), F32)],
        cost_estimate=pl.CostEstimate(
            flops=60 * HEADS * slots * slots * HD // 4, bytes_accessed=10**7, transcendentals=0
        ),
    )(length, low, grad, lse_rows, cosine, sine)


def expert_kernel(
    gate_pre_ref, lift_ref, ups_ref, gates_ref, gate_ref, up_ref, down_ref,
    gated_ref, gate_grad_ref, lift_grad_ref, back_ref, slot_ref,
):
    act_grad = jnp.dot(ups_ref[0], down_ref[0], preferred_element_type=F32)
    gate_pre, lift_pre, gates = gate_pre_ref[0], lift_ref[0], gates_ref[0]
    sigmoid_gate = jax.nn.sigmoid(gate_pre)
    silu_gate = gate_pre * sigmoid_gate
    activated = silu_gate * lift_pre
    slot_ref[0] = jnp.sum(act_grad * activated, axis=-1, keepdims=True)
    gated_ref[0] = (activated * gates).astype(BF16)
    act_grad = act_grad * gates
    gate_pre_grad = (
        act_grad * lift_pre * (sigmoid_gate + silu_gate * (1.0 - sigmoid_gate))
    ).astype(BF16)
    lift_pre_grad = (act_grad * silu_gate).astype(BF16)
    gate_grad_ref[0] = gate_pre_grad
    lift_grad_ref[0] = lift_pre_grad
    back_ref[0] = (
        dot_last(gate_pre_grad, gate_ref[0]) + dot_last(lift_pre_grad, up_ref[0])
    ).astype(BF16)


def expert_block(*shape):
    return pl.BlockSpec((1,) + shape, lambda x: (x, 0, 0))


def expert_core(gate_pre, lift_pre, ups, gates, gate_full, up_full, down_full):
    experts, rows, width = ups.shape
    hidden = gate_pre.shape[-1]
    narrow, wide = expert_block(rows, hidden), expert_block(rows, width)
    weight, single = expert_block(width, hidden), expert_block(rows, 1)
    low = jax.ShapeDtypeStruct((experts, rows, hidden), BF16)
    return pl.pallas_call(
        expert_kernel,
        grid=(experts,),
        in_specs=[narrow, narrow, wide, single, weight, weight, weight],
        out_specs=[narrow, narrow, narrow, wide, single],
        out_shape=[
            low,
            low,
            low,
            jax.ShapeDtypeStruct((experts, rows, width), BF16),
            jax.ShapeDtypeStruct((experts, rows, 1), F32),
        ],
        compiler_params=pltpu.CompilerParams(vmem_limit_bytes=VMEM_BYTES),
        cost_estimate=pl.CostEstimate(
            flops=6 * experts * rows * width * hidden, bytes_accessed=60 * 10**6, transcendentals=0
        ),
    )(gate_pre, lift_pre, ups, gates, gate_full, up_full, down_full)


def weight_kernel(
    low_ref, high_ref, ups_ref, gated_ref, gate_grad_ref, lift_grad_ref, down_ref,
    out_ref, grads_ref,
):
    out_ref[0] = dot_last(gated_ref[0], down_ref[0]).astype(BF16)
    rows_t = jnp.concatenate([low_ref[0].T, high_ref[0].T], axis=0)
    grads_ref[0, 0] = jnp.dot(
        rows_t, gate_grad_ref[0], preferred_element_type=F32
    ).astype(BF16)
    grads_ref[1, 0] = jnp.dot(
        rows_t, lift_grad_ref[0], preferred_element_type=F32
    ).astype(BF16)
    grads_ref[2, 0] = jnp.dot(
        ups_ref[0].T, gated_ref[0], preferred_element_type=F32
    ).astype(BF16)


def expert_weights(low, high, ups, gated, gate_grad, lift_grad, down_full):
    experts, count, width = ups.shape
    hidden = gated.shape[-1]
    narrow, wide = expert_block(count, hidden), expert_block(count, width)
    weight, half = expert_block(width, hidden), expert_block(count, width // 2)
    return pl.pallas_call(
        weight_kernel,
        grid=(experts,),
        in_specs=[half, half, wide, narrow, narrow, narrow, weight],
        out_specs=[wide, pl.BlockSpec((3, 1, width, hidden), lambda x: (0, x, 0, 0))],
        out_shape=[
            jax.ShapeDtypeStruct((experts, count, width), BF16),
            jax.ShapeDtypeStruct((3, experts, width, hidden), BF16),
        ],
        compiler_params=pltpu.CompilerParams(vmem_limit_bytes=VMEM_BYTES),
        cost_estimate=pl.CostEstimate(
            flops=8 * experts * count * width * hidden, bytes_accessed=60 * 10**6, transcendentals=0
        ),
    )(low, high, ups, gated, gate_grad, lift_grad, down_full)


def body(
    tokens,
    lengths,
    routes,
    priority,
    first_gain,
    query_weight,
    key_weight,
    value_weight,
    merge_weight,
    router_weight,
    second_gain,
    gate_weight,
    up_weight,
    down_weight,
    cotangent,
):
    slots = tokens.shape[1]
    width = tokens.shape[2]
    groups = lax.axis_size("expert")
    expert_count = router_weight.shape[1]
    capacity = 5 * slots * TOP // (8 * expert_count)
    q_cols, k_cols = HEADS * HD, KV_HEADS * HD
    side_cols = 128

    def gather_shard(value, axis=0):
        return lax.all_gather(value, "shard", axis=axis, tiled=True)

    def scatter_all(part, ahead=None):
        part = part.astype(BF16).reshape(groups, -1, part.shape[-1])
        part = lax.psum_scatter(part, "shard", scatter_dimension=1, tiled=True)
        part, ahead = lax.optimization_barrier((part, ahead))
        me = lax.axis_index("expert")
        order = [
            lax.dynamic_index_in_dim(part, lax.rem(me - p + groups, groups), 0, keepdims=False)
            for p in range(groups)
        ]
        return direct_scatter(order), ahead

    side = jnp.concatenate(
        [router_weight, first_gain[:, None], second_gain[:, None]], axis=1
    )
    side = jnp.pad(side, ((0, 0), (0, side_cols - expert_count - 2)))
    pairs = KV_HEADS // 2
    pair_cols = [0, q_cols // pairs, (q_cols + k_cols) // pairs, (q_cols + 2 * k_cols) // pairs]
    columns = []
    for pair in range(pairs):
        for weight in (query_weight, key_weight, value_weight):
            span = weight.shape[1] // pairs
            columns.append(weight[:, pair * span : (pair + 1) * span])
    first_set = gather_shard(jnp.concatenate(columns + [side], axis=1))
    merge_full = gather_shard(merge_weight)
    tables = jnp.concatenate(
        [routes[0].T, priority, jnp.broadcast_to(lengths[:, None], (1, slots))], axis=0
    )
    tables = jnp.stack(direct_gather(tables)).transpose(0, 2, 1)
    mid = groups // 2
    early_up, early_down = line_hops(cotangent[0], 0, mid)
    gate_full = gather_shard(gate_weight, 1)
    up_full = gather_shard(up_weight, 1)
    down_full = gather_shard(down_weight, 1)

    group = lax.axis_index("expert")
    own_experts = group * EXP_DEV + jnp.arange(EXP_DEV, dtype=jnp.int32)
    spread = jax.vmap(
        lambda t: dispatch_matrix(t[:, :TOP], t[:, TOP], t[0, TOP + 1], own_experts, capacity)
    )(tables)

    first_set, spread = lax.optimization_barrier((first_set, spread))
    qkv_full = first_set[:, : q_cols + 2 * k_cols]
    side_full = first_set[:, q_cols + 2 * k_cols :]
    router_full = side_full[:, :expert_count]
    gain_first = side_full[:, expert_count].astype(F32)
    gain_second = side_full[:, expert_count + 1].astype(F32)

    inputs = tokens[0].astype(F32)
    length = lengths[0]
    positions = jnp.arange(slots, dtype=jnp.int32)
    live_rows = (positions < length).astype(F32)[:, None]
    cosine, sine_table = rope_tables(slots)
    rms_one = lax.rsqrt(jnp.mean(inputs * inputs, axis=-1, keepdims=True) + EPS)
    unit_one = inputs * rms_one
    normed_one = (unit_one * gain_first).astype(BF16)
    qkv = jnp.dot(normed_one, qkv_full, preferred_element_type=F32)
    mixed, qkv_low, lse = attend(lengths, qkv, cosine, sine_table)
    mixed, early_up, early_down = lax.optimization_barrier((mixed, early_up, early_down))
    later_up, later_down = line_hops(
        cotangent[0], mid, held=(early_up[-1], early_down[-1])
    )
    upstream_all = jnp.stack(
        line_order(cotangent[0], early_up + later_up, early_down + later_down)
    )
    attended = jnp.dot(mixed, merge_full, preferred_element_type=F32)
    hidden = inputs + live_rows * attended
    rms_two = lax.rsqrt(jnp.mean(hidden * hidden, axis=-1, keepdims=True) + EPS)
    unit_two = hidden * rms_two
    normed_two = (unit_two * gain_second).astype(BF16)

    logits = jnp.dot(normed_two, router_full, preferred_element_type=F32)
    chosen = (
        routes[0][:, :, None] == jnp.arange(expert_count, dtype=jnp.int32)[None, None, :]
    ).astype(F32)
    chosen_any = jnp.sum(chosen, axis=1)
    masked = jnp.where(chosen_any > 0, logits, NEGATIVE)
    peak = jnp.max(masked, axis=-1, keepdims=True)
    exp_logits = jnp.exp(masked - peak) * chosen_any
    gate_dense = exp_logits / jnp.sum(exp_logits, axis=-1, keepdims=True)

    gates_all = jnp.stack(direct_gather(gate_dense.T))
    gates_own = lax.dynamic_slice_in_dim(gates_all, group * EXP_DEV, EXP_DEV, axis=1)
    slot_gate = jnp.sum(spread.astype(F32) * gates_own[:, :, None, :], axis=-1)
    gates = slot_gate.transpose(1, 0, 2).reshape(EXP_DEV, groups * capacity, 1)

    def dispatch(blocks):
        taken = jnp.einsum("sxct,std->xscd", spread, blocks, preferred_element_type=F32)
        return taken.astype(BF16).reshape(EXP_DEV, groups * capacity, blocks.shape[-1])

    ups = dispatch(upstream_all)
    step = width // AG_PARTS
    rows, gate_pre, lift_pre = [], 0.0, 0.0
    for part in range(AG_PARTS):
        cut = slice(part * step, (part + 1) * step)
        piece = dispatch(jnp.stack(line_gather(normed_two[:, cut])))
        rows.append(piece)
        gate_pre = gate_pre + jnp.einsum(
            "xrd,xdf->xrf", piece, gate_full[:, cut], preferred_element_type=F32
        )
        lift_pre = lift_pre + jnp.einsum(
            "xrd,xdf->xrf", piece, up_full[:, cut], preferred_element_type=F32
        )
    gated, gate_pre_grad, lift_pre_grad, back_rows, slot_grad = expert_core(
        gate_pre, lift_pre, ups, gates, gate_full, up_full, down_full
    )

    def combine(slot_rows):
        slot_rows = slot_rows.astype(BF16).reshape(EXP_DEV, groups, capacity, -1)
        return [
            jnp.einsum("xct,xcd->td", spread[p], slot_rows[:, p], preferred_element_type=F32)
            for p in range(groups)
        ]

    slot_grad = slot_grad.reshape(EXP_DEV, groups, capacity).transpose(1, 0, 2)
    token_grad = jnp.sum(spread.astype(F32) * slot_grad[:, :, :, None], axis=2)
    token_grad = lax.dynamic_update_slice_in_dim(
        jnp.zeros((groups, expert_count, slots), F32), token_grad, group * EXP_DEV, axis=1
    )
    slot_back = direct_scatter([token_grad[p] for p in range(groups)]).T
    step = width // RS_PARTS
    back_total = []
    for part in range(RS_PARTS):
        cut = slice(part * step, (part + 1) * step)
        back_total.append(line_scatter(combine(back_rows[:, :, cut])))
    produced, expert_grads = expert_weights(
        rows[0], rows[1], ups, gated, gate_pre_grad, lift_pre_grad, down_full
    )
    expert_grads = lax.psum_scatter(
        expert_grads.reshape(3 * EXP_DEV, width, -1), "shard", scatter_dimension=1, tiled=True
    )
    produced = combine(produced)
    produced = [part.astype(BF16) for part in produced]
    back_total, produced = lax.optimization_barrier((back_total, produced))
    back_total = jnp.concatenate(back_total, axis=1)
    sums = scatter_hops(produced, 0, 1)

    upstream = cotangent[0].astype(F32)
    picked_grad = gate_dense * (
        slot_back - jnp.sum(gate_dense * slot_back, axis=-1, keepdims=True)
    )
    logit_grad = picked_grad.astype(BF16)
    router_part = jnp.einsum("ld,le->de", normed_two, logit_grad, preferred_element_type=F32)
    normed_two_grad = jnp.einsum("le,de->ld", logit_grad, router_full, preferred_element_type=F32)
    normed_two_grad = normed_two_grad + back_total
    scaled_two = normed_two_grad * gain_second
    second_gain_part = jnp.sum(normed_two_grad * unit_two, axis=0)
    hidden_grad = upstream + rms_two * (
        scaled_two - unit_two * jnp.mean(scaled_two * unit_two, axis=-1, keepdims=True)
    )
    attended_grad = (live_rows * hidden_grad).astype(BF16)

    merge_part = jnp.einsum("lh,ld->hd", mixed, attended_grad, preferred_element_type=F32)
    merge_part, expert_grads = lax.optimization_barrier((merge_part, expert_grads))
    merge_grad, _ = scatter_all(merge_part)
    gate_grad, up_grad, down_grad = jnp.split(expert_grads.astype(F32), 3)
    mixed_grad = jnp.einsum(
        "ld,hd->lh", attended_grad, merge_full, preferred_element_type=F32
    ).astype(BF16)
    sums, mixed_grad = lax.optimization_barrier((sums, mixed_grad))
    sums = scatter_hops(produced, 1, mid, sums)
    qkv_grad = attend_back(lengths, qkv_low, mixed_grad, lse, cosine, sine_table)
    sums, qkv_grad = lax.optimization_barrier((sums, qkv_grad))
    sums = scatter_hops(produced, mid, groups - 1, sums)
    qkv_part = jnp.einsum("ld,lh->dh", normed_one, qkv_grad, preferred_element_type=F32)
    normed_one_grad = jnp.einsum("lh,dh->ld", qkv_grad, qkv_full, preferred_element_type=F32)
    scaled_one = normed_one_grad * gain_first
    first_gain_part = jnp.sum(normed_one_grad * unit_one, axis=0)
    input_grad = hidden_grad + rms_one * (
        scaled_one - unit_one * jnp.mean(scaled_one * unit_one, axis=-1, keepdims=True)
    )
    side_part = jnp.concatenate(
        [router_part, first_gain_part[:, None], second_gain_part[:, None]], axis=1
    )
    side_part = jnp.pad(side_part, ((0, 0), (0, side_cols - expert_count - 2)))
    block_output = (
        hidden + produced[0].astype(F32) + sums[0].astype(F32) + sums[1].astype(F32)
    )
    reduced, (merge_grad, block_output) = scatter_all(
        jnp.concatenate([qkv_part, side_part], axis=1), (merge_grad, block_output)
    )
    side_grad = reduced[:, q_cols + 2 * k_cols :]
    by_pair = reduced[:, : q_cols + 2 * k_cols].reshape(reduced.shape[0], pairs, -1)
    query_grad, key_grad, value_grad = [
        by_pair[:, :, start:stop].reshape(reduced.shape[0], -1)
        for start, stop in zip(pair_cols[:-1], pair_cols[1:])
    ]
    return (
        block_output[None],
        input_grad[None],
        side_grad[:, expert_count],
        query_grad,
        key_grad,
        value_grad,
        merge_grad,
        side_grad[:, :expert_count],
        side_grad[:, expert_count + 1],
        gate_grad,
        up_grad,
        down_grad,
    )


def solution(mesh):
    both = ("expert", "shard")
    in_specs = (
        P(both, None, None),
        P(both),
        P(both, None, None),
        P(both, None),
        P("shard"),
        P("shard", None),
        P("shard", None),
        P("shard", None),
        P("shard", None),
        P("shard", None),
        P("shard"),
        P("expert", "shard", None),
        P("expert", "shard", None),
        P("expert", "shard", None),
        P(both, None, None),
    )
    out_specs = (
        P(both, None, None),
        P(both, None, None),
        P(both),
        P(both, None),
        P(both, None),
        P(both, None),
        P(both, None),
        P(both, None),
        P(both),
        P("expert", "shard", None),
        P("expert", "shard", None),
        P("expert", "shard", None),
    )
    return jax.shard_map(body, mesh=mesh, in_specs=in_specs, out_specs=out_specs, check_vma=False)
```

```python
import functools

import jax
import jax.numpy as jnp
from jax import lax
from jax.experimental import pallas as pl
from jax.experimental.pallas import tpu as pltpu
from jax.sharding import PartitionSpec as P

HEADS = 24
KV_HEADS = 8
HD = 64
TOP = 8
EXP_DEV = 5
SHARE = HEADS // KV_HEADS
Q_BLOCK = 128
VMEM_BYTES = 60 * 2**20
CHUNKS = 4
COLS = 256

EPS = 1e-05
THETA = 10000.0
NEGATIVE = -1e30
RS_PARTS = 2
F32 = jnp.float32
BF16 = jnp.bfloat16


def rope_tables(slots):
    frequency = THETA ** (-jnp.arange(HD // 2, dtype=F32) * 2.0 / HD)
    angles = jnp.arange(slots, dtype=F32)[:, None] * frequency[None, :]
    cosine, sine = jnp.cos(angles), jnp.sin(angles)
    return (
        jnp.concatenate([cosine] * 4, axis=1),
        jnp.concatenate([-sine, sine, -sine, sine], axis=1),
    )


def dispatch_matrix(routes, priority, length, expert_ids, capacity):
    slots = routes.shape[0]
    positions = jnp.arange(slots, dtype=jnp.int32)
    live = positions < length
    named = jnp.any(routes[:, :, None] == expert_ids[None, None, :], axis=1) & live[:, None]
    earlier = (priority[None, :] < priority[:, None]).astype(BF16)
    slot = jnp.dot(earlier, named.astype(BF16), preferred_element_type=F32).astype(jnp.int32)
    slot = jnp.where(named, slot, capacity)
    return (
        slot.T[:, None, :] == jnp.arange(capacity, dtype=jnp.int32)[None, :, None]
    ).astype(BF16)


def shift_perm(count, shift):
    return [(i, (i + shift) % count) for i in range(count)]


def direct_gather(block):
    count = lax.axis_size("expert")
    return [block] + [
        lax.ppermute(block, "expert", shift_perm(count, k)) for k in range(1, count)
    ]


def direct_scatter(parts):
    count = lax.axis_size("expert")
    total = parts[0].astype(F32)
    for k in range(1, count):
        total = total + lax.ppermute(parts[k], "expert", shift_perm(count, -k)).astype(F32)
    return total


def line_gather(block):
    return line_order(block, *line_hops(block))


def line_hops(block, first=0, last=None, held=None):
    count = lax.axis_size("expert")
    last = count - 1 if last is None else last
    held_up, held_down = (block, block) if held is None else held
    up, down = [], []
    for step in range(first, last):
        held_up = lax.ppermute(
            held_up, "expert", [(i, i + 1) for i in range(step, count - 1)]
        )
        held_down = lax.ppermute(
            held_down, "expert", [(i + 1, i) for i in range(0, count - 1 - step)]
        )
        up.append(held_up)
        down.append(held_down)
    return up, down


def line_order(block, up, down):
    count = lax.axis_size("expert")
    me = lax.axis_index("expert")
    return [block] + [
        jnp.where(me > k, up[k], down[count - 2 - k]) for k in range(count - 1)
    ]


def line_scatter(parts):
    held_up, held_down = scatter_hops(parts)
    return parts[0].astype(F32) + held_up.astype(F32) + held_down.astype(F32)


def scatter_hops(parts, first=0, last=None, held=None):
    count = lax.axis_size("expert")
    last = count - 1 if last is None else last
    held_up, held_down = (None, None) if held is None else held
    for step in range(first, last):
        piece_up = parts[step + 1]
        piece_down = parts[count - 1 - step]
        if step:
            piece_up = piece_up.astype(F32) + held_up.astype(F32)
            piece_down = piece_down.astype(F32) + held_down.astype(F32)
        held_up = lax.ppermute(
            piece_up.astype(BF16), "expert", [(i, i + 1) for i in range(step + 1)]
        )
        held_down = lax.ppermute(
            piece_down.astype(BF16),
            "expert",
            [(i + 1, i) for i in range(count - 2 - step, count - 1)],
        )
    return held_up, held_down


def turn(values, cosine, sine):
    first = lax.broadcasted_iota(jnp.int32, (1, 2 * HD), 1) % HD < HD // 2
    out = []
    for start in range(0, values.shape[1], 2 * HD):
        part = values[:, start : start + 2 * HD]
        other = jnp.where(
            first, pltpu.roll(part, 2 * HD - HD // 2, 1), pltpu.roll(part, HD // 2, 1)
        )
        out.append(part * cosine + other * sine)
    return out[0] if len(out) == 1 else jnp.concatenate(out, axis=1)


def last_keys(block, length):
    lane = lax.broadcasted_iota(jnp.int32, (1, SHARE * Q_BLOCK), 1)
    return jnp.minimum(block * Q_BLOCK + lane % Q_BLOCK, length - 1)


def head_block(values, pair_head, block):
    rows = slice(block * Q_BLOCK, (block + 1) * Q_BLOCK)
    heads = range(pair_head * SHARE, (pair_head + 1) * SHARE)
    return jnp.concatenate([values[rows, h * HD : (h + 1) * HD] for h in heads], axis=0)


def rows_of_heads(parts):
    tall = [
        part[:, g * Q_BLOCK : (g + 1) * Q_BLOCK] for part in parts for g in range(SHARE)
    ]
    return jnp.concatenate(tall, axis=0).T


def dot_last(a, b):
    return lax.dot_general(a, b, (((1,), (1,)), ((), ())), preferred_element_type=F32)


def attend_kernel(length_ref, qkv_ref, cos_ref, sin_ref, mixed_ref, low_ref, lse_ref):
    length = length_ref[0]
    slots = qkv_ref.shape[0]
    q_cols = 2 * SHARE * HD
    k_end = q_cols + 2 * HD
    cosine, sine = cos_ref[...], sin_ref[...]
    queries = (turn(qkv_ref[:, :q_cols], cosine, sine) * HD**-0.5).astype(BF16)
    keys = turn(qkv_ref[:, q_cols:k_end], cosine, sine).astype(BF16)
    values = qkv_ref[:, k_end:]
    low_ref[:, :q_cols] = queries
    low_ref[:, q_cols:k_end] = keys
    low_ref[:, k_end:] = values.astype(BF16)
    values_t = values.T.astype(BF16)
    blocks = slots // Q_BLOCK
    for block in range(blocks):
        span = (block + 1) * Q_BLOCK
        limit = last_keys(block, length)
        key_id = lax.broadcasted_iota(jnp.int32, (span, 1), 0)
        parts = []
        for head in range(2):
            scores = dot_last(
                keys[:span, head * HD : (head + 1) * HD], head_block(queries, head, block)
            )
            scores = jnp.where(key_id <= limit, scores, NEGATIVE)
            peak = jnp.max(scores, axis=0, keepdims=True)
            exp_scores = jnp.exp(scores - peak)
            total = jnp.sum(exp_scores, axis=0, keepdims=True)
            lse_ref[0, pl.ds(head * blocks + block, 1), :] = peak + jnp.log(total)
            part = jnp.dot(
                values_t[head * HD : (head + 1) * HD, :span],
                exp_scores.astype(BF16),
                preferred_element_type=F32,
            )
            parts.append(part / total)
        mixed_ref[block * Q_BLOCK : span, :] = rows_of_heads(parts).astype(BF16)


def attend_back_kernel(
    length_ref, low_ref, grad_ref, lse_ref, cos_ref, sin_ref, out_ref, dk_ref, dv_ref
):
    length = length_ref[0]
    slots = low_ref.shape[0]
    q_cols = 2 * SHARE * HD
    k_end = q_cols + 2 * HD
    cosine, sine = cos_ref[...], -sin_ref[...]
    queries = low_ref[:, :q_cols]
    keys = low_ref[:, q_cols:k_end]
    values = low_ref[:, k_end:]
    grad = grad_ref[...]
    keys_t = keys.astype(F32).T.astype(BF16)
    dk_ref[...] = jnp.zeros_like(dk_ref)
    dv_ref[...] = jnp.zeros_like(dv_ref)
    blocks = slots // Q_BLOCK
    for block in range(blocks):
        rows = slice(block * Q_BLOCK, (block + 1) * Q_BLOCK)
        span = (block + 1) * Q_BLOCK
        limit = last_keys(block, length)
        key_id = lax.broadcasted_iota(jnp.int32, (span, 1), 0)
        parts = []
        for head in range(2):
            cols = slice(head * HD, (head + 1) * HD)
            query = head_block(queries, head, block)
            out_grad = head_block(grad, head, block)
            scores = dot_last(keys[:span, cols], query)
            scores = jnp.where(key_id <= limit, scores, NEGATIVE)
            probs = jnp.exp(scores - lse_ref[0, pl.ds(head * blocks + block, 1), :])
            prob_back = dot_last(values[:span, cols], out_grad)
            mean = jnp.sum(probs * prob_back, axis=0, keepdims=True)
            score_grad = (probs * (prob_back - mean)).astype(BF16)
            dv_ref[head, :span, :] += jnp.dot(
                probs.astype(BF16), out_grad, preferred_element_type=F32
            )
            dk_ref[head, :span, :] += jnp.dot(score_grad, query, preferred_element_type=F32)
            parts.append(
                jnp.dot(keys_t[cols, :span], score_grad, preferred_element_type=F32)
                * HD**-0.5
            )
        out_ref[rows, :q_cols] = turn(rows_of_heads(parts), cosine[rows], sine[rows]).astype(
            BF16
        )
    key_grad = jnp.concatenate([dk_ref[0], dk_ref[1]], axis=1)
    out_ref[:, q_cols:k_end] = turn(key_grad, cosine, sine).astype(BF16)
    out_ref[:, k_end:] = jnp.concatenate([dv_ref[0], dv_ref[1]], axis=1).astype(BF16)


def column_block(slots, columns):
    return pl.BlockSpec((slots, columns), lambda p: (0, p))


def attention_specs(slots):
    pairs = KV_HEADS // 2
    q_cols, cols = 2 * SHARE * HD, 2 * (SHARE + 2) * HD
    blocks = slots // Q_BLOCK
    whole = pl.BlockSpec((slots, 2 * HD), lambda p: (0, 0))
    lse = pl.BlockSpec((1, 2 * blocks, SHARE * Q_BLOCK), lambda p: (p, 0, 0))
    scalar = pl.BlockSpec(memory_space=pltpu.SMEM)
    return pairs, q_cols, cols, blocks, whole, lse, scalar


def attend(length, qkv, cosine, sine):
    slots = qkv.shape[0]
    pairs, q_cols, cols, blocks, whole, lse, scalar = attention_specs(slots)
    return pl.pallas_call(
        attend_kernel,
        grid=(pairs,),
        in_specs=[scalar, column_block(slots, cols), whole, whole],
        out_specs=[column_block(slots, q_cols), column_block(slots, cols), lse],
        out_shape=[
            jax.ShapeDtypeStruct((slots, pairs * q_cols), BF16),
            jax.ShapeDtypeStruct((slots, pairs * cols), BF16),
            jax.ShapeDtypeStruct((pairs, 2 * blocks, SHARE * Q_BLOCK), F32),
        ],
        cost_estimate=pl.CostEstimate(
            flops=24 * HEADS * slots * slots * HD // 4, bytes_accessed=10**7, transcendentals=0
        ),
    )(length, qkv, cosine, sine)


def attend_back(length, low, grad, lse_rows, cosine, sine):
    slots = low.shape[0]
    pairs, q_cols, cols, blocks, whole, lse, scalar = attention_specs(slots)
    return pl.pallas_call(
        attend_back_kernel,
        grid=(pairs,),
        in_specs=[scalar, column_block(slots, cols), column_block(slots, q_cols), lse, whole, whole],
        out_specs=column_block(slots, cols),
        out_shape=jax.ShapeDtypeStruct((slots, pairs * cols), BF16),
        scratch_shapes=[pltpu.VMEM((2, slots, HD), F32), pltpu.VMEM((2, slots, HD), F32)],
        cost_estimate=pl.CostEstimate(
            flops=60 * HEADS * slots * slots * HD // 4, bytes_accessed=10**7, transcendentals=0
        ),
    )(length, low, grad, lse_rows, cosine, sine)


def expert_kernel(
    gate_pre_ref, lift_ref, ups_ref, gates_ref, gate_ref, up_ref, down_ref,
    gated_ref, gate_grad_ref, lift_grad_ref, back_ref, slot_ref,
):
    act_grad = jnp.dot(ups_ref[0], down_ref[0], preferred_element_type=F32)
    gate_pre, lift_pre, gates = gate_pre_ref[0], lift_ref[0], gates_ref[0]
    sigmoid_gate = jax.nn.sigmoid(gate_pre)
    silu_gate = gate_pre * sigmoid_gate
    activated = silu_gate * lift_pre
    slot_ref[0] = jnp.sum(act_grad * activated, axis=-1, keepdims=True)
    gated_ref[0] = (activated * gates).astype(BF16)
    act_grad = act_grad * gates
    gate_pre_grad = (
        act_grad * lift_pre * (sigmoid_gate + silu_gate * (1.0 - sigmoid_gate))
    ).astype(BF16)
    lift_pre_grad = (act_grad * silu_gate).astype(BF16)
    gate_grad_ref[0] = gate_pre_grad
    lift_grad_ref[0] = lift_pre_grad
    back_ref[0] = (
        dot_last(gate_pre_grad, gate_ref[0]) + dot_last(lift_pre_grad, up_ref[0])
    ).astype(BF16)


def expert_block(*shape):
    return pl.BlockSpec((1,) + shape, lambda x: (x, 0, 0))


def expert_core(gate_pre, lift_pre, ups, gates, gate_full, up_full, down_full):
    experts, rows, width = ups.shape
    hidden = gate_pre.shape[-1]
    narrow, wide = expert_block(rows, hidden), expert_block(rows, width)
    weight, single = expert_block(width, hidden), expert_block(rows, 1)
    low = jax.ShapeDtypeStruct((experts, rows, hidden), BF16)
    return pl.pallas_call(
        expert_kernel,
        grid=(experts,),
        in_specs=[narrow, narrow, wide, single, weight, weight, weight],
        out_specs=[narrow, narrow, narrow, wide, single],
        out_shape=[
            low,
            low,
            low,
            jax.ShapeDtypeStruct((experts, rows, width), BF16),
            jax.ShapeDtypeStruct((experts, rows, 1), F32),
        ],
        compiler_params=pltpu.CompilerParams(vmem_limit_bytes=VMEM_BYTES),
        cost_estimate=pl.CostEstimate(
            flops=6 * experts * rows * width * hidden, bytes_accessed=60 * 10**6, transcendentals=0
        ),
    )(gate_pre, lift_pre, ups, gates, gate_full, up_full, down_full)


def weight_kernel(
    rows_ref, ups_ref, gated_ref, gate_grad_ref, lift_grad_ref, down_ref, out_ref, grads_ref
):
    out_ref[0] = dot_last(gated_ref[0], down_ref[0]).astype(BF16)
    rows_t = rows_ref[0].T
    grads_ref[0, 0] = jnp.dot(
        rows_t, gate_grad_ref[0], preferred_element_type=F32
    ).astype(BF16)
    grads_ref[1, 0] = jnp.dot(
        rows_t, lift_grad_ref[0], preferred_element_type=F32
    ).astype(BF16)
    grads_ref[2, 0] = jnp.dot(
        ups_ref[0].T, gated_ref[0], preferred_element_type=F32
    ).astype(BF16)


def expert_weights(rows, ups, gated, gate_grad, lift_grad, down_full):
    experts, count, width = ups.shape
    hidden = gated.shape[-1]
    narrow, wide = expert_block(count, hidden), expert_block(count, width)
    weight = expert_block(width, hidden)
    return pl.pallas_call(
        weight_kernel,
        grid=(experts,),
        in_specs=[wide, wide, narrow, narrow, narrow, weight],
        out_specs=[wide, pl.BlockSpec((3, 1, width, hidden), lambda x: (0, x, 0, 0))],
        out_shape=[
            jax.ShapeDtypeStruct((experts, count, width), BF16),
            jax.ShapeDtypeStruct((3, experts, width, hidden), BF16),
        ],
        compiler_params=pltpu.CompilerParams(vmem_limit_bytes=VMEM_BYTES),
        cost_estimate=pl.CostEstimate(
            flops=8 * experts * count * width * hidden, bytes_accessed=60 * 10**6, transcendentals=0
        ),
    )(rows, ups, gated, gate_grad, lift_grad, down_full)


def line_copy(source, target, sems, step, up, chunk):
    send_sems, recv_sems = sems
    side = 0 if up else 1
    me = lax.axis_index("expert")
    return pltpu.make_async_remote_copy(
        src_ref=source,
        dst_ref=target,
        send_sem=send_sems.at[side, step, chunk],
        recv_sem=recv_sems.at[side, step, chunk],
        device_id={"expert": me + 1 if up else me - 1},
        device_id_type=pl.DeviceIdType.MESH,
    )


def greet_line(count):
    me = lax.axis_index("expert")
    barrier = pltpu.get_barrier_semaphore()
    for up in (True, False):
        there = me < count - 1 if up else me > 0

        @pl.when(there)
        def _():
            pl.semaphore_signal(
                barrier,
                inc=1,
                device_id={"expert": me + 1 if up else me - 1},
                device_id_type=pl.DeviceIdType.MESH,
            )

    ends = (me == 0) | (me == count - 1)

    @pl.when(ends)
    def _():
        pl.semaphore_wait(barrier, 1)

    @pl.when(jnp.logical_not(ends))
    def _():
        pl.semaphore_wait(barrier, 2)


def gather_line(count, own, held, chunks, sems, work):
    me = lax.axis_index("expert")

    def after(step, up):
        return me + step < count if up else me - step >= 0

    def place(step, up):
        return step if up else count - step

    for chunk in range(chunks):
        for up in (True, False):

            @pl.when(after(1, up))
            def _():
                line_copy(own(chunk), held(place(1, up), chunk), sems, 0, up, chunk).start()

    work(0)
    for step in range(1, count):
        for chunk in range(chunks):
            for up in (True, False):
                here = held(place(step, up), chunk)

                @pl.when(after(step, not up))
                def _():
                    line_copy(here, here, sems, step - 1, up, chunk).wait_recv()

                if step < count - 1:

                    @pl.when(after(step, not up) & after(1, up))
                    def _():
                        there = held(place(step + 1, up), chunk)
                        line_copy(here, there, sems, step, up, chunk).start()

        for up in (True, False):

            @pl.when(after(step, not up))
            def _():
                work(place(step, up))

    for step in range(count - 1):
        for chunk in range(chunks):
            for up in (True, False):

                @pl.when(after(step, not up) & after(1, up))
                def _():
                    source = held(place(step, up), chunk) if step else own(chunk)
                    line_copy(
                        source, held(place(step + 1, up), chunk), sems, step, up, chunk
                    ).wait_send()


def early_kernel(count, columns, block_ref, held_ref, send_sems, recv_sems):
    greet_line(count)
    tall = block_ref.shape[0] // CHUNKS

    def rows(chunk):
        return pl.ds(chunk * tall, tall)

    gather_line(
        count,
        lambda c: block_ref.at[rows(c), pl.ds(0, columns)],
        lambda p, c: held_ref.at[p - 1, rows(c), :],
        CHUNKS,
        (send_sems, recv_sems),
        lambda p: None,
    )


def early_gather(block, columns):
    count = lax.axis_size("expert")
    slots = block.shape[0]
    sems = pltpu.SemaphoreType.DMA((2, count - 1, CHUNKS))
    sent = 2 * (count - 1) * slots * columns
    return pl.pallas_call(
        functools.partial(early_kernel, count, columns),
        in_specs=[pl.BlockSpec(memory_space=pltpu.VMEM)],
        out_specs=pl.BlockSpec(memory_space=pl.ANY),
        out_shape=jax.ShapeDtypeStruct((count - 1, slots, columns), BF16),
        scratch_shapes=[sems, sems],
        compiler_params=pltpu.CompilerParams(
            collective_id=0, has_side_effects=True, vmem_limit_bytes=VMEM_BYTES
        ),
        cost_estimate=pl.CostEstimate(flops=0, bytes_accessed=40 * sent, transcendentals=0),
    )(block)


def dispatch_kernel(
    count, normed_ref, block_ref, early_ref, spread_ref, rows_ref, ups_ref,
    held_ref, late_ref, send_sems, recv_sems,
):
    greet_line(count)
    slots = normed_ref.shape[0]
    columns = early_ref.shape[-1]
    tall = slots // CHUNKS
    capacity = rows_ref.shape[1] // count

    def cut(chunk):
        return pl.ds(chunk % CHUNKS * tall, tall)

    def own(chunk):
        if chunk < CHUNKS:
            return normed_ref.at[cut(chunk), :]
        return block_ref.at[cut(chunk), pl.ds(columns, block_ref.shape[1] - columns)]

    def held(place, chunk):
        ref = held_ref if chunk < CHUNKS else late_ref
        return ref.at[place - 1, cut(chunk), :]

    def work(place):
        if place == 0:
            sources = [normed_ref[...], block_ref[...]]
        else:
            sources = [held_ref[place - 1], early_ref[place - 1], late_ref[place - 1]]
        at = slice(place * capacity, (place + 1) * capacity)
        for expert in range(EXP_DEV):
            pick = spread_ref[place, expert]
            taken = [jnp.dot(pick, s, preferred_element_type=F32).astype(BF16) for s in sources]
            rows_ref[expert, at, :] = taken[0]
            if place == 0:
                ups_ref[expert, at, :] = taken[1]
            else:
                ups_ref[expert, at, :columns] = taken[1]
                ups_ref[expert, at, columns:] = taken[2]

    gather_line(count, own, held, 2 * CHUNKS, (send_sems, recv_sems), work)


def gather_dispatch(normed, block, early, spread):
    count = lax.axis_size("expert")
    slots, width = normed.shape
    columns = early.shape[-1]
    capacity = spread.shape[2]
    rows = jax.ShapeDtypeStruct((EXP_DEV, count * capacity, width), BF16)
    vmem = pl.BlockSpec(memory_space=pltpu.VMEM)
    sems = pltpu.SemaphoreType.DMA((2, count - 1, 2 * CHUNKS))
    sent = 2 * (count - 1) * slots * (2 * width - columns)
    return pl.pallas_call(
        functools.partial(dispatch_kernel, count),
        in_specs=[vmem] * 4,
        out_specs=[vmem] * 2,
        out_shape=[rows, rows],
        scratch_shapes=[
            pltpu.VMEM((count - 1, slots, width), BF16),
            pltpu.VMEM((count - 1, slots, width - columns), BF16),
            sems,
            sems,
        ],
        compiler_params=pltpu.CompilerParams(
            collective_id=1, has_side_effects=True, vmem_limit_bytes=VMEM_BYTES
        ),
        cost_estimate=pl.CostEstimate(flops=0, bytes_accessed=40 * sent, transcendentals=0),
    )(normed, block, early, spread)


def projection_kernel(mixed_ref, normed_ref, merge_ref, qkv_ref, side_ref, out_ref, turned_ref):
    step = pl.program_id(0)
    merge_steps = mixed_ref.shape[1] // COLS
    steps = pl.num_programs(0)

    @pl.when(step == 0)
    def _():
        turned_ref[...] = mixed_ref[...].T

    @pl.when(step == merge_steps)
    def _():
        turned_ref[...] = normed_ref[...].T

    @pl.when(step < merge_steps)
    def _():
        out_ref[0] = jnp.dot(
            turned_ref[...], merge_ref[...], preferred_element_type=F32
        ).astype(BF16)

    @pl.when((step >= merge_steps) & (step < steps - 1))
    def _():
        out_ref[0] = jnp.dot(
            turned_ref[...], qkv_ref[...], preferred_element_type=F32
        ).astype(BF16)

    @pl.when(step == steps - 1)
    def _():
        out_ref[0] = side_ref[...]


def projection_terms(mixed, normed, attended_grad, qkv_grad, side):
    slots, width = mixed.shape
    first, second = attended_grad.shape[1] // COLS, qkv_grad.shape[1] // COLS
    whole = pl.BlockSpec((slots, width), lambda j: (0, 0))
    return pl.pallas_call(
        projection_kernel,
        grid=(first + second + 1,),
        in_specs=[
            whole,
            whole,
            pl.BlockSpec((slots, COLS), lambda j: (0, jnp.minimum(j, first - 1))),
            pl.BlockSpec((slots, COLS), lambda j: (0, jnp.clip(j - first, 0, second - 1))),
            pl.BlockSpec((width, COLS), lambda j: (0, 0)),
        ],
        out_specs=pl.BlockSpec((1, width, COLS), lambda j: (j, 0, 0)),
        out_shape=jax.ShapeDtypeStruct((first + second + 1, width, COLS), BF16),
        scratch_shapes=[pltpu.VMEM((width, slots), BF16)],
        cost_estimate=pl.CostEstimate(
            flops=2 * slots * width * (first + second) * COLS,
            bytes_accessed=2 * 10**7,
            transcendentals=0,
        ),
    )(mixed, normed, attended_grad, qkv_grad, side)


def body(
    tokens,
    lengths,
    routes,
    priority,
    first_gain,
    query_weight,
    key_weight,
    value_weight,
    merge_weight,
    router_weight,
    second_gain,
    gate_weight,
    up_weight,
    down_weight,
    cotangent,
):
    slots = tokens.shape[1]
    width = tokens.shape[2]
    groups = lax.axis_size("expert")
    expert_count = router_weight.shape[1]
    capacity = 5 * slots * TOP // (8 * expert_count)
    q_cols, k_cols = HEADS * HD, KV_HEADS * HD
    side_cols = 128

    def gather_shard(value, axis=0):
        return lax.all_gather(value, "shard", axis=axis, tiled=True)

    def scatter_all(part, ahead=None):
        planes, _, columns = part.shape
        part = lax.psum_scatter(
            part.reshape(planes * groups, -1, columns), "shard", scatter_dimension=1, tiled=True
        ).reshape(planes, groups, -1, columns)
        part, ahead = lax.optimization_barrier((part, ahead))
        me = lax.axis_index("expert")
        order = [
            lax.dynamic_index_in_dim(part, lax.rem(me - p + groups, groups), 1, keepdims=False)
            for p in range(groups)
        ]
        return direct_scatter(order), ahead

    side = jnp.concatenate(
        [router_weight, first_gain[:, None], second_gain[:, None]], axis=1
    )
    side = jnp.pad(side, ((0, 0), (0, side_cols - expert_count - 2)))
    pairs = KV_HEADS // 2
    pair_cols = [0, q_cols // pairs, (q_cols + k_cols) // pairs, (q_cols + 2 * k_cols) // pairs]
    columns = []
    for pair in range(pairs):
        for weight in (query_weight, key_weight, value_weight):
            span = weight.shape[1] // pairs
            columns.append(weight[:, pair * span : (pair + 1) * span])
    first_set = gather_shard(jnp.concatenate(columns + [side], axis=1))
    merge_full = gather_shard(merge_weight)
    tables = jnp.concatenate(
        [routes[0].T, priority, jnp.broadcast_to(lengths[:, None], (1, slots))], axis=0
    )
    tables = jnp.stack(direct_gather(tables)).transpose(0, 2, 1)
    mid = groups // 2
    early_columns = 2 * width // 3
    early = early_gather(cotangent[0], early_columns)
    gate_full = gather_shard(gate_weight, 1)
    up_full = gather_shard(up_weight, 1)
    down_full = gather_shard(down_weight, 1)

    group = lax.axis_index("expert")
    own_experts = group * EXP_DEV + jnp.arange(EXP_DEV, dtype=jnp.int32)
    spread = jax.vmap(
        lambda t: dispatch_matrix(t[:, :TOP], t[:, TOP], t[0, TOP + 1], own_experts, capacity)
    )(tables)

    first_set, spread, early = lax.optimization_barrier((first_set, spread, early))
    qkv_full = first_set[:, : q_cols + 2 * k_cols]
    side_full = first_set[:, q_cols + 2 * k_cols :]
    router_full = side_full[:, :expert_count]
    gain_first = side_full[:, expert_count].astype(F32)
    gain_second = side_full[:, expert_count + 1].astype(F32)

    inputs = tokens[0].astype(F32)
    length = lengths[0]
    positions = jnp.arange(slots, dtype=jnp.int32)
    live_rows = (positions < length).astype(F32)[:, None]
    cosine, sine_table = rope_tables(slots)
    rms_one = lax.rsqrt(jnp.mean(inputs * inputs, axis=-1, keepdims=True) + EPS)
    unit_one = inputs * rms_one
    normed_one = (unit_one * gain_first).astype(BF16)
    qkv = jnp.dot(normed_one, qkv_full, preferred_element_type=F32)
    mixed, qkv_low, lse = attend(lengths, qkv, cosine, sine_table)
    attended = jnp.dot(mixed, merge_full, preferred_element_type=F32)
    hidden = inputs + live_rows * attended
    rms_two = lax.rsqrt(jnp.mean(hidden * hidden, axis=-1, keepdims=True) + EPS)
    unit_two = hidden * rms_two
    normed_two = (unit_two * gain_second).astype(BF16)

    logits = jnp.dot(normed_two, router_full, preferred_element_type=F32)
    chosen = (
        routes[0][:, :, None] == jnp.arange(expert_count, dtype=jnp.int32)[None, None, :]
    ).astype(F32)
    chosen_any = jnp.sum(chosen, axis=1)
    masked = jnp.where(chosen_any > 0, logits, NEGATIVE)
    peak = jnp.max(masked, axis=-1, keepdims=True)
    exp_logits = jnp.exp(masked - peak) * chosen_any
    gate_dense = exp_logits / jnp.sum(exp_logits, axis=-1, keepdims=True)

    gates_all = jnp.stack(direct_gather(gate_dense.T))
    gates_own = lax.dynamic_slice_in_dim(gates_all, group * EXP_DEV, EXP_DEV, axis=1)
    slot_gate = jnp.sum(spread.astype(F32) * gates_own[:, :, None, :], axis=-1)
    gates = slot_gate.transpose(1, 0, 2).reshape(EXP_DEV, groups * capacity, 1)

    rows, ups = gather_dispatch(normed_two, cotangent[0], early, spread)
    gate_pre = jnp.einsum("xrd,xdf->xrf", rows, gate_full, preferred_element_type=F32)
    lift_pre = jnp.einsum("xrd,xdf->xrf", rows, up_full, preferred_element_type=F32)
    gated, gate_pre_grad, lift_pre_grad, back_rows, slot_grad = expert_core(
        gate_pre, lift_pre, ups, gates, gate_full, up_full, down_full
    )

    def combine(slot_rows):
        slot_rows = slot_rows.astype(BF16).reshape(EXP_DEV, groups, capacity, -1)
        return [
            jnp.einsum("xct,xcd->td", spread[p], slot_rows[:, p], preferred_element_type=F32)
            for p in range(groups)
        ]

    slot_grad = slot_grad.reshape(EXP_DEV, groups, capacity).transpose(1, 0, 2)
    token_grad = jnp.sum(spread.astype(F32) * slot_grad[:, :, :, None], axis=2)
    token_grad = lax.dynamic_update_slice_in_dim(
        jnp.zeros((groups, expert_count, slots), F32), token_grad, group * EXP_DEV, axis=1
    )
    slot_back = direct_scatter([token_grad[p] for p in range(groups)]).T
    step = width // RS_PARTS
    back_parts = [
        combine(back_rows[:, :, part * step : (part + 1) * step]) for part in range(RS_PARTS)
    ]
    back_parts, gated = lax.optimization_barrier((back_parts, gated))
    back_held = [scatter_hops(parts, 0, 1) for parts in back_parts]
    produced, expert_grads = expert_weights(
        rows, ups, gated, gate_pre_grad, lift_pre_grad, down_full
    )
    expert_grads, back_held[0] = lax.optimization_barrier((expert_grads, back_held[0]))
    back_total = []
    for parts, held in zip(back_parts, back_held):
        held_up, held_down = scatter_hops(parts, 1, groups - 1, held)
        back_total.append(parts[0] + held_up.astype(F32) + held_down.astype(F32))
    expert_grads = lax.psum_scatter(
        expert_grads.reshape(3 * EXP_DEV, width, -1), "shard", scatter_dimension=1, tiled=True
    )
    produced = combine(produced)
    produced = [part.astype(BF16) for part in produced]
    back_total, produced = lax.optimization_barrier((back_total, produced))
    back_total = jnp.concatenate(back_total, axis=1)
    sums = scatter_hops(produced, 0, 1)

    upstream = cotangent[0].astype(F32)
    picked_grad = gate_dense * (
        slot_back - jnp.sum(gate_dense * slot_back, axis=-1, keepdims=True)
    )
    logit_grad = picked_grad.astype(BF16)
    router_part = jnp.einsum("ld,le->de", normed_two, logit_grad, preferred_element_type=F32)
    normed_two_grad = jnp.einsum("le,de->ld", logit_grad, router_full, preferred_element_type=F32)
    normed_two_grad = normed_two_grad + back_total
    scaled_two = normed_two_grad * gain_second
    second_gain_part = jnp.sum(normed_two_grad * unit_two, axis=0)
    hidden_grad = upstream + rms_two * (
        scaled_two - unit_two * jnp.mean(scaled_two * unit_two, axis=-1, keepdims=True)
    )
    attended_grad = (live_rows * hidden_grad).astype(BF16)

    mixed_grad = jnp.einsum(
        "ld,hd->lh", attended_grad, merge_full, preferred_element_type=F32
    ).astype(BF16)
    sums, mixed_grad = lax.optimization_barrier((sums, mixed_grad))
    sums = scatter_hops(produced, 1, mid, sums)
    qkv_grad = attend_back(lengths, qkv_low, mixed_grad, lse, cosine, sine_table)
    sums, qkv_grad = lax.optimization_barrier((sums, qkv_grad))
    sums = scatter_hops(produced, mid, groups - 1, sums)
    side_part = jnp.concatenate([router_part, second_gain_part[:, None]], axis=1)
    side_part = jnp.pad(side_part, ((0, 0), (0, COLS - expert_count - 1))).astype(BF16)
    terms = projection_terms(mixed, normed_one, attended_grad, qkv_grad, side_part)
    terms, expert_grads = lax.optimization_barrier((terms, expert_grads))
    normed_one_grad = jnp.einsum("lh,dh->ld", qkv_grad, qkv_full, preferred_element_type=F32)
    scaled_one = normed_one_grad * gain_first
    input_grad = hidden_grad + rms_one * (
        scaled_one - unit_one * jnp.mean(scaled_one * unit_one, axis=-1, keepdims=True)
    )
    block_output = (
        hidden + produced[0].astype(F32) + sums[0].astype(F32) + sums[1].astype(F32)
    )
    gate_grad, up_grad, down_grad = jnp.split(expert_grads.astype(F32), 3)
    reduced, (block_output, input_grad) = scatter_all(terms, (block_output, input_grad))
    own_rows = reduced.shape[1]
    reduced = reduced.transpose(1, 0, 2).reshape(own_rows, -1)
    place = (group * lax.axis_size("shard") + lax.axis_index("shard")) * own_rows
    merge_grad, qkv_reduced, side_grad = jnp.split(
        reduced, [width, width + q_cols + 2 * k_cols], axis=1
    )
    own_weights = lax.dynamic_slice_in_dim(qkv_full, place, own_rows, axis=0).astype(F32)
    own_gain = lax.dynamic_slice_in_dim(gain_first, place, own_rows)
    first_gain_grad = jnp.sum(own_weights * qkv_reduced, axis=1) / own_gain
    by_pair = qkv_reduced.reshape(own_rows, pairs, -1)
    query_grad, key_grad, value_grad = [
        by_pair[:, :, start:stop].reshape(own_rows, -1)
        for start, stop in zip(pair_cols[:-1], pair_cols[1:])
    ]
    return (
        block_output[None],
        input_grad[None],
        first_gain_grad,
        query_grad,
        key_grad,
        value_grad,
        merge_grad,
        side_grad[:, :expert_count],
        side_grad[:, expert_count],
        gate_grad,
        up_grad,
        down_grad,
    )


def solution(mesh):
    both = ("expert", "shard")
    in_specs = (
        P(both, None, None),
        P(both),
        P(both, None, None),
        P(both, None),
        P("shard"),
        P("shard", None),
        P("shard", None),
        P("shard", None),
        P("shard", None),
        P("shard", None),
        P("shard"),
        P("expert", "shard", None),
        P("expert", "shard", None),
        P("expert", "shard", None),
        P(both, None, None),
    )
    out_specs = (
        P(both, None, None),
        P(both, None, None),
        P(both),
        P(both, None),
        P(both, None),
        P(both, None),
        P(both, None),
        P(both, None),
        P(both),
        P("expert", "shard", None),
        P("expert", "shard", None),
        P("expert", "shard", None),
    )
    return jax.shard_map(body, mesh=mesh, in_specs=in_specs, out_specs=out_specs, check_vma=False)
```

```python
import functools

import jax
import jax.numpy as jnp
from jax import lax
from jax.experimental import pallas as pl
from jax.experimental.pallas import tpu as pltpu
from jax.sharding import PartitionSpec as P

HEADS = 24
KV_HEADS = 8
HD = 64
TOP = 8
EXP_DEV = 5
SHARE = HEADS // KV_HEADS
Q_BLOCK = 128
VMEM_BYTES = 60 * 2**20
CHUNKS = 4
COLS = 256

EPS = 1e-05
THETA = 10000.0
NEGATIVE = -1e30
RS_PARTS = 2
F32 = jnp.float32
BF16 = jnp.bfloat16


def rope_tables(slots):
    frequency = THETA ** (-jnp.arange(HD // 2, dtype=F32) * 2.0 / HD)
    angles = jnp.arange(slots, dtype=F32)[:, None] * frequency[None, :]
    cosine, sine = jnp.cos(angles), jnp.sin(angles)
    return (
        jnp.concatenate([cosine] * 4, axis=1),
        jnp.concatenate([-sine, sine, -sine, sine], axis=1),
    )


def dispatch_matrix(routes, priority, length, expert_ids, capacity):
    slots = routes.shape[0]
    positions = jnp.arange(slots, dtype=jnp.int32)
    live = positions < length
    named = jnp.any(routes[:, :, None] == expert_ids[None, None, :], axis=1) & live[:, None]
    earlier = (priority[None, :] < priority[:, None]).astype(BF16)
    slot = jnp.dot(earlier, named.astype(BF16), preferred_element_type=F32).astype(jnp.int32)
    slot = jnp.where(named, slot, capacity)
    return (
        slot.T[:, None, :] == jnp.arange(capacity, dtype=jnp.int32)[None, :, None]
    ).astype(BF16)


def shift_perm(count, shift):
    return [(i, (i + shift) % count) for i in range(count)]


def direct_gather(block):
    count = lax.axis_size("expert")
    return [block] + [
        lax.ppermute(block, "expert", shift_perm(count, k)) for k in range(1, count)
    ]


def direct_scatter(parts):
    count = lax.axis_size("expert")
    total = parts[0].astype(F32)
    for k in range(1, count):
        total = total + lax.ppermute(parts[k], "expert", shift_perm(count, -k)).astype(F32)
    return total


def line_gather(block):
    return line_order(block, *line_hops(block))


def line_hops(block, first=0, last=None, held=None):
    count = lax.axis_size("expert")
    last = count - 1 if last is None else last
    held_up, held_down = (block, block) if held is None else held
    up, down = [], []
    for step in range(first, last):
        held_up = lax.ppermute(
            held_up, "expert", [(i, i + 1) for i in range(step, count - 1)]
        )
        held_down = lax.ppermute(
            held_down, "expert", [(i + 1, i) for i in range(0, count - 1 - step)]
        )
        up.append(held_up)
        down.append(held_down)
    return up, down


def line_order(block, up, down):
    count = lax.axis_size("expert")
    me = lax.axis_index("expert")
    return [block] + [
        jnp.where(me > k, up[k], down[count - 2 - k]) for k in range(count - 1)
    ]


def line_scatter(parts):
    held_up, held_down = scatter_hops(parts)
    return parts[0].astype(F32) + held_up.astype(F32) + held_down.astype(F32)


def scatter_hops(parts, first=0, last=None, held=None):
    count = lax.axis_size("expert")
    last = count - 1 if last is None else last
    held_up, held_down = (None, None) if held is None else held
    for step in range(first, last):
        piece_up = parts[step + 1]
        piece_down = parts[count - 1 - step]
        if step:
            piece_up = piece_up.astype(F32) + held_up.astype(F32)
            piece_down = piece_down.astype(F32) + held_down.astype(F32)
        held_up = lax.ppermute(
            piece_up.astype(BF16), "expert", [(i, i + 1) for i in range(step + 1)]
        )
        held_down = lax.ppermute(
            piece_down.astype(BF16),
            "expert",
            [(i + 1, i) for i in range(count - 2 - step, count - 1)],
        )
    return held_up, held_down


def turn(values, cosine, sine):
    first = lax.broadcasted_iota(jnp.int32, (1, 2 * HD), 1) % HD < HD // 2
    out = []
    for start in range(0, values.shape[1], 2 * HD):
        part = values[:, start : start + 2 * HD]
        other = jnp.where(
            first, pltpu.roll(part, 2 * HD - HD // 2, 1), pltpu.roll(part, HD // 2, 1)
        )
        out.append(part * cosine + other * sine)
    return out[0] if len(out) == 1 else jnp.concatenate(out, axis=1)


def last_keys(block, length):
    lane = lax.broadcasted_iota(jnp.int32, (1, SHARE * Q_BLOCK), 1)
    return jnp.minimum(block * Q_BLOCK + lane % Q_BLOCK, length - 1)


def head_block(values, pair_head, block):
    rows = slice(block * Q_BLOCK, (block + 1) * Q_BLOCK)
    heads = range(pair_head * SHARE, (pair_head + 1) * SHARE)
    return jnp.concatenate([values[rows, h * HD : (h + 1) * HD] for h in heads], axis=0)


def rows_of_heads(parts):
    tall = [
        part[:, g * Q_BLOCK : (g + 1) * Q_BLOCK] for part in parts for g in range(SHARE)
    ]
    return jnp.concatenate(tall, axis=0).T


def dot_last(a, b):
    return lax.dot_general(a, b, (((1,), (1,)), ((), ())), preferred_element_type=F32)


def attend_kernel(
    length_ref, q_ref, k_ref, v_ref, cos_ref, sin_ref,
    mixed_ref, q_low_ref, k_low_ref, v_low_ref, lse_ref,
):
    length = length_ref[0]
    slots = q_ref.shape[0]
    cosine, sine = cos_ref[...], sin_ref[...]
    queries = (turn(q_ref[...], cosine, sine) * HD**-0.5).astype(BF16)
    keys = turn(k_ref[...], cosine, sine).astype(BF16)
    values = v_ref[...]
    q_low_ref[...] = queries
    k_low_ref[...] = keys
    v_low_ref[...] = values.astype(BF16)
    values_t = values.T.astype(BF16)
    blocks = slots // Q_BLOCK
    for block in range(blocks):
        span = (block + 1) * Q_BLOCK
        limit = last_keys(block, length)
        key_id = lax.broadcasted_iota(jnp.int32, (span, 1), 0)
        parts = []
        for head in range(2):
            scores = dot_last(
                keys[:span, head * HD : (head + 1) * HD], head_block(queries, head, block)
            )
            scores = jnp.where(key_id <= limit, scores, NEGATIVE)
            peak = jnp.max(scores, axis=0, keepdims=True)
            exp_scores = jnp.exp(scores - peak)
            total = jnp.sum(exp_scores, axis=0, keepdims=True)
            lse_ref[0, pl.ds(head * blocks + block, 1), :] = peak + jnp.log(total)
            part = jnp.dot(
                values_t[head * HD : (head + 1) * HD, :span],
                exp_scores.astype(BF16),
                preferred_element_type=F32,
            )
            parts.append(part / total)
        mixed_ref[block * Q_BLOCK : span, :] = rows_of_heads(parts).astype(BF16)


def attend_back_kernel(
    length_ref, q_ref, k_ref, v_ref, grad_ref, lse_ref, cos_ref, sin_ref, out_ref, dk_ref, dv_ref
):
    length = length_ref[0]
    slots, q_cols = q_ref.shape
    pairs = pl.num_programs(0)
    pair = pl.program_id(0)
    q_at = pl.ds(pl.multiple_of(pair * q_cols, 2 * HD), q_cols)
    k_at = pl.ds(pl.multiple_of(pairs * q_cols + pair * 2 * HD, 2 * HD), 2 * HD)
    v_at = pl.ds(pl.multiple_of(pairs * (q_cols + 2 * HD) + pair * 2 * HD, 2 * HD), 2 * HD)
    cosine, sine = cos_ref[...], -sin_ref[...]
    queries, keys, values = q_ref[...], k_ref[...], v_ref[...]
    grad = grad_ref[...]
    keys_t = keys.astype(F32).T.astype(BF16)
    dk_ref[...] = jnp.zeros_like(dk_ref)
    dv_ref[...] = jnp.zeros_like(dv_ref)
    blocks = slots // Q_BLOCK
    for block in range(blocks):
        rows = slice(block * Q_BLOCK, (block + 1) * Q_BLOCK)
        span = (block + 1) * Q_BLOCK
        limit = last_keys(block, length)
        key_id = lax.broadcasted_iota(jnp.int32, (span, 1), 0)
        parts = []
        for head in range(2):
            cols = slice(head * HD, (head + 1) * HD)
            query = head_block(queries, head, block)
            out_grad = head_block(grad, head, block)
            scores = dot_last(keys[:span, cols], query)
            scores = jnp.where(key_id <= limit, scores, NEGATIVE)
            probs = jnp.exp(scores - lse_ref[0, pl.ds(head * blocks + block, 1), :])
            prob_back = dot_last(values[:span, cols], out_grad)
            mean = jnp.sum(probs * prob_back, axis=0, keepdims=True)
            score_grad = (probs * (prob_back - mean)).astype(BF16)
            dv_ref[head, :span, :] += jnp.dot(
                probs.astype(BF16), out_grad, preferred_element_type=F32
            )
            dk_ref[head, :span, :] += jnp.dot(score_grad, query, preferred_element_type=F32)
            parts.append(
                jnp.dot(keys_t[cols, :span], score_grad, preferred_element_type=F32)
                * HD**-0.5
            )
        out_ref[rows, q_at] = turn(rows_of_heads(parts), cosine[rows], sine[rows]).astype(
            BF16
        )
    key_grad = jnp.concatenate([dk_ref[0], dk_ref[1]], axis=1)
    out_ref[:, k_at] = turn(key_grad, cosine, sine).astype(BF16)
    out_ref[:, v_at] = jnp.concatenate([dv_ref[0], dv_ref[1]], axis=1).astype(BF16)


def column_block(slots, columns, first=0):
    return pl.BlockSpec((slots, columns), lambda p: (0, first + p))


def attention_specs(slots):
    pairs = KV_HEADS // 2
    q_cols, cols = 2 * SHARE * HD, 2 * (SHARE + 2) * HD
    blocks = slots // Q_BLOCK
    whole = pl.BlockSpec((slots, 2 * HD), lambda p: (0, 0))
    lse = pl.BlockSpec((1, 2 * blocks, SHARE * Q_BLOCK), lambda p: (p, 0, 0))
    scalar = pl.BlockSpec(memory_space=pltpu.SMEM)
    return pairs, q_cols, cols, blocks, whole, lse, scalar


def attend(length, qkv, cosine, sine):
    slots = qkv.shape[0]
    pairs, q_cols, cols, blocks, whole, lse, scalar = attention_specs(slots)
    queries, keys = column_block(slots, q_cols), column_block(slots, 2 * HD)
    key_first = pairs * q_cols // (2 * HD)
    low_keys = jax.ShapeDtypeStruct((slots, pairs * 2 * HD), BF16)
    low_queries = jax.ShapeDtypeStruct((slots, pairs * q_cols), BF16)
    return pl.pallas_call(
        attend_kernel,
        grid=(pairs,),
        in_specs=[
            scalar,
            queries,
            column_block(slots, 2 * HD, key_first),
            column_block(slots, 2 * HD, key_first + pairs),
            whole,
            whole,
        ],
        out_specs=[queries, queries, keys, keys, lse],
        out_shape=[
            low_queries,
            low_queries,
            low_keys,
            low_keys,
            jax.ShapeDtypeStruct((pairs, 2 * blocks, SHARE * Q_BLOCK), F32),
        ],
        cost_estimate=pl.CostEstimate(
            flops=24 * HEADS * slots * slots * HD // 4, bytes_accessed=10**7, transcendentals=0
        ),
    )(length, qkv, qkv, qkv, cosine, sine)


def attend_back(length, queries, keys, values, grad, lse_rows, cosine, sine):
    slots = grad.shape[0]
    pairs, q_cols, cols, blocks, whole, lse, scalar = attention_specs(slots)
    wide, narrow = column_block(slots, q_cols), column_block(slots, 2 * HD)
    return pl.pallas_call(
        attend_back_kernel,
        grid=(pairs,),
        in_specs=[scalar, wide, narrow, narrow, wide, lse, whole, whole],
        out_specs=pl.BlockSpec((slots, pairs * cols), lambda p: (0, 0)),
        out_shape=jax.ShapeDtypeStruct((slots, pairs * cols), BF16),
        scratch_shapes=[pltpu.VMEM((2, slots, HD), F32), pltpu.VMEM((2, slots, HD), F32)],
        cost_estimate=pl.CostEstimate(
            flops=60 * HEADS * slots * slots * HD // 4, bytes_accessed=10**7, transcendentals=0
        ),
    )(length, queries, keys, values, grad, lse_rows, cosine, sine)


def expert_kernel(
    gate_pre_ref, lift_ref, ups_ref, gates_ref, gate_ref, up_ref, down_ref,
    gated_ref, gate_grad_ref, lift_grad_ref, back_ref, slot_ref,
):
    act_grad = jnp.dot(ups_ref[0], down_ref[0], preferred_element_type=F32)
    gate_pre, lift_pre, gates = gate_pre_ref[0], lift_ref[0], gates_ref[0]
    sigmoid_gate = jax.nn.sigmoid(gate_pre)
    silu_gate = gate_pre * sigmoid_gate
    activated = silu_gate * lift_pre
    slot_ref[0] = jnp.sum(act_grad * activated, axis=-1, keepdims=True)
    gated_ref[0] = (activated * gates).astype(BF16)
    act_grad = act_grad * gates
    gate_pre_grad = (
        act_grad * lift_pre * (sigmoid_gate + silu_gate * (1.0 - sigmoid_gate))
    ).astype(BF16)
    lift_pre_grad = (act_grad * silu_gate).astype(BF16)
    gate_grad_ref[0] = gate_pre_grad
    lift_grad_ref[0] = lift_pre_grad
    back_ref[0] = (
        dot_last(gate_pre_grad, gate_ref[0]) + dot_last(lift_pre_grad, up_ref[0])
    ).astype(BF16)


def expert_block(*shape, first=0):
    return pl.BlockSpec((1,) + shape, lambda x: (first + x, 0, 0))


def first_kernel(rows_ref, gate_ref, up_ref, gate_pre_ref, lift_ref):
    rows = rows_ref[0]
    gate_pre_ref[0] = jnp.dot(rows, gate_ref[0], preferred_element_type=F32)
    lift_ref[0] = jnp.dot(rows, up_ref[0], preferred_element_type=F32)


def expert_first(rows, both_full):
    experts, count, width = rows.shape
    hidden = both_full.shape[-1]
    narrow, weight = expert_block(count, hidden), expert_block(width, hidden)
    shape = jax.ShapeDtypeStruct((experts, count, hidden), F32)
    return pl.pallas_call(
        first_kernel,
        grid=(experts,),
        in_specs=[
            expert_block(count, width), weight, expert_block(width, hidden, first=experts)
        ],
        out_specs=[narrow, narrow],
        out_shape=[shape, shape],
        compiler_params=pltpu.CompilerParams(vmem_limit_bytes=VMEM_BYTES),
        cost_estimate=pl.CostEstimate(
            flops=4 * experts * count * width * hidden, bytes_accessed=35 * 10**6, transcendentals=0
        ),
    )(rows, both_full, both_full)


def pick_kernel(spread_ref, block_ref, out_ref):
    for expert in range(EXP_DEV):
        out_ref[expert] = jnp.dot(
            spread_ref[0, expert], block_ref[0], preferred_element_type=F32
        ).astype(BF16)


def pick_rows(spread, blocks):
    count, experts, capacity, slots = spread.shape
    width = blocks.shape[-1]
    return pl.pallas_call(
        pick_kernel,
        grid=(count,),
        in_specs=[
            pl.BlockSpec((1, experts, capacity, slots), lambda s: (s, 0, 0, 0)),
            pl.BlockSpec((1, slots, width), lambda s: (s, 0, 0)),
        ],
        out_specs=pl.BlockSpec((experts, capacity, width), lambda s: (0, s, 0)),
        out_shape=jax.ShapeDtypeStruct((experts, count * capacity, width), BF16),
        cost_estimate=pl.CostEstimate(
            flops=2 * count * experts * capacity * slots * width,
            bytes_accessed=17 * 10**6,
            transcendentals=0,
        ),
    )(spread, blocks)


def expert_core(gate_pre, lift_pre, ups, gates, both_full, down_full):
    experts, rows, width = ups.shape
    hidden = gate_pre.shape[-1]
    narrow, wide = expert_block(rows, hidden), expert_block(rows, width)
    weight, single = expert_block(width, hidden), expert_block(rows, 1)
    low = jax.ShapeDtypeStruct((experts, rows, hidden), BF16)
    return pl.pallas_call(
        expert_kernel,
        grid=(experts,),
        in_specs=[
            narrow, narrow, wide, single,
            weight, expert_block(width, hidden, first=experts), weight,
        ],
        out_specs=[narrow, narrow, narrow, wide, single],
        out_shape=[
            low,
            low,
            low,
            jax.ShapeDtypeStruct((experts, rows, width), BF16),
            jax.ShapeDtypeStruct((experts, rows, 1), F32),
        ],
        compiler_params=pltpu.CompilerParams(vmem_limit_bytes=VMEM_BYTES),
        cost_estimate=pl.CostEstimate(
            flops=6 * experts * rows * width * hidden, bytes_accessed=60 * 10**6, transcendentals=0
        ),
    )(gate_pre, lift_pre, ups, gates, both_full, both_full, down_full)


def weight_kernel(
    rows_ref, ups_ref, gated_ref, gate_grad_ref, lift_grad_ref, down_ref, out_ref, grads_ref
):
    out_ref[0] = dot_last(gated_ref[0], down_ref[0]).astype(BF16)
    rows_t = rows_ref[0].T
    grads_ref[0, 0] = jnp.dot(
        rows_t, gate_grad_ref[0], preferred_element_type=F32
    ).astype(BF16)
    grads_ref[1, 0] = jnp.dot(
        rows_t, lift_grad_ref[0], preferred_element_type=F32
    ).astype(BF16)
    grads_ref[2, 0] = jnp.dot(
        ups_ref[0].T, gated_ref[0], preferred_element_type=F32
    ).astype(BF16)


def expert_weights(rows, ups, gated, gate_grad, lift_grad, down_full):
    experts, count, width = ups.shape
    hidden = gated.shape[-1]
    narrow, wide = expert_block(count, hidden), expert_block(count, width)
    weight = expert_block(width, hidden)
    return pl.pallas_call(
        weight_kernel,
        grid=(experts,),
        in_specs=[wide, wide, narrow, narrow, narrow, weight],
        out_specs=[wide, pl.BlockSpec((3, 1, width, hidden), lambda x: (0, x, 0, 0))],
        out_shape=[
            jax.ShapeDtypeStruct((experts, count, width), BF16),
            jax.ShapeDtypeStruct((3, experts, width, hidden), BF16),
        ],
        compiler_params=pltpu.CompilerParams(vmem_limit_bytes=VMEM_BYTES),
        cost_estimate=pl.CostEstimate(
            flops=8 * experts * count * width * hidden, bytes_accessed=60 * 10**6, transcendentals=0
        ),
    )(rows, ups, gated, gate_grad, lift_grad, down_full)


def line_copy(source, target, sems, step, up, chunk):
    send_sems, recv_sems = sems
    side = 0 if up else 1
    me = lax.axis_index("expert")
    return pltpu.make_async_remote_copy(
        src_ref=source,
        dst_ref=target,
        send_sem=send_sems.at[side, step, chunk],
        recv_sem=recv_sems.at[side, step, chunk],
        device_id={"expert": me + 1 if up else me - 1},
        device_id_type=pl.DeviceIdType.MESH,
    )


def greet_line(count):
    me = lax.axis_index("expert")
    barrier = pltpu.get_barrier_semaphore()
    for up in (True, False):
        there = me < count - 1 if up else me > 0

        @pl.when(there)
        def _():
            pl.semaphore_signal(
                barrier,
                inc=1,
                device_id={"expert": me + 1 if up else me - 1},
                device_id_type=pl.DeviceIdType.MESH,
            )

    ends = (me == 0) | (me == count - 1)

    @pl.when(ends)
    def _():
        pl.semaphore_wait(barrier, 1)

    @pl.when(jnp.logical_not(ends))
    def _():
        pl.semaphore_wait(barrier, 2)


def gather_line(count, own, held, chunks, sems, work):
    me = lax.axis_index("expert")

    def after(step, up):
        return me + step < count if up else me - step >= 0

    def place(step, up):
        return step if up else count - step

    for chunk in range(chunks):
        for up in (True, False):

            @pl.when(after(1, up))
            def _():
                line_copy(own(chunk), held(place(1, up), chunk), sems, 0, up, chunk).start()

    work(0)
    for step in range(1, count):
        for chunk in range(chunks):
            for up in (True, False):
                here = held(place(step, up), chunk)

                @pl.when(after(step, not up))
                def _():
                    line_copy(here, here, sems, step - 1, up, chunk).wait_recv()

                if step < count - 1:

                    @pl.when(after(step, not up) & after(1, up))
                    def _():
                        there = held(place(step + 1, up), chunk)
                        line_copy(here, there, sems, step, up, chunk).start()

        for up in (True, False):

            @pl.when(after(step, not up))
            def _():
                work(place(step, up))

    for step in range(count - 1):
        for chunk in range(chunks):
            for up in (True, False):

                @pl.when(after(step, not up) & after(1, up))
                def _():
                    source = held(place(step, up), chunk) if step else own(chunk)
                    line_copy(
                        source, held(place(step + 1, up), chunk), sems, step, up, chunk
                    ).wait_send()


def dispatch_kernel(
    count, normed_ref, spread_ref, rows_ref, held_ref, send_sems, recv_sems
):
    greet_line(count)
    tall = normed_ref.shape[0] // CHUNKS
    capacity = rows_ref.shape[1] // count

    def cut(chunk):
        return pl.ds(chunk * tall, tall)

    def work(place):
        source = held_ref[place - 1] if place else normed_ref[...]
        for expert in range(EXP_DEV):
            rows_ref[expert, place * capacity : (place + 1) * capacity, :] = jnp.dot(
                spread_ref[place, expert], source, preferred_element_type=F32
            ).astype(BF16)

    gather_line(
        count,
        lambda c: normed_ref.at[cut(c), :],
        lambda p, c: held_ref.at[p - 1, cut(c), :],
        CHUNKS,
        (send_sems, recv_sems),
        work,
    )


def gather_dispatch(normed, spread):
    count = lax.axis_size("expert")
    slots, width = normed.shape
    capacity = spread.shape[2]
    vmem = pl.BlockSpec(memory_space=pltpu.VMEM)
    sems = pltpu.SemaphoreType.DMA((2, count - 1, CHUNKS))
    sent = 2 * (count - 1) * slots * width
    return pl.pallas_call(
        functools.partial(dispatch_kernel, count),
        in_specs=[vmem] * 2,
        out_specs=vmem,
        out_shape=jax.ShapeDtypeStruct((EXP_DEV, count * capacity, width), BF16),
        scratch_shapes=[pltpu.VMEM((count - 1, slots, width), BF16), sems, sems],
        compiler_params=pltpu.CompilerParams(
            collective_id=0, has_side_effects=True, vmem_limit_bytes=VMEM_BYTES
        ),
        cost_estimate=pl.CostEstimate(flops=0, bytes_accessed=40 * sent, transcendentals=0),
    )(normed, spread)


def projection_kernel(mixed_ref, normed_ref, merge_ref, qkv_ref, side_ref, out_ref, turned_ref):
    step = pl.program_id(0)
    merge_steps = mixed_ref.shape[1] // COLS
    steps = pl.num_programs(0)

    @pl.when(step == 0)
    def _():
        turned_ref[...] = mixed_ref[...].T

    @pl.when(step == merge_steps)
    def _():
        turned_ref[...] = normed_ref[...].T

    @pl.when(step < merge_steps)
    def _():
        out_ref[0] = jnp.dot(
            turned_ref[...], merge_ref[...], preferred_element_type=F32
        ).astype(BF16)

    @pl.when((step >= merge_steps) & (step < steps - 1))
    def _():
        out_ref[0] = jnp.dot(
            turned_ref[...], qkv_ref[...], preferred_element_type=F32
        ).astype(BF16)

    @pl.when(step == steps - 1)
    def _():
        out_ref[0] = side_ref[...]


def projection_terms(mixed, normed, attended_grad, qkv_grad, side):
    slots, width = mixed.shape
    first, second = attended_grad.shape[1] // COLS, qkv_grad.shape[1] // COLS
    whole = pl.BlockSpec((slots, width), lambda j: (0, 0))
    return pl.pallas_call(
        projection_kernel,
        grid=(first + second + 1,),
        in_specs=[
            whole,
            whole,
            pl.BlockSpec((slots, COLS), lambda j: (0, jnp.minimum(j, first - 1))),
            pl.BlockSpec((slots, COLS), lambda j: (0, jnp.clip(j - first, 0, second - 1))),
            pl.BlockSpec((width, COLS), lambda j: (0, 0)),
        ],
        out_specs=pl.BlockSpec((1, width, COLS), lambda j: (j, 0, 0)),
        out_shape=jax.ShapeDtypeStruct((first + second + 1, width, COLS), BF16),
        scratch_shapes=[pltpu.VMEM((width, slots), BF16)],
        cost_estimate=pl.CostEstimate(
            flops=2 * slots * width * (first + second) * COLS,
            bytes_accessed=2 * 10**7,
            transcendentals=0,
        ),
    )(mixed, normed, attended_grad, qkv_grad, side)


def body(
    tokens,
    lengths,
    routes,
    priority,
    first_gain,
    query_weight,
    key_weight,
    value_weight,
    merge_weight,
    router_weight,
    second_gain,
    gate_weight,
    up_weight,
    down_weight,
    cotangent,
):
    slots = tokens.shape[1]
    width = tokens.shape[2]
    groups = lax.axis_size("expert")
    expert_count = router_weight.shape[1]
    capacity = 5 * slots * TOP // (8 * expert_count)
    q_cols, k_cols = HEADS * HD, KV_HEADS * HD
    side_cols = 128

    def gather_shard(value, axis=0):
        return lax.all_gather(value, "shard", axis=axis, tiled=True)

    def scatter_all(part, ahead=None):
        planes, _, columns = part.shape
        part = lax.psum_scatter(
            part.reshape(planes * groups, -1, columns), "shard", scatter_dimension=1, tiled=True
        ).reshape(planes, groups, -1, columns)
        part, ahead = lax.optimization_barrier((part, ahead))
        me = lax.axis_index("expert")
        order = [
            lax.dynamic_index_in_dim(part, lax.rem(me - p + groups, groups), 1, keepdims=False)
            for p in range(groups)
        ]
        return direct_scatter(order), ahead

    side = jnp.concatenate(
        [router_weight, first_gain[:, None], second_gain[:, None]], axis=1
    )
    side = jnp.pad(side, ((0, 0), (0, side_cols - expert_count - 2)))
    first_set = gather_shard(
        jnp.concatenate([query_weight, key_weight, value_weight, side], axis=1)
    )
    merge_full = gather_shard(merge_weight)
    tables = jnp.concatenate(
        [routes[0].T, priority, jnp.broadcast_to(lengths[:, None], (1, slots))], axis=0
    )
    tables = jnp.stack(direct_gather(tables)).transpose(0, 2, 1)
    mid = groups // 2
    early_up, early_down = line_hops(cotangent[0], 0, mid)
    both_full = gather_shard(jnp.concatenate([gate_weight, up_weight], axis=0), 1)
    down_full = gather_shard(down_weight, 1)

    group = lax.axis_index("expert")
    own_experts = group * EXP_DEV + jnp.arange(EXP_DEV, dtype=jnp.int32)
    spread = jax.vmap(
        lambda t: dispatch_matrix(t[:, :TOP], t[:, TOP], t[0, TOP + 1], own_experts, capacity)
    )(tables)

    first_set, spread = lax.optimization_barrier((first_set, spread))
    qkv_full = first_set[:, : q_cols + 2 * k_cols]
    side_full = first_set[:, q_cols + 2 * k_cols :]
    router_full = side_full[:, :expert_count]
    gain_first = side_full[:, expert_count].astype(F32)
    gain_second = side_full[:, expert_count + 1].astype(F32)

    inputs = tokens[0].astype(F32)
    length = lengths[0]
    positions = jnp.arange(slots, dtype=jnp.int32)
    live_rows = (positions < length).astype(F32)[:, None]
    cosine, sine_table = rope_tables(slots)
    rms_one = lax.rsqrt(jnp.mean(inputs * inputs, axis=-1, keepdims=True) + EPS)
    unit_one = inputs * rms_one
    normed_one = (unit_one * gain_first).astype(BF16)
    qkv = jnp.dot(normed_one, qkv_full, preferred_element_type=F32)
    mixed, *low_parts, lse = attend(lengths, qkv, cosine, sine_table)
    mixed, early_up, early_down = lax.optimization_barrier((mixed, early_up, early_down))
    later_up, later_down = line_hops(
        cotangent[0], mid, held=(early_up[-1], early_down[-1])
    )
    upstream_all = jnp.stack(
        line_order(cotangent[0], early_up + later_up, early_down + later_down)
    )
    attended = jnp.dot(mixed, merge_full, preferred_element_type=F32)
    hidden = inputs + live_rows * attended
    rms_two = lax.rsqrt(jnp.mean(hidden * hidden, axis=-1, keepdims=True) + EPS)
    unit_two = hidden * rms_two
    normed_two = (unit_two * gain_second).astype(BF16)

    logits = jnp.dot(normed_two, router_full, preferred_element_type=F32)
    chosen = (
        routes[0][:, :, None] == jnp.arange(expert_count, dtype=jnp.int32)[None, None, :]
    ).astype(F32)
    chosen_any = jnp.sum(chosen, axis=1)
    masked = jnp.where(chosen_any > 0, logits, NEGATIVE)
    peak = jnp.max(masked, axis=-1, keepdims=True)
    exp_logits = jnp.exp(masked - peak) * chosen_any
    gate_dense = exp_logits / jnp.sum(exp_logits, axis=-1, keepdims=True)

    gates_all = jnp.stack(direct_gather(gate_dense.T))
    gates_own = lax.dynamic_slice_in_dim(gates_all, group * EXP_DEV, EXP_DEV, axis=1)
    slot_gate = jnp.sum(spread.astype(F32) * gates_own[:, :, None, :], axis=-1)
    gates = slot_gate.transpose(1, 0, 2).reshape(EXP_DEV, groups * capacity, 1)

    rows = gather_dispatch(normed_two, spread)
    gate_pre, lift_pre = expert_first(rows, both_full)
    ups = pick_rows(spread, upstream_all)
    gated, gate_pre_grad, lift_pre_grad, back_rows, slot_grad = expert_core(
        gate_pre, lift_pre, ups, gates, both_full, down_full
    )

    def combine(slot_rows):
        slot_rows = slot_rows.astype(BF16).reshape(EXP_DEV, groups, capacity, -1)
        return [
            jnp.einsum("xct,xcd->td", spread[p], slot_rows[:, p], preferred_element_type=F32)
            for p in range(groups)
        ]

    slot_grad = slot_grad.reshape(EXP_DEV, groups, capacity).transpose(1, 0, 2)
    token_grad = jnp.sum(spread.astype(F32) * slot_grad[:, :, :, None], axis=2)
    token_grad = lax.dynamic_update_slice_in_dim(
        jnp.zeros((groups, expert_count, slots), F32), token_grad, group * EXP_DEV, axis=1
    )
    slot_back = direct_scatter([token_grad[p] for p in range(groups)]).T
    step = width // RS_PARTS
    back_parts = [
        combine(back_rows[:, :, part * step : (part + 1) * step]) for part in range(RS_PARTS)
    ]
    back_parts, gated = lax.optimization_barrier((back_parts, gated))
    back_held = [scatter_hops(parts, 0, 1) for parts in back_parts]
    produced, expert_grads = expert_weights(
        rows, ups, gated, gate_pre_grad, lift_pre_grad, down_full
    )
    expert_grads, back_held[0] = lax.optimization_barrier((expert_grads, back_held[0]))
    back_total = []
    for parts, held in zip(back_parts, back_held):
        held_up, held_down = scatter_hops(parts, 1, groups - 1, held)
        back_total.append(parts[0] + held_up.astype(F32) + held_down.astype(F32))
    expert_grads = lax.psum_scatter(
        expert_grads.reshape(3 * EXP_DEV, width, -1), "shard", scatter_dimension=1, tiled=True
    )
    produced = combine(produced)
    produced = [part.astype(BF16) for part in produced]
    back_total, produced = lax.optimization_barrier((back_total, produced))
    back_total = jnp.concatenate(back_total, axis=1)
    sums = scatter_hops(produced, 0, 1)

    upstream = cotangent[0].astype(F32)
    picked_grad = gate_dense * (
        slot_back - jnp.sum(gate_dense * slot_back, axis=-1, keepdims=True)
    )
    logit_grad = picked_grad.astype(BF16)
    router_part = jnp.einsum("ld,le->de", normed_two, logit_grad, preferred_element_type=F32)
    normed_two_grad = jnp.einsum("le,de->ld", logit_grad, router_full, preferred_element_type=F32)
    normed_two_grad = normed_two_grad + back_total
    scaled_two = normed_two_grad * gain_second
    second_gain_part = jnp.sum(normed_two_grad * unit_two, axis=0)
    hidden_grad = upstream + rms_two * (
        scaled_two - unit_two * jnp.mean(scaled_two * unit_two, axis=-1, keepdims=True)
    )
    attended_grad = (live_rows * hidden_grad).astype(BF16)

    mixed_grad = jnp.einsum(
        "ld,hd->lh", attended_grad, merge_full, preferred_element_type=F32
    ).astype(BF16)
    qkv_grad = attend_back(lengths, *low_parts, mixed_grad, lse, cosine, sine_table)
    sums, qkv_grad = lax.optimization_barrier((sums, qkv_grad))
    sums = scatter_hops(produced, 1, mid, sums)
    side_part = jnp.concatenate([router_part, second_gain_part[:, None]], axis=1)
    side_part = jnp.pad(side_part, ((0, 0), (0, COLS - expert_count - 1))).astype(BF16)
    terms = projection_terms(mixed, normed_one, attended_grad, qkv_grad, side_part)
    terms, expert_grads, sums = lax.optimization_barrier((terms, expert_grads, sums))
    sums = scatter_hops(produced, mid, groups - 1, sums)
    normed_one_grad = jnp.einsum("lh,dh->ld", qkv_grad, qkv_full, preferred_element_type=F32)
    scaled_one = normed_one_grad * gain_first
    input_grad = hidden_grad + rms_one * (
        scaled_one - unit_one * jnp.mean(scaled_one * unit_one, axis=-1, keepdims=True)
    )
    block_output = (
        hidden + produced[0].astype(F32) + sums[0].astype(F32) + sums[1].astype(F32)
    )
    gate_grad, up_grad, down_grad = jnp.split(expert_grads.astype(F32), 3)
    reduced, (block_output, input_grad) = scatter_all(terms, (block_output, input_grad))
    own_rows = reduced.shape[1]
    reduced = reduced.transpose(1, 0, 2).reshape(own_rows, -1)
    place = (group * lax.axis_size("shard") + lax.axis_index("shard")) * own_rows
    merge_grad, qkv_reduced, side_grad = jnp.split(
        reduced, [width, width + q_cols + 2 * k_cols], axis=1
    )
    own_weights = lax.dynamic_slice_in_dim(qkv_full, place, own_rows, axis=0).astype(F32)
    own_gain = lax.dynamic_slice_in_dim(gain_first, place, own_rows)
    first_gain_grad = jnp.sum(own_weights * qkv_reduced, axis=1) / own_gain
    query_grad, key_grad, value_grad = jnp.split(qkv_reduced, [q_cols, q_cols + k_cols], axis=1)
    return (
        block_output[None],
        input_grad[None],
        first_gain_grad,
        query_grad,
        key_grad,
        value_grad,
        merge_grad,
        side_grad[:, :expert_count],
        side_grad[:, expert_count],
        gate_grad,
        up_grad,
        down_grad,
    )


def solution(mesh):
    both = ("expert", "shard")
    in_specs = (
        P(both, None, None),
        P(both),
        P(both, None, None),
        P(both, None),
        P("shard"),
        P("shard", None),
        P("shard", None),
        P("shard", None),
        P("shard", None),
        P("shard", None),
        P("shard"),
        P("expert", "shard", None),
        P("expert", "shard", None),
        P("expert", "shard", None),
        P(both, None, None),
    )
    out_specs = (
        P(both, None, None),
        P(both, None, None),
        P(both),
        P(both, None),
        P(both, None),
        P(both, None),
        P(both, None),
        P(both, None),
        P(both),
        P("expert", "shard", None),
        P("expert", "shard", None),
        P("expert", "shard", None),
    )
    return jax.shard_map(body, mesh=mesh, in_specs=in_specs, out_specs=out_specs, check_vma=False)
```

```python
import functools

import jax
import jax.numpy as jnp
import numpy as np
from jax import lax
from jax.experimental import pallas as pl
from jax.experimental.pallas import tpu as pltpu
from jax.sharding import PartitionSpec as P

HEADS = 24
KV_HEADS = 8
HD = 64
TOP = 8
EXP_DEV = 5
SHARE = HEADS // KV_HEADS
Q_BLOCK = 128
VMEM_BYTES = 63 * 2**20
CHUNKS = 4
COLS = 256

EPS = 1e-05
THETA = 10000.0
NEGATIVE = -1e30
F32 = jnp.float32
BF16 = jnp.bfloat16


def rope_tables(slots):
    frequency = THETA ** (-np.arange(HD // 2, dtype=np.float32) * np.float32(2.0) / HD)
    angles = np.arange(slots, dtype=np.float32)[:, None] * frequency.astype(np.float32)[None, :]
    cosine, sine = np.cos(angles), np.sin(angles)
    return (
        jnp.asarray(np.concatenate([cosine] * 4, axis=1), F32),
        jnp.asarray(np.concatenate([-sine, sine, -sine, sine], axis=1), F32),
    )


def dispatch_matrix(routes, priority, length, expert_ids, capacity):
    slots = routes.shape[0]
    positions = jnp.arange(slots, dtype=jnp.int32)
    live = positions < length
    named = jnp.any(routes[:, :, None] == expert_ids[None, None, :], axis=1) & live[:, None]
    earlier = (priority[None, :] < priority[:, None]).astype(BF16)
    slot = jnp.dot(earlier, named.astype(BF16), preferred_element_type=F32).astype(jnp.int32)
    slot = jnp.where(named, slot, capacity)
    return (
        slot.T[:, None, :] == jnp.arange(capacity, dtype=jnp.int32)[None, :, None]
    ).astype(BF16)


def shift_perm(count, shift):
    return [(i, (i + shift) % count) for i in range(count)]


def direct_gather(block):
    count = lax.axis_size("expert")
    return [block] + [
        lax.ppermute(block, "expert", shift_perm(count, k)) for k in range(1, count)
    ]


def direct_scatter(parts):
    count = lax.axis_size("expert")
    total = parts[0].astype(F32)
    for k in range(1, count):
        total = total + lax.ppermute(parts[k], "expert", shift_perm(count, -k)).astype(F32)
    return total


def line_hops(block, first=0, last=None, held=None):
    count = lax.axis_size("expert")
    last = count - 1 if last is None else last
    held_up, held_down = (block, block) if held is None else held
    up, down = [], []
    for step in range(first, last):
        held_up = lax.ppermute(
            held_up, "expert", [(i, i + 1) for i in range(step, count - 1)]
        )
        held_down = lax.ppermute(
            held_down, "expert", [(i + 1, i) for i in range(0, count - 1 - step)]
        )
        up.append(held_up)
        down.append(held_down)
    return up, down


def scatter_hops(parts, first=0, last=None, held=None):
    count = lax.axis_size("expert")
    last = count - 1 if last is None else last
    held_up, held_down = (None, None) if held is None else held
    for step in range(first, last):
        piece_up = parts[step + 1]
        piece_down = parts[count - 1 - step]
        if step:
            piece_up = piece_up.astype(F32) + held_up.astype(F32)
            piece_down = piece_down.astype(F32) + held_down.astype(F32)
        held_up = lax.ppermute(
            piece_up.astype(BF16), "expert", [(i, i + 1) for i in range(step + 1)]
        )
        held_down = lax.ppermute(
            piece_down.astype(BF16),
            "expert",
            [(i + 1, i) for i in range(count - 2 - step, count - 1)],
        )
    return held_up, held_down


def turn(values, cosine, sine):
    first = lax.broadcasted_iota(jnp.int32, (1, 2 * HD), 1) % HD < HD // 2
    out = []
    for start in range(0, values.shape[1], 2 * HD):
        part = values[:, start : start + 2 * HD]
        other = jnp.where(
            first, pltpu.roll(part, 2 * HD - HD // 2, 1), pltpu.roll(part, HD // 2, 1)
        )
        out.append(part * cosine + other * sine)
    return out[0] if len(out) == 1 else jnp.concatenate(out, axis=1)


def last_keys(block, length):
    lane = lax.broadcasted_iota(jnp.int32, (1, SHARE * Q_BLOCK), 1)
    return jnp.minimum(block * Q_BLOCK + lane % Q_BLOCK, length - 1)


def head_block(values, pair_head, block):
    rows = slice(block * Q_BLOCK, (block + 1) * Q_BLOCK)
    heads = range(pair_head * SHARE, (pair_head + 1) * SHARE)
    return jnp.concatenate([values[rows, h * HD : (h + 1) * HD] for h in heads], axis=0)


def rows_of_heads(parts):
    tall = [
        part[:, g * Q_BLOCK : (g + 1) * Q_BLOCK] for part in parts for g in range(SHARE)
    ]
    return jnp.concatenate(tall, axis=0).T


def dot_last(a, b):
    return lax.dot_general(a, b, (((1,), (1,)), ((), ())), preferred_element_type=F32)


def attend_kernel(
    length_ref, q_ref, k_ref, v_ref, cos_ref, sin_ref,
    mixed_ref, q_low_ref, k_low_ref, v_low_ref, lse_ref,
):
    length = length_ref[0]
    slots = q_ref.shape[0]
    cosine, sine = cos_ref[...], sin_ref[...]
    queries = (turn(q_ref[...], cosine, sine) * HD**-0.5).astype(BF16)
    keys = turn(k_ref[...], cosine, sine).astype(BF16)
    values = v_ref[...]
    q_low_ref[...] = queries
    k_low_ref[...] = keys
    v_low_ref[...] = values.astype(BF16)
    values_t = values.T.astype(BF16)
    blocks = slots // Q_BLOCK
    for block in range(blocks):
        span = (block + 1) * Q_BLOCK
        limit = last_keys(block, length)
        key_id = lax.broadcasted_iota(jnp.int32, (span, 1), 0)
        parts = []
        for head in range(2):
            scores = dot_last(
                keys[:span, head * HD : (head + 1) * HD], head_block(queries, head, block)
            )
            scores = jnp.where(key_id <= limit, scores, NEGATIVE)
            peak = jnp.max(scores, axis=0, keepdims=True)
            exp_scores = jnp.exp(scores - peak)
            total = jnp.sum(exp_scores, axis=0, keepdims=True)
            lse_ref[0, pl.ds(head * blocks + block, 1), :] = peak + jnp.log(total)
            part = jnp.dot(
                values_t[head * HD : (head + 1) * HD, :span],
                exp_scores.astype(BF16),
                preferred_element_type=F32,
            )
            parts.append(part / total)
        mixed_ref[block * Q_BLOCK : span, :] = rows_of_heads(parts).astype(BF16)


def attend_back_kernel(
    length_ref, q_ref, k_ref, v_ref, grad_ref, lse_ref, cos_ref, sin_ref, out_ref, dk_ref, dv_ref
):
    length = length_ref[0]
    slots, q_cols = q_ref.shape
    pairs = pl.num_programs(0)
    pair = pl.program_id(0)
    q_at = pl.ds(pl.multiple_of(pair * q_cols, 2 * HD), q_cols)
    k_at = pl.ds(pl.multiple_of(pairs * q_cols + pair * 2 * HD, 2 * HD), 2 * HD)
    v_at = pl.ds(pl.multiple_of(pairs * (q_cols + 2 * HD) + pair * 2 * HD, 2 * HD), 2 * HD)
    cosine, sine = cos_ref[...], -sin_ref[...]
    queries, keys, values = q_ref[...], k_ref[...], v_ref[...]
    grad = grad_ref[...]
    keys_t = keys.astype(F32).T.astype(BF16)
    dk_ref[...] = jnp.zeros_like(dk_ref)
    dv_ref[...] = jnp.zeros_like(dv_ref)
    blocks = slots // Q_BLOCK
    for block in range(blocks):
        rows = slice(block * Q_BLOCK, (block + 1) * Q_BLOCK)
        span = (block + 1) * Q_BLOCK
        limit = last_keys(block, length)
        key_id = lax.broadcasted_iota(jnp.int32, (span, 1), 0)
        parts = []
        for head in range(2):
            cols = slice(head * HD, (head + 1) * HD)
            query = head_block(queries, head, block)
            out_grad = head_block(grad, head, block)
            scores = dot_last(keys[:span, cols], query)
            scores = jnp.where(key_id <= limit, scores, NEGATIVE)
            probs = jnp.exp(scores - lse_ref[0, pl.ds(head * blocks + block, 1), :])
            prob_back = dot_last(values[:span, cols], out_grad)
            mean = jnp.sum(probs * prob_back, axis=0, keepdims=True)
            score_grad = (probs * (prob_back - mean)).astype(BF16)
            dv_ref[head, :span, :] += jnp.dot(
                probs.astype(BF16), out_grad, preferred_element_type=F32
            )
            dk_ref[head, :span, :] += jnp.dot(score_grad, query, preferred_element_type=F32)
            parts.append(
                jnp.dot(keys_t[cols, :span], score_grad, preferred_element_type=F32)
                * HD**-0.5
            )
        out_ref[rows, q_at] = turn(rows_of_heads(parts), cosine[rows], sine[rows]).astype(
            BF16
        )
    key_grad = jnp.concatenate([dk_ref[0], dk_ref[1]], axis=1)
    out_ref[:, k_at] = turn(key_grad, cosine, sine).astype(BF16)
    out_ref[:, v_at] = jnp.concatenate([dv_ref[0], dv_ref[1]], axis=1).astype(BF16)


def column_block(slots, columns, first=0):
    return pl.BlockSpec((slots, columns), lambda p: (0, first + p))


def attention_specs(slots):
    pairs = KV_HEADS // 2
    q_cols, cols = 2 * SHARE * HD, 2 * (SHARE + 2) * HD
    blocks = slots // Q_BLOCK
    whole = pl.BlockSpec((slots, 2 * HD), lambda p: (0, 0))
    lse = pl.BlockSpec((1, 2 * blocks, SHARE * Q_BLOCK), lambda p: (p, 0, 0))
    scalar = pl.BlockSpec(memory_space=pltpu.SMEM)
    return pairs, q_cols, cols, blocks, whole, lse, scalar


def attend(length, qkv, cosine, sine):
    slots = qkv.shape[0]
    pairs, q_cols, cols, blocks, whole, lse, scalar = attention_specs(slots)
    queries, keys = column_block(slots, q_cols), column_block(slots, 2 * HD)
    key_first = pairs * q_cols // (2 * HD)
    low_keys = jax.ShapeDtypeStruct((slots, pairs * 2 * HD), BF16)
    low_queries = jax.ShapeDtypeStruct((slots, pairs * q_cols), BF16)
    return pl.pallas_call(
        attend_kernel,
        grid=(pairs,),
        in_specs=[
            scalar,
            queries,
            column_block(slots, 2 * HD, key_first),
            column_block(slots, 2 * HD, key_first + pairs),
            whole,
            whole,
        ],
        out_specs=[queries, queries, keys, keys, lse],
        out_shape=[
            low_queries,
            low_queries,
            low_keys,
            low_keys,
            jax.ShapeDtypeStruct((pairs, 2 * blocks, SHARE * Q_BLOCK), F32),
        ],
        cost_estimate=pl.CostEstimate(
            flops=24 * HEADS * slots * slots * HD // 4, bytes_accessed=10**7, transcendentals=0
        ),
    )(length, qkv, qkv, qkv, cosine, sine)


def attend_back(length, queries, keys, values, grad, lse_rows, cosine, sine):
    slots = grad.shape[0]
    pairs, q_cols, cols, blocks, whole, lse, scalar = attention_specs(slots)
    wide, narrow = column_block(slots, q_cols), column_block(slots, 2 * HD)
    return pl.pallas_call(
        attend_back_kernel,
        grid=(pairs,),
        in_specs=[scalar, wide, narrow, narrow, wide, lse, whole, whole],
        out_specs=pl.BlockSpec((slots, pairs * cols), lambda p: (0, 0)),
        out_shape=jax.ShapeDtypeStruct((slots, pairs * cols), BF16),
        scratch_shapes=[pltpu.VMEM((2, slots, HD), F32), pltpu.VMEM((2, slots, HD), F32)],
        cost_estimate=pl.CostEstimate(
            flops=60 * HEADS * slots * slots * HD // 4, bytes_accessed=10**7, transcendentals=0
        ),
    )(length, queries, keys, values, grad, lse_rows, cosine, sine)


def expert_kernel(
    gate_pre_ref, lift_ref, ups_ref, gates_ref, gate_ref, up_ref, down_ref, spread_ref,
    gated_ref, gate_grad_ref, lift_grad_ref, parts_ref, slot_ref,
    total_ref, stage_ref, sems,
):
    act_grad = jnp.dot(ups_ref[0], down_ref[0], preferred_element_type=F32)
    gate_pre, lift_pre, gates = gate_pre_ref[0], lift_ref[0], gates_ref[0]
    sigmoid_gate = jax.nn.sigmoid(gate_pre)
    silu_gate = gate_pre * sigmoid_gate
    activated = silu_gate * lift_pre
    slot_ref[0] = jnp.sum(act_grad * activated, axis=-1, keepdims=True)
    gated_ref[0] = (activated * gates).astype(BF16)
    act_grad = act_grad * gates
    gate_pre_grad = (
        act_grad * lift_pre * (sigmoid_gate + silu_gate * (1.0 - sigmoid_gate))
    ).astype(BF16)
    lift_pre_grad = (act_grad * silu_gate).astype(BF16)
    gate_grad_ref[0] = gate_pre_grad
    lift_grad_ref[0] = lift_pre_grad
    back = (
        dot_last(gate_pre_grad, gate_ref[0]) + dot_last(lift_pre_grad, up_ref[0])
    ).astype(BF16)
    step = pl.program_id(0)
    count, _, capacity, _ = spread_ref.shape
    for place in range(count):
        part = jnp.dot(
            spread_ref[place, 0].T,
            back[place * capacity : (place + 1) * capacity],
            preferred_element_type=F32,
        )

        @pl.when(step == 0)
        def _():
            total_ref[place] = part

        @pl.when(step > 0)
        def _():
            total_ref[place] += part

    @pl.when(step == pl.num_programs(0) - 1)
    def _():
        copies = [
            pltpu.make_async_copy(
                stage_ref.at[place % 2], parts_ref.at[place], sems.at[place % 2]
            )
            for place in range(count)
        ]
        for place in range(count):
            if place > 1:
                copies[place - 2].wait()
            stage_ref[place % 2] = total_ref[place].astype(BF16)
            copies[place].start()
        for copy in copies[-2:]:
            copy.wait()


def expert_block(*shape, first=0):
    return pl.BlockSpec((1,) + shape, lambda x: (first + x, 0, 0))


def first_kernel(rows_ref, gate_ref, up_ref, gate_pre_ref, lift_ref):
    rows = rows_ref[0]
    gate_pre_ref[0] = jnp.dot(rows, gate_ref[0], preferred_element_type=F32)
    lift_ref[0] = jnp.dot(rows, up_ref[0], preferred_element_type=F32)


def expert_first(rows, both_full):
    experts, count, width = rows.shape
    hidden = both_full.shape[-1]
    narrow, weight = expert_block(count, hidden), expert_block(width, hidden)
    shape = jax.ShapeDtypeStruct((experts, count, hidden), F32)
    return pl.pallas_call(
        first_kernel,
        grid=(experts,),
        in_specs=[
            expert_block(count, width), weight, expert_block(width, hidden, first=experts)
        ],
        out_specs=[narrow, narrow],
        out_shape=[shape, shape],
        compiler_params=pltpu.CompilerParams(vmem_limit_bytes=VMEM_BYTES),
        cost_estimate=pl.CostEstimate(
            flops=4 * experts * count * width * hidden, bytes_accessed=35 * 10**6, transcendentals=0
        ),
    )(rows, both_full, both_full)


def expert_core(gate_pre, lift_pre, ups, gates, both_full, down_full, spread):
    experts, rows, width = ups.shape
    count, _, capacity, slots = spread.shape
    hidden = gate_pre.shape[-1]
    narrow, wide = expert_block(rows, hidden), expert_block(rows, width)
    weight, single = expert_block(width, hidden), expert_block(rows, 1)
    low = jax.ShapeDtypeStruct((experts, rows, hidden), BF16)
    return pl.pallas_call(
        expert_kernel,
        grid=(experts,),
        in_specs=[
            narrow, narrow, wide, single,
            weight, expert_block(width, hidden, first=experts), weight,
            pl.BlockSpec((count, 1, capacity, slots), lambda x: (0, x, 0, 0)),
        ],
        out_specs=[narrow, narrow, narrow, pl.BlockSpec(memory_space=pl.ANY), single],
        out_shape=[
            low,
            low,
            low,
            jax.ShapeDtypeStruct((count, slots, width), BF16),
            jax.ShapeDtypeStruct((experts, rows, 1), F32),
        ],
        scratch_shapes=[
            pltpu.VMEM((count, slots, width), F32),
            pltpu.VMEM((2, slots, width), BF16),
            pltpu.SemaphoreType.DMA((2,)),
        ],
        compiler_params=pltpu.CompilerParams(vmem_limit_bytes=VMEM_BYTES),
        cost_estimate=pl.CostEstimate(
            flops=8 * experts * rows * width * hidden, bytes_accessed=60 * 10**6, transcendentals=0
        ),
    )(gate_pre, lift_pre, ups, gates, both_full, both_full, down_full, spread)


def weight_kernel(
    rows_ref, ups_ref, gated_ref, gate_grad_ref, lift_grad_ref, down_ref, out_ref, grads_ref
):
    out_ref[0] = dot_last(gated_ref[0], down_ref[0]).astype(BF16)
    rows_t = rows_ref[0].T
    grads_ref[0, 0] = jnp.dot(
        rows_t, gate_grad_ref[0], preferred_element_type=F32
    ).astype(BF16)
    grads_ref[1, 0] = jnp.dot(
        rows_t, lift_grad_ref[0], preferred_element_type=F32
    ).astype(BF16)
    grads_ref[2, 0] = jnp.dot(
        ups_ref[0].T, gated_ref[0], preferred_element_type=F32
    ).astype(BF16)


def expert_weights(rows, ups, gated, gate_grad, lift_grad, down_full):
    experts, count, width = ups.shape
    hidden = gated.shape[-1]
    narrow, wide = expert_block(count, hidden), expert_block(count, width)
    weight = expert_block(width, hidden)
    return pl.pallas_call(
        weight_kernel,
        grid=(experts,),
        in_specs=[wide, wide, narrow, narrow, narrow, weight],
        out_specs=[wide, pl.BlockSpec((3, 1, width, hidden), lambda x: (0, x, 0, 0))],
        out_shape=[
            jax.ShapeDtypeStruct((experts, count, width), BF16),
            jax.ShapeDtypeStruct((3, experts, width, hidden), BF16),
        ],
        compiler_params=pltpu.CompilerParams(vmem_limit_bytes=VMEM_BYTES),
        cost_estimate=pl.CostEstimate(
            flops=8 * experts * count * width * hidden, bytes_accessed=60 * 10**6, transcendentals=0
        ),
    )(rows, ups, gated, gate_grad, lift_grad, down_full)


def line_copy(source, target, sems, step, up, chunk):
    send_sems, recv_sems = sems
    side = 0 if up else 1
    me = lax.axis_index("expert")
    return pltpu.make_async_remote_copy(
        src_ref=source,
        dst_ref=target,
        send_sem=send_sems.at[side, step, chunk],
        recv_sem=recv_sems.at[side, step, chunk],
        device_id={"expert": me + 1 if up else me - 1},
        device_id_type=pl.DeviceIdType.MESH,
    )


def greet_line(count):
    me = lax.axis_index("expert")
    barrier = pltpu.get_barrier_semaphore()
    for up in (True, False):
        there = me < count - 1 if up else me > 0

        @pl.when(there)
        def _():
            pl.semaphore_signal(
                barrier,
                inc=1,
                device_id={"expert": me + 1 if up else me - 1},
                device_id_type=pl.DeviceIdType.MESH,
            )

    ends = (me == 0) | (me == count - 1)

    @pl.when(ends)
    def _():
        pl.semaphore_wait(barrier, 1)

    @pl.when(jnp.logical_not(ends))
    def _():
        pl.semaphore_wait(barrier, 2)


def gather_line(count, own, held, chunks, sems, work):
    me = lax.axis_index("expert")

    def after(step, up):
        return me + step < count if up else me - step >= 0

    def place(step, up):
        return step if up else count - step

    for chunk in range(chunks):
        for up in (True, False):

            @pl.when(after(1, up))
            def _():
                line_copy(own(chunk), held(place(1, up), chunk), sems, 0, up, chunk).start()

    work(0, True)
    for step in range(1, count):
        for chunk in range(chunks):
            for up in (True, False):
                here = held(place(step, up), chunk)

                @pl.when(after(step, not up))
                def _():
                    line_copy(here, here, sems, step - 1, up, chunk).wait_recv()

                if step < count - 1:

                    @pl.when(after(step, not up) & after(1, up))
                    def _():
                        there = held(place(step + 1, up), chunk)
                        line_copy(here, there, sems, step, up, chunk).start()

        for up in (True, False):

            @pl.when(after(step, not up))
            def _():
                work(place(step, up), up)

    for step in range(count - 1):
        for chunk in range(chunks):
            for up in (True, False):

                @pl.when(after(step, not up) & after(1, up))
                def _():
                    source = held(place(step, up), chunk) if step else own(chunk)
                    line_copy(
                        source, held(place(step + 1, up), chunk), sems, step, up, chunk
                    ).wait_send()


def early_kernel(count, columns, block_ref, held_ref, send_sems, recv_sems):
    greet_line(count)
    tall = block_ref.shape[0] // CHUNKS

    def rows(chunk):
        return pl.ds(chunk * tall, tall)

    gather_line(
        count,
        lambda c: block_ref.at[rows(c), pl.ds(0, columns)],
        lambda p, c: held_ref.at[p - 1, rows(c), :],
        CHUNKS,
        (send_sems, recv_sems),
        lambda place, up: None,
    )


def early_gather(block, columns):
    count = lax.axis_size("expert")
    slots = block.shape[0]
    sems = pltpu.SemaphoreType.DMA((2, count - 1, CHUNKS))
    sent = 2 * (count - 1) * slots * columns
    return pl.pallas_call(
        functools.partial(early_kernel, count, columns),
        in_specs=[pl.BlockSpec(memory_space=pltpu.VMEM)],
        out_specs=pl.BlockSpec(memory_space=pl.ANY),
        out_shape=jax.ShapeDtypeStruct((count - 1, slots, columns), BF16),
        scratch_shapes=[sems, sems],
        compiler_params=pltpu.CompilerParams(
            collective_id=1, has_side_effects=True, vmem_limit_bytes=VMEM_BYTES
        ),
        cost_estimate=pl.CostEstimate(flops=0, bytes_accessed=40 * sent, transcendentals=0),
    )(block)


def dispatch_kernel(count, normed_ref, block_ref, early_ref, spread_ref, *refs):
    late_up, late_down = refs[: count - 1], refs[count - 1 : 2 * (count - 1)]
    rows_ref, ups_ref, held_ref, send_sems, recv_sems = refs[2 * (count - 1) :]
    greet_line(count)
    tall = normed_ref.shape[0] // CHUNKS
    capacity = rows_ref.shape[1] // count
    columns = early_ref.shape[-1]

    def cut(chunk):
        return pl.ds(chunk * tall, tall)

    def work(place, up):
        if place:
            late = late_up[place - 1] if up else late_down[count - place - 1]
            source = held_ref[place - 1]
            grads = [early_ref[place - 1], late[...]]
        else:
            source = normed_ref[...]
            grads = [block_ref[:, :columns], block_ref[:, columns:]]
        at = slice(place * capacity, (place + 1) * capacity)
        for expert in range(EXP_DEV):
            pick = spread_ref[place, expert]
            taken = [
                jnp.dot(pick, s, preferred_element_type=F32).astype(BF16)
                for s in [source] + grads
            ]
            rows_ref[expert, at, :] = taken[0]
            ups_ref[expert, at, :columns] = taken[1]
            ups_ref[expert, at, columns:] = taken[2]

    gather_line(
        count,
        lambda c: normed_ref.at[cut(c), :],
        lambda p, c: held_ref.at[p - 1, cut(c), :],
        CHUNKS,
        (send_sems, recv_sems),
        work,
    )


def gather_dispatch(normed, block, early, late_up, late_down, spread):
    count = lax.axis_size("expert")
    slots, width = normed.shape
    capacity = spread.shape[2]
    vmem = pl.BlockSpec(memory_space=pltpu.VMEM)
    sems = pltpu.SemaphoreType.DMA((2, count - 1, CHUNKS))
    sent = 2 * (count - 1) * slots * width
    rows = jax.ShapeDtypeStruct((EXP_DEV, count * capacity, width), BF16)
    return pl.pallas_call(
        functools.partial(dispatch_kernel, count),
        in_specs=[vmem] * (4 + 2 * (count - 1)),
        out_specs=[vmem] * 2,
        out_shape=[rows, rows],
        scratch_shapes=[pltpu.VMEM((count - 1, slots, width), BF16), sems, sems],
        compiler_params=pltpu.CompilerParams(
            collective_id=0, has_side_effects=True, vmem_limit_bytes=VMEM_BYTES
        ),
        cost_estimate=pl.CostEstimate(flops=0, bytes_accessed=40 * sent, transcendentals=0),
    )(normed, block, early, spread, *late_up, *late_down)


def sum_kernel(
    count, parts_ref, produced_ref, spread_ref, out_ref, produced_out,
    held_ref, stage_ref, stage_sems, send_sems, recv_sems,
):
    greet_line(count)
    me = lax.axis_index("expert")
    slots = out_ref.shape[0]
    tall = slots // CHUNKS
    sems = (send_sems, recv_sems)

    def after(step, up):
        return me + step < count if up else me - step >= 0

    def cut(chunk):
        return pl.ds(chunk * tall, tall)

    def held(step, up, chunk):
        return held_ref.at[0 if up else 1, step, cut(chunk), :]

    def own(step, up, chunk):
        return parts_ref.at[count - step if up else step, cut(chunk), :]

    def combine():
        capacity = produced_ref.shape[1] // count
        copies = []
        for place in range(count):
            at = slice(place * capacity, (place + 1) * capacity)
            pick = spread_ref[place].reshape(EXP_DEV * capacity, slots).T
            rows = produced_ref[:, at, :].reshape(EXP_DEV * capacity, -1)
            if place > 1:
                copies[place - 2].wait()
            stage_ref[place % 2] = jnp.dot(pick, rows, preferred_element_type=F32).astype(BF16)
            copies.append(
                pltpu.make_async_copy(
                    stage_ref.at[place % 2], produced_out.at[place], stage_sems.at[place % 2]
                )
            )
            copies[place].start()
        for copy in copies[-2:]:
            copy.wait()

    for step in range(count - 1, 0, -1):
        if step == count - 2:
            combine()
        for chunk in range(CHUNKS):
            for up in (True, False):
                there = held(step - 1, up, chunk)

                @pl.when(after(step, up) & jnp.logical_not(after(1, not up)))
                def _():
                    line_copy(own(step, up, chunk), there, sems, step - 1, up, chunk).start()

                if step < count - 1:
                    here = held(step, up, chunk)

                    @pl.when(after(step, up) & after(1, not up))
                    def _():
                        line_copy(here, here, sems, step, up, chunk).wait_recv()
                        here[...] = (
                            here[...].astype(F32) + own(step, up, chunk)[...].astype(F32)
                        ).astype(BF16)
                        line_copy(here, there, sems, step - 1, up, chunk).start()

    for chunk in range(CHUNKS):
        rows = cut(chunk)
        out_ref[rows, :] = parts_ref[0, rows, :].astype(F32)
        for up in (True, False):
            here = held(0, up, chunk)

            @pl.when(after(1, not up))
            def _():
                line_copy(here, here, sems, 0, up, chunk).wait_recv()
                out_ref[rows, :] += here[...].astype(F32)

    for step in range(count - 1, 0, -1):
        for chunk in range(CHUNKS):
            for up in (True, False):

                @pl.when(after(step, up))
                def _():
                    source = own(step, up, chunk)
                    line_copy(
                        source, held(step - 1, up, chunk), sems, step - 1, up, chunk
                    ).wait_send()


def line_sum(parts, produced, spread):
    count, slots, width = parts.shape
    vmem = pl.BlockSpec(memory_space=pltpu.VMEM)
    sems = pltpu.SemaphoreType.DMA((2, count - 1, CHUNKS))
    return pl.pallas_call(
        functools.partial(sum_kernel, count),
        in_specs=[vmem] * 3,
        out_specs=[vmem, pl.BlockSpec(memory_space=pl.ANY)],
        out_shape=[
            jax.ShapeDtypeStruct((slots, width), F32),
            jax.ShapeDtypeStruct((count, slots, width), BF16),
        ],
        scratch_shapes=[
            pltpu.VMEM((2, count - 1, slots, width), BF16),
            pltpu.VMEM((2, slots, width), BF16),
            pltpu.SemaphoreType.DMA((2,)),
            sems,
            sems,
        ],
        compiler_params=pltpu.CompilerParams(
            collective_id=2, has_side_effects=True, vmem_limit_bytes=VMEM_BYTES
        ),
        cost_estimate=pl.CostEstimate(
            flops=0, bytes_accessed=80 * (count - 1) * slots * width, transcendentals=0
        ),
    )(parts, produced, spread)


def projection_kernel(mixed_ref, normed_ref, merge_ref, qkv_ref, side_ref, out_ref, turned_ref):
    step = pl.program_id(0)
    merge_steps = mixed_ref.shape[1] // COLS
    steps = pl.num_programs(0)

    @pl.when(step == 0)
    def _():
        turned_ref[...] = mixed_ref[...].T

    @pl.when(step == merge_steps)
    def _():
        turned_ref[...] = normed_ref[...].T

    @pl.when(step < merge_steps)
    def _():
        out_ref[0] = jnp.dot(
            turned_ref[...], merge_ref[...], preferred_element_type=F32
        ).astype(BF16)

    @pl.when((step >= merge_steps) & (step < steps - 1))
    def _():
        out_ref[0] = jnp.dot(
            turned_ref[...], qkv_ref[...], preferred_element_type=F32
        ).astype(BF16)

    @pl.when(step == steps - 1)
    def _():
        out_ref[0] = side_ref[...]


def projection_terms(mixed, normed, attended_grad, qkv_grad, side):
    slots, width = mixed.shape
    first, second = attended_grad.shape[1] // COLS, qkv_grad.shape[1] // COLS
    whole = pl.BlockSpec((slots, width), lambda j: (0, 0))
    return pl.pallas_call(
        projection_kernel,
        grid=(first + second + 1,),
        in_specs=[
            whole,
            whole,
            pl.BlockSpec((slots, COLS), lambda j: (0, jnp.minimum(j, first - 1))),
            pl.BlockSpec((slots, COLS), lambda j: (0, jnp.clip(j - first, 0, second - 1))),
            pl.BlockSpec((width, COLS), lambda j: (0, 0)),
        ],
        out_specs=pl.BlockSpec((1, width, COLS), lambda j: (j, 0, 0)),
        out_shape=jax.ShapeDtypeStruct((first + second + 1, width, COLS), BF16),
        scratch_shapes=[pltpu.VMEM((width, slots), BF16)],
        cost_estimate=pl.CostEstimate(
            flops=2 * slots * width * (first + second) * COLS,
            bytes_accessed=2 * 10**7,
            transcendentals=0,
        ),
    )(mixed, normed, attended_grad, qkv_grad, side)


def body(
    tokens,
    lengths,
    routes,
    priority,
    first_gain,
    query_weight,
    key_weight,
    value_weight,
    merge_weight,
    router_weight,
    second_gain,
    gate_weight,
    up_weight,
    down_weight,
    cotangent,
):
    slots = tokens.shape[1]
    width = tokens.shape[2]
    groups = lax.axis_size("expert")
    expert_count = router_weight.shape[1]
    capacity = 5 * slots * TOP // (8 * expert_count)
    q_cols, k_cols = HEADS * HD, KV_HEADS * HD
    side_cols = 128

    def gather_shard(value, axis=0):
        return lax.all_gather(value, "shard", axis=axis, tiled=True)

    def scatter_all(part, ahead=None):
        planes, _, columns = part.shape
        part = lax.psum_scatter(
            part.reshape(planes * groups, -1, columns), "shard", scatter_dimension=1, tiled=True
        ).reshape(planes, groups, -1, columns)
        part, ahead = lax.optimization_barrier((part, ahead))
        me = lax.axis_index("expert")
        order = [
            lax.dynamic_index_in_dim(part, lax.rem(me - p + groups, groups), 1, keepdims=False)
            for p in range(groups)
        ]
        return direct_scatter(order), ahead

    side = jnp.concatenate(
        [router_weight, first_gain[:, None], second_gain[:, None]], axis=1
    )
    side = jnp.pad(side, ((0, 0), (0, side_cols - expert_count - 2)))
    first_set = gather_shard(
        jnp.concatenate([query_weight, key_weight, value_weight, side], axis=1)
    )
    merge_full = gather_shard(merge_weight)
    tables = jnp.concatenate(
        [routes[0].T, priority, jnp.broadcast_to(lengths[:, None], (1, slots))], axis=0
    )
    tables = jnp.stack(direct_gather(tables)).transpose(0, 2, 1)
    mid = groups // 2
    early_columns = 7 * width // 12
    early = early_gather(cotangent[0], early_columns)
    late_block, tokens, gate_weight, tables, early = lax.optimization_barrier(
        (cotangent[0][:, early_columns:], tokens, gate_weight, tables, early)
    )
    late_up, late_down = line_hops(late_block, 0, 1)
    both_full = gather_shard(jnp.concatenate([gate_weight, up_weight], axis=0), 1)
    down_full = gather_shard(down_weight, 1)

    group = lax.axis_index("expert")
    own_experts = group * EXP_DEV + jnp.arange(EXP_DEV, dtype=jnp.int32)
    spread = jax.vmap(
        lambda t: dispatch_matrix(t[:, :TOP], t[:, TOP], t[0, TOP + 1], own_experts, capacity)
    )(tables)

    qkv_full = first_set[:, : q_cols + 2 * k_cols]
    side_full = first_set[:, q_cols + 2 * k_cols :]
    router_full = side_full[:, :expert_count]
    gain_first = side_full[:, expert_count].astype(F32)
    gain_second = side_full[:, expert_count + 1].astype(F32)

    inputs = tokens[0].astype(F32)
    length = lengths[0]
    positions = jnp.arange(slots, dtype=jnp.int32)
    live_rows = (positions < length).astype(F32)[:, None]
    cosine, sine_table = rope_tables(slots)
    rms_one = lax.rsqrt(jnp.mean(inputs * inputs, axis=-1, keepdims=True) + EPS)
    unit_one = inputs * rms_one
    normed_one = (unit_one * gain_first).astype(BF16)
    qkv = jnp.dot(normed_one, qkv_full, preferred_element_type=F32)
    mixed, *low_parts, lse = attend(lengths, qkv, cosine, sine_table)
    mixed, late_up, late_down = lax.optimization_barrier((mixed, late_up, late_down))
    later_up, later_down = line_hops(late_block, 1, held=(late_up[-1], late_down[-1]))
    attended = jnp.dot(mixed, merge_full, preferred_element_type=F32)
    hidden = inputs + live_rows * attended
    rms_two = lax.rsqrt(jnp.mean(hidden * hidden, axis=-1, keepdims=True) + EPS)
    unit_two = hidden * rms_two
    normed_two = (unit_two * gain_second).astype(BF16)

    logits = jnp.dot(normed_two, router_full, preferred_element_type=F32)
    chosen = (
        routes[0][:, :, None] == jnp.arange(expert_count, dtype=jnp.int32)[None, None, :]
    ).astype(F32)
    chosen_any = jnp.sum(chosen, axis=1)
    masked = jnp.where(chosen_any > 0, logits, NEGATIVE)
    peak = jnp.max(masked, axis=-1, keepdims=True)
    exp_logits = jnp.exp(masked - peak) * chosen_any
    gate_dense = exp_logits / jnp.sum(exp_logits, axis=-1, keepdims=True)

    gates_all = jnp.stack(direct_gather(gate_dense.T))
    gates_own = lax.dynamic_slice_in_dim(gates_all, group * EXP_DEV, EXP_DEV, axis=1)
    slot_gate = jnp.sum(spread.astype(F32) * gates_own[:, :, None, :], axis=-1)
    gates = slot_gate.transpose(1, 0, 2).reshape(EXP_DEV, groups * capacity, 1)

    rows, ups = gather_dispatch(
        normed_two, cotangent[0], early, late_up + later_up, late_down + later_down, spread
    )
    gate_pre, lift_pre = expert_first(rows, both_full)
    gated, gate_pre_grad, lift_pre_grad, back_parts, slot_grad = expert_core(
        gate_pre, lift_pre, ups, gates, both_full, down_full, spread
    )

    slot_grad = slot_grad.reshape(EXP_DEV, groups, capacity).transpose(1, 0, 2)
    token_grad = jnp.sum(spread.astype(F32) * slot_grad[:, :, :, None], axis=2)
    token_grad = lax.dynamic_update_slice_in_dim(
        jnp.zeros((groups, expert_count, slots), F32), token_grad, group * EXP_DEV, axis=1
    )
    slot_back = direct_scatter([token_grad[p] for p in range(groups)]).T
    produced, expert_grads = expert_weights(
        rows, ups, gated, gate_pre_grad, lift_pre_grad, down_full
    )
    back_parts, expert_grads = lax.optimization_barrier((back_parts, expert_grads))
    back_total, produced = line_sum(back_parts, produced, spread)
    expert_grads = lax.psum_scatter(
        expert_grads.reshape(3 * EXP_DEV, width, -1), "shard", scatter_dimension=1, tiled=True
    )
    sums = scatter_hops(produced, 0, 1)

    upstream = cotangent[0].astype(F32)
    picked_grad = gate_dense * (
        slot_back - jnp.sum(gate_dense * slot_back, axis=-1, keepdims=True)
    )
    logit_grad = picked_grad.astype(BF16)
    router_part = jnp.einsum("ld,le->de", normed_two, logit_grad, preferred_element_type=F32)
    normed_two_grad = jnp.einsum("le,de->ld", logit_grad, router_full, preferred_element_type=F32)
    normed_two_grad = normed_two_grad + back_total
    scaled_two = normed_two_grad * gain_second
    second_gain_part = jnp.sum(normed_two_grad * unit_two, axis=0)
    hidden_grad = upstream + rms_two * (
        scaled_two - unit_two * jnp.mean(scaled_two * unit_two, axis=-1, keepdims=True)
    )
    attended_grad = (live_rows * hidden_grad).astype(BF16)

    mixed_grad = jnp.einsum(
        "ld,hd->lh", attended_grad, merge_full, preferred_element_type=F32
    ).astype(BF16)
    qkv_grad = attend_back(lengths, *low_parts, mixed_grad, lse, cosine, sine_table)
    sums, qkv_grad = lax.optimization_barrier((sums, qkv_grad))
    sums = scatter_hops(produced, 1, mid, sums)
    side_part = jnp.concatenate([router_part, second_gain_part[:, None]], axis=1)
    side_part = jnp.pad(side_part, ((0, 0), (0, COLS - expert_count - 1))).astype(BF16)
    terms = projection_terms(mixed, normed_one, attended_grad, qkv_grad, side_part)
    terms, expert_grads, sums = lax.optimization_barrier((terms, expert_grads, sums))
    sums = scatter_hops(produced, mid, groups - 1, sums)
    normed_one_grad = jnp.einsum("lh,dh->ld", qkv_grad, qkv_full, preferred_element_type=F32)
    scaled_one = normed_one_grad * gain_first
    input_grad = hidden_grad + rms_one * (
        scaled_one - unit_one * jnp.mean(scaled_one * unit_one, axis=-1, keepdims=True)
    )
    block_output = (
        hidden + produced[0].astype(F32) + sums[0].astype(F32) + sums[1].astype(F32)
    )
    gate_grad, up_grad, down_grad = jnp.split(expert_grads.astype(F32), 3)
    reduced, (block_output, input_grad) = scatter_all(terms, (block_output, input_grad))
    own_rows = reduced.shape[1]
    reduced = reduced.transpose(1, 0, 2).reshape(own_rows, -1)
    place = (group * lax.axis_size("shard") + lax.axis_index("shard")) * own_rows
    merge_grad, qkv_reduced, side_grad = jnp.split(
        reduced, [width, width + q_cols + 2 * k_cols], axis=1
    )
    own_weights = lax.dynamic_slice_in_dim(qkv_full, place, own_rows, axis=0).astype(F32)
    own_gain = lax.dynamic_slice_in_dim(gain_first, place, own_rows)
    first_gain_grad = jnp.sum(own_weights * qkv_reduced, axis=1) / own_gain
    query_grad, key_grad, value_grad = jnp.split(qkv_reduced, [q_cols, q_cols + k_cols], axis=1)
    return (
        block_output[None],
        input_grad[None],
        first_gain_grad,
        query_grad,
        key_grad,
        value_grad,
        merge_grad,
        side_grad[:, :expert_count],
        side_grad[:, expert_count],
        gate_grad,
        up_grad,
        down_grad,
    )


def solution(mesh):
    both = ("expert", "shard")
    in_specs = (
        P(both, None, None),
        P(both),
        P(both, None, None),
        P(both, None),
        P("shard"),
        P("shard", None),
        P("shard", None),
        P("shard", None),
        P("shard", None),
        P("shard", None),
        P("shard"),
        P("expert", "shard", None),
        P("expert", "shard", None),
        P("expert", "shard", None),
        P(both, None, None),
    )
    out_specs = (
        P(both, None, None),
        P(both, None, None),
        P(both),
        P(both, None),
        P(both, None),
        P(both, None),
        P(both, None),
        P(both, None),
        P(both),
        P("expert", "shard", None),
        P("expert", "shard", None),
        P("expert", "shard", None),
    )
    return jax.shard_map(body, mesh=mesh, in_specs=in_specs, out_specs=out_specs, check_vma=False)
```

```python
import functools

import jax
import jax.numpy as jnp
import numpy as np
from jax import lax
from jax.experimental import pallas as pl
from jax.experimental.pallas import tpu as pltpu
from jax.sharding import PartitionSpec as P

HEADS = 24
KV_HEADS = 8
HD = 64
TOP = 8
EXP_DEV = 5
SHARE = HEADS // KV_HEADS
Q_BLOCK = 128
VMEM_BYTES = 63 * 2**20
CHUNKS = 4
COLS = 256

EPS = 1e-05
THETA = 10000.0
NEGATIVE = -1e30
F32 = jnp.float32
BF16 = jnp.bfloat16


def rope_tables(slots):
    frequency = THETA ** (-np.arange(HD // 2, dtype=np.float32) * np.float32(2.0) / HD)
    angles = np.arange(slots, dtype=np.float32)[:, None] * frequency.astype(np.float32)[None, :]
    cosine, sine = np.cos(angles), np.sin(angles)
    return (
        jnp.asarray(np.concatenate([cosine] * 4, axis=1), F32),
        jnp.asarray(np.concatenate([-sine, sine, -sine, sine], axis=1), F32),
    )


def dispatch_matrix(routes, priority, length, expert_ids, capacity):
    slots = routes.shape[0]
    positions = jnp.arange(slots, dtype=jnp.int32)
    live = positions < length
    named = jnp.any(routes[:, :, None] == expert_ids[None, None, :], axis=1) & live[:, None]
    earlier = (priority[None, :] < priority[:, None]).astype(BF16)
    slot = jnp.dot(earlier, named.astype(BF16), preferred_element_type=F32).astype(jnp.int32)
    slot = jnp.where(named, slot, capacity)
    return (
        slot.T[:, None, :] == jnp.arange(capacity, dtype=jnp.int32)[None, :, None]
    ).astype(BF16)


def shift_perm(count, shift):
    return [(i, (i + shift) % count) for i in range(count)]


def direct_gather(block):
    count = lax.axis_size("expert")
    return [block] + [
        lax.ppermute(block, "expert", shift_perm(count, k)) for k in range(1, count)
    ]


def direct_scatter(parts):
    count = lax.axis_size("expert")
    total = parts[0].astype(F32)
    for k in range(1, count):
        total = total + lax.ppermute(parts[k], "expert", shift_perm(count, -k)).astype(F32)
    return total


def line_hops(block, first=0, last=None, held=None):
    count = lax.axis_size("expert")
    last = count - 1 if last is None else last
    held_up, held_down = (block, block) if held is None else held
    up, down = [], []
    for step in range(first, last):
        held_up = lax.ppermute(
            held_up, "expert", [(i, i + 1) for i in range(step, count - 1)]
        )
        held_down = lax.ppermute(
            held_down, "expert", [(i + 1, i) for i in range(0, count - 1 - step)]
        )
        up.append(held_up)
        down.append(held_down)
    return up, down


def scatter_hops(parts, first=0, last=None, held=None):
    count = lax.axis_size("expert")
    last = count - 1 if last is None else last
    held_up, held_down = (None, None) if held is None else held
    for step in range(first, last):
        piece_up = parts[step + 1]
        piece_down = parts[count - 1 - step]
        if step:
            piece_up = piece_up.astype(F32) + held_up.astype(F32)
            piece_down = piece_down.astype(F32) + held_down.astype(F32)
        held_up = lax.ppermute(
            piece_up.astype(BF16), "expert", [(i, i + 1) for i in range(step + 1)]
        )
        held_down = lax.ppermute(
            piece_down.astype(BF16),
            "expert",
            [(i + 1, i) for i in range(count - 2 - step, count - 1)],
        )
    return held_up, held_down


def turn(values, cosine, sine):
    first = lax.broadcasted_iota(jnp.int32, (1, 2 * HD), 1) % HD < HD // 2
    out = []
    for start in range(0, values.shape[1], 2 * HD):
        part = values[:, start : start + 2 * HD]
        other = jnp.where(
            first, pltpu.roll(part, 2 * HD - HD // 2, 1), pltpu.roll(part, HD // 2, 1)
        )
        out.append(part * cosine + other * sine)
    return out[0] if len(out) == 1 else jnp.concatenate(out, axis=1)


def last_keys(block, length):
    lane = lax.broadcasted_iota(jnp.int32, (1, SHARE * Q_BLOCK), 1)
    return jnp.minimum(block * Q_BLOCK + lane % Q_BLOCK, length - 1)


def head_block(values, pair_head, block):
    rows = slice(block * Q_BLOCK, (block + 1) * Q_BLOCK)
    heads = range(pair_head * SHARE, (pair_head + 1) * SHARE)
    return jnp.concatenate([values[rows, h * HD : (h + 1) * HD] for h in heads], axis=0)


def rows_of_heads(parts):
    tall = [
        part[:, g * Q_BLOCK : (g + 1) * Q_BLOCK] for part in parts for g in range(SHARE)
    ]
    return jnp.concatenate(tall, axis=0).T


def dot_last(a, b):
    return lax.dot_general(a, b, (((1,), (1,)), ((), ())), preferred_element_type=F32)


def attend_kernel(
    length_ref, q_ref, k_ref, v_ref, cos_ref, sin_ref,
    mixed_ref, q_low_ref, k_low_ref, v_low_ref, lse_ref,
):
    length = length_ref[0]
    slots = q_ref.shape[0]
    cosine, sine = cos_ref[...], sin_ref[...]
    queries = (turn(q_ref[...], cosine, sine) * HD**-0.5).astype(BF16)
    keys = turn(k_ref[...], cosine, sine).astype(BF16)
    values = v_ref[...]
    q_low_ref[...] = queries
    k_low_ref[...] = keys
    v_low_ref[...] = values.astype(BF16)
    values_t = values.T.astype(BF16)
    blocks = slots // Q_BLOCK
    for block in range(blocks):
        span = (block + 1) * Q_BLOCK
        limit = last_keys(block, length)
        key_id = lax.broadcasted_iota(jnp.int32, (span, 1), 0)
        parts = []
        for head in range(2):
            scores = dot_last(
                keys[:span, head * HD : (head + 1) * HD], head_block(queries, head, block)
            )
            scores = jnp.where(key_id <= limit, scores, NEGATIVE)
            peak = jnp.max(scores, axis=0, keepdims=True)
            exp_scores = jnp.exp(scores - peak)
            total = jnp.sum(exp_scores, axis=0, keepdims=True)
            lse_ref[0, pl.ds(head * blocks + block, 1), :] = peak + jnp.log(total)
            part = jnp.dot(
                values_t[head * HD : (head + 1) * HD, :span],
                exp_scores.astype(BF16),
                preferred_element_type=F32,
            )
            parts.append(part / total)
        mixed_ref[block * Q_BLOCK : span, :] = rows_of_heads(parts).astype(BF16)


def attend_back_kernel(
    length_ref, q_ref, k_ref, v_ref, grad_ref, lse_ref, cos_ref, sin_ref, out_ref, dk_ref, dv_ref
):
    length = length_ref[0]
    slots, q_cols = q_ref.shape
    pairs = pl.num_programs(0)
    pair = pl.program_id(0)
    q_at = pl.ds(pl.multiple_of(pair * q_cols, 2 * HD), q_cols)
    k_at = pl.ds(pl.multiple_of(pairs * q_cols + pair * 2 * HD, 2 * HD), 2 * HD)
    v_at = pl.ds(pl.multiple_of(pairs * (q_cols + 2 * HD) + pair * 2 * HD, 2 * HD), 2 * HD)
    cosine, sine = cos_ref[...], -sin_ref[...]
    queries, keys, values = q_ref[...], k_ref[...], v_ref[...]
    grad = grad_ref[...]
    keys_t = keys.astype(F32).T.astype(BF16)
    dk_ref[...] = jnp.zeros_like(dk_ref)
    dv_ref[...] = jnp.zeros_like(dv_ref)
    blocks = slots // Q_BLOCK
    for block in range(blocks):
        rows = slice(block * Q_BLOCK, (block + 1) * Q_BLOCK)
        span = (block + 1) * Q_BLOCK
        limit = last_keys(block, length)
        key_id = lax.broadcasted_iota(jnp.int32, (span, 1), 0)
        parts = []
        for head in range(2):
            cols = slice(head * HD, (head + 1) * HD)
            query = head_block(queries, head, block)
            out_grad = head_block(grad, head, block)
            scores = dot_last(keys[:span, cols], query)
            scores = jnp.where(key_id <= limit, scores, NEGATIVE)
            probs = jnp.exp(scores - lse_ref[0, pl.ds(head * blocks + block, 1), :])
            prob_back = dot_last(values[:span, cols], out_grad)
            mean = jnp.sum(probs * prob_back, axis=0, keepdims=True)
            score_grad = (probs * (prob_back - mean)).astype(BF16)
            dv_ref[head, :span, :] += jnp.dot(
                probs.astype(BF16), out_grad, preferred_element_type=F32
            )
            dk_ref[head, :span, :] += jnp.dot(score_grad, query, preferred_element_type=F32)
            parts.append(
                jnp.dot(keys_t[cols, :span], score_grad, preferred_element_type=F32)
                * HD**-0.5
            )
        out_ref[rows, q_at] = turn(rows_of_heads(parts), cosine[rows], sine[rows]).astype(
            BF16
        )
    key_grad = jnp.concatenate([dk_ref[0], dk_ref[1]], axis=1)
    out_ref[:, k_at] = turn(key_grad, cosine, sine).astype(BF16)
    out_ref[:, v_at] = jnp.concatenate([dv_ref[0], dv_ref[1]], axis=1).astype(BF16)


def column_block(slots, columns, first=0):
    return pl.BlockSpec((slots, columns), lambda p: (0, first + p))


def attention_specs(slots):
    pairs = KV_HEADS // 2
    q_cols, cols = 2 * SHARE * HD, 2 * (SHARE + 2) * HD
    blocks = slots // Q_BLOCK
    whole = pl.BlockSpec((slots, 2 * HD), lambda p: (0, 0))
    lse = pl.BlockSpec((1, 2 * blocks, SHARE * Q_BLOCK), lambda p: (p, 0, 0))
    scalar = pl.BlockSpec(memory_space=pltpu.SMEM)
    return pairs, q_cols, cols, blocks, whole, lse, scalar


def attend(length, qkv, cosine, sine):
    slots = qkv.shape[0]
    pairs, q_cols, cols, blocks, whole, lse, scalar = attention_specs(slots)
    queries, keys = column_block(slots, q_cols), column_block(slots, 2 * HD)
    key_first = pairs * q_cols // (2 * HD)
    low_keys = jax.ShapeDtypeStruct((slots, pairs * 2 * HD), BF16)
    low_queries = jax.ShapeDtypeStruct((slots, pairs * q_cols), BF16)
    return pl.pallas_call(
        attend_kernel,
        grid=(pairs,),
        in_specs=[
            scalar,
            queries,
            column_block(slots, 2 * HD, key_first),
            column_block(slots, 2 * HD, key_first + pairs),
            whole,
            whole,
        ],
        out_specs=[queries, queries, keys, keys, lse],
        out_shape=[
            low_queries,
            low_queries,
            low_keys,
            low_keys,
            jax.ShapeDtypeStruct((pairs, 2 * blocks, SHARE * Q_BLOCK), F32),
        ],
        cost_estimate=pl.CostEstimate(
            flops=24 * HEADS * slots * slots * HD // 4, bytes_accessed=10**7, transcendentals=0
        ),
    )(length, qkv, qkv, qkv, cosine, sine)


def attend_back(length, queries, keys, values, grad, lse_rows, cosine, sine):
    slots = grad.shape[0]
    pairs, q_cols, cols, blocks, whole, lse, scalar = attention_specs(slots)
    wide, narrow = column_block(slots, q_cols), column_block(slots, 2 * HD)
    return pl.pallas_call(
        attend_back_kernel,
        grid=(pairs,),
        in_specs=[scalar, wide, narrow, narrow, wide, lse, whole, whole],
        out_specs=pl.BlockSpec((slots, pairs * cols), lambda p: (0, 0)),
        out_shape=jax.ShapeDtypeStruct((slots, pairs * cols), BF16),
        scratch_shapes=[pltpu.VMEM((2, slots, HD), F32), pltpu.VMEM((2, slots, HD), F32)],
        cost_estimate=pl.CostEstimate(
            flops=60 * HEADS * slots * slots * HD // 4, bytes_accessed=10**7, transcendentals=0
        ),
    )(length, queries, keys, values, grad, lse_rows, cosine, sine)


def stage_out(count, make, stage_ref, targets, sems):
    copies = [
        pltpu.make_async_copy(stage_ref.at[p % 2], targets(p), sems.at[p % 2])
        for p in range(count)
    ]
    for p in range(count):
        if p > 1:
            copies[p - 2].wait()
        stage_ref[p % 2] = make(p)
        copies[p].start()
    for copy in copies[-2:]:
        copy.wait()


def token_sum(spread_ref, rows_ref, place):
    capacity = rows_ref.shape[1] // spread_ref.shape[0]
    pick = spread_ref[place].reshape(EXP_DEV * capacity, -1).T
    rows = rows_ref[:, place * capacity : (place + 1) * capacity, :]
    return jnp.dot(
        pick, rows.reshape(EXP_DEV * capacity, -1), preferred_element_type=F32
    ).astype(BF16)


def expert_kernel(
    rows_ref, ups_ref, gates_ref, gate_ref, up_ref, down_ref, spread_ref,
    gated_ref, gate_grad_ref, lift_grad_ref, parts_ref, slot_ref,
    back_ref, stage_ref, sems,
):
    rows, gates = rows_ref[0], gates_ref[0]
    gate_pre = jnp.dot(rows, gate_ref[0], preferred_element_type=F32)
    lift_pre = jnp.dot(rows, up_ref[0], preferred_element_type=F32)
    act_grad = jnp.dot(ups_ref[0], down_ref[0], preferred_element_type=F32)
    sigmoid_gate = jax.nn.sigmoid(gate_pre)
    silu_gate = gate_pre * sigmoid_gate
    activated = silu_gate * lift_pre
    slot_ref[0] = jnp.sum(act_grad * activated, axis=-1, keepdims=True)
    gated_ref[0] = (activated * gates).astype(BF16)
    act_grad = act_grad * gates
    gate_pre_grad = (
        act_grad * lift_pre * (sigmoid_gate + silu_gate * (1.0 - sigmoid_gate))
    ).astype(BF16)
    lift_pre_grad = (act_grad * silu_gate).astype(BF16)
    gate_grad_ref[0] = gate_pre_grad
    lift_grad_ref[0] = lift_pre_grad
    step = pl.program_id(0)
    back_ref[step] = (
        dot_last(gate_pre_grad, gate_ref[0]) + dot_last(lift_pre_grad, up_ref[0])
    ).astype(BF16)

    @pl.when(step == pl.num_programs(0) - 1)
    def _():
        stage_out(
            spread_ref.shape[0],
            lambda p: token_sum(spread_ref, back_ref, p),
            stage_ref,
            lambda p: parts_ref.at[p],
            sems,
        )


def expert_block(*shape, first=0):
    return pl.BlockSpec((1,) + shape, lambda x: (first + x, 0, 0))


def expert_core(rows, ups, gates, both_full, down_full, spread):
    experts, total, width = ups.shape
    count, _, capacity, slots = spread.shape
    hidden = down_full.shape[-1]
    narrow, wide = expert_block(total, hidden), expert_block(total, width)
    weight, single = expert_block(width, hidden), expert_block(total, 1)
    low = jax.ShapeDtypeStruct((experts, total, hidden), BF16)
    return pl.pallas_call(
        expert_kernel,
        grid=(experts,),
        in_specs=[
            wide, wide, single,
            weight, expert_block(width, hidden, first=experts), weight,
            pl.BlockSpec(spread.shape, lambda x: (0, 0, 0, 0)),
        ],
        out_specs=[narrow, narrow, narrow, pl.BlockSpec(memory_space=pl.ANY), single],
        out_shape=[
            low,
            low,
            low,
            jax.ShapeDtypeStruct((count, slots, width), BF16),
            jax.ShapeDtypeStruct((experts, total, 1), F32),
        ],
        scratch_shapes=[
            pltpu.VMEM((experts, total, width), BF16),
            pltpu.VMEM((2, slots, width), BF16),
            pltpu.SemaphoreType.DMA((2,)),
        ],
        compiler_params=pltpu.CompilerParams(vmem_limit_bytes=VMEM_BYTES),
        cost_estimate=pl.CostEstimate(
            flops=12 * experts * total * width * hidden,
            bytes_accessed=60 * 10**6,
            transcendentals=0,
        ),
    )(rows, ups, gates, both_full, both_full, down_full, spread)


def weight_kernel(
    rows_ref, ups_ref, gated_ref, gate_grad_ref, lift_grad_ref, down_ref, out_ref, grads_ref
):
    out_ref[0] = dot_last(gated_ref[0], down_ref[0]).astype(BF16)
    rows_t = rows_ref[0].T
    grads_ref[0, 0] = jnp.dot(
        rows_t, gate_grad_ref[0], preferred_element_type=F32
    ).astype(BF16)
    grads_ref[1, 0] = jnp.dot(
        rows_t, lift_grad_ref[0], preferred_element_type=F32
    ).astype(BF16)
    grads_ref[2, 0] = jnp.dot(
        ups_ref[0].T, gated_ref[0], preferred_element_type=F32
    ).astype(BF16)


def expert_weights(rows, ups, gated, gate_grad, lift_grad, down_full):
    experts, count, width = ups.shape
    hidden = gated.shape[-1]
    narrow, wide = expert_block(count, hidden), expert_block(count, width)
    weight = expert_block(width, hidden)
    return pl.pallas_call(
        weight_kernel,
        grid=(experts,),
        in_specs=[wide, wide, narrow, narrow, narrow, weight],
        out_specs=[wide, pl.BlockSpec((3, 1, width, hidden), lambda x: (0, x, 0, 0))],
        out_shape=[
            jax.ShapeDtypeStruct((experts, count, width), BF16),
            jax.ShapeDtypeStruct((3, experts, width, hidden), BF16),
        ],
        compiler_params=pltpu.CompilerParams(vmem_limit_bytes=VMEM_BYTES),
        cost_estimate=pl.CostEstimate(
            flops=8 * experts * count * width * hidden, bytes_accessed=60 * 10**6, transcendentals=0
        ),
    )(rows, ups, gated, gate_grad, lift_grad, down_full)


def line_copy(source, target, sems, step, up, chunk):
    send_sems, recv_sems = sems
    side = 0 if up else 1
    me = lax.axis_index("expert")
    return pltpu.make_async_remote_copy(
        src_ref=source,
        dst_ref=target,
        send_sem=send_sems.at[side, step, chunk],
        recv_sem=recv_sems.at[side, step, chunk],
        device_id={"expert": me + 1 if up else me - 1},
        device_id_type=pl.DeviceIdType.MESH,
    )


def greet_line(count):
    me = lax.axis_index("expert")
    barrier = pltpu.get_barrier_semaphore()
    for up in (True, False):
        there = me < count - 1 if up else me > 0

        @pl.when(there)
        def _():
            pl.semaphore_signal(
                barrier,
                inc=1,
                device_id={"expert": me + 1 if up else me - 1},
                device_id_type=pl.DeviceIdType.MESH,
            )

    ends = (me == 0) | (me == count - 1)

    @pl.when(ends)
    def _():
        pl.semaphore_wait(barrier, 1)

    @pl.when(jnp.logical_not(ends))
    def _():
        pl.semaphore_wait(barrier, 2)


def gather_line(count, own, held, chunks, sems, work):
    me = lax.axis_index("expert")

    def after(step, up):
        return me + step < count if up else me - step >= 0

    def place(step, up):
        return step if up else count - step

    for chunk in range(chunks):
        for up in (True, False):

            @pl.when(after(1, up))
            def _():
                line_copy(own(chunk), held(place(1, up), chunk), sems, 0, up, chunk).start()

    work(0, True)
    for step in range(1, count):
        for chunk in range(chunks):
            for up in (True, False):
                here = held(place(step, up), chunk)

                @pl.when(after(step, not up))
                def _():
                    line_copy(here, here, sems, step - 1, up, chunk).wait_recv()

                if step < count - 1:

                    @pl.when(after(step, not up) & after(1, up))
                    def _():
                        there = held(place(step + 1, up), chunk)
                        line_copy(here, there, sems, step, up, chunk).start()

        for up in (True, False):

            @pl.when(after(step, not up))
            def _():
                work(place(step, up), up)

    for step in range(count - 1):
        for chunk in range(chunks):
            for up in (True, False):

                @pl.when(after(step, not up) & after(1, up))
                def _():
                    source = held(place(step, up), chunk) if step else own(chunk)
                    line_copy(
                        source, held(place(step + 1, up), chunk), sems, step, up, chunk
                    ).wait_send()


def early_kernel(count, columns, block_ref, held_ref, send_sems, recv_sems):
    greet_line(count)
    tall = block_ref.shape[0] // CHUNKS

    def rows(chunk):
        return pl.ds(chunk * tall, tall)

    gather_line(
        count,
        lambda c: block_ref.at[rows(c), pl.ds(0, columns)],
        lambda p, c: held_ref.at[p - 1, rows(c), :],
        CHUNKS,
        (send_sems, recv_sems),
        lambda place, up: None,
    )


def early_gather(block, columns):
    count = lax.axis_size("expert")
    slots = block.shape[0]
    sems = pltpu.SemaphoreType.DMA((2, count - 1, CHUNKS))
    sent = 2 * (count - 1) * slots * columns
    return pl.pallas_call(
        functools.partial(early_kernel, count, columns),
        in_specs=[pl.BlockSpec(memory_space=pltpu.VMEM)],
        out_specs=pl.BlockSpec(memory_space=pl.ANY),
        out_shape=jax.ShapeDtypeStruct((count - 1, slots, columns), BF16),
        scratch_shapes=[sems, sems],
        compiler_params=pltpu.CompilerParams(
            collective_id=1, has_side_effects=True, vmem_limit_bytes=VMEM_BYTES
        ),
        cost_estimate=pl.CostEstimate(flops=0, bytes_accessed=40 * sent, transcendentals=0),
    )(block)


def dispatch_kernel(count, normed_ref, block_ref, early_ref, spread_ref, *refs):
    late_up, late_down = refs[: count - 1], refs[count - 1 : 2 * (count - 1)]
    rows_ref, ups_ref, held_ref, send_sems, recv_sems = refs[2 * (count - 1) :]
    greet_line(count)
    tall = normed_ref.shape[0] // CHUNKS
    capacity = rows_ref.shape[1] // count
    columns = early_ref.shape[-1]

    def cut(chunk):
        return pl.ds(chunk * tall, tall)

    def work(place, up):
        if place:
            late = late_up[place - 1] if up else late_down[count - place - 1]
            source = held_ref[place - 1]
            grads = [early_ref[place - 1], late[...]]
        else:
            source = normed_ref[...]
            grads = [block_ref[:, :columns], block_ref[:, columns:]]
        at = slice(place * capacity, (place + 1) * capacity)
        for expert in range(EXP_DEV):
            pick = spread_ref[place, expert]
            taken = [
                jnp.dot(pick, s, preferred_element_type=F32).astype(BF16)
                for s in [source] + grads
            ]
            rows_ref[expert, at, :] = taken[0]
            ups_ref[expert, at, :columns] = taken[1]
            ups_ref[expert, at, columns:] = taken[2]

    gather_line(
        count,
        lambda c: normed_ref.at[cut(c), :],
        lambda p, c: held_ref.at[p - 1, cut(c), :],
        CHUNKS,
        (send_sems, recv_sems),
        work,
    )


def gather_dispatch(normed, block, early, late_up, late_down, spread):
    count = lax.axis_size("expert")
    slots, width = normed.shape
    capacity = spread.shape[2]
    vmem = pl.BlockSpec(memory_space=pltpu.VMEM)
    sems = pltpu.SemaphoreType.DMA((2, count - 1, CHUNKS))
    sent = 2 * (count - 1) * slots * width
    rows = jax.ShapeDtypeStruct((EXP_DEV, count * capacity, width), BF16)
    return pl.pallas_call(
        functools.partial(dispatch_kernel, count),
        in_specs=[vmem] * (4 + 2 * (count - 1)),
        out_specs=[vmem] * 2,
        out_shape=[rows, rows],
        scratch_shapes=[pltpu.VMEM((count - 1, slots, width), BF16), sems, sems],
        compiler_params=pltpu.CompilerParams(
            collective_id=0, has_side_effects=True, vmem_limit_bytes=VMEM_BYTES
        ),
        cost_estimate=pl.CostEstimate(flops=0, bytes_accessed=40 * sent, transcendentals=0),
    )(normed, block, early, spread, *late_up, *late_down)


def sum_line(count, own, held, out, sems, fill):
    me = lax.axis_index("expert")

    def after(step, up):
        return me + step < count if up else me - step >= 0

    for step in range(count - 1, 0, -1):
        if step == count - 2:
            fill()
        for chunk in range(CHUNKS):
            for up in (True, False):
                there = held(step - 1, up, chunk)

                @pl.when(after(step, up) & jnp.logical_not(after(1, not up)))
                def _():
                    line_copy(own(step, up, chunk), there, sems, step - 1, up, chunk).start()

                if step < count - 1:
                    here = held(step, up, chunk)

                    @pl.when(after(step, up) & after(1, not up))
                    def _():
                        line_copy(here, here, sems, step, up, chunk).wait_recv()
                        here[...] = (
                            here[...].astype(F32) + own(step, up, chunk)[...].astype(F32)
                        ).astype(BF16)
                        line_copy(here, there, sems, step - 1, up, chunk).start()

    for chunk in range(CHUNKS):
        result = out(chunk)
        result[...] = own(0, True, chunk)[...].astype(F32)
        for up in (True, False):
            here = held(0, up, chunk)

            @pl.when(after(1, not up))
            def _():
                line_copy(here, here, sems, 0, up, chunk).wait_recv()
                result[...] += here[...].astype(F32)

    for step in range(count - 1, 0, -1):
        for chunk in range(CHUNKS):
            for up in (True, False):

                @pl.when(after(step, up))
                def _():
                    source = own(step, up, chunk)
                    line_copy(
                        source, held(step - 1, up, chunk), sems, step - 1, up, chunk
                    ).wait_send()


def sum_kernel(count, parts_ref, produced_ref, spread_ref, out_ref, *refs):
    produced_out = refs[:count]
    held_ref, stage_ref, stage_sems, send_sems, recv_sems = refs[count:]
    greet_line(count)
    tall = out_ref.shape[0] // CHUNKS

    def cut(chunk):
        return pl.ds(chunk * tall, tall)

    sum_line(
        count,
        lambda step, up, c: parts_ref.at[(count - step) % count if up else step, cut(c), :],
        lambda step, up, c: held_ref.at[0 if up else 1, step, cut(c), :],
        lambda c: out_ref.at[cut(c), :],
        (send_sems, recv_sems),
        lambda: stage_out(
            count,
            lambda p: token_sum(spread_ref, produced_ref, p),
            stage_ref,
            lambda p: produced_out[p],
            stage_sems,
        ),
    )


def line_sum(parts, produced, spread):
    count, slots, width = parts.shape
    vmem = pl.BlockSpec(memory_space=pltpu.VMEM)
    sems = pltpu.SemaphoreType.DMA((2, count - 1, CHUNKS))
    total, *produced = pl.pallas_call(
        functools.partial(sum_kernel, count),
        in_specs=[vmem] * 3,
        out_specs=[vmem] + [pl.BlockSpec(memory_space=pl.ANY)] * count,
        out_shape=[jax.ShapeDtypeStruct((slots, width), F32)]
        + [jax.ShapeDtypeStruct((slots, width), BF16)] * count,
        scratch_shapes=[
            pltpu.VMEM((2, count - 1, slots, width), BF16),
            pltpu.VMEM((2, slots, width), BF16),
            pltpu.SemaphoreType.DMA((2,)),
            sems,
            sems,
        ],
        compiler_params=pltpu.CompilerParams(
            collective_id=2, has_side_effects=True, vmem_limit_bytes=VMEM_BYTES
        ),
        cost_estimate=pl.CostEstimate(
            flops=0, bytes_accessed=80 * (count - 1) * slots * width, transcendentals=0
        ),
    )(parts, produced, spread)
    return total, produced


def last_kernel(count, parts_ref, out_ref, held_ref, send_sems, recv_sems):
    greet_line(count)
    me = lax.axis_index("expert")
    planes = out_ref.shape[0]
    edges = [planes * c // CHUNKS for c in range(CHUNKS + 1)]

    def cut(chunk):
        return pl.ds(edges[chunk], edges[chunk + 1] - edges[chunk])

    sum_line(
        count,
        lambda step, up, c: parts_ref.at[cut(c), me + step if up else me - step],
        lambda step, up, c: held_ref.at[0 if up else 1, step, cut(c)],
        lambda c: out_ref.at[cut(c)],
        (send_sems, recv_sems),
        lambda: None,
    )


def last_sum(parts):
    planes, count, rows, columns = parts.shape
    vmem = pl.BlockSpec(memory_space=pltpu.VMEM)
    sems = pltpu.SemaphoreType.DMA((2, count - 1, CHUNKS))
    return pl.pallas_call(
        functools.partial(last_kernel, count),
        in_specs=[vmem],
        out_specs=vmem,
        out_shape=jax.ShapeDtypeStruct((planes, rows, columns), F32),
        scratch_shapes=[pltpu.VMEM((2, count - 1, planes, rows, columns), BF16), sems, sems],
        compiler_params=pltpu.CompilerParams(
            collective_id=3, has_side_effects=True, vmem_limit_bytes=VMEM_BYTES
        ),
        cost_estimate=pl.CostEstimate(
            flops=0, bytes_accessed=80 * parts.size, transcendentals=0
        ),
    )(parts)


def projection_kernel(mixed_ref, normed_ref, merge_ref, qkv_ref, side_ref, out_ref, turned_ref):
    step = pl.program_id(0)
    merge_steps = mixed_ref.shape[1] // COLS
    steps = pl.num_programs(0)

    @pl.when(step == 0)
    def _():
        turned_ref[...] = mixed_ref[...].T

    @pl.when(step == merge_steps)
    def _():
        turned_ref[...] = normed_ref[...].T

    @pl.when(step < merge_steps)
    def _():
        out_ref[0] = jnp.dot(
            turned_ref[...], merge_ref[...], preferred_element_type=F32
        ).astype(BF16)

    @pl.when((step >= merge_steps) & (step < steps - 1))
    def _():
        out_ref[0] = jnp.dot(
            turned_ref[...], qkv_ref[...], preferred_element_type=F32
        ).astype(BF16)

    @pl.when(step == steps - 1)
    def _():
        out_ref[0] = side_ref[...]


def projection_terms(mixed, normed, attended_grad, qkv_grad, side):
    slots, width = mixed.shape
    first, second = attended_grad.shape[1] // COLS, qkv_grad.shape[1] // COLS
    whole = pl.BlockSpec((slots, width), lambda j: (0, 0))
    return pl.pallas_call(
        projection_kernel,
        grid=(first + second + 1,),
        in_specs=[
            whole,
            whole,
            pl.BlockSpec((slots, COLS), lambda j: (0, jnp.minimum(j, first - 1))),
            pl.BlockSpec((slots, COLS), lambda j: (0, jnp.clip(j - first, 0, second - 1))),
            pl.BlockSpec((width, COLS), lambda j: (0, 0)),
        ],
        out_specs=pl.BlockSpec((1, width, COLS), lambda j: (j, 0, 0)),
        out_shape=jax.ShapeDtypeStruct((first + second + 1, width, COLS), BF16),
        scratch_shapes=[pltpu.VMEM((width, slots), BF16)],
        cost_estimate=pl.CostEstimate(
            flops=2 * slots * width * (first + second) * COLS,
            bytes_accessed=2 * 10**7,
            transcendentals=0,
        ),
    )(mixed, normed, attended_grad, qkv_grad, side)


def body(
    tokens,
    lengths,
    routes,
    priority,
    first_gain,
    query_weight,
    key_weight,
    value_weight,
    merge_weight,
    router_weight,
    second_gain,
    gate_weight,
    up_weight,
    down_weight,
    cotangent,
):
    slots = tokens.shape[1]
    width = tokens.shape[2]
    groups = lax.axis_size("expert")
    expert_count = router_weight.shape[1]
    capacity = 5 * slots * TOP // (8 * expert_count)
    q_cols, k_cols = HEADS * HD, KV_HEADS * HD
    side_cols = 128

    def gather_shard(value, axis=0):
        return lax.all_gather(value, "shard", axis=axis, tiled=True)

    def scatter_all(part, ahead=None):
        planes, _, columns = part.shape
        part = lax.psum_scatter(
            part.reshape(planes * groups, -1, columns), "shard", scatter_dimension=1, tiled=True
        ).reshape(planes, groups, -1, columns)
        part, ahead = lax.optimization_barrier((part, ahead))
        return last_sum(part), ahead

    side = jnp.concatenate(
        [router_weight, first_gain[:, None], second_gain[:, None]], axis=1
    )
    side = jnp.pad(side, ((0, 0), (0, side_cols - expert_count - 2)))
    first_set = gather_shard(
        jnp.concatenate([query_weight, key_weight, value_weight, side], axis=1)
    )
    merge_full = gather_shard(merge_weight)
    tables = jnp.concatenate(
        [routes[0].T, priority, jnp.broadcast_to(lengths[:, None], (1, slots))], axis=0
    )
    tables = jnp.stack(direct_gather(tables)).transpose(0, 2, 1)
    mid = groups // 2
    early_columns = 7 * width // 12
    early = early_gather(cotangent[0], early_columns)
    late_block, tokens, gate_weight, tables, early = lax.optimization_barrier(
        (cotangent[0][:, early_columns:], tokens, gate_weight, tables, early)
    )
    late_up, late_down = line_hops(late_block, 0, 1)
    both_full = gather_shard(jnp.concatenate([gate_weight, up_weight], axis=0), 1)
    down_full = gather_shard(down_weight, 1)

    group = lax.axis_index("expert")
    own_experts = group * EXP_DEV + jnp.arange(EXP_DEV, dtype=jnp.int32)
    spread = jax.vmap(
        lambda t: dispatch_matrix(t[:, :TOP], t[:, TOP], t[0, TOP + 1], own_experts, capacity)
    )(tables)

    qkv_full = first_set[:, : q_cols + 2 * k_cols]
    side_full = first_set[:, q_cols + 2 * k_cols :]
    router_full = side_full[:, :expert_count]
    gain_first = side_full[:, expert_count].astype(F32)
    gain_second = side_full[:, expert_count + 1].astype(F32)

    inputs = tokens[0].astype(F32)
    length = lengths[0]
    positions = jnp.arange(slots, dtype=jnp.int32)
    live_rows = (positions < length).astype(F32)[:, None]
    cosine, sine_table = rope_tables(slots)
    rms_one = lax.rsqrt(jnp.mean(inputs * inputs, axis=-1, keepdims=True) + EPS)
    unit_one = inputs * rms_one
    normed_one = (unit_one * gain_first).astype(BF16)
    qkv = jnp.dot(normed_one, qkv_full, preferred_element_type=F32)
    qkv, late_up, late_down = lax.optimization_barrier((qkv, late_up, late_down))
    next_up, next_down = line_hops(late_block, 1, 2, (late_up[-1], late_down[-1]))
    mixed, *low_parts, lse = attend(lengths, qkv, cosine, sine_table)
    mixed, next_up, next_down = lax.optimization_barrier((mixed, next_up, next_down))
    last_up, last_down = line_hops(late_block, 2, held=(next_up[-1], next_down[-1]))
    late_up, late_down = late_up + next_up + last_up, late_down + next_down + last_down
    attended = jnp.dot(mixed, merge_full, preferred_element_type=F32)
    hidden = inputs + live_rows * attended
    rms_two = lax.rsqrt(jnp.mean(hidden * hidden, axis=-1, keepdims=True) + EPS)
    unit_two = hidden * rms_two
    normed_two = (unit_two * gain_second).astype(BF16)

    logits = jnp.dot(normed_two, router_full, preferred_element_type=F32)
    chosen = (
        routes[0][:, :, None] == jnp.arange(expert_count, dtype=jnp.int32)[None, None, :]
    ).astype(F32)
    chosen_any = jnp.sum(chosen, axis=1)
    masked = jnp.where(chosen_any > 0, logits, NEGATIVE)
    peak = jnp.max(masked, axis=-1, keepdims=True)
    exp_logits = jnp.exp(masked - peak) * chosen_any
    gate_dense = exp_logits / jnp.sum(exp_logits, axis=-1, keepdims=True)

    gates_all = direct_gather(gate_dense.T)
    rows, ups = gather_dispatch(
        normed_two, cotangent[0], early, late_up, late_down, spread
    )
    gates_all, rows = lax.optimization_barrier((gates_all, rows))
    gates_all = jnp.stack(gates_all)
    gates_own = lax.dynamic_slice_in_dim(gates_all, group * EXP_DEV, EXP_DEV, axis=1)
    slot_gate = jnp.sum(spread.astype(F32) * gates_own[:, :, None, :], axis=-1)
    gates = slot_gate.transpose(1, 0, 2).reshape(EXP_DEV, groups * capacity, 1)

    gated, gate_pre_grad, lift_pre_grad, back_parts, slot_grad = expert_core(
        rows, ups, gates, both_full, down_full, spread
    )

    slot_grad = slot_grad.reshape(EXP_DEV, groups, capacity).transpose(1, 0, 2)
    token_grad = jnp.sum(spread.astype(F32) * slot_grad[:, :, :, None], axis=2)
    token_grad = lax.dynamic_update_slice_in_dim(
        jnp.zeros((groups, expert_count, slots), F32), token_grad, group * EXP_DEV, axis=1
    )
    slot_back = direct_scatter([token_grad[p] for p in range(groups)]).T
    produced, expert_grads = expert_weights(
        rows, ups, gated, gate_pre_grad, lift_pre_grad, down_full
    )
    back_parts, expert_grads = lax.optimization_barrier((back_parts, expert_grads))
    back_total, produced = line_sum(back_parts, produced, spread)
    expert_grads = lax.psum_scatter(
        expert_grads.reshape(3 * EXP_DEV, width, -1), "shard", scatter_dimension=1, tiled=True
    )
    sums = scatter_hops(produced, 0, 1)

    upstream = cotangent[0].astype(F32)
    picked_grad = gate_dense * (
        slot_back - jnp.sum(gate_dense * slot_back, axis=-1, keepdims=True)
    )
    logit_grad = picked_grad.astype(BF16)
    router_part = jnp.einsum("ld,le->de", normed_two, logit_grad, preferred_element_type=F32)
    normed_two_grad = jnp.einsum("le,de->ld", logit_grad, router_full, preferred_element_type=F32)
    normed_two_grad = normed_two_grad + back_total
    scaled_two = normed_two_grad * gain_second
    second_gain_part = jnp.sum(normed_two_grad * unit_two, axis=0)
    hidden_grad = upstream + rms_two * (
        scaled_two - unit_two * jnp.mean(scaled_two * unit_two, axis=-1, keepdims=True)
    )
    attended_grad = (live_rows * hidden_grad).astype(BF16)

    mixed_grad = jnp.einsum(
        "ld,hd->lh", attended_grad, merge_full, preferred_element_type=F32
    ).astype(BF16)
    qkv_grad = attend_back(lengths, *low_parts, mixed_grad, lse, cosine, sine_table)
    sums, qkv_grad = lax.optimization_barrier((sums, qkv_grad))
    sums = scatter_hops(produced, 1, mid, sums)
    side_part = jnp.concatenate([router_part, second_gain_part[:, None]], axis=1)
    side_part = jnp.pad(side_part, ((0, 0), (0, COLS - expert_count - 1))).astype(BF16)
    terms = projection_terms(mixed, normed_one, attended_grad, qkv_grad, side_part)
    terms, expert_grads, sums = lax.optimization_barrier((terms, expert_grads, sums))
    sums = scatter_hops(produced, mid, groups - 1, sums)
    normed_one_grad = jnp.einsum("lh,dh->ld", qkv_grad, qkv_full, preferred_element_type=F32)
    scaled_one = normed_one_grad * gain_first
    input_grad = hidden_grad + rms_one * (
        scaled_one - unit_one * jnp.mean(scaled_one * unit_one, axis=-1, keepdims=True)
    )
    block_output = (
        hidden + produced[0].astype(F32) + sums[0].astype(F32) + sums[1].astype(F32)
    )
    gate_grad, up_grad, down_grad = jnp.split(expert_grads.astype(F32), 3)
    reduced, (block_output, input_grad) = scatter_all(terms, (block_output, input_grad))
    own_rows = reduced.shape[1]
    reduced = reduced.transpose(1, 0, 2).reshape(own_rows, -1)
    place = (group * lax.axis_size("shard") + lax.axis_index("shard")) * own_rows
    merge_grad, qkv_reduced, side_grad = jnp.split(
        reduced, [width, width + q_cols + 2 * k_cols], axis=1
    )
    own_weights = lax.dynamic_slice_in_dim(qkv_full, place, own_rows, axis=0).astype(F32)
    own_gain = lax.dynamic_slice_in_dim(gain_first, place, own_rows)
    first_gain_grad = jnp.sum(own_weights * qkv_reduced, axis=1) / own_gain
    query_grad, key_grad, value_grad = jnp.split(qkv_reduced, [q_cols, q_cols + k_cols], axis=1)
    return (
        block_output[None],
        input_grad[None],
        first_gain_grad,
        query_grad,
        key_grad,
        value_grad,
        merge_grad,
        side_grad[:, :expert_count],
        side_grad[:, expert_count],
        gate_grad,
        up_grad,
        down_grad,
    )


def solution(mesh):
    both = ("expert", "shard")
    in_specs = (
        P(both, None, None),
        P(both),
        P(both, None, None),
        P(both, None),
        P("shard"),
        P("shard", None),
        P("shard", None),
        P("shard", None),
        P("shard", None),
        P("shard", None),
        P("shard"),
        P("expert", "shard", None),
        P("expert", "shard", None),
        P("expert", "shard", None),
        P(both, None, None),
    )
    out_specs = (
        P(both, None, None),
        P(both, None, None),
        P(both),
        P(both, None),
        P(both, None),
        P(both, None),
        P(both, None),
        P(both, None),
        P(both),
        P("expert", "shard", None),
        P("expert", "shard", None),
        P("expert", "shard", None),
    )
    return jax.shard_map(body, mesh=mesh, in_specs=in_specs, out_specs=out_specs, check_vma=False)
```

```python
import functools

import jax
import jax.numpy as jnp
import numpy as np
from jax import lax
from jax.experimental import pallas as pl
from jax.experimental.pallas import tpu as pltpu
from jax.sharding import PartitionSpec as P

HEADS = 24
KV_HEADS = 8
HD = 64
TOP = 8
EXP_DEV = 5
SHARE = HEADS // KV_HEADS
Q_BLOCK = 128
VMEM_BYTES = 63 * 2**20
CHUNKS = 4
COLS = 256

EPS = 1e-05
THETA = 10000.0
NEGATIVE = -1e30
F32 = jnp.float32
BF16 = jnp.bfloat16


def rope_tables(slots):
    frequency = THETA ** (-np.arange(HD // 2, dtype=np.float32) * np.float32(2.0) / HD)
    angles = np.arange(slots, dtype=np.float32)[:, None] * frequency.astype(np.float32)[None, :]
    cosine, sine = np.cos(angles), np.sin(angles)
    return (
        jnp.asarray(np.concatenate([cosine] * 4, axis=1), F32),
        jnp.asarray(np.concatenate([-sine, sine, -sine, sine], axis=1), F32),
    )


def dispatch_matrix(routes, priority, length, expert_ids, capacity):
    slots = routes.shape[0]
    positions = jnp.arange(slots, dtype=jnp.int32)
    live = positions < length
    named = jnp.any(routes[:, :, None] == expert_ids[None, None, :], axis=1) & live[:, None]
    earlier = (priority[None, :] < priority[:, None]).astype(BF16)
    slot = jnp.dot(earlier, named.astype(BF16), preferred_element_type=F32).astype(jnp.int32)
    slot = jnp.where(named, slot, capacity)
    return (
        slot.T[:, None, :] == jnp.arange(capacity, dtype=jnp.int32)[None, :, None]
    ).astype(BF16)


def shift_perm(count, shift):
    return [(i, (i + shift) % count) for i in range(count)]


def direct_scatter(parts):
    count = lax.axis_size("expert")
    total = parts[0].astype(F32)
    for k in range(1, count):
        total = total + lax.ppermute(parts[k], "expert", shift_perm(count, -k)).astype(F32)
    return total


def line_hops(block, first=0, last=None, held=None):
    count = lax.axis_size("expert")
    last = count - 1 if last is None else last
    held_up, held_down = (block, block) if held is None else held
    up, down = [], []
    for step in range(first, last):
        held_up = lax.ppermute(
            held_up, "expert", [(i, i + 1) for i in range(step, count - 1)]
        )
        held_down = lax.ppermute(
            held_down, "expert", [(i + 1, i) for i in range(0, count - 1 - step)]
        )
        up.append(held_up)
        down.append(held_down)
    return up, down


def scatter_hops(parts, first=0, last=None, held=None):
    count = lax.axis_size("expert")
    last = count - 1 if last is None else last
    held_up, held_down = (None, None) if held is None else held
    for step in range(first, last):
        piece_up = parts[step + 1]
        piece_down = parts[count - 1 - step]
        if step:
            piece_up = piece_up.astype(F32) + held_up.astype(F32)
            piece_down = piece_down.astype(F32) + held_down.astype(F32)
        held_up = lax.ppermute(
            piece_up.astype(BF16), "expert", [(i, i + 1) for i in range(step + 1)]
        )
        held_down = lax.ppermute(
            piece_down.astype(BF16),
            "expert",
            [(i + 1, i) for i in range(count - 2 - step, count - 1)],
        )
    return held_up, held_down


def turn(values, cosine, sine):
    first = lax.broadcasted_iota(jnp.int32, (1, 2 * HD), 1) % HD < HD // 2
    out = []
    for start in range(0, values.shape[1], 2 * HD):
        part = values[:, start : start + 2 * HD]
        other = jnp.where(
            first, pltpu.roll(part, 2 * HD - HD // 2, 1), pltpu.roll(part, HD // 2, 1)
        )
        out.append(part * cosine + other * sine)
    return out[0] if len(out) == 1 else jnp.concatenate(out, axis=1)


def last_keys(block, length):
    lane = lax.broadcasted_iota(jnp.int32, (1, SHARE * Q_BLOCK), 1)
    return jnp.minimum(block * Q_BLOCK + lane % Q_BLOCK, length - 1)


def head_block(values, pair_head, block):
    rows = slice(block * Q_BLOCK, (block + 1) * Q_BLOCK)
    heads = range(pair_head * SHARE, (pair_head + 1) * SHARE)
    return jnp.concatenate([values[rows, h * HD : (h + 1) * HD] for h in heads], axis=0)


def rows_of_heads(parts):
    tall = [
        part[:, g * Q_BLOCK : (g + 1) * Q_BLOCK] for part in parts for g in range(SHARE)
    ]
    return jnp.concatenate(tall, axis=0).T


def dot_last(a, b):
    return lax.dot_general(a, b, (((1,), (1,)), ((), ())), preferred_element_type=F32)


def attend_kernel(
    length_ref, q_ref, k_ref, v_ref, cos_ref, sin_ref,
    mixed_ref, q_low_ref, k_low_ref, v_low_ref, lse_ref,
):
    length = length_ref[0]
    slots = q_ref.shape[0]
    cosine, sine = cos_ref[...], sin_ref[...]
    queries = (turn(q_ref[...], cosine, sine) * HD**-0.5).astype(BF16)
    keys = turn(k_ref[...], cosine, sine).astype(BF16)
    values = v_ref[...]
    q_low_ref[...] = queries
    k_low_ref[...] = keys
    v_low_ref[...] = values.astype(BF16)
    values_t = values.T.astype(BF16)
    blocks = slots // Q_BLOCK
    for block in range(blocks):
        span = (block + 1) * Q_BLOCK
        limit = last_keys(block, length)
        key_id = lax.broadcasted_iota(jnp.int32, (span, 1), 0)
        parts = []
        for head in range(2):
            scores = dot_last(
                keys[:span, head * HD : (head + 1) * HD], head_block(queries, head, block)
            )
            scores = jnp.where(key_id <= limit, scores, NEGATIVE)
            peak = jnp.max(scores, axis=0, keepdims=True)
            exp_scores = jnp.exp(scores - peak)
            total = jnp.sum(exp_scores, axis=0, keepdims=True)
            lse_ref[0, pl.ds(head * blocks + block, 1), :] = peak + jnp.log(total)
            part = jnp.dot(
                values_t[head * HD : (head + 1) * HD, :span],
                exp_scores.astype(BF16),
                preferred_element_type=F32,
            )
            parts.append(part / total)
        mixed_ref[block * Q_BLOCK : span, :] = rows_of_heads(parts).astype(BF16)


def attend_back_kernel(
    length_ref, q_ref, k_ref, v_ref, grad_ref, lse_ref, cos_ref, sin_ref, out_ref, dk_ref, dv_ref
):
    length = length_ref[0]
    slots, q_cols = q_ref.shape
    pairs = pl.num_programs(0)
    pair = pl.program_id(0)
    q_at = pl.ds(pl.multiple_of(pair * q_cols, 2 * HD), q_cols)
    k_at = pl.ds(pl.multiple_of(pairs * q_cols + pair * 2 * HD, 2 * HD), 2 * HD)
    v_at = pl.ds(pl.multiple_of(pairs * (q_cols + 2 * HD) + pair * 2 * HD, 2 * HD), 2 * HD)
    cosine, sine = cos_ref[...], -sin_ref[...]
    queries, keys, values = q_ref[...], k_ref[...], v_ref[...]
    grad = grad_ref[...]
    keys_t = keys.astype(F32).T.astype(BF16)
    dk_ref[...] = jnp.zeros_like(dk_ref)
    dv_ref[...] = jnp.zeros_like(dv_ref)
    blocks = slots // Q_BLOCK
    for block in range(blocks):
        rows = slice(block * Q_BLOCK, (block + 1) * Q_BLOCK)
        span = (block + 1) * Q_BLOCK
        limit = last_keys(block, length)
        key_id = lax.broadcasted_iota(jnp.int32, (span, 1), 0)
        parts = []
        for head in range(2):
            cols = slice(head * HD, (head + 1) * HD)
            query = head_block(queries, head, block)
            out_grad = head_block(grad, head, block)
            scores = dot_last(keys[:span, cols], query)
            scores = jnp.where(key_id <= limit, scores, NEGATIVE)
            probs = jnp.exp(scores - lse_ref[0, pl.ds(head * blocks + block, 1), :])
            prob_back = dot_last(values[:span, cols], out_grad)
            mean = jnp.sum(probs * prob_back, axis=0, keepdims=True)
            score_grad = (probs * (prob_back - mean)).astype(BF16)
            dv_ref[head, :span, :] += jnp.dot(
                probs.astype(BF16), out_grad, preferred_element_type=F32
            )
            dk_ref[head, :span, :] += jnp.dot(score_grad, query, preferred_element_type=F32)
            parts.append(
                jnp.dot(keys_t[cols, :span], score_grad, preferred_element_type=F32)
                * HD**-0.5
            )
        out_ref[rows, q_at] = turn(rows_of_heads(parts), cosine[rows], sine[rows]).astype(
            BF16
        )
    key_grad = jnp.concatenate([dk_ref[0], dk_ref[1]], axis=1)
    out_ref[:, k_at] = turn(key_grad, cosine, sine).astype(BF16)
    out_ref[:, v_at] = jnp.concatenate([dv_ref[0], dv_ref[1]], axis=1).astype(BF16)


def column_block(slots, columns, first=0):
    return pl.BlockSpec((slots, columns), lambda p: (0, first + p))


def attention_specs(slots):
    pairs = KV_HEADS // 2
    q_cols, cols = 2 * SHARE * HD, 2 * (SHARE + 2) * HD
    blocks = slots // Q_BLOCK
    whole = pl.BlockSpec((slots, 2 * HD), lambda p: (0, 0))
    lse = pl.BlockSpec((1, 2 * blocks, SHARE * Q_BLOCK), lambda p: (p, 0, 0))
    scalar = pl.BlockSpec(memory_space=pltpu.SMEM)
    return pairs, q_cols, cols, blocks, whole, lse, scalar


def attend(length, qkv, cosine, sine):
    slots = qkv.shape[0]
    pairs, q_cols, cols, blocks, whole, lse, scalar = attention_specs(slots)
    queries, keys = column_block(slots, q_cols), column_block(slots, 2 * HD)
    key_first = pairs * q_cols // (2 * HD)
    low_keys = jax.ShapeDtypeStruct((slots, pairs * 2 * HD), BF16)
    low_queries = jax.ShapeDtypeStruct((slots, pairs * q_cols), BF16)
    return pl.pallas_call(
        attend_kernel,
        grid=(pairs,),
        in_specs=[
            scalar,
            queries,
            column_block(slots, 2 * HD, key_first),
            column_block(slots, 2 * HD, key_first + pairs),
            whole,
            whole,
        ],
        out_specs=[queries, queries, keys, keys, lse],
        out_shape=[
            low_queries,
            low_queries,
            low_keys,
            low_keys,
            jax.ShapeDtypeStruct((pairs, 2 * blocks, SHARE * Q_BLOCK), F32),
        ],
        cost_estimate=pl.CostEstimate(
            flops=24 * HEADS * slots * slots * HD // 4, bytes_accessed=10**7, transcendentals=0
        ),
    )(length, qkv, qkv, qkv, cosine, sine)


def attend_back(length, queries, keys, values, grad, lse_rows, cosine, sine):
    slots = grad.shape[0]
    pairs, q_cols, cols, blocks, whole, lse, scalar = attention_specs(slots)
    wide, narrow = column_block(slots, q_cols), column_block(slots, 2 * HD)
    return pl.pallas_call(
        attend_back_kernel,
        grid=(pairs,),
        in_specs=[scalar, wide, narrow, narrow, wide, lse, whole, whole],
        out_specs=pl.BlockSpec((slots, pairs * cols), lambda p: (0, 0)),
        out_shape=jax.ShapeDtypeStruct((slots, pairs * cols), BF16),
        scratch_shapes=[pltpu.VMEM((2, slots, HD), F32), pltpu.VMEM((2, slots, HD), F32)],
        cost_estimate=pl.CostEstimate(
            flops=60 * HEADS * slots * slots * HD // 4, bytes_accessed=10**7, transcendentals=0
        ),
    )(length, queries, keys, values, grad, lse_rows, cosine, sine)


def stage_out(count, make, stage_ref, targets, sems):
    copies = [
        pltpu.make_async_copy(stage_ref.at[p % 2], targets(p), sems.at[p % 2])
        for p in range(count)
    ]
    for p in range(count):
        if p > 1:
            copies[p - 2].wait()
        stage_ref[p % 2] = make(p)
        copies[p].start()
    for copy in copies[-2:]:
        copy.wait()


def token_sum(spread_ref, rows_ref, place):
    capacity = rows_ref.shape[1] // spread_ref.shape[0]
    pick = spread_ref[place].reshape(EXP_DEV * capacity, -1).T
    rows = rows_ref[:, place * capacity : (place + 1) * capacity, :]
    return jnp.dot(
        pick, rows.reshape(EXP_DEV * capacity, -1), preferred_element_type=F32
    ).astype(BF16)


def expert_kernel(
    rows_ref, ups_ref, gates_ref, gate_ref, up_ref, down_ref, spread_ref,
    gated_ref, gate_grad_ref, lift_grad_ref, parts_ref, slot_ref,
    back_ref, stage_ref, sems,
):
    rows, gates = rows_ref[0], gates_ref[0]
    gate_pre = jnp.dot(rows, gate_ref[0], preferred_element_type=F32)
    lift_pre = jnp.dot(rows, up_ref[0], preferred_element_type=F32)
    act_grad = jnp.dot(ups_ref[0], down_ref[0], preferred_element_type=F32)
    sigmoid_gate = jax.nn.sigmoid(gate_pre)
    silu_gate = gate_pre * sigmoid_gate
    activated = silu_gate * lift_pre
    slot_ref[0] = jnp.sum(act_grad * activated, axis=-1, keepdims=True)
    gated_ref[0] = (activated * gates).astype(BF16)
    act_grad = act_grad * gates
    gate_pre_grad = (
        act_grad * lift_pre * (sigmoid_gate + silu_gate * (1.0 - sigmoid_gate))
    ).astype(BF16)
    lift_pre_grad = (act_grad * silu_gate).astype(BF16)
    gate_grad_ref[0] = gate_pre_grad
    lift_grad_ref[0] = lift_pre_grad
    step = pl.program_id(0)
    back_ref[step] = (
        dot_last(gate_pre_grad, gate_ref[0]) + dot_last(lift_pre_grad, up_ref[0])
    ).astype(BF16)

    @pl.when(step == pl.num_programs(0) - 1)
    def _():
        stage_out(
            spread_ref.shape[0],
            lambda p: token_sum(spread_ref, back_ref, p),
            stage_ref,
            lambda p: parts_ref.at[p],
            sems,
        )


def expert_block(*shape, first=0):
    return pl.BlockSpec((1,) + shape, lambda x: (first + x, 0, 0))


def expert_core(rows, ups, gates, both_full, down_full, spread):
    experts, total, width = ups.shape
    count, _, capacity, slots = spread.shape
    hidden = down_full.shape[-1]
    narrow, wide = expert_block(total, hidden), expert_block(total, width)
    weight, single = expert_block(width, hidden), expert_block(total, 1)
    low = jax.ShapeDtypeStruct((experts, total, hidden), BF16)
    return pl.pallas_call(
        expert_kernel,
        grid=(experts,),
        in_specs=[
            wide, wide, single,
            weight, expert_block(width, hidden, first=experts), weight,
            pl.BlockSpec(spread.shape, lambda x: (0, 0, 0, 0)),
        ],
        out_specs=[narrow, narrow, narrow, pl.BlockSpec(memory_space=pl.ANY), single],
        out_shape=[
            low,
            low,
            low,
            jax.ShapeDtypeStruct((count, slots, width), BF16),
            jax.ShapeDtypeStruct((experts, total, 1), F32),
        ],
        scratch_shapes=[
            pltpu.VMEM((experts, total, width), BF16),
            pltpu.VMEM((2, slots, width), BF16),
            pltpu.SemaphoreType.DMA((2,)),
        ],
        compiler_params=pltpu.CompilerParams(vmem_limit_bytes=VMEM_BYTES),
        cost_estimate=pl.CostEstimate(
            flops=12 * experts * total * width * hidden,
            bytes_accessed=60 * 10**6,
            transcendentals=0,
        ),
    )(rows, ups, gates, both_full, both_full, down_full, spread)


def weight_kernel(rows_ref, ups_ref, gated_ref, gate_grad_ref, lift_grad_ref, grads_ref):
    rows_t = rows_ref[0].T
    grads_ref[0, 0] = jnp.dot(
        rows_t, gate_grad_ref[0], preferred_element_type=F32
    ).astype(BF16)
    grads_ref[1, 0] = jnp.dot(
        rows_t, lift_grad_ref[0], preferred_element_type=F32
    ).astype(BF16)
    grads_ref[2, 0] = jnp.dot(
        ups_ref[0].T, gated_ref[0], preferred_element_type=F32
    ).astype(BF16)


def expert_weights(rows, ups, gated, gate_grad, lift_grad):
    experts, count, width = ups.shape
    hidden = gated.shape[-1]
    narrow, wide = expert_block(count, hidden), expert_block(count, width)
    return pl.pallas_call(
        weight_kernel,
        grid=(experts,),
        in_specs=[wide, wide, narrow, narrow, narrow],
        out_specs=pl.BlockSpec((3, 1, width, hidden), lambda x: (0, x, 0, 0)),
        out_shape=jax.ShapeDtypeStruct((3, experts, width, hidden), BF16),
        compiler_params=pltpu.CompilerParams(vmem_limit_bytes=VMEM_BYTES),
        cost_estimate=pl.CostEstimate(
            flops=6 * experts * count * width * hidden, bytes_accessed=50 * 10**6, transcendentals=0
        ),
    )(rows, ups, gated, gate_grad, lift_grad)


def line_copy(source, target, sems, step, up, chunk):
    send_sems, recv_sems = sems
    side = 0 if up else 1
    me = lax.axis_index("expert")
    return pltpu.make_async_remote_copy(
        src_ref=source,
        dst_ref=target,
        send_sem=send_sems.at[side, step, chunk],
        recv_sem=recv_sems.at[side, step, chunk],
        device_id={"expert": me + 1 if up else me - 1},
        device_id_type=pl.DeviceIdType.MESH,
    )


def greet_line(count):
    me = lax.axis_index("expert")
    barrier = pltpu.get_barrier_semaphore()
    for up in (True, False):
        there = me < count - 1 if up else me > 0

        @pl.when(there)
        def _():
            pl.semaphore_signal(
                barrier,
                inc=1,
                device_id={"expert": me + 1 if up else me - 1},
                device_id_type=pl.DeviceIdType.MESH,
            )

    ends = (me == 0) | (me == count - 1)

    @pl.when(ends)
    def _():
        pl.semaphore_wait(barrier, 1)

    @pl.when(jnp.logical_not(ends))
    def _():
        pl.semaphore_wait(barrier, 2)


def gather_line(count, own, held, chunks, sems, work):
    me = lax.axis_index("expert")

    def after(step, up):
        return me + step < count if up else me - step >= 0

    def place(step, up):
        return step if up else count - step

    for chunk in range(chunks):
        for up in (True, False):

            @pl.when(after(1, up))
            def _():
                line_copy(own(chunk), held(place(1, up), chunk), sems, 0, up, chunk).start()

    work(0, True)
    for step in range(1, count):
        for chunk in range(chunks):
            for up in (True, False):
                here = held(place(step, up), chunk)

                @pl.when(after(step, not up))
                def _():
                    line_copy(here, here, sems, step - 1, up, chunk).wait_recv()

                if step < count - 1:

                    @pl.when(after(step, not up) & after(1, up))
                    def _():
                        there = held(place(step + 1, up), chunk)
                        line_copy(here, there, sems, step, up, chunk).start()

        for up in (True, False):

            @pl.when(after(step, not up))
            def _():
                work(place(step, up), up)

    for step in range(count - 1):
        for chunk in range(chunks):
            for up in (True, False):

                @pl.when(after(step, not up) & after(1, up))
                def _():
                    source = held(place(step, up), chunk) if step else own(chunk)
                    line_copy(
                        source, held(place(step + 1, up), chunk), sems, step, up, chunk
                    ).wait_send()


def early_kernel(
    count, columns, block_ref, tables_ref, gate_ref, up_ref,
    held_ref, tables_out, late_ref, both_ref,
    both_vmem, local_sems, send_sems, recv_sems,
):
    greet_line(count)
    tall = block_ref.shape[0] // CHUNKS
    experts = gate_ref.shape[0]

    def rows(chunk):
        return pl.ds(chunk * tall, tall)

    def own(chunk):
        if chunk == CHUNKS:
            return tables_ref
        return block_ref.at[rows(chunk), pl.ds(0, columns)]

    def held(place, chunk):
        if chunk == CHUNKS:
            return tables_out.at[place - 1]
        return held_ref.at[place - 1, rows(chunk), :]

    def work(place, up):
        if place:
            return
        loads = [
            pltpu.make_async_copy(gate_ref, both_vmem.at[pl.ds(0, experts)], local_sems.at[0]),
            pltpu.make_async_copy(up_ref, both_vmem.at[pl.ds(experts, experts)], local_sems.at[1]),
        ]
        late = pltpu.make_async_copy(
            block_ref.at[:, pl.ds(columns, block_ref.shape[1] - columns)],
            late_ref,
            local_sems.at[2],
        )
        store = pltpu.make_async_copy(both_vmem, both_ref, local_sems.at[3])
        for copy in loads + [late]:
            copy.start()
        for copy in loads:
            copy.wait()
        store.start()
        late.wait()
        store.wait()

    gather_line(count, own, held, CHUNKS + 1, (send_sems, recv_sems), work)


def early_gather(block, tables, gate_weight, up_weight, columns):
    count = lax.axis_size("expert")
    slots, width = block.shape
    sems = pltpu.SemaphoreType.DMA((2, count - 1, CHUNKS + 1))
    sent = 2 * (count - 1) * slots * columns
    vmem, anywhere = pl.BlockSpec(memory_space=pltpu.VMEM), pl.BlockSpec(memory_space=pl.ANY)
    both = (2 * gate_weight.shape[0],) + gate_weight.shape[1:]
    return pl.pallas_call(
        functools.partial(early_kernel, count, columns),
        in_specs=[vmem, vmem, anywhere, anywhere],
        out_specs=[anywhere] * 4,
        out_shape=[
            jax.ShapeDtypeStruct((count - 1, slots, columns), BF16),
            jax.ShapeDtypeStruct((count - 1,) + tables.shape, jnp.int32),
            jax.ShapeDtypeStruct((slots, width - columns), BF16),
            jax.ShapeDtypeStruct(both, BF16),
        ],
        scratch_shapes=[pltpu.VMEM(both, BF16), pltpu.SemaphoreType.DMA((4,)), sems, sems],
        compiler_params=pltpu.CompilerParams(
            collective_id=1, has_side_effects=True, vmem_limit_bytes=VMEM_BYTES
        ),
        cost_estimate=pl.CostEstimate(flops=0, bytes_accessed=40 * sent, transcendentals=0),
    )(block, tables, gate_weight, up_weight)


def dispatch_kernel(count, normed_ref, gates_ref, *refs):
    sources = refs[: 2 * count + 1]
    rows_out, ups_out, gates_out, rows_ref, ups_ref, held_ref = refs[2 * count + 1 : 2 * count + 7]
    loaded = refs[2 * count + 7 : 4 * count + 8]
    load_sems, store_sems, send_sems, recv_sems = refs[4 * count + 8 :]
    block_ref, early_ref, spread_ref = loaded[:3]
    late_up, late_down = loaded[3 : count + 2], loaded[count + 2 :]
    greet_line(count)
    tall = normed_ref.shape[0] // CHUNKS
    capacity = rows_ref.shape[1] // count
    columns = early_ref.shape[-1]
    loads = [
        pltpu.make_async_copy(source, target, load_sems.at[k])
        for k, (source, target) in enumerate(zip(sources, loaded))
    ]

    def cut(chunk):
        return pl.ds(chunk * tall, tall)

    def own(chunk):
        return gates_ref if chunk == CHUNKS else normed_ref.at[cut(chunk), :]

    def held(place, chunk):
        if chunk == CHUNKS:
            return gates_out.at[place - 1]
        return held_ref.at[place - 1, cut(chunk), :]

    def stores(place):
        at = pl.ds(place * capacity, capacity)
        return [
            pltpu.make_async_copy(
                full.at[:, at, :], target.at[:, at, :], store_sems.at[k, place]
            )
            for k, (full, target) in enumerate([(rows_ref, rows_out), (ups_ref, ups_out)])
        ]

    def work(place, up):
        if place:
            late = late_up[place - 1] if up else late_down[count - place - 1]
            source = held_ref[place - 1]
            grads = [early_ref[place - 1], late[...]]
        else:
            for copy in loads:
                copy.start()
            for copy in loads:
                copy.wait()
            source = normed_ref[...]
            grads = [block_ref[:, :columns], block_ref[:, columns:]]
        at = slice(place * capacity, (place + 1) * capacity)
        for expert in range(EXP_DEV):
            pick = spread_ref[place, expert]
            taken = [
                jnp.dot(pick, s, preferred_element_type=F32).astype(BF16)
                for s in [source] + grads
            ]
            rows_ref[expert, at, :] = taken[0]
            ups_ref[expert, at, :columns] = taken[1]
            ups_ref[expert, at, columns:] = taken[2]
        for copy in stores(place):
            copy.start()

    gather_line(count, own, held, CHUNKS + 1, (send_sems, recv_sems), work)
    for place in range(count):
        for copy in stores(place):
            copy.wait()


def gather_dispatch(normed, gates, block, early, late_up, late_down, spread):
    count = lax.axis_size("expert")
    slots, width = normed.shape
    capacity = spread.shape[2]
    vmem, anywhere = pl.BlockSpec(memory_space=pltpu.VMEM), pl.BlockSpec(memory_space=pl.ANY)
    sems = pltpu.SemaphoreType.DMA((2, count - 1, CHUNKS + 1))
    sent = 2 * (count - 1) * slots * width
    full = (EXP_DEV, count * capacity, width)
    sources = [block, early, spread, *late_up, *late_down]
    return pl.pallas_call(
        functools.partial(dispatch_kernel, count),
        in_specs=[vmem] * 2 + [anywhere] * len(sources),
        out_specs=[anywhere] * 3,
        out_shape=[
            jax.ShapeDtypeStruct(full, BF16),
            jax.ShapeDtypeStruct(full, BF16),
            jax.ShapeDtypeStruct((count - 1,) + gates.shape, F32),
        ],
        scratch_shapes=[
            pltpu.VMEM(full, BF16),
            pltpu.VMEM(full, BF16),
            pltpu.VMEM((count - 1, slots, width), BF16),
        ]
        + [pltpu.VMEM(source.shape, BF16) for source in sources]
        + [
            pltpu.SemaphoreType.DMA((len(sources),)),
            pltpu.SemaphoreType.DMA((2, count)),
            sems,
            sems,
        ],
        compiler_params=pltpu.CompilerParams(
            collective_id=0, has_side_effects=True, vmem_limit_bytes=VMEM_BYTES
        ),
        cost_estimate=pl.CostEstimate(flops=0, bytes_accessed=40 * sent, transcendentals=0),
    )(normed, gates, *sources)


def sum_line(count, first, own, held, out, sems, fill):
    me = lax.axis_index("expert")

    def after(step, up):
        return me + step < count if up else me - step >= 0

    for step in range(count - 1, 0, -1):
        if step == count - 2:
            fill()
        for chunk in range(CHUNKS):
            for up in (True, False):
                there = held(step - 1, up, chunk)

                @pl.when(after(step, up) & jnp.logical_not(after(1, not up)))
                def _():
                    line_copy(first(step, up, chunk), there, sems, step - 1, up, chunk).start()

                if step < count - 1:
                    here = held(step, up, chunk)

                    @pl.when(after(step, up) & after(1, not up))
                    def _():
                        line_copy(here, here, sems, step, up, chunk).wait_recv()
                        here[...] = (
                            here[...].astype(F32) + own(step, up, chunk)[...].astype(F32)
                        ).astype(BF16)
                        line_copy(here, there, sems, step - 1, up, chunk).start()

    for chunk in range(CHUNKS):
        result = out(chunk)
        result[...] = own(0, True, chunk)[...].astype(F32)
        for up in (True, False):
            here = held(0, up, chunk)

            @pl.when(after(1, not up))
            def _():
                line_copy(here, here, sems, 0, up, chunk).wait_recv()
                result[...] += here[...].astype(F32)

    for step in range(count - 1, 0, -1):
        for chunk in range(CHUNKS):
            for up in (True, False):

                @pl.when(after(step, up))
                def _():
                    source = first(step, up, chunk)
                    line_copy(
                        source, held(step - 1, up, chunk), sems, step - 1, up, chunk
                    ).wait_send()


def sum_kernel(count, parts_ref, gated_ref, down_ref, spread_ref, out_ref, *refs):
    produced_out = refs[:count]
    held_ref, *loaded = refs[count : count + 5]
    stage_ref, stage_sems, load_sems, send_sems, recv_sems = refs[count + 5 :]
    parts, gated, down, spread = loaded
    greet_line(count)
    tall = out_ref.shape[0] // CHUNKS
    capacity = gated.shape[1] // count
    loads = [
        pltpu.make_async_copy(source, target, load_sems.at[k])
        for k, (source, target) in enumerate(
            zip([parts_ref, gated_ref, down_ref, spread_ref], loaded)
        )
    ]

    def cut(chunk):
        return pl.ds(chunk * tall, tall)

    def part(ref):
        return lambda step, up, c: ref.at[(count - step) % count if up else step, cut(c), :]

    def produced(place):
        at = slice(place * capacity, (place + 1) * capacity)
        rows = [dot_last(gated[x, at, :], down[x]).astype(BF16) for x in range(EXP_DEV)]
        pick = spread[place].reshape(EXP_DEV * capacity, -1).T
        return jnp.dot(
            pick, jnp.concatenate(rows, axis=0), preferred_element_type=F32
        ).astype(BF16)

    def fill():
        for copy in loads:
            copy.start()
        for copy in loads:
            copy.wait()
        stage_out(count, produced, stage_ref, lambda p: produced_out[p], stage_sems)

    sum_line(
        count,
        part(parts_ref),
        part(parts),
        lambda step, up, c: held_ref.at[0 if up else 1, step, cut(c), :],
        lambda c: out_ref.at[cut(c), :],
        (send_sems, recv_sems),
        fill,
    )


def line_sum(parts, gated, down_full, spread):
    count, slots, width = parts.shape
    vmem, anywhere = pl.BlockSpec(memory_space=pltpu.VMEM), pl.BlockSpec(memory_space=pl.ANY)
    sems = pltpu.SemaphoreType.DMA((2, count - 1, CHUNKS))
    sources = [parts, gated, down_full, spread]
    total, *produced = pl.pallas_call(
        functools.partial(sum_kernel, count),
        in_specs=[anywhere] * 4,
        out_specs=[vmem] + [anywhere] * count,
        out_shape=[jax.ShapeDtypeStruct((slots, width), F32)]
        + [jax.ShapeDtypeStruct((slots, width), BF16)] * count,
        scratch_shapes=[pltpu.VMEM((2, count - 1, slots, width), BF16)]
        + [pltpu.VMEM(source.shape, BF16) for source in sources]
        + [
            pltpu.VMEM((2, slots, width), BF16),
            pltpu.SemaphoreType.DMA((2,)),
            pltpu.SemaphoreType.DMA((4,)),
            sems,
            sems,
        ],
        compiler_params=pltpu.CompilerParams(
            collective_id=2, has_side_effects=True, vmem_limit_bytes=VMEM_BYTES
        ),
        cost_estimate=pl.CostEstimate(
            flops=0, bytes_accessed=80 * (count - 1) * slots * width, transcendentals=0
        ),
    )(*sources)
    return total, produced


def last_kernel(count, parts_ref, out_ref, held_ref, send_sems, recv_sems):
    greet_line(count)
    me = lax.axis_index("expert")
    planes = out_ref.shape[0]
    edges = [planes * c // CHUNKS for c in range(CHUNKS + 1)]

    def cut(chunk):
        return pl.ds(edges[chunk], edges[chunk + 1] - edges[chunk])

    def own(step, up, chunk):
        return parts_ref.at[cut(chunk), me + step if up else me - step]

    sum_line(
        count,
        own,
        own,
        lambda step, up, c: held_ref.at[0 if up else 1, step, cut(c)],
        lambda c: out_ref.at[cut(c)],
        (send_sems, recv_sems),
        lambda: None,
    )


def last_sum(parts):
    planes, count, rows, columns = parts.shape
    vmem = pl.BlockSpec(memory_space=pltpu.VMEM)
    sems = pltpu.SemaphoreType.DMA((2, count - 1, CHUNKS))
    return pl.pallas_call(
        functools.partial(last_kernel, count),
        in_specs=[vmem],
        out_specs=vmem,
        out_shape=jax.ShapeDtypeStruct((planes, rows, columns), F32),
        scratch_shapes=[pltpu.VMEM((2, count - 1, planes, rows, columns), BF16), sems, sems],
        compiler_params=pltpu.CompilerParams(
            collective_id=3, has_side_effects=True, vmem_limit_bytes=VMEM_BYTES
        ),
        cost_estimate=pl.CostEstimate(
            flops=0, bytes_accessed=80 * parts.size, transcendentals=0
        ),
    )(parts)


def projection_kernel(mixed_ref, normed_ref, merge_ref, qkv_ref, side_ref, out_ref, turned_ref):
    step = pl.program_id(0)
    merge_steps = mixed_ref.shape[1] // COLS
    steps = pl.num_programs(0)

    @pl.when(step == 0)
    def _():
        turned_ref[...] = mixed_ref[...].T

    @pl.when(step == merge_steps)
    def _():
        turned_ref[...] = normed_ref[...].T

    @pl.when(step < merge_steps)
    def _():
        out_ref[0] = jnp.dot(
            turned_ref[...], merge_ref[...], preferred_element_type=F32
        ).astype(BF16)

    @pl.when((step >= merge_steps) & (step < steps - 1))
    def _():
        out_ref[0] = jnp.dot(
            turned_ref[...], qkv_ref[...], preferred_element_type=F32
        ).astype(BF16)

    @pl.when(step == steps - 1)
    def _():
        out_ref[0] = side_ref[...]


def projection_terms(mixed, normed, attended_grad, qkv_grad, side):
    slots, width = mixed.shape
    first, second = attended_grad.shape[1] // COLS, qkv_grad.shape[1] // COLS
    whole = pl.BlockSpec((slots, width), lambda j: (0, 0))
    return pl.pallas_call(
        projection_kernel,
        grid=(first + second + 1,),
        in_specs=[
            whole,
            whole,
            pl.BlockSpec((slots, COLS), lambda j: (0, jnp.minimum(j, first - 1))),
            pl.BlockSpec((slots, COLS), lambda j: (0, jnp.clip(j - first, 0, second - 1))),
            pl.BlockSpec((width, COLS), lambda j: (0, 0)),
        ],
        out_specs=pl.BlockSpec((1, width, COLS), lambda j: (j, 0, 0)),
        out_shape=jax.ShapeDtypeStruct((first + second + 1, width, COLS), BF16),
        scratch_shapes=[pltpu.VMEM((width, slots), BF16)],
        cost_estimate=pl.CostEstimate(
            flops=2 * slots * width * (first + second) * COLS,
            bytes_accessed=2 * 10**7,
            transcendentals=0,
        ),
    )(mixed, normed, attended_grad, qkv_grad, side)


def body(
    tokens,
    lengths,
    routes,
    priority,
    first_gain,
    query_weight,
    key_weight,
    value_weight,
    merge_weight,
    router_weight,
    second_gain,
    gate_weight,
    up_weight,
    down_weight,
    cotangent,
):
    slots = tokens.shape[1]
    width = tokens.shape[2]
    groups = lax.axis_size("expert")
    expert_count = router_weight.shape[1]
    capacity = 5 * slots * TOP // (8 * expert_count)
    q_cols, k_cols = HEADS * HD, KV_HEADS * HD
    side_cols = 128

    def gather_shard(value, axis=0):
        return lax.all_gather(value, "shard", axis=axis, tiled=True)

    def scatter_all(part, ahead=None):
        planes, _, columns = part.shape
        part = lax.psum_scatter(
            part.reshape(planes * groups, -1, columns), "shard", scatter_dimension=1, tiled=True
        ).reshape(planes, groups, -1, columns)
        part, ahead = lax.optimization_barrier((part, ahead))
        return last_sum(part), ahead

    side = jnp.concatenate(
        [router_weight, first_gain[:, None], second_gain[:, None]], axis=1
    )
    side = jnp.pad(side, ((0, 0), (0, side_cols - expert_count - 2)))
    first_set = gather_shard(
        jnp.concatenate([query_weight, key_weight, value_weight, side], axis=1)
    )
    merge_full = gather_shard(merge_weight)
    tables = jnp.concatenate(
        [routes[0].T, priority, jnp.broadcast_to(lengths[:, None], (1, slots))], axis=0
    )
    mid = groups // 2
    early_columns = 7 * width // 12
    early, other_tables, late_block, both = early_gather(
        cotangent[0], tables, gate_weight, up_weight, early_columns
    )
    tables = jnp.concatenate([tables[None], other_tables], axis=0).transpose(0, 2, 1)
    tokens, late_block = lax.optimization_barrier((tokens, late_block))
    late_up, late_down = line_hops(late_block, 0, 1)
    both_full = gather_shard(both, 1)
    down_full = gather_shard(down_weight, 1)

    group = lax.axis_index("expert")
    own_experts = group * EXP_DEV + jnp.arange(EXP_DEV, dtype=jnp.int32)
    spread = jax.vmap(
        lambda t: dispatch_matrix(t[:, :TOP], t[:, TOP], t[0, TOP + 1], own_experts, capacity)
    )(tables)

    qkv_full = first_set[:, : q_cols + 2 * k_cols]
    side_full = first_set[:, q_cols + 2 * k_cols :]
    router_full = side_full[:, :expert_count]
    gain_first = side_full[:, expert_count].astype(F32)
    gain_second = side_full[:, expert_count + 1].astype(F32)

    inputs = tokens[0].astype(F32)
    length = lengths[0]
    positions = jnp.arange(slots, dtype=jnp.int32)
    live_rows = (positions < length).astype(F32)[:, None]
    cosine, sine_table = rope_tables(slots)
    rms_one = lax.rsqrt(jnp.mean(inputs * inputs, axis=-1, keepdims=True) + EPS)
    unit_one = inputs * rms_one
    normed_one = (unit_one * gain_first).astype(BF16)
    qkv = jnp.dot(normed_one, qkv_full, preferred_element_type=F32)
    qkv, late_up, late_down = lax.optimization_barrier((qkv, late_up, late_down))
    next_up, next_down = line_hops(late_block, 1, 2, (late_up[-1], late_down[-1]))
    mixed, *low_parts, lse = attend(lengths, qkv, cosine, sine_table)
    mixed, next_up, next_down = lax.optimization_barrier((mixed, next_up, next_down))
    last_up, last_down = line_hops(late_block, 2, held=(next_up[-1], next_down[-1]))
    late_up, late_down = late_up + next_up + last_up, late_down + next_down + last_down
    attended = jnp.dot(mixed, merge_full, preferred_element_type=F32)
    hidden = inputs + live_rows * attended
    rms_two = lax.rsqrt(jnp.mean(hidden * hidden, axis=-1, keepdims=True) + EPS)
    unit_two = hidden * rms_two
    normed_two = (unit_two * gain_second).astype(BF16)

    logits = jnp.dot(normed_two, router_full, preferred_element_type=F32)
    chosen = (
        routes[0][:, :, None] == jnp.arange(expert_count, dtype=jnp.int32)[None, None, :]
    ).astype(F32)
    chosen_any = jnp.sum(chosen, axis=1)
    masked = jnp.where(chosen_any > 0, logits, NEGATIVE)
    peak = jnp.max(masked, axis=-1, keepdims=True)
    exp_logits = jnp.exp(masked - peak) * chosen_any
    gate_dense = exp_logits / jnp.sum(exp_logits, axis=-1, keepdims=True)

    gates = gate_dense.T
    rows, ups, other_gates = gather_dispatch(
        normed_two, gates, cotangent[0], early, late_up, late_down, spread
    )
    gates_all = jnp.concatenate([gates[None], other_gates], axis=0)
    gates_own = lax.dynamic_slice_in_dim(gates_all, group * EXP_DEV, EXP_DEV, axis=1)
    slot_gate = jnp.sum(spread.astype(F32) * gates_own[:, :, None, :], axis=-1)
    gates = slot_gate.transpose(1, 0, 2).reshape(EXP_DEV, groups * capacity, 1)

    gated, gate_pre_grad, lift_pre_grad, back_parts, slot_grad = expert_core(
        rows, ups, gates, both_full, down_full, spread
    )

    slot_grad = slot_grad.reshape(EXP_DEV, groups, capacity).transpose(1, 0, 2)
    token_grad = jnp.sum(spread.astype(F32) * slot_grad[:, :, :, None], axis=2)
    token_grad = lax.dynamic_update_slice_in_dim(
        jnp.zeros((groups, expert_count, slots), F32), token_grad, group * EXP_DEV, axis=1
    )
    slot_back = direct_scatter([token_grad[p] for p in range(groups)]).T
    expert_grads = expert_weights(rows, ups, gated, gate_pre_grad, lift_pre_grad)
    back_parts, expert_grads = lax.optimization_barrier((back_parts, expert_grads))
    back_total, produced = line_sum(back_parts, gated, down_full, spread)
    expert_grads = lax.psum_scatter(
        expert_grads.reshape(3 * EXP_DEV, width, -1), "shard", scatter_dimension=1, tiled=True
    )
    sums = scatter_hops(produced, 0, 1)

    upstream = cotangent[0].astype(F32)
    picked_grad = gate_dense * (
        slot_back - jnp.sum(gate_dense * slot_back, axis=-1, keepdims=True)
    )
    logit_grad = picked_grad.astype(BF16)
    router_part = jnp.einsum("ld,le->de", normed_two, logit_grad, preferred_element_type=F32)
    normed_two_grad = jnp.einsum("le,de->ld", logit_grad, router_full, preferred_element_type=F32)
    normed_two_grad = normed_two_grad + back_total
    scaled_two = normed_two_grad * gain_second
    second_gain_part = jnp.sum(normed_two_grad * unit_two, axis=0)
    hidden_grad = upstream + rms_two * (
        scaled_two - unit_two * jnp.mean(scaled_two * unit_two, axis=-1, keepdims=True)
    )
    attended_grad = (live_rows * hidden_grad).astype(BF16)

    mixed_grad = jnp.einsum(
        "ld,hd->lh", attended_grad, merge_full, preferred_element_type=F32
    ).astype(BF16)
    qkv_grad = attend_back(lengths, *low_parts, mixed_grad, lse, cosine, sine_table)
    sums, qkv_grad = lax.optimization_barrier((sums, qkv_grad))
    sums = scatter_hops(produced, 1, mid, sums)
    side_part = jnp.concatenate([router_part, second_gain_part[:, None]], axis=1)
    side_part = jnp.pad(side_part, ((0, 0), (0, COLS - expert_count - 1))).astype(BF16)
    terms = projection_terms(mixed, normed_one, attended_grad, qkv_grad, side_part)
    terms, expert_grads, sums = lax.optimization_barrier((terms, expert_grads, sums))
    sums = scatter_hops(produced, mid, groups - 1, sums)
    normed_one_grad = jnp.einsum("lh,dh->ld", qkv_grad, qkv_full, preferred_element_type=F32)
    scaled_one = normed_one_grad * gain_first
    input_grad = hidden_grad + rms_one * (
        scaled_one - unit_one * jnp.mean(scaled_one * unit_one, axis=-1, keepdims=True)
    )
    block_output = (
        hidden + produced[0].astype(F32) + sums[0].astype(F32) + sums[1].astype(F32)
    )
    gate_grad, up_grad, down_grad = jnp.split(expert_grads.astype(F32), 3)
    reduced, (block_output, input_grad) = scatter_all(terms, (block_output, input_grad))
    own_rows = reduced.shape[1]
    reduced = reduced.transpose(1, 0, 2).reshape(own_rows, -1)
    place = (group * lax.axis_size("shard") + lax.axis_index("shard")) * own_rows
    merge_grad, qkv_reduced, side_grad = jnp.split(
        reduced, [width, width + q_cols + 2 * k_cols], axis=1
    )
    own_weights = lax.dynamic_slice_in_dim(qkv_full, place, own_rows, axis=0).astype(F32)
    own_gain = lax.dynamic_slice_in_dim(gain_first, place, own_rows)
    first_gain_grad = jnp.sum(own_weights * qkv_reduced, axis=1) / own_gain
    query_grad, key_grad, value_grad = jnp.split(qkv_reduced, [q_cols, q_cols + k_cols], axis=1)
    return (
        block_output[None],
        input_grad[None],
        first_gain_grad,
        query_grad,
        key_grad,
        value_grad,
        merge_grad,
        side_grad[:, :expert_count],
        side_grad[:, expert_count],
        gate_grad,
        up_grad,
        down_grad,
    )


def solution(mesh):
    both = ("expert", "shard")
    in_specs = (
        P(both, None, None),
        P(both),
        P(both, None, None),
        P(both, None),
        P("shard"),
        P("shard", None),
        P("shard", None),
        P("shard", None),
        P("shard", None),
        P("shard", None),
        P("shard"),
        P("expert", "shard", None),
        P("expert", "shard", None),
        P("expert", "shard", None),
        P(both, None, None),
    )
    out_specs = (
        P(both, None, None),
        P(both, None, None),
        P(both),
        P(both, None),
        P(both, None),
        P(both, None),
        P(both, None),
        P(both, None),
        P(both),
        P("expert", "shard", None),
        P("expert", "shard", None),
        P("expert", "shard", None),
    )
    return jax.shard_map(body, mesh=mesh, in_specs=in_specs, out_specs=out_specs, check_vma=False)
```

```python
import functools

import jax
import jax.numpy as jnp
import numpy as np
from jax import lax
from jax.experimental import pallas as pl
from jax.experimental.pallas import tpu as pltpu
from jax.sharding import PartitionSpec as P

HEADS = 24
KV_HEADS = 8
HD = 64
TOP = 8
EXP_DEV = 5
SHARE = HEADS // KV_HEADS
Q_BLOCK = 128
VMEM_BYTES = 63 * 2**20
CHUNKS = 4
COLS = 256

EPS = 1e-05
THETA = 10000.0
NEGATIVE = -1e30
F32 = jnp.float32
BF16 = jnp.bfloat16


def rope_tables(slots):
    frequency = THETA ** (-np.arange(HD // 2, dtype=np.float32) * np.float32(2.0) / HD)
    angles = np.arange(slots, dtype=np.float32)[:, None] * frequency.astype(np.float32)[None, :]
    cosine, sine = np.cos(angles), np.sin(angles)
    return (
        jnp.asarray(np.concatenate([cosine] * 4, axis=1), F32),
        jnp.asarray(np.concatenate([-sine, sine, -sine, sine], axis=1), F32),
    )


def dispatch_matrix(routes, priority, length, expert_ids, capacity):
    slots = routes.shape[0]
    positions = jnp.arange(slots, dtype=jnp.int32)
    live = positions < length
    named = jnp.any(routes[:, :, None] == expert_ids[None, None, :], axis=1) & live[:, None]
    earlier = (priority[None, :] < priority[:, None]).astype(BF16)
    slot = jnp.dot(earlier, named.astype(BF16), preferred_element_type=F32).astype(jnp.int32)
    slot = jnp.where(named, slot, capacity)
    return (
        slot.T[:, None, :] == jnp.arange(capacity, dtype=jnp.int32)[None, :, None]
    ).astype(BF16)


def line_hops(block, first=0, last=None, held=None):
    count = lax.axis_size("expert")
    last = count - 1 if last is None else last
    held_up, held_down = (block, block) if held is None else held
    up, down = [], []
    for step in range(first, last):
        held_up = lax.ppermute(
            held_up, "expert", [(i, i + 1) for i in range(step, count - 1)]
        )
        held_down = lax.ppermute(
            held_down, "expert", [(i + 1, i) for i in range(0, count - 1 - step)]
        )
        up.append(held_up)
        down.append(held_down)
    return up, down


def scatter_hops(parts, first=0, last=None, held=None):
    count = lax.axis_size("expert")
    last = count - 1 if last is None else last
    held_up, held_down = (None, None) if held is None else held
    for step in range(first, last):
        piece_up = parts[step + 1]
        piece_down = parts[count - 1 - step]
        if step:
            piece_up = piece_up.astype(F32) + held_up.astype(F32)
            piece_down = piece_down.astype(F32) + held_down.astype(F32)
        held_up = lax.ppermute(
            piece_up.astype(BF16), "expert", [(i, i + 1) for i in range(step + 1)]
        )
        held_down = lax.ppermute(
            piece_down.astype(BF16),
            "expert",
            [(i + 1, i) for i in range(count - 2 - step, count - 1)],
        )
    return held_up, held_down


def turn(values, cosine, sine):
    first = lax.broadcasted_iota(jnp.int32, (1, 2 * HD), 1) % HD < HD // 2
    out = []
    for start in range(0, values.shape[1], 2 * HD):
        part = values[:, start : start + 2 * HD]
        other = jnp.where(
            first, pltpu.roll(part, 2 * HD - HD // 2, 1), pltpu.roll(part, HD // 2, 1)
        )
        out.append(part * cosine + other * sine)
    return out[0] if len(out) == 1 else jnp.concatenate(out, axis=1)


def last_keys(block, length):
    lane = lax.broadcasted_iota(jnp.int32, (1, SHARE * Q_BLOCK), 1)
    return jnp.minimum(block * Q_BLOCK + lane % Q_BLOCK, length - 1)


def head_block(values, pair_head, block):
    rows = slice(block * Q_BLOCK, (block + 1) * Q_BLOCK)
    heads = range(pair_head * SHARE, (pair_head + 1) * SHARE)
    return jnp.concatenate([values[rows, h * HD : (h + 1) * HD] for h in heads], axis=0)


def rows_of_heads(parts):
    tall = [
        part[:, g * Q_BLOCK : (g + 1) * Q_BLOCK] for part in parts for g in range(SHARE)
    ]
    return jnp.concatenate(tall, axis=0).T


def dot_last(a, b):
    return lax.dot_general(a, b, (((1,), (1,)), ((), ())), preferred_element_type=F32)


def attend_kernel(
    length_ref, q_ref, k_ref, v_ref, cos_ref, sin_ref,
    mixed_ref, q_low_ref, k_low_ref, v_low_ref, lse_ref,
):
    length = length_ref[0]
    slots = q_ref.shape[0]
    cosine, sine = cos_ref[...], sin_ref[...]
    queries = (turn(q_ref[...], cosine, sine) * HD**-0.5).astype(BF16)
    keys = turn(k_ref[...], cosine, sine).astype(BF16)
    values = v_ref[...]
    q_low_ref[...] = queries
    k_low_ref[...] = keys
    v_low_ref[...] = values.astype(BF16)
    values_t = values.T.astype(BF16)
    blocks = slots // Q_BLOCK
    for block in range(blocks):
        span = (block + 1) * Q_BLOCK
        limit = last_keys(block, length)
        key_id = lax.broadcasted_iota(jnp.int32, (span, 1), 0)
        parts = []
        for head in range(2):
            scores = dot_last(
                keys[:span, head * HD : (head + 1) * HD], head_block(queries, head, block)
            )
            scores = jnp.where(key_id <= limit, scores, NEGATIVE)
            peak = jnp.max(scores, axis=0, keepdims=True)
            exp_scores = jnp.exp(scores - peak)
            total = jnp.sum(exp_scores, axis=0, keepdims=True)
            lse_ref[0, pl.ds(head * blocks + block, 1), :] = peak + jnp.log(total)
            part = jnp.dot(
                values_t[head * HD : (head + 1) * HD, :span],
                exp_scores.astype(BF16),
                preferred_element_type=F32,
            )
            parts.append(part / total)
        mixed_ref[block * Q_BLOCK : span, :] = rows_of_heads(parts).astype(BF16)


def attend_back_kernel(
    length_ref, q_ref, k_ref, v_ref, grad_ref, lse_ref, cos_ref, sin_ref, out_ref, dk_ref, dv_ref
):
    length = length_ref[0]
    slots, q_cols = q_ref.shape
    pairs = pl.num_programs(0)
    pair = pl.program_id(0)
    q_at = pl.ds(pl.multiple_of(pair * q_cols, 2 * HD), q_cols)
    k_at = pl.ds(pl.multiple_of(pairs * q_cols + pair * 2 * HD, 2 * HD), 2 * HD)
    v_at = pl.ds(pl.multiple_of(pairs * (q_cols + 2 * HD) + pair * 2 * HD, 2 * HD), 2 * HD)
    cosine, sine = cos_ref[...], -sin_ref[...]
    queries, keys, values = q_ref[...], k_ref[...], v_ref[...]
    grad = grad_ref[...]
    keys_t = keys.astype(F32).T.astype(BF16)
    dk_ref[...] = jnp.zeros_like(dk_ref)
    dv_ref[...] = jnp.zeros_like(dv_ref)
    blocks = slots // Q_BLOCK
    for block in range(blocks):
        rows = slice(block * Q_BLOCK, (block + 1) * Q_BLOCK)
        span = (block + 1) * Q_BLOCK
        limit = last_keys(block, length)
        key_id = lax.broadcasted_iota(jnp.int32, (span, 1), 0)
        parts = []
        for head in range(2):
            cols = slice(head * HD, (head + 1) * HD)
            query = head_block(queries, head, block)
            out_grad = head_block(grad, head, block)
            scores = dot_last(keys[:span, cols], query)
            scores = jnp.where(key_id <= limit, scores, NEGATIVE)
            probs = jnp.exp(scores - lse_ref[0, pl.ds(head * blocks + block, 1), :])
            prob_back = dot_last(values[:span, cols], out_grad)
            mean = jnp.sum(probs * prob_back, axis=0, keepdims=True)
            score_grad = (probs * (prob_back - mean)).astype(BF16)
            dv_ref[head, :span, :] += jnp.dot(
                probs.astype(BF16), out_grad, preferred_element_type=F32
            )
            dk_ref[head, :span, :] += jnp.dot(score_grad, query, preferred_element_type=F32)
            parts.append(
                jnp.dot(keys_t[cols, :span], score_grad, preferred_element_type=F32)
                * HD**-0.5
            )
        out_ref[rows, q_at] = turn(rows_of_heads(parts), cosine[rows], sine[rows]).astype(
            BF16
        )
    key_grad = jnp.concatenate([dk_ref[0], dk_ref[1]], axis=1)
    out_ref[:, k_at] = turn(key_grad, cosine, sine).astype(BF16)
    out_ref[:, v_at] = jnp.concatenate([dv_ref[0], dv_ref[1]], axis=1).astype(BF16)


def column_block(slots, columns, first=0):
    return pl.BlockSpec((slots, columns), lambda p: (0, first + p))


def attention_specs(slots):
    pairs = KV_HEADS // 2
    q_cols, cols = 2 * SHARE * HD, 2 * (SHARE + 2) * HD
    blocks = slots // Q_BLOCK
    whole = pl.BlockSpec((slots, 2 * HD), lambda p: (0, 0))
    lse = pl.BlockSpec((1, 2 * blocks, SHARE * Q_BLOCK), lambda p: (p, 0, 0))
    scalar = pl.BlockSpec(memory_space=pltpu.SMEM)
    return pairs, q_cols, cols, blocks, whole, lse, scalar


def attend(length, qkv, cosine, sine):
    slots = qkv.shape[0]
    pairs, q_cols, cols, blocks, whole, lse, scalar = attention_specs(slots)
    queries, keys = column_block(slots, q_cols), column_block(slots, 2 * HD)
    key_first = pairs * q_cols // (2 * HD)
    low_keys = jax.ShapeDtypeStruct((slots, pairs * 2 * HD), BF16)
    low_queries = jax.ShapeDtypeStruct((slots, pairs * q_cols), BF16)
    return pl.pallas_call(
        attend_kernel,
        grid=(pairs,),
        in_specs=[
            scalar,
            queries,
            column_block(slots, 2 * HD, key_first),
            column_block(slots, 2 * HD, key_first + pairs),
            whole,
            whole,
        ],
        out_specs=[queries, queries, keys, keys, lse],
        out_shape=[
            low_queries,
            low_queries,
            low_keys,
            low_keys,
            jax.ShapeDtypeStruct((pairs, 2 * blocks, SHARE * Q_BLOCK), F32),
        ],
        cost_estimate=pl.CostEstimate(
            flops=24 * HEADS * slots * slots * HD // 4, bytes_accessed=10**7, transcendentals=0
        ),
    )(length, qkv, qkv, qkv, cosine, sine)


def attend_back(length, queries, keys, values, grad, lse_rows, cosine, sine):
    slots = grad.shape[0]
    pairs, q_cols, cols, blocks, whole, lse, scalar = attention_specs(slots)
    wide, narrow = column_block(slots, q_cols), column_block(slots, 2 * HD)
    return pl.pallas_call(
        attend_back_kernel,
        grid=(pairs,),
        in_specs=[scalar, wide, narrow, narrow, wide, lse, whole, whole],
        out_specs=pl.BlockSpec((slots, pairs * cols), lambda p: (0, 0)),
        out_shape=jax.ShapeDtypeStruct((slots, pairs * cols), BF16),
        scratch_shapes=[pltpu.VMEM((2, slots, HD), F32), pltpu.VMEM((2, slots, HD), F32)],
        cost_estimate=pl.CostEstimate(
            flops=60 * HEADS * slots * slots * HD // 4, bytes_accessed=10**7, transcendentals=0
        ),
    )(length, queries, keys, values, grad, lse_rows, cosine, sine)


def stage_out(count, make, stage_ref, targets, sems):
    copies = [
        pltpu.make_async_copy(stage_ref.at[p % 2], targets(p), sems.at[p % 2])
        for p in range(count)
    ]
    for p in range(count):
        if p > 1:
            copies[p - 2].wait()
        stage_ref[p % 2] = make(p)
        copies[p].start()
    for copy in copies[-2:]:
        copy.wait()


def token_sum(spread_ref, rows_ref, place):
    capacity = rows_ref.shape[1] // spread_ref.shape[0]
    pick = spread_ref[place].reshape(EXP_DEV * capacity, -1).T
    rows = rows_ref[:, place * capacity : (place + 1) * capacity, :]
    return jnp.dot(
        pick, rows.reshape(EXP_DEV * capacity, -1), preferred_element_type=F32
    ).astype(BF16)


def expert_kernel(
    rows_ref, ups_ref, gates_ref, gate_ref, up_ref, down_ref, spread_ref,
    gated_ref, gate_grad_ref, lift_grad_ref, parts_ref, slot_ref,
    back_ref, stage_ref, sems,
):
    rows, gates = rows_ref[0], gates_ref[0]
    gate_pre = jnp.dot(rows, gate_ref[0], preferred_element_type=F32)
    lift_pre = jnp.dot(rows, up_ref[0], preferred_element_type=F32)
    act_grad = jnp.dot(ups_ref[0], down_ref[0], preferred_element_type=F32)
    sigmoid_gate = jax.nn.sigmoid(gate_pre)
    silu_gate = gate_pre * sigmoid_gate
    activated = silu_gate * lift_pre
    slot_ref[0] = jnp.sum(act_grad * activated, axis=-1, keepdims=True)
    gated_ref[0] = (activated * gates).astype(BF16)
    act_grad = act_grad * gates
    gate_pre_grad = (
        act_grad * lift_pre * (sigmoid_gate + silu_gate * (1.0 - sigmoid_gate))
    ).astype(BF16)
    lift_pre_grad = (act_grad * silu_gate).astype(BF16)
    gate_grad_ref[0] = gate_pre_grad
    lift_grad_ref[0] = lift_pre_grad
    step = pl.program_id(0)
    back_ref[step] = (
        dot_last(gate_pre_grad, gate_ref[0]) + dot_last(lift_pre_grad, up_ref[0])
    ).astype(BF16)

    @pl.when(step == pl.num_programs(0) - 1)
    def _():
        stage_out(
            spread_ref.shape[0],
            lambda p: token_sum(spread_ref, back_ref, p),
            stage_ref,
            lambda p: parts_ref.at[p],
            sems,
        )


def expert_block(*shape, first=0):
    return pl.BlockSpec((1,) + shape, lambda x: (first + x, 0, 0))


def expert_core(rows, ups, gates, both_full, down_full, spread):
    experts, total, width = ups.shape
    count, _, capacity, slots = spread.shape
    hidden = down_full.shape[-1]
    narrow, wide = expert_block(total, hidden), expert_block(total, width)
    weight, single = expert_block(width, hidden), expert_block(total, 1)
    low = jax.ShapeDtypeStruct((experts, total, hidden), BF16)
    return pl.pallas_call(
        expert_kernel,
        grid=(experts,),
        in_specs=[
            wide, wide, single,
            weight, expert_block(width, hidden, first=experts), weight,
            pl.BlockSpec(spread.shape, lambda x: (0, 0, 0, 0)),
        ],
        out_specs=[narrow, narrow, narrow, pl.BlockSpec(memory_space=pl.ANY), single],
        out_shape=[
            low,
            low,
            low,
            jax.ShapeDtypeStruct((count, slots, width), BF16),
            jax.ShapeDtypeStruct((experts, total, 1), F32),
        ],
        scratch_shapes=[
            pltpu.VMEM((experts, total, width), BF16),
            pltpu.VMEM((2, slots, width), BF16),
            pltpu.SemaphoreType.DMA((2,)),
        ],
        compiler_params=pltpu.CompilerParams(vmem_limit_bytes=VMEM_BYTES),
        cost_estimate=pl.CostEstimate(
            flops=12 * experts * total * width * hidden,
            bytes_accessed=60 * 10**6,
            transcendentals=0,
        ),
    )(rows, ups, gates, both_full, both_full, down_full, spread)


def weight_kernel(rows_ref, ups_ref, gated_ref, gate_grad_ref, lift_grad_ref, grads_ref):
    rows_t = rows_ref[0].T
    grads_ref[0, 0] = jnp.dot(
        rows_t, gate_grad_ref[0], preferred_element_type=F32
    ).astype(BF16)
    grads_ref[1, 0] = jnp.dot(
        rows_t, lift_grad_ref[0], preferred_element_type=F32
    ).astype(BF16)
    grads_ref[2, 0] = jnp.dot(
        ups_ref[0].T, gated_ref[0], preferred_element_type=F32
    ).astype(BF16)


def expert_weights(rows, ups, gated, gate_grad, lift_grad):
    experts, count, width = ups.shape
    hidden = gated.shape[-1]
    narrow, wide = expert_block(count, hidden), expert_block(count, width)
    return pl.pallas_call(
        weight_kernel,
        grid=(experts,),
        in_specs=[wide, wide, narrow, narrow, narrow],
        out_specs=pl.BlockSpec((3, 1, width, hidden), lambda x: (0, x, 0, 0)),
        out_shape=jax.ShapeDtypeStruct((3, experts, width, hidden), BF16),
        compiler_params=pltpu.CompilerParams(vmem_limit_bytes=VMEM_BYTES),
        cost_estimate=pl.CostEstimate(
            flops=6 * experts * count * width * hidden, bytes_accessed=50 * 10**6, transcendentals=0
        ),
    )(rows, ups, gated, gate_grad, lift_grad)


def line_copy(source, target, sems, step, up, chunk):
    send_sems, recv_sems = sems
    side = 0 if up else 1
    me = lax.axis_index("expert")
    return pltpu.make_async_remote_copy(
        src_ref=source,
        dst_ref=target,
        send_sem=send_sems.at[side, step, chunk],
        recv_sem=recv_sems.at[side, step, chunk],
        device_id={"expert": me + 1 if up else me - 1},
        device_id_type=pl.DeviceIdType.MESH,
    )


def greet_line(count):
    me = lax.axis_index("expert")
    barrier = pltpu.get_barrier_semaphore()
    for up in (True, False):
        there = me < count - 1 if up else me > 0

        @pl.when(there)
        def _():
            pl.semaphore_signal(
                barrier,
                inc=1,
                device_id={"expert": me + 1 if up else me - 1},
                device_id_type=pl.DeviceIdType.MESH,
            )

    ends = (me == 0) | (me == count - 1)

    @pl.when(ends)
    def _():
        pl.semaphore_wait(barrier, 1)

    @pl.when(jnp.logical_not(ends))
    def _():
        pl.semaphore_wait(barrier, 2)


def gather_line(count, own, held, chunks, sems, work, short=0):
    me = lax.axis_index("expert")

    def after(step, up):
        return me + step < count if up else me - step >= 0

    def place(step, up):
        return step if up else count - step

    def reach(chunk):
        return count - 1 if chunk < chunks - short else 1

    for chunk in range(chunks):
        for up in (True, False):

            @pl.when(after(1, up))
            def _():
                line_copy(own(chunk), held(place(1, up), chunk), sems, 0, up, chunk).start()

    work(0, True)
    for step in range(1, count):
        for chunk in range(chunks):
            for up in (True, False):
                if step > reach(chunk):
                    continue
                here = held(place(step, up), chunk)

                @pl.when(after(step, not up))
                def _():
                    line_copy(here, here, sems, step - 1, up, chunk).wait_recv()

                if step < reach(chunk):

                    @pl.when(after(step, not up) & after(1, up))
                    def _():
                        there = held(place(step + 1, up), chunk)
                        line_copy(here, there, sems, step, up, chunk).start()

        for up in (True, False):

            @pl.when(after(step, not up))
            def _():
                work(place(step, up), up)

    for step in range(count - 1):
        for chunk in range(chunks):
            for up in (True, False):
                if step >= reach(chunk):
                    continue

                @pl.when(after(step, not up) & after(1, up))
                def _():
                    source = held(place(step, up), chunk) if step else own(chunk)
                    line_copy(
                        source, held(place(step + 1, up), chunk), sems, step, up, chunk
                    ).wait_send()


def early_kernel(
    count, columns, block_ref, tables_ref, gate_ref, up_ref,
    held_ref, tables_out, late_up, late_down, both_ref,
    both_vmem, local_sems, send_sems, recv_sems,
):
    greet_line(count)
    tall = block_ref.shape[0] // CHUNKS
    experts = gate_ref.shape[0]

    def rows(chunk):
        return pl.ds(chunk * tall, tall)

    def own(chunk):
        if chunk == CHUNKS:
            return tables_ref
        if chunk > CHUNKS:
            late = block_ref.shape[1] - columns
            return block_ref.at[rows(chunk - CHUNKS - 1), pl.ds(columns, late)]
        return block_ref.at[rows(chunk), pl.ds(0, columns)]

    def held(place, chunk):
        if chunk == CHUNKS:
            return tables_out.at[place - 1]
        if chunk > CHUNKS:
            late = late_up if place == 1 else late_down
            return late.at[rows(chunk - CHUNKS - 1), :]
        return held_ref.at[place - 1, rows(chunk), :]

    def work(place, up):
        if place:
            return
        loads = [
            pltpu.make_async_copy(gate_ref, both_vmem.at[pl.ds(0, experts)], local_sems.at[0]),
            pltpu.make_async_copy(up_ref, both_vmem.at[pl.ds(experts, experts)], local_sems.at[1]),
        ]
        store = pltpu.make_async_copy(both_vmem, both_ref, local_sems.at[2])
        for copy in loads:
            copy.start()
        for copy in loads:
            copy.wait()
        store.start()
        store.wait()

    gather_line(
        count, own, held, 2 * CHUNKS + 1, (send_sems, recv_sems), work, short=CHUNKS
    )


def early_gather(block, tables, gate_weight, up_weight, columns):
    count = lax.axis_size("expert")
    slots, width = block.shape
    sems = pltpu.SemaphoreType.DMA((2, count - 1, 2 * CHUNKS + 1))
    sent = 2 * (count - 1) * slots * columns
    vmem, anywhere = pl.BlockSpec(memory_space=pltpu.VMEM), pl.BlockSpec(memory_space=pl.ANY)
    both = (2 * gate_weight.shape[0],) + gate_weight.shape[1:]
    return pl.pallas_call(
        functools.partial(early_kernel, count, columns),
        in_specs=[vmem, vmem, anywhere, anywhere],
        out_specs=[anywhere] * 5,
        out_shape=[
            jax.ShapeDtypeStruct((count - 1, slots, columns), BF16),
            jax.ShapeDtypeStruct((count - 1,) + tables.shape, jnp.int32),
            jax.ShapeDtypeStruct((slots, width - columns), BF16),
            jax.ShapeDtypeStruct((slots, width - columns), BF16),
            jax.ShapeDtypeStruct(both, BF16),
        ],
        scratch_shapes=[pltpu.VMEM(both, BF16), pltpu.SemaphoreType.DMA((3,)), sems, sems],
        compiler_params=pltpu.CompilerParams(
            collective_id=1, has_side_effects=True, vmem_limit_bytes=VMEM_BYTES
        ),
        cost_estimate=pl.CostEstimate(flops=0, bytes_accessed=40 * sent, transcendentals=0),
    )(block, tables, gate_weight, up_weight)


def dispatch_kernel(count, normed_ref, gates_ref, *refs):
    sources = refs[: 2 * count + 1]
    rows_out, ups_out, gates_out, rows_ref, ups_ref, held_ref = refs[2 * count + 1 : 2 * count + 7]
    loaded = refs[2 * count + 7 : 4 * count + 8]
    load_sems, store_sems, send_sems, recv_sems = refs[4 * count + 8 :]
    block_ref, early_ref, spread_ref = loaded[:3]
    late_up, late_down = loaded[3 : count + 2], loaded[count + 2 :]
    greet_line(count)
    tall = normed_ref.shape[0] // CHUNKS
    capacity = rows_ref.shape[1] // count
    columns = early_ref.shape[-1]
    loads = [
        pltpu.make_async_copy(source, target, load_sems.at[k])
        for k, (source, target) in enumerate(zip(sources, loaded))
    ]

    def cut(chunk):
        return pl.ds(chunk * tall, tall)

    def own(chunk):
        return gates_ref if chunk == CHUNKS else normed_ref.at[cut(chunk), :]

    def held(place, chunk):
        if chunk == CHUNKS:
            return gates_out.at[place - 1]
        return held_ref.at[place - 1, cut(chunk), :]

    def stores(place):
        at = pl.ds(place * capacity, capacity)
        return [
            pltpu.make_async_copy(
                full.at[:, at, :], target.at[:, at, :], store_sems.at[k, place]
            )
            for k, (full, target) in enumerate([(rows_ref, rows_out), (ups_ref, ups_out)])
        ]

    def work(place, up):
        if place:
            late = late_up[place - 1] if up else late_down[count - place - 1]
            source = held_ref[place - 1]
            grads = [early_ref[place - 1], late[...]]
        else:
            for copy in loads:
                copy.start()
            for copy in loads:
                copy.wait()
            source = normed_ref[...]
            grads = [block_ref[:, :columns], block_ref[:, columns:]]
        at = slice(place * capacity, (place + 1) * capacity)
        for expert in range(EXP_DEV):
            pick = spread_ref[place, expert]
            taken = [
                jnp.dot(pick, s, preferred_element_type=F32).astype(BF16)
                for s in [source] + grads
            ]
            rows_ref[expert, at, :] = taken[0]
            ups_ref[expert, at, :columns] = taken[1]
            ups_ref[expert, at, columns:] = taken[2]
        for copy in stores(place):
            copy.start()

    gather_line(count, own, held, CHUNKS + 1, (send_sems, recv_sems), work)
    for place in range(count):
        for copy in stores(place):
            copy.wait()


def gather_dispatch(normed, gates, block, early, late_up, late_down, spread):
    count = lax.axis_size("expert")
    slots, width = normed.shape
    capacity = spread.shape[2]
    vmem, anywhere = pl.BlockSpec(memory_space=pltpu.VMEM), pl.BlockSpec(memory_space=pl.ANY)
    sems = pltpu.SemaphoreType.DMA((2, count - 1, CHUNKS + 1))
    sent = 2 * (count - 1) * slots * width
    full = (EXP_DEV, count * capacity, width)
    sources = [block, early, spread, *late_up, *late_down]
    return pl.pallas_call(
        functools.partial(dispatch_kernel, count),
        in_specs=[vmem] * 2 + [anywhere] * len(sources),
        out_specs=[anywhere] * 3,
        out_shape=[
            jax.ShapeDtypeStruct(full, BF16),
            jax.ShapeDtypeStruct(full, BF16),
            jax.ShapeDtypeStruct((count - 1,) + gates.shape, F32),
        ],
        scratch_shapes=[
            pltpu.VMEM(full, BF16),
            pltpu.VMEM(full, BF16),
            pltpu.VMEM((count - 1, slots, width), BF16),
        ]
        + [pltpu.VMEM(source.shape, BF16) for source in sources]
        + [
            pltpu.SemaphoreType.DMA((len(sources),)),
            pltpu.SemaphoreType.DMA((2, count)),
            sems,
            sems,
        ],
        compiler_params=pltpu.CompilerParams(
            collective_id=0, has_side_effects=True, vmem_limit_bytes=VMEM_BYTES
        ),
        cost_estimate=pl.CostEstimate(flops=0, bytes_accessed=40 * sent, transcendentals=0),
    )(normed, gates, *sources)


def sum_line(count, chunks, first, own, held, out, sems, fill):
    me = lax.axis_index("expert")

    def after(step, up):
        return me + step < count if up else me - step >= 0

    for step in range(count - 1, 0, -1):
        if step == count - 2:
            fill()
        for chunk in range(chunks):
            for up in (True, False):
                there = held(step - 1, up, chunk)

                @pl.when(after(step, up) & jnp.logical_not(after(1, not up)))
                def _():
                    line_copy(first(step, up, chunk), there, sems, step - 1, up, chunk).start()

                if step < count - 1:
                    here = held(step, up, chunk)

                    @pl.when(after(step, up) & after(1, not up))
                    def _():
                        line_copy(here, here, sems, step, up, chunk).wait_recv()
                        here[...] = (
                            here[...].astype(F32) + own(step, up, chunk)[...].astype(F32)
                        ).astype(here.dtype)
                        line_copy(here, there, sems, step - 1, up, chunk).start()

    for chunk in range(chunks):
        result = out(chunk)
        result[...] = own(0, True, chunk)[...].astype(F32)
        for up in (True, False):
            here = held(0, up, chunk)

            @pl.when(after(1, not up))
            def _():
                line_copy(here, here, sems, 0, up, chunk).wait_recv()
                result[...] += here[...].astype(F32)

    for step in range(count - 1, 0, -1):
        for chunk in range(chunks):
            for up in (True, False):

                @pl.when(after(step, up))
                def _():
                    source = first(step, up, chunk)
                    line_copy(
                        source, held(step - 1, up, chunk), sems, step - 1, up, chunk
                    ).wait_send()


def sum_kernel(
    count, slot_ref, parts_ref, gated_ref, down_ref, spread_ref, out_ref, slot_out, *refs
):
    produced_out = refs[:count]
    held_ref, *loaded = refs[count : count + 5]
    slot_held, stage_ref, stage_sems, load_sems, send_sems, recv_sems = refs[count + 5 :]
    parts, gated, down, spread = loaded
    greet_line(count)
    tall = out_ref.shape[0] // CHUNKS
    capacity = gated.shape[1] // count
    loads = [
        pltpu.make_async_copy(source, target, load_sems.at[k])
        for k, (source, target) in enumerate(
            zip([parts_ref, gated_ref, down_ref, spread_ref], loaded)
        )
    ]

    def cut(chunk):
        return pl.ds(chunk * tall, tall)

    def part(ref):
        def pick(step, up, chunk):
            place = (count - step) % count if up else step
            return slot_ref.at[place] if chunk == CHUNKS else ref.at[place, cut(chunk), :]

        return pick

    def held(step, up, chunk):
        side = 0 if up else 1
        if chunk == CHUNKS:
            return slot_held.at[side, step]
        return held_ref.at[side, step, cut(chunk), :]

    def produced(place):
        at = slice(place * capacity, (place + 1) * capacity)
        rows = [dot_last(gated[x, at, :], down[x]).astype(BF16) for x in range(EXP_DEV)]
        pick = spread[place].reshape(EXP_DEV * capacity, -1).T
        return jnp.dot(
            pick, jnp.concatenate(rows, axis=0), preferred_element_type=F32
        ).astype(BF16)

    def fill():
        for copy in loads:
            copy.start()
        for copy in loads:
            copy.wait()
        stage_out(count, produced, stage_ref, lambda p: produced_out[p], stage_sems)

    sum_line(
        count,
        CHUNKS + 1,
        part(parts_ref),
        part(parts),
        held,
        lambda c: slot_out if c == CHUNKS else out_ref.at[cut(c), :],
        (send_sems, recv_sems),
        fill,
    )


def line_sum(slot_parts, parts, gated, down_full, spread):
    count, slots, width = parts.shape
    vmem, anywhere = pl.BlockSpec(memory_space=pltpu.VMEM), pl.BlockSpec(memory_space=pl.ANY)
    sems = pltpu.SemaphoreType.DMA((2, count - 1, CHUNKS + 1))
    sources = [parts, gated, down_full, spread]
    total, slot_total, *produced = pl.pallas_call(
        functools.partial(sum_kernel, count),
        in_specs=[vmem] + [anywhere] * 4,
        out_specs=[vmem] * 2 + [anywhere] * count,
        out_shape=[
            jax.ShapeDtypeStruct((slots, width), F32),
            jax.ShapeDtypeStruct(slot_parts.shape[1:], F32),
        ]
        + [jax.ShapeDtypeStruct((slots, width), BF16)] * count,
        scratch_shapes=[pltpu.VMEM((2, count - 1, slots, width), BF16)]
        + [pltpu.VMEM(source.shape, BF16) for source in sources]
        + [
            pltpu.VMEM((2, count - 1) + slot_parts.shape[1:], F32),
            pltpu.VMEM((2, slots, width), BF16),
            pltpu.SemaphoreType.DMA((2,)),
            pltpu.SemaphoreType.DMA((4,)),
            sems,
            sems,
        ],
        compiler_params=pltpu.CompilerParams(
            collective_id=2, has_side_effects=True, vmem_limit_bytes=VMEM_BYTES
        ),
        cost_estimate=pl.CostEstimate(
            flops=0, bytes_accessed=80 * (count - 1) * slots * width, transcendentals=0
        ),
    )(slot_parts, *sources)
    return total, slot_total, produced


def last_kernel(count, parts_ref, out_ref, held_ref, send_sems, recv_sems):
    greet_line(count)
    me = lax.axis_index("expert")
    planes = out_ref.shape[0]
    edges = [planes * c // CHUNKS for c in range(CHUNKS + 1)]

    def cut(chunk):
        return pl.ds(edges[chunk], edges[chunk + 1] - edges[chunk])

    def own(step, up, chunk):
        return parts_ref.at[cut(chunk), me + step if up else me - step]

    sum_line(
        count,
        CHUNKS,
        own,
        own,
        lambda step, up, c: held_ref.at[0 if up else 1, step, cut(c)],
        lambda c: out_ref.at[cut(c)],
        (send_sems, recv_sems),
        lambda: None,
    )


def last_sum(parts):
    planes, count, rows, columns = parts.shape
    vmem = pl.BlockSpec(memory_space=pltpu.VMEM)
    sems = pltpu.SemaphoreType.DMA((2, count - 1, CHUNKS))
    return pl.pallas_call(
        functools.partial(last_kernel, count),
        in_specs=[vmem],
        out_specs=vmem,
        out_shape=jax.ShapeDtypeStruct((planes, rows, columns), F32),
        scratch_shapes=[pltpu.VMEM((2, count - 1, planes, rows, columns), BF16), sems, sems],
        compiler_params=pltpu.CompilerParams(
            collective_id=3, has_side_effects=True, vmem_limit_bytes=VMEM_BYTES
        ),
        cost_estimate=pl.CostEstimate(
            flops=0, bytes_accessed=80 * parts.size, transcendentals=0
        ),
    )(parts)


def projection_kernel(
    mixed_ref, normed_ref, merge_ref, qkv_ref, side_ref, out_ref, turned_ref, stage_ref, sems
):
    step = pl.program_id(0)
    steps = pl.num_programs(0)
    merge_steps = mixed_ref.shape[1] // (2 * COLS)
    slot = step % 2

    def store(at):
        return pltpu.make_async_copy(
            stage_ref.at[at % 2], out_ref.at[pl.ds(2 * at, 2)], sems.at[at % 2]
        )

    def fill(rhs_ref):
        for half in range(2):
            stage_ref[slot, half] = jnp.dot(
                turned_ref[...],
                rhs_ref[:, half * COLS : (half + 1) * COLS],
                preferred_element_type=F32,
            ).astype(BF16)

    @pl.when(step == 0)
    def _():
        turned_ref[...] = mixed_ref[...].T

    @pl.when(step == merge_steps)
    def _():
        turned_ref[...] = normed_ref[...].T

    @pl.when(step >= 2)
    def _():
        store(step - 2).wait()

    @pl.when(step < merge_steps)
    def _():
        fill(merge_ref)

    @pl.when(step >= merge_steps)
    def _():
        fill(qkv_ref)

    store(step).start()

    @pl.when(step == steps - 1)
    def _():
        side = pltpu.make_async_copy(side_ref, out_ref.at[2 * steps], sems.at[2])
        side.start()
        store(step - 1).wait()
        store(step).wait()
        side.wait()


def projection_terms(mixed, normed, attended_grad, qkv_grad, side):
    slots, width = mixed.shape
    wide = 2 * COLS
    first, second = attended_grad.shape[1] // wide, qkv_grad.shape[1] // wide
    whole = pl.BlockSpec((slots, width), lambda j: (0, 0))
    return pl.pallas_call(
        projection_kernel,
        grid=(first + second,),
        in_specs=[
            whole,
            whole,
            pl.BlockSpec((slots, wide), lambda j: (0, jnp.minimum(j, first - 1))),
            pl.BlockSpec((slots, wide), lambda j: (0, jnp.maximum(j - first, 0))),
            pl.BlockSpec((width, COLS), lambda j: (0, 0)),
        ],
        out_specs=pl.BlockSpec(memory_space=pl.ANY),
        out_shape=jax.ShapeDtypeStruct((2 * (first + second) + 1, width, COLS), BF16),
        scratch_shapes=[
            pltpu.VMEM((width, slots), BF16),
            pltpu.VMEM((2, 2, width, COLS), BF16),
            pltpu.SemaphoreType.DMA((3,)),
        ],
        cost_estimate=pl.CostEstimate(
            flops=2 * slots * width * (first + second) * wide,
            bytes_accessed=2 * 10**7,
            transcendentals=0,
        ),
    )(mixed, normed, attended_grad, qkv_grad, side)


def body(
    tokens,
    lengths,
    routes,
    priority,
    first_gain,
    query_weight,
    key_weight,
    value_weight,
    merge_weight,
    router_weight,
    second_gain,
    gate_weight,
    up_weight,
    down_weight,
    cotangent,
):
    slots = tokens.shape[1]
    width = tokens.shape[2]
    groups = lax.axis_size("expert")
    expert_count = router_weight.shape[1]
    capacity = 5 * slots * TOP // (8 * expert_count)
    q_cols, k_cols = HEADS * HD, KV_HEADS * HD
    side_cols = 128

    def gather_shard(value, axis=0):
        return lax.all_gather(value, "shard", axis=axis, tiled=True)

    def scatter_all(part, ahead=None):
        planes, _, columns = part.shape
        part = lax.psum_scatter(
            part.reshape(planes * groups, -1, columns), "shard", scatter_dimension=1, tiled=True
        ).reshape(planes, groups, -1, columns)
        part, ahead = lax.optimization_barrier((part, ahead))
        return last_sum(part), ahead

    side = jnp.concatenate(
        [router_weight, first_gain[:, None], second_gain[:, None]], axis=1
    )
    side = jnp.pad(side, ((0, 0), (0, side_cols - expert_count - 2)))
    first_set = gather_shard(
        jnp.concatenate([query_weight, key_weight, value_weight, side], axis=1)
    )
    merge_full = gather_shard(merge_weight)
    tables = jnp.concatenate(
        [routes[0].T, priority, jnp.broadcast_to(lengths[:, None], (1, slots))], axis=0
    )
    early_columns = width // 2
    early, other_tables, first_up, first_down, both = early_gather(
        cotangent[0], tables, gate_weight, up_weight, early_columns
    )
    tables = jnp.concatenate([tables[None], other_tables], axis=0).transpose(0, 2, 1)
    tokens, first_up, first_down = lax.optimization_barrier((tokens, first_up, first_down))
    next_up, next_down = line_hops(None, 1, 2, (first_up, first_down))
    both_full = gather_shard(both, 1)
    down_full = gather_shard(down_weight, 1)

    group = lax.axis_index("expert")
    own_experts = group * EXP_DEV + jnp.arange(EXP_DEV, dtype=jnp.int32)
    spread = jax.vmap(
        lambda t: dispatch_matrix(t[:, :TOP], t[:, TOP], t[0, TOP + 1], own_experts, capacity)
    )(tables)

    qkv_full = first_set[:, : q_cols + 2 * k_cols]
    side_full = first_set[:, q_cols + 2 * k_cols :]
    router_full = side_full[:, :expert_count]
    gain_first = side_full[:, expert_count].astype(F32)
    gain_second = side_full[:, expert_count + 1].astype(F32)

    inputs = tokens[0].astype(F32)
    length = lengths[0]
    positions = jnp.arange(slots, dtype=jnp.int32)
    live_rows = (positions < length).astype(F32)[:, None]
    cosine, sine_table = rope_tables(slots)
    rms_one = lax.rsqrt(jnp.mean(inputs * inputs, axis=-1, keepdims=True) + EPS)
    unit_one = inputs * rms_one
    normed_one = (unit_one * gain_first).astype(BF16)
    qkv = jnp.dot(normed_one, qkv_full, preferred_element_type=F32)
    qkv, next_up, next_down = lax.optimization_barrier((qkv, next_up, next_down))
    last_up, last_down = line_hops(None, 2, held=(next_up[-1], next_down[-1]))
    mixed, *low_parts, lse = attend(lengths, qkv, cosine, sine_table)
    late_up = [first_up] + next_up + last_up
    late_down = [first_down] + next_down + last_down
    attended = jnp.dot(mixed, merge_full, preferred_element_type=F32)
    hidden = inputs + live_rows * attended
    rms_two = lax.rsqrt(jnp.mean(hidden * hidden, axis=-1, keepdims=True) + EPS)
    unit_two = hidden * rms_two
    normed_two = (unit_two * gain_second).astype(BF16)

    logits = jnp.dot(normed_two, router_full, preferred_element_type=F32)
    chosen = (
        routes[0][:, :, None] == jnp.arange(expert_count, dtype=jnp.int32)[None, None, :]
    ).astype(F32)
    chosen_any = jnp.sum(chosen, axis=1)
    masked = jnp.where(chosen_any > 0, logits, NEGATIVE)
    peak = jnp.max(masked, axis=-1, keepdims=True)
    exp_logits = jnp.exp(masked - peak) * chosen_any
    gate_dense = exp_logits / jnp.sum(exp_logits, axis=-1, keepdims=True)

    gates = gate_dense.T
    rows, ups, other_gates = gather_dispatch(
        normed_two, gates, cotangent[0], early, late_up, late_down, spread
    )
    gates_all = jnp.concatenate([gates[None], other_gates], axis=0)
    gates_own = lax.dynamic_slice_in_dim(gates_all, group * EXP_DEV, EXP_DEV, axis=1)
    slot_gate = jnp.sum(spread.astype(F32) * gates_own[:, :, None, :], axis=-1)
    gates = slot_gate.transpose(1, 0, 2).reshape(EXP_DEV, groups * capacity, 1)

    gated, gate_pre_grad, lift_pre_grad, back_parts, slot_grad = expert_core(
        rows, ups, gates, both_full, down_full, spread
    )

    slot_grad = slot_grad.reshape(EXP_DEV, groups, capacity).transpose(1, 0, 2)
    token_grad = jnp.sum(spread.astype(F32) * slot_grad[:, :, :, None], axis=2)
    token_grad = lax.dynamic_update_slice_in_dim(
        jnp.zeros((groups, expert_count, slots), F32), token_grad, group * EXP_DEV, axis=1
    )
    expert_grads = expert_weights(rows, ups, gated, gate_pre_grad, lift_pre_grad)
    back_parts, expert_grads = lax.optimization_barrier((back_parts, expert_grads))
    back_total, slot_back, produced = line_sum(
        token_grad, back_parts, gated, down_full, spread
    )
    slot_back = slot_back.T
    expert_grads = lax.psum_scatter(
        expert_grads.reshape(3 * EXP_DEV, width, -1), "shard", scatter_dimension=1, tiled=True
    )
    sums = scatter_hops(produced, 0, 1)

    upstream = cotangent[0].astype(F32)
    picked_grad = gate_dense * (
        slot_back - jnp.sum(gate_dense * slot_back, axis=-1, keepdims=True)
    )
    logit_grad = picked_grad.astype(BF16)
    router_part = jnp.einsum("ld,le->de", normed_two, logit_grad, preferred_element_type=F32)
    normed_two_grad = jnp.einsum("le,de->ld", logit_grad, router_full, preferred_element_type=F32)
    normed_two_grad = normed_two_grad + back_total
    scaled_two = normed_two_grad * gain_second
    second_gain_part = jnp.sum(normed_two_grad * unit_two, axis=0)
    hidden_grad = upstream + rms_two * (
        scaled_two - unit_two * jnp.mean(scaled_two * unit_two, axis=-1, keepdims=True)
    )
    attended_grad = (live_rows * hidden_grad).astype(BF16)

    mixed_grad = jnp.einsum(
        "ld,hd->lh", attended_grad, merge_full, preferred_element_type=F32
    ).astype(BF16)
    qkv_grad = attend_back(lengths, *low_parts, mixed_grad, lse, cosine, sine_table)
    side_part = jnp.concatenate([router_part, second_gain_part[:, None]], axis=1)
    side_part = jnp.pad(side_part, ((0, 0), (0, COLS - expert_count - 1))).astype(BF16)
    terms = projection_terms(mixed, normed_one, attended_grad, qkv_grad, side_part)
    terms, expert_grads = lax.optimization_barrier((terms, expert_grads))
    sums, qkv_grad, terms = lax.optimization_barrier((sums, qkv_grad, terms))
    sums = scatter_hops(produced, 1, groups - 1, sums)
    normed_one_grad = jnp.einsum("lh,dh->ld", qkv_grad, qkv_full, preferred_element_type=F32)
    scaled_one = normed_one_grad * gain_first
    input_grad = hidden_grad + rms_one * (
        scaled_one - unit_one * jnp.mean(scaled_one * unit_one, axis=-1, keepdims=True)
    )
    block_output = (
        hidden + produced[0].astype(F32) + sums[0].astype(F32) + sums[1].astype(F32)
    )
    gate_grad, up_grad, down_grad = jnp.split(expert_grads.astype(F32), 3)
    reduced, (block_output, input_grad) = scatter_all(terms, (block_output, input_grad))
    own_rows = reduced.shape[1]
    reduced = reduced.transpose(1, 0, 2).reshape(own_rows, -1)
    place = (group * lax.axis_size("shard") + lax.axis_index("shard")) * own_rows
    merge_grad, qkv_reduced, side_grad = jnp.split(
        reduced, [width, width + q_cols + 2 * k_cols], axis=1
    )
    own_weights = lax.dynamic_slice_in_dim(qkv_full, place, own_rows, axis=0).astype(F32)
    own_gain = lax.dynamic_slice_in_dim(gain_first, place, own_rows)
    first_gain_grad = jnp.sum(own_weights * qkv_reduced, axis=1) / own_gain
    query_grad, key_grad, value_grad = jnp.split(qkv_reduced, [q_cols, q_cols + k_cols], axis=1)
    return (
        block_output[None],
        input_grad[None],
        first_gain_grad,
        query_grad,
        key_grad,
        value_grad,
        merge_grad,
        side_grad[:, :expert_count],
        side_grad[:, expert_count],
        gate_grad,
        up_grad,
        down_grad,
    )


def solution(mesh):
    both = ("expert", "shard")
    in_specs = (
        P(both, None, None),
        P(both),
        P(both, None, None),
        P(both, None),
        P("shard"),
        P("shard", None),
        P("shard", None),
        P("shard", None),
        P("shard", None),
        P("shard", None),
        P("shard"),
        P("expert", "shard", None),
        P("expert", "shard", None),
        P("expert", "shard", None),
        P(both, None, None),
    )
    out_specs = (
        P(both, None, None),
        P(both, None, None),
        P(both),
        P(both, None),
        P(both, None),
        P(both, None),
        P(both, None),
        P(both, None),
        P(both),
        P("expert", "shard", None),
        P("expert", "shard", None),
        P("expert", "shard", None),
    )
    return jax.shard_map(body, mesh=mesh, in_specs=in_specs, out_specs=out_specs, check_vma=False)
```

```python
import functools

import jax
import jax.numpy as jnp
import numpy as np
from jax import lax
from jax.experimental import pallas as pl
from jax.experimental.pallas import tpu as pltpu
from jax.sharding import PartitionSpec as P

HEADS = 24
KV_HEADS = 8
HD = 64
TOP = 8
EXP_DEV = 5
SHARE = HEADS // KV_HEADS
Q_BLOCK = 128
VMEM_BYTES = 63 * 2**20
CHUNKS = 4
COLS = 256

EPS = 1e-05
THETA = 10000.0
NEGATIVE = -1e30
F32 = jnp.float32
BF16 = jnp.bfloat16


def rope_tables(slots):
    frequency = THETA ** (-np.arange(HD // 2, dtype=np.float32) * np.float32(2.0) / HD)
    angles = np.arange(slots, dtype=np.float32)[:, None] * frequency.astype(np.float32)[None, :]
    cosine, sine = np.cos(angles), np.sin(angles)
    return (
        jnp.asarray(np.concatenate([cosine] * 4, axis=1), F32),
        jnp.asarray(np.concatenate([-sine, sine, -sine, sine], axis=1), F32),
    )


def dispatch_matrix(routes, priority, length, expert_ids, capacity):
    slots = routes.shape[0]
    positions = jnp.arange(slots, dtype=jnp.int32)
    live = positions < length
    named = jnp.any(routes[:, :, None] == expert_ids[None, None, :], axis=1) & live[:, None]
    earlier = (priority[None, :] < priority[:, None]).astype(BF16)
    slot = jnp.dot(earlier, named.astype(BF16), preferred_element_type=F32).astype(jnp.int32)
    slot = jnp.where(named, slot, capacity)
    return (
        slot.T[:, None, :] == jnp.arange(capacity, dtype=jnp.int32)[None, :, None]
    ).astype(BF16)


def line_hops(block, first=0, last=None, held=None):
    count = lax.axis_size("expert")
    last = count - 1 if last is None else last
    held_up, held_down = (block, block) if held is None else held
    up, down = [], []
    for step in range(first, last):
        held_up = lax.ppermute(
            held_up, "expert", [(i, i + 1) for i in range(step, count - 1)]
        )
        held_down = lax.ppermute(
            held_down, "expert", [(i + 1, i) for i in range(0, count - 1 - step)]
        )
        up.append(held_up)
        down.append(held_down)
    return up, down


def scatter_hops(parts, first=0, last=None, held=None):
    count = lax.axis_size("expert")
    last = count - 1 if last is None else last
    held_up, held_down = (None, None) if held is None else held
    for step in range(first, last):
        piece_up = parts[step + 1]
        piece_down = parts[count - 1 - step]
        if step:
            piece_up = piece_up.astype(F32) + held_up.astype(F32)
            piece_down = piece_down.astype(F32) + held_down.astype(F32)
        held_up = lax.ppermute(
            piece_up.astype(BF16), "expert", [(i, i + 1) for i in range(step + 1)]
        )
        held_down = lax.ppermute(
            piece_down.astype(BF16),
            "expert",
            [(i + 1, i) for i in range(count - 2 - step, count - 1)],
        )
    return held_up, held_down


def turn(values, cosine, sine):
    first = lax.broadcasted_iota(jnp.int32, (1, 2 * HD), 1) % HD < HD // 2
    out = []
    for start in range(0, values.shape[1], 2 * HD):
        part = values[:, start : start + 2 * HD]
        other = jnp.where(
            first, pltpu.roll(part, 2 * HD - HD // 2, 1), pltpu.roll(part, HD // 2, 1)
        )
        out.append(part * cosine + other * sine)
    return out[0] if len(out) == 1 else jnp.concatenate(out, axis=1)


def last_keys(block, length):
    lane = lax.broadcasted_iota(jnp.int32, (1, SHARE * Q_BLOCK), 1)
    return jnp.minimum(block * Q_BLOCK + lane % Q_BLOCK, length - 1)


def head_block(values, pair_head, block):
    rows = slice(block * Q_BLOCK, (block + 1) * Q_BLOCK)
    heads = range(pair_head * SHARE, (pair_head + 1) * SHARE)
    return jnp.concatenate([values[rows, h * HD : (h + 1) * HD] for h in heads], axis=0)


def rows_of_heads(parts):
    tall = [
        part[:, g * Q_BLOCK : (g + 1) * Q_BLOCK] for part in parts for g in range(SHARE)
    ]
    return jnp.concatenate(tall, axis=0).T


def dot_last(a, b):
    return lax.dot_general(a, b, (((1,), (1,)), ((), ())), preferred_element_type=F32)


def attend_kernel(
    length_ref, q_ref, k_ref, v_ref, cos_ref, sin_ref,
    mixed_ref, q_low_ref, k_low_ref, v_low_ref, lse_ref,
):
    length = length_ref[0]
    slots = q_ref.shape[0]
    cosine, sine = cos_ref[...], sin_ref[...]
    queries = (turn(q_ref[...], cosine, sine) * HD**-0.5).astype(BF16)
    keys = turn(k_ref[...], cosine, sine).astype(BF16)
    values = v_ref[...]
    q_low_ref[...] = queries
    k_low_ref[...] = keys
    v_low_ref[...] = values.astype(BF16)
    values_t = values.T.astype(BF16)
    blocks = slots // Q_BLOCK
    for block in range(blocks):
        span = (block + 1) * Q_BLOCK
        limit = last_keys(block, length)
        key_id = lax.broadcasted_iota(jnp.int32, (span, 1), 0)
        parts = []
        for head in range(2):
            scores = dot_last(
                keys[:span, head * HD : (head + 1) * HD], head_block(queries, head, block)
            )
            scores = jnp.where(key_id <= limit, scores, NEGATIVE)
            peak = jnp.max(scores, axis=0, keepdims=True)
            exp_scores = jnp.exp(scores - peak)
            total = jnp.sum(exp_scores, axis=0, keepdims=True)
            lse_ref[0, pl.ds(head * blocks + block, 1), :] = peak + jnp.log(total)
            part = jnp.dot(
                values_t[head * HD : (head + 1) * HD, :span],
                exp_scores.astype(BF16),
                preferred_element_type=F32,
            )
            parts.append(part / total)
        mixed_ref[block * Q_BLOCK : span, :] = rows_of_heads(parts).astype(BF16)


def attend_back_kernel(
    length_ref, q_ref, k_ref, v_ref, grad_ref, lse_ref, cos_ref, sin_ref, out_ref, dk_ref, dv_ref
):
    length = length_ref[0]
    slots, q_cols = q_ref.shape
    pairs = pl.num_programs(0)
    pair = pl.program_id(0)
    q_at = pl.ds(pl.multiple_of(pair * q_cols, 2 * HD), q_cols)
    k_at = pl.ds(pl.multiple_of(pairs * q_cols + pair * 2 * HD, 2 * HD), 2 * HD)
    v_at = pl.ds(pl.multiple_of(pairs * (q_cols + 2 * HD) + pair * 2 * HD, 2 * HD), 2 * HD)
    cosine, sine = cos_ref[...], -sin_ref[...]
    queries, keys, values = q_ref[...], k_ref[...], v_ref[...]
    grad = grad_ref[...]
    keys_t = keys.astype(F32).T.astype(BF16)
    dk_ref[...] = jnp.zeros_like(dk_ref)
    dv_ref[...] = jnp.zeros_like(dv_ref)
    blocks = slots // Q_BLOCK
    for block in range(blocks):
        rows = slice(block * Q_BLOCK, (block + 1) * Q_BLOCK)
        span = (block + 1) * Q_BLOCK
        limit = last_keys(block, length)
        key_id = lax.broadcasted_iota(jnp.int32, (span, 1), 0)
        parts = []
        for head in range(2):
            cols = slice(head * HD, (head + 1) * HD)
            query = head_block(queries, head, block)
            out_grad = head_block(grad, head, block)
            scores = dot_last(keys[:span, cols], query)
            scores = jnp.where(key_id <= limit, scores, NEGATIVE)
            probs = jnp.exp(scores - lse_ref[0, pl.ds(head * blocks + block, 1), :])
            prob_back = dot_last(values[:span, cols], out_grad)
            mean = jnp.sum(probs * prob_back, axis=0, keepdims=True)
            score_grad = (probs * (prob_back - mean)).astype(BF16)
            dv_ref[head, :span, :] += jnp.dot(
                probs.astype(BF16), out_grad, preferred_element_type=F32
            )
            dk_ref[head, :span, :] += jnp.dot(score_grad, query, preferred_element_type=F32)
            parts.append(
                jnp.dot(keys_t[cols, :span], score_grad, preferred_element_type=F32)
                * HD**-0.5
            )
        out_ref[rows, q_at] = turn(rows_of_heads(parts), cosine[rows], sine[rows]).astype(
            BF16
        )
    key_grad = jnp.concatenate([dk_ref[0], dk_ref[1]], axis=1)
    out_ref[:, k_at] = turn(key_grad, cosine, sine).astype(BF16)
    out_ref[:, v_at] = jnp.concatenate([dv_ref[0], dv_ref[1]], axis=1).astype(BF16)


def column_block(slots, columns, first=0):
    return pl.BlockSpec((slots, columns), lambda p: (0, first + p))


def attention_specs(slots):
    pairs = KV_HEADS // 2
    q_cols, cols = 2 * SHARE * HD, 2 * (SHARE + 2) * HD
    blocks = slots // Q_BLOCK
    whole = pl.BlockSpec((slots, 2 * HD), lambda p: (0, 0))
    lse = pl.BlockSpec((1, 2 * blocks, SHARE * Q_BLOCK), lambda p: (p, 0, 0))
    scalar = pl.BlockSpec(memory_space=pltpu.SMEM)
    return pairs, q_cols, cols, blocks, whole, lse, scalar


def attend(length, qkv, cosine, sine):
    slots = qkv.shape[0]
    pairs, q_cols, cols, blocks, whole, lse, scalar = attention_specs(slots)
    queries, keys = column_block(slots, q_cols), column_block(slots, 2 * HD)
    key_first = pairs * q_cols // (2 * HD)
    low_keys = jax.ShapeDtypeStruct((slots, pairs * 2 * HD), BF16)
    low_queries = jax.ShapeDtypeStruct((slots, pairs * q_cols), BF16)
    return pl.pallas_call(
        attend_kernel,
        grid=(pairs,),
        in_specs=[
            scalar,
            queries,
            column_block(slots, 2 * HD, key_first),
            column_block(slots, 2 * HD, key_first + pairs),
            whole,
            whole,
        ],
        out_specs=[queries, queries, keys, keys, lse],
        out_shape=[
            low_queries,
            low_queries,
            low_keys,
            low_keys,
            jax.ShapeDtypeStruct((pairs, 2 * blocks, SHARE * Q_BLOCK), F32),
        ],
        cost_estimate=pl.CostEstimate(
            flops=24 * HEADS * slots * slots * HD // 4, bytes_accessed=10**7, transcendentals=0
        ),
    )(length, qkv, qkv, qkv, cosine, sine)


def attend_back(length, queries, keys, values, grad, lse_rows, cosine, sine):
    slots = grad.shape[0]
    pairs, q_cols, cols, blocks, whole, lse, scalar = attention_specs(slots)
    wide, narrow = column_block(slots, q_cols), column_block(slots, 2 * HD)
    return pl.pallas_call(
        attend_back_kernel,
        grid=(pairs,),
        in_specs=[scalar, wide, narrow, narrow, wide, lse, whole, whole],
        out_specs=pl.BlockSpec((slots, pairs * cols), lambda p: (0, 0)),
        out_shape=jax.ShapeDtypeStruct((slots, pairs * cols), BF16),
        scratch_shapes=[pltpu.VMEM((2, slots, HD), F32), pltpu.VMEM((2, slots, HD), F32)],
        cost_estimate=pl.CostEstimate(
            flops=60 * HEADS * slots * slots * HD // 4, bytes_accessed=10**7, transcendentals=0
        ),
    )(length, queries, keys, values, grad, lse_rows, cosine, sine)


def stage_out(count, make, stage_ref, targets, sems):
    copies = [
        pltpu.make_async_copy(stage_ref.at[p % 2], targets(p), sems.at[p % 2])
        for p in range(count)
    ]
    for p in range(count):
        if p > 1:
            copies[p - 2].wait()
        stage_ref[p % 2] = make(p)
        copies[p].start()
    for copy in copies[-2:]:
        copy.wait()


def token_sum(spread_ref, rows_ref, place):
    capacity = rows_ref.shape[1] // spread_ref.shape[0]
    pick = spread_ref[place].reshape(EXP_DEV * capacity, -1).T
    rows = rows_ref[:, place * capacity : (place + 1) * capacity, :]
    return jnp.dot(
        pick, rows.reshape(EXP_DEV * capacity, -1), preferred_element_type=F32
    ).astype(BF16)


def expert_kernel(
    rows_ref, ups_ref, gates_ref, gate_ref, up_ref, down_ref, spread_ref,
    gated_ref, gate_grad_ref, lift_grad_ref, parts_ref, slot_ref,
    back_ref, stage_ref, sems,
):
    rows, gates = rows_ref[0], gates_ref[0]
    gate_pre = jnp.dot(rows, gate_ref[0], preferred_element_type=F32)
    lift_pre = jnp.dot(rows, up_ref[0], preferred_element_type=F32)
    act_grad = jnp.dot(ups_ref[0], down_ref[0], preferred_element_type=F32)
    sigmoid_gate = jax.nn.sigmoid(gate_pre)
    silu_gate = gate_pre * sigmoid_gate
    activated = silu_gate * lift_pre
    slot_ref[0] = jnp.sum(act_grad * activated, axis=-1, keepdims=True)
    gated_ref[0] = (activated * gates).astype(BF16)
    act_grad = act_grad * gates
    gate_pre_grad = (
        act_grad * lift_pre * (sigmoid_gate + silu_gate * (1.0 - sigmoid_gate))
    ).astype(BF16)
    lift_pre_grad = (act_grad * silu_gate).astype(BF16)
    gate_grad_ref[0] = gate_pre_grad
    lift_grad_ref[0] = lift_pre_grad
    step = pl.program_id(0)
    back_ref[step] = (
        dot_last(gate_pre_grad, gate_ref[0]) + dot_last(lift_pre_grad, up_ref[0])
    ).astype(BF16)

    @pl.when(step == pl.num_programs(0) - 1)
    def _():
        stage_out(
            spread_ref.shape[0],
            lambda p: token_sum(spread_ref, back_ref, p),
            stage_ref,
            lambda p: parts_ref.at[p],
            sems,
        )


def expert_block(*shape, first=0):
    return pl.BlockSpec((1,) + shape, lambda x: (first + x, 0, 0))


def expert_core(rows, ups, gates, both_full, down_full, spread):
    experts, total, width = ups.shape
    count, _, capacity, slots = spread.shape
    hidden = down_full.shape[-1]
    narrow, wide = expert_block(total, hidden), expert_block(total, width)
    weight, single = expert_block(width, hidden), expert_block(total, 1)
    low = jax.ShapeDtypeStruct((experts, total, hidden), BF16)
    return pl.pallas_call(
        expert_kernel,
        grid=(experts,),
        in_specs=[
            wide, wide, single,
            weight, expert_block(width, hidden, first=experts), weight,
            pl.BlockSpec(spread.shape, lambda x: (0, 0, 0, 0)),
        ],
        out_specs=[narrow, narrow, narrow, pl.BlockSpec(memory_space=pl.ANY), single],
        out_shape=[
            low,
            low,
            low,
            jax.ShapeDtypeStruct((count, slots, width), BF16),
            jax.ShapeDtypeStruct((experts, total, 1), F32),
        ],
        scratch_shapes=[
            pltpu.VMEM((experts, total, width), BF16),
            pltpu.VMEM((2, slots, width), BF16),
            pltpu.SemaphoreType.DMA((2,)),
        ],
        compiler_params=pltpu.CompilerParams(vmem_limit_bytes=VMEM_BYTES),
        cost_estimate=pl.CostEstimate(
            flops=12 * experts * total * width * hidden,
            bytes_accessed=60 * 10**6,
            transcendentals=0,
        ),
    )(rows, ups, gates, both_full, both_full, down_full, spread)


def weight_kernel(rows_ref, ups_ref, gated_ref, gate_grad_ref, lift_grad_ref, grads_ref):
    rows_t = rows_ref[0].T
    grads_ref[0, 0] = jnp.dot(
        rows_t, gate_grad_ref[0], preferred_element_type=F32
    ).astype(BF16)
    grads_ref[1, 0] = jnp.dot(
        rows_t, lift_grad_ref[0], preferred_element_type=F32
    ).astype(BF16)
    grads_ref[2, 0] = jnp.dot(
        ups_ref[0].T, gated_ref[0], preferred_element_type=F32
    ).astype(BF16)


def expert_weights(rows, ups, gated, gate_grad, lift_grad):
    experts, count, width = ups.shape
    hidden = gated.shape[-1]
    narrow, wide = expert_block(count, hidden), expert_block(count, width)
    return pl.pallas_call(
        weight_kernel,
        grid=(experts,),
        in_specs=[wide, wide, narrow, narrow, narrow],
        out_specs=pl.BlockSpec((3, 1, width, hidden), lambda x: (0, x, 0, 0)),
        out_shape=jax.ShapeDtypeStruct((3, experts, width, hidden), BF16),
        compiler_params=pltpu.CompilerParams(vmem_limit_bytes=VMEM_BYTES),
        cost_estimate=pl.CostEstimate(
            flops=6 * experts * count * width * hidden, bytes_accessed=50 * 10**6, transcendentals=0
        ),
    )(rows, ups, gated, gate_grad, lift_grad)


def line_copy(source, target, sems, step, up, chunk):
    send_sems, recv_sems = sems
    side = 0 if up else 1
    me = lax.axis_index("expert")
    return pltpu.make_async_remote_copy(
        src_ref=source,
        dst_ref=target,
        send_sem=send_sems.at[side, step, chunk],
        recv_sem=recv_sems.at[side, step, chunk],
        device_id={"expert": me + 1 if up else me - 1},
        device_id_type=pl.DeviceIdType.MESH,
    )


def greet_line(count):
    me = lax.axis_index("expert")
    barrier = pltpu.get_barrier_semaphore()
    for up in (True, False):
        there = me < count - 1 if up else me > 0

        @pl.when(there)
        def _():
            pl.semaphore_signal(
                barrier,
                inc=1,
                device_id={"expert": me + 1 if up else me - 1},
                device_id_type=pl.DeviceIdType.MESH,
            )

    ends = (me == 0) | (me == count - 1)

    @pl.when(ends)
    def _():
        pl.semaphore_wait(barrier, 1)

    @pl.when(jnp.logical_not(ends))
    def _():
        pl.semaphore_wait(barrier, 2)


def gather_line(count, own, held, chunks, sems, work, short=0):
    me = lax.axis_index("expert")

    def after(step, up):
        return me + step < count if up else me - step >= 0

    def place(step, up):
        return step if up else count - step

    def reach(chunk):
        return count - 1 if chunk < chunks - short else 1

    for chunk in range(chunks):
        for up in (True, False):

            @pl.when(after(1, up))
            def _():
                line_copy(own(chunk), held(place(1, up), chunk), sems, 0, up, chunk).start()

    work(0, True)
    for step in range(1, count):
        for chunk in range(chunks):
            for up in (True, False):
                if step > reach(chunk):
                    continue
                here = held(place(step, up), chunk)

                @pl.when(after(step, not up))
                def _():
                    line_copy(here, here, sems, step - 1, up, chunk).wait_recv()

                if step < reach(chunk):

                    @pl.when(after(step, not up) & after(1, up))
                    def _():
                        there = held(place(step + 1, up), chunk)
                        line_copy(here, there, sems, step, up, chunk).start()

        for up in (True, False):

            @pl.when(after(step, not up))
            def _():
                work(place(step, up), up)

    for step in range(count - 1):
        for chunk in range(chunks):
            for up in (True, False):
                if step >= reach(chunk):
                    continue

                @pl.when(after(step, not up) & after(1, up))
                def _():
                    source = held(place(step, up), chunk) if step else own(chunk)
                    line_copy(
                        source, held(place(step + 1, up), chunk), sems, step, up, chunk
                    ).wait_send()


def early_kernel(
    count, columns, block_ref, tables_ref, gate_ref, up_ref,
    held_ref, tables_out, late_up, late_down, both_ref,
    both_vmem, local_sems, send_sems, recv_sems,
):
    greet_line(count)
    tall = block_ref.shape[0] // CHUNKS
    experts = gate_ref.shape[0]

    def rows(chunk):
        return pl.ds(chunk * tall, tall)

    def own(chunk):
        if chunk == CHUNKS:
            return tables_ref
        if chunk > CHUNKS:
            late = block_ref.shape[1] - columns
            return block_ref.at[rows(chunk - CHUNKS - 1), pl.ds(columns, late)]
        return block_ref.at[rows(chunk), pl.ds(0, columns)]

    def held(place, chunk):
        if chunk == CHUNKS:
            return tables_out.at[place - 1]
        if chunk > CHUNKS:
            late = late_up if place == 1 else late_down
            return late.at[rows(chunk - CHUNKS - 1), :]
        return held_ref.at[place - 1, rows(chunk), :]

    def work(place, up):
        if place:
            return
        loads = [
            pltpu.make_async_copy(gate_ref, both_vmem.at[pl.ds(0, experts)], local_sems.at[0]),
            pltpu.make_async_copy(up_ref, both_vmem.at[pl.ds(experts, experts)], local_sems.at[1]),
        ]
        store = pltpu.make_async_copy(both_vmem, both_ref, local_sems.at[2])
        for copy in loads:
            copy.start()
        for copy in loads:
            copy.wait()
        store.start()
        store.wait()

    gather_line(
        count, own, held, 2 * CHUNKS + 1, (send_sems, recv_sems), work, short=CHUNKS
    )


def early_gather(block, tables, gate_weight, up_weight, columns):
    count = lax.axis_size("expert")
    slots, width = block.shape
    sems = pltpu.SemaphoreType.DMA((2, count - 1, 2 * CHUNKS + 1))
    sent = 2 * (count - 1) * slots * columns
    vmem, anywhere = pl.BlockSpec(memory_space=pltpu.VMEM), pl.BlockSpec(memory_space=pl.ANY)
    both = (2 * gate_weight.shape[0],) + gate_weight.shape[1:]
    return pl.pallas_call(
        functools.partial(early_kernel, count, columns),
        in_specs=[vmem, vmem, anywhere, anywhere],
        out_specs=[anywhere] * 5,
        out_shape=[
            jax.ShapeDtypeStruct((count - 1, slots, columns), BF16),
            jax.ShapeDtypeStruct((count - 1,) + tables.shape, jnp.int32),
            jax.ShapeDtypeStruct((slots, width - columns), BF16),
            jax.ShapeDtypeStruct((slots, width - columns), BF16),
            jax.ShapeDtypeStruct(both, BF16),
        ],
        scratch_shapes=[pltpu.VMEM(both, BF16), pltpu.SemaphoreType.DMA((3,)), sems, sems],
        compiler_params=pltpu.CompilerParams(
            collective_id=1, has_side_effects=True, vmem_limit_bytes=VMEM_BYTES
        ),
        cost_estimate=pl.CostEstimate(flops=0, bytes_accessed=40 * sent, transcendentals=0),
    )(block, tables, gate_weight, up_weight)


def dispatch_kernel(count, normed_ref, gates_ref, *refs):
    sources = refs[: 2 * count + 1]
    rows_out, ups_out, gates_out, rows_ref, ups_ref, held_ref = refs[2 * count + 1 : 2 * count + 7]
    loaded = refs[2 * count + 7 : 4 * count + 8]
    load_sems, store_sems, send_sems, recv_sems = refs[4 * count + 8 :]
    block_ref, early_ref, spread_ref = loaded[:3]
    late_up, late_down = loaded[3 : count + 2], loaded[count + 2 :]
    greet_line(count)
    tall = normed_ref.shape[0] // CHUNKS
    capacity = rows_ref.shape[1] // count
    columns = early_ref.shape[-1]
    loads = [
        pltpu.make_async_copy(source, target, load_sems.at[k])
        for k, (source, target) in enumerate(zip(sources, loaded))
    ]

    def cut(chunk):
        return pl.ds(chunk * tall, tall)

    def own(chunk):
        return gates_ref if chunk == CHUNKS else normed_ref.at[cut(chunk), :]

    def held(place, chunk):
        if chunk == CHUNKS:
            return gates_out.at[place - 1]
        return held_ref.at[place - 1, cut(chunk), :]

    def stores(place):
        at = pl.ds(place * capacity, capacity)
        return [
            pltpu.make_async_copy(
                full.at[:, at, :], target.at[:, at, :], store_sems.at[k, place]
            )
            for k, (full, target) in enumerate([(rows_ref, rows_out), (ups_ref, ups_out)])
        ]

    def work(place, up):
        if place:
            late = late_up[place - 1] if up else late_down[count - place - 1]
            source = held_ref[place - 1]
            grads = [early_ref[place - 1], late[...]]
        else:
            for copy in loads:
                copy.start()
            for copy in loads:
                copy.wait()
            source = normed_ref[...]
            grads = [block_ref[:, :columns], block_ref[:, columns:]]
        at = slice(place * capacity, (place + 1) * capacity)
        for expert in range(EXP_DEV):
            pick = spread_ref[place, expert]
            taken = [
                jnp.dot(pick, s, preferred_element_type=F32).astype(BF16)
                for s in [source] + grads
            ]
            rows_ref[expert, at, :] = taken[0]
            ups_ref[expert, at, :columns] = taken[1]
            ups_ref[expert, at, columns:] = taken[2]
        for copy in stores(place):
            copy.start()

    gather_line(count, own, held, CHUNKS + 1, (send_sems, recv_sems), work)
    for place in range(count):
        for copy in stores(place):
            copy.wait()


def gather_dispatch(normed, gates, block, early, late_up, late_down, spread):
    count = lax.axis_size("expert")
    slots, width = normed.shape
    capacity = spread.shape[2]
    vmem, anywhere = pl.BlockSpec(memory_space=pltpu.VMEM), pl.BlockSpec(memory_space=pl.ANY)
    sems = pltpu.SemaphoreType.DMA((2, count - 1, CHUNKS + 1))
    sent = 2 * (count - 1) * slots * width
    full = (EXP_DEV, count * capacity, width)
    sources = [block, early, spread, *late_up, *late_down]
    return pl.pallas_call(
        functools.partial(dispatch_kernel, count),
        in_specs=[vmem] * 2 + [anywhere] * len(sources),
        out_specs=[anywhere] * 3,
        out_shape=[
            jax.ShapeDtypeStruct(full, BF16),
            jax.ShapeDtypeStruct(full, BF16),
            jax.ShapeDtypeStruct((count - 1,) + gates.shape, F32),
        ],
        scratch_shapes=[
            pltpu.VMEM(full, BF16),
            pltpu.VMEM(full, BF16),
            pltpu.VMEM((count - 1, slots, width), BF16),
        ]
        + [pltpu.VMEM(source.shape, BF16) for source in sources]
        + [
            pltpu.SemaphoreType.DMA((len(sources),)),
            pltpu.SemaphoreType.DMA((2, count)),
            sems,
            sems,
        ],
        compiler_params=pltpu.CompilerParams(
            collective_id=0, has_side_effects=True, vmem_limit_bytes=VMEM_BYTES
        ),
        cost_estimate=pl.CostEstimate(flops=0, bytes_accessed=40 * sent, transcendentals=0),
    )(normed, gates, *sources)


def sum_line(count, chunks, first, own, held, out, sems, fill):
    me = lax.axis_index("expert")

    def after(step, up):
        return me + step < count if up else me - step >= 0

    for step in range(count - 1, 0, -1):
        if step == count - 2:
            fill()
        for chunk in range(chunks):
            for up in (True, False):
                there = held(step - 1, up, chunk)

                @pl.when(after(step, up) & jnp.logical_not(after(1, not up)))
                def _():
                    line_copy(first(step, up, chunk), there, sems, step - 1, up, chunk).start()

                if step < count - 1:
                    here = held(step, up, chunk)

                    @pl.when(after(step, up) & after(1, not up))
                    def _():
                        line_copy(here, here, sems, step, up, chunk).wait_recv()
                        here[...] = (
                            here[...].astype(F32) + own(step, up, chunk)[...].astype(F32)
                        ).astype(here.dtype)
                        line_copy(here, there, sems, step - 1, up, chunk).start()

    for chunk in range(chunks):
        result = out(chunk)
        result[...] = own(0, True, chunk)[...].astype(F32)
        for up in (True, False):
            here = held(0, up, chunk)

            @pl.when(after(1, not up))
            def _():
                line_copy(here, here, sems, 0, up, chunk).wait_recv()
                result[...] += here[...].astype(F32)

    for step in range(count - 1, 0, -1):
        for chunk in range(chunks):
            for up in (True, False):

                @pl.when(after(step, up))
                def _():
                    source = first(step, up, chunk)
                    line_copy(
                        source, held(step - 1, up, chunk), sems, step - 1, up, chunk
                    ).wait_send()


def sum_kernel(
    count, slot_ref, parts_ref, gated_ref, down_ref, spread_ref, out_ref, slot_out, *refs
):
    produced_out = refs[:count]
    held_ref, *loaded = refs[count : count + 5]
    slot_held, stage_ref, stage_sems, load_sems, send_sems, recv_sems = refs[count + 5 :]
    parts, gated, down, spread = loaded
    greet_line(count)
    tall = out_ref.shape[0] // CHUNKS
    capacity = gated.shape[1] // count
    loads = [
        pltpu.make_async_copy(source, target, load_sems.at[k])
        for k, (source, target) in enumerate(
            zip([parts_ref, gated_ref, down_ref, spread_ref], loaded)
        )
    ]

    def cut(chunk):
        return pl.ds(chunk * tall, tall)

    def part(ref):
        def pick(step, up, chunk):
            place = (count - step) % count if up else step
            return slot_ref.at[place] if chunk == CHUNKS else ref.at[place, cut(chunk), :]

        return pick

    def held(step, up, chunk):
        side = 0 if up else 1
        if chunk == CHUNKS:
            return slot_held.at[side, step]
        return held_ref.at[side, step, cut(chunk), :]

    def produced(place):
        at = slice(place * capacity, (place + 1) * capacity)
        rows = [dot_last(gated[x, at, :], down[x]).astype(BF16) for x in range(EXP_DEV)]
        pick = spread[place].reshape(EXP_DEV * capacity, -1).T
        return jnp.dot(
            pick, jnp.concatenate(rows, axis=0), preferred_element_type=F32
        ).astype(BF16)

    def fill():
        for copy in loads:
            copy.start()
        for copy in loads:
            copy.wait()
        stage_out(count, produced, stage_ref, lambda p: produced_out[p], stage_sems)

    sum_line(
        count,
        CHUNKS + 1,
        part(parts_ref),
        part(parts),
        held,
        lambda c: slot_out if c == CHUNKS else out_ref.at[cut(c), :],
        (send_sems, recv_sems),
        fill,
    )


def line_sum(slot_parts, parts, gated, down_full, spread):
    count, slots, width = parts.shape
    vmem, anywhere = pl.BlockSpec(memory_space=pltpu.VMEM), pl.BlockSpec(memory_space=pl.ANY)
    sems = pltpu.SemaphoreType.DMA((2, count - 1, CHUNKS + 1))
    sources = [parts, gated, down_full, spread]
    total, slot_total, *produced = pl.pallas_call(
        functools.partial(sum_kernel, count),
        in_specs=[vmem] + [anywhere] * 4,
        out_specs=[vmem] * 2 + [anywhere] * count,
        out_shape=[
            jax.ShapeDtypeStruct((slots, width), F32),
            jax.ShapeDtypeStruct(slot_parts.shape[1:], F32),
        ]
        + [jax.ShapeDtypeStruct((slots, width), BF16)] * count,
        scratch_shapes=[pltpu.VMEM((2, count - 1, slots, width), BF16)]
        + [pltpu.VMEM(source.shape, BF16) for source in sources]
        + [
            pltpu.VMEM((2, count - 1) + slot_parts.shape[1:], F32),
            pltpu.VMEM((2, slots, width), BF16),
            pltpu.SemaphoreType.DMA((2,)),
            pltpu.SemaphoreType.DMA((4,)),
            sems,
            sems,
        ],
        compiler_params=pltpu.CompilerParams(
            collective_id=2, has_side_effects=True, vmem_limit_bytes=VMEM_BYTES
        ),
        cost_estimate=pl.CostEstimate(
            flops=0, bytes_accessed=80 * (count - 1) * slots * width, transcendentals=0
        ),
    )(slot_parts, *sources)
    return total, slot_total, produced


def last_kernel(count, parts_ref, out_ref, held_ref, send_sems, recv_sems):
    greet_line(count)
    me = lax.axis_index("expert")
    planes = out_ref.shape[0]
    edges = [planes * c // CHUNKS for c in range(CHUNKS + 1)]

    def cut(chunk):
        return pl.ds(edges[chunk], edges[chunk + 1] - edges[chunk])

    def own(step, up, chunk):
        return parts_ref.at[cut(chunk), me + step if up else me - step]

    sum_line(
        count,
        CHUNKS,
        own,
        own,
        lambda step, up, c: held_ref.at[0 if up else 1, step, cut(c)],
        lambda c: out_ref.at[cut(c)],
        (send_sems, recv_sems),
        lambda: None,
    )


def last_sum(parts):
    planes, count, rows, columns = parts.shape
    vmem = pl.BlockSpec(memory_space=pltpu.VMEM)
    sems = pltpu.SemaphoreType.DMA((2, count - 1, CHUNKS))
    return pl.pallas_call(
        functools.partial(last_kernel, count),
        in_specs=[vmem],
        out_specs=vmem,
        out_shape=jax.ShapeDtypeStruct((planes, rows, columns), F32),
        scratch_shapes=[pltpu.VMEM((2, count - 1, planes, rows, columns), BF16), sems, sems],
        compiler_params=pltpu.CompilerParams(
            collective_id=3, has_side_effects=True, vmem_limit_bytes=VMEM_BYTES
        ),
        cost_estimate=pl.CostEstimate(
            flops=0, bytes_accessed=80 * parts.size, transcendentals=0
        ),
    )(parts)


def norm_back_kernel(
    length_ref, logit_ref, side_ref, back_ref, hidden_ref, upstream_ref, gain_ref, merge_ref,
    hidden_grad_ref, attended_ref, mixed_ref, gain_grad_ref,
):
    step = pl.program_id(0)
    rows = hidden_ref.shape[0]
    hidden = hidden_ref[...]
    rms = lax.rsqrt(jnp.mean(hidden * hidden, axis=-1, keepdims=True) + EPS)
    unit = hidden * rms
    grad = dot_last(logit_ref[...], side_ref[...]) + back_ref[...]
    gain_part = jnp.sum(grad * unit, axis=0, keepdims=True)

    @pl.when(step == 0)
    def _():
        gain_grad_ref[...] = gain_part

    @pl.when(step > 0)
    def _():
        gain_grad_ref[...] += gain_part

    scaled = grad * gain_ref[...]
    hidden_grad = upstream_ref[...].astype(F32) + rms * (
        scaled - unit * jnp.mean(scaled * unit, axis=-1, keepdims=True)
    )
    hidden_grad_ref[...] = hidden_grad
    position = step * rows + lax.broadcasted_iota(jnp.int32, (rows, 1), 0)
    attended = jnp.where(position < length_ref[0], hidden_grad, 0.0).astype(BF16)
    attended_ref[...] = attended
    mixed_ref[...] = dot_last(attended, merge_ref[...]).astype(BF16)


def norm_back(length, logit_grad, first_set, back_total, hidden, upstream, gain, merge_full):
    slots, width = hidden.shape
    lanes = logit_grad.shape[1]
    side_block = first_set.shape[1] // lanes - 1
    rows = pl.BlockSpec((Q_BLOCK, width), lambda j: (j, 0))
    single = pl.BlockSpec((1, width), lambda j: (0, 0))
    low = jax.ShapeDtypeStruct((slots, width), BF16)
    return pl.pallas_call(
        norm_back_kernel,
        grid=(slots // Q_BLOCK,),
        in_specs=[
            pl.BlockSpec(memory_space=pltpu.SMEM),
            pl.BlockSpec((Q_BLOCK, lanes), lambda j: (j, 0)),
            pl.BlockSpec((width, lanes), lambda j: (0, side_block)),
            rows,
            rows,
            rows,
            single,
            pl.BlockSpec((width, width), lambda j: (0, 0)),
        ],
        out_specs=[rows, rows, rows, single],
        out_shape=[
            jax.ShapeDtypeStruct((slots, width), F32),
            low,
            low,
            jax.ShapeDtypeStruct((1, width), F32),
        ],
        cost_estimate=pl.CostEstimate(
            flops=2 * slots * width * width, bytes_accessed=2 * 10**7, transcendentals=0
        ),
    )(length, logit_grad, first_set, back_total, hidden, upstream, gain, merge_full)


def projection_kernel(
    mixed_ref, normed_ref, merge_ref, qkv_ref, side_ref, out_ref, turned_ref, stage_ref, sems
):
    step = pl.program_id(0)
    steps = pl.num_programs(0)
    merge_steps = mixed_ref.shape[1] // (2 * COLS)
    slot = step % 2

    def store(at):
        return pltpu.make_async_copy(
            stage_ref.at[at % 2], out_ref.at[pl.ds(2 * at, 2)], sems.at[at % 2]
        )

    def fill(rhs_ref):
        for half in range(2):
            stage_ref[slot, half] = jnp.dot(
                turned_ref[...],
                rhs_ref[:, half * COLS : (half + 1) * COLS],
                preferred_element_type=F32,
            ).astype(BF16)

    @pl.when(step == 0)
    def _():
        turned_ref[...] = mixed_ref[...].T

    @pl.when(step == merge_steps)
    def _():
        turned_ref[...] = normed_ref[...].T

    @pl.when(step >= 2)
    def _():
        store(step - 2).wait()

    @pl.when(step < merge_steps)
    def _():
        fill(merge_ref)

    @pl.when(step >= merge_steps)
    def _():
        fill(qkv_ref)

    store(step).start()

    @pl.when(step == steps - 1)
    def _():
        side = pltpu.make_async_copy(side_ref, out_ref.at[2 * steps], sems.at[2])
        side.start()
        store(step - 1).wait()
        store(step).wait()
        side.wait()


def projection_terms(mixed, normed, attended_grad, qkv_grad, side):
    slots, width = mixed.shape
    wide = 2 * COLS
    first, second = attended_grad.shape[1] // wide, qkv_grad.shape[1] // wide
    whole = pl.BlockSpec((slots, width), lambda j: (0, 0))
    return pl.pallas_call(
        projection_kernel,
        grid=(first + second,),
        in_specs=[
            whole,
            whole,
            pl.BlockSpec((slots, wide), lambda j: (0, jnp.minimum(j, first - 1))),
            pl.BlockSpec((slots, wide), lambda j: (0, jnp.maximum(j - first, 0))),
            pl.BlockSpec((width, COLS), lambda j: (0, 0)),
        ],
        out_specs=pl.BlockSpec(memory_space=pl.ANY),
        out_shape=jax.ShapeDtypeStruct((2 * (first + second) + 1, width, COLS), BF16),
        scratch_shapes=[
            pltpu.VMEM((width, slots), BF16),
            pltpu.VMEM((2, 2, width, COLS), BF16),
            pltpu.SemaphoreType.DMA((3,)),
        ],
        cost_estimate=pl.CostEstimate(
            flops=2 * slots * width * (first + second) * wide,
            bytes_accessed=2 * 10**7,
            transcendentals=0,
        ),
    )(mixed, normed, attended_grad, qkv_grad, side)


def body(
    tokens,
    lengths,
    routes,
    priority,
    first_gain,
    query_weight,
    key_weight,
    value_weight,
    merge_weight,
    router_weight,
    second_gain,
    gate_weight,
    up_weight,
    down_weight,
    cotangent,
):
    slots = tokens.shape[1]
    width = tokens.shape[2]
    groups = lax.axis_size("expert")
    expert_count = router_weight.shape[1]
    capacity = 5 * slots * TOP // (8 * expert_count)
    q_cols, k_cols = HEADS * HD, KV_HEADS * HD
    side_cols = 128

    def gather_shard(value, axis=0):
        return lax.all_gather(value, "shard", axis=axis, tiled=True)

    def scatter_all(part, ahead=None):
        planes, _, columns = part.shape
        part = lax.psum_scatter(
            part.reshape(planes * groups, -1, columns), "shard", scatter_dimension=1, tiled=True
        ).reshape(planes, groups, -1, columns)
        part, ahead = lax.optimization_barrier((part, ahead))
        return last_sum(part), ahead

    side = jnp.concatenate(
        [router_weight, first_gain[:, None], second_gain[:, None]], axis=1
    )
    side = jnp.pad(side, ((0, 0), (0, side_cols - expert_count - 2)))
    first_set = gather_shard(
        jnp.concatenate([query_weight, key_weight, value_weight, side], axis=1)
    )
    merge_full = gather_shard(merge_weight)
    tables = jnp.concatenate(
        [routes[0].T, priority, jnp.broadcast_to(lengths[:, None], (1, slots))], axis=0
    )
    early_columns = 5 * width // 12
    early, other_tables, first_up, first_down, both = early_gather(
        cotangent[0], tables, gate_weight, up_weight, early_columns
    )
    tables = jnp.concatenate([tables[None], other_tables], axis=0).transpose(0, 2, 1)
    tokens, first_up, first_down = lax.optimization_barrier((tokens, first_up, first_down))
    next_up, next_down = line_hops(None, 1, 2, (first_up, first_down))
    both_full = gather_shard(both, 1)
    down_full = gather_shard(down_weight, 1)

    group = lax.axis_index("expert")
    own_experts = group * EXP_DEV + jnp.arange(EXP_DEV, dtype=jnp.int32)
    spread = jax.vmap(
        lambda t: dispatch_matrix(t[:, :TOP], t[:, TOP], t[0, TOP + 1], own_experts, capacity)
    )(tables)

    qkv_full = first_set[:, : q_cols + 2 * k_cols]
    side_full = first_set[:, q_cols + 2 * k_cols :]
    router_full = side_full[:, :expert_count]
    gain_first = side_full[:, expert_count].astype(F32)
    gain_second = side_full[:, expert_count + 1].astype(F32)

    inputs = tokens[0].astype(F32)
    length = lengths[0]
    positions = jnp.arange(slots, dtype=jnp.int32)
    live_rows = (positions < length).astype(F32)[:, None]
    cosine, sine_table = rope_tables(slots)
    rms_one = lax.rsqrt(jnp.mean(inputs * inputs, axis=-1, keepdims=True) + EPS)
    unit_one = inputs * rms_one
    normed_one = (unit_one * gain_first).astype(BF16)
    qkv = jnp.dot(normed_one, qkv_full, preferred_element_type=F32)
    qkv, next_up, next_down = lax.optimization_barrier((qkv, next_up, next_down))
    last_up, last_down = line_hops(None, 2, held=(next_up[-1], next_down[-1]))
    mixed, *low_parts, lse = attend(lengths, qkv, cosine, sine_table)
    late_up = [first_up] + next_up + last_up
    late_down = [first_down] + next_down + last_down
    attended = jnp.dot(mixed, merge_full, preferred_element_type=F32)
    hidden = inputs + live_rows * attended
    rms_two = lax.rsqrt(jnp.mean(hidden * hidden, axis=-1, keepdims=True) + EPS)
    unit_two = hidden * rms_two
    normed_two = (unit_two * gain_second).astype(BF16)

    logits = jnp.dot(normed_two, router_full, preferred_element_type=F32)
    chosen = (
        routes[0][:, :, None] == jnp.arange(expert_count, dtype=jnp.int32)[None, None, :]
    ).astype(F32)
    chosen_any = jnp.sum(chosen, axis=1)
    masked = jnp.where(chosen_any > 0, logits, NEGATIVE)
    peak = jnp.max(masked, axis=-1, keepdims=True)
    exp_logits = jnp.exp(masked - peak) * chosen_any
    gate_dense = exp_logits / jnp.sum(exp_logits, axis=-1, keepdims=True)

    gates = gate_dense.T
    rows, ups, other_gates = gather_dispatch(
        normed_two, gates, cotangent[0], early, late_up, late_down, spread
    )
    gates_all = jnp.concatenate([gates[None], other_gates], axis=0)
    gates_own = lax.dynamic_slice_in_dim(gates_all, group * EXP_DEV, EXP_DEV, axis=1)
    slot_gate = jnp.sum(spread.astype(F32) * gates_own[:, :, None, :], axis=-1)
    gates = slot_gate.transpose(1, 0, 2).reshape(EXP_DEV, groups * capacity, 1)

    gated, gate_pre_grad, lift_pre_grad, back_parts, slot_grad = expert_core(
        rows, ups, gates, both_full, down_full, spread
    )

    slot_grad = slot_grad.reshape(EXP_DEV, groups, capacity).transpose(1, 0, 2)
    token_grad = jnp.sum(spread.astype(F32) * slot_grad[:, :, :, None], axis=2)
    token_grad = lax.dynamic_update_slice_in_dim(
        jnp.zeros((groups, expert_count, slots), F32), token_grad, group * EXP_DEV, axis=1
    )
    expert_grads = expert_weights(rows, ups, gated, gate_pre_grad, lift_pre_grad)
    back_parts, expert_grads = lax.optimization_barrier((back_parts, expert_grads))
    back_total, slot_back, produced = line_sum(
        token_grad, back_parts, gated, down_full, spread
    )
    slot_back = slot_back.T
    expert_grads = lax.psum_scatter(
        expert_grads.reshape(3 * EXP_DEV, width, -1), "shard", scatter_dimension=1, tiled=True
    )
    sums = scatter_hops(produced, 0, 1)

    picked_grad = gate_dense * (
        slot_back - jnp.sum(gate_dense * slot_back, axis=-1, keepdims=True)
    )
    logit_grad = jnp.pad(
        picked_grad.astype(BF16), ((0, 0), (0, side_cols - expert_count))
    )
    hidden_grad, attended_grad, mixed_grad, second_gain_part = norm_back(
        lengths, logit_grad, first_set, back_total, hidden, cotangent[0],
        gain_second[None], merge_full,
    )
    side_part = jnp.einsum("ld,le->de", normed_two, logit_grad, preferred_element_type=F32)
    side_part = jnp.where(
        jnp.arange(side_cols) == expert_count, second_gain_part[0][:, None], side_part
    )
    side_part = jnp.pad(side_part, ((0, 0), (0, COLS - side_cols))).astype(BF16)

    qkv_grad = attend_back(lengths, *low_parts, mixed_grad, lse, cosine, sine_table)
    terms = projection_terms(mixed, normed_one, attended_grad, qkv_grad, side_part)
    terms, expert_grads = lax.optimization_barrier((terms, expert_grads))
    sums, qkv_grad, terms = lax.optimization_barrier((sums, qkv_grad, terms))
    sums = scatter_hops(produced, 1, groups - 1, sums)
    normed_one_grad = jnp.einsum("lh,dh->ld", qkv_grad, qkv_full, preferred_element_type=F32)
    scaled_one = normed_one_grad * gain_first
    input_grad = hidden_grad + rms_one * (
        scaled_one - unit_one * jnp.mean(scaled_one * unit_one, axis=-1, keepdims=True)
    )
    block_output = (
        hidden + produced[0].astype(F32) + sums[0].astype(F32) + sums[1].astype(F32)
    )
    gate_grad, up_grad, down_grad = jnp.split(expert_grads.astype(F32), 3)
    reduced, (block_output, input_grad) = scatter_all(terms, (block_output, input_grad))
    own_rows = reduced.shape[1]
    reduced = reduced.transpose(1, 0, 2).reshape(own_rows, -1)
    place = (group * lax.axis_size("shard") + lax.axis_index("shard")) * own_rows
    merge_grad, qkv_reduced, side_grad = jnp.split(
        reduced, [width, width + q_cols + 2 * k_cols], axis=1
    )
    own_weights = lax.dynamic_slice_in_dim(qkv_full, place, own_rows, axis=0).astype(F32)
    own_gain = lax.dynamic_slice_in_dim(gain_first, place, own_rows)
    first_gain_grad = jnp.sum(own_weights * qkv_reduced, axis=1) / own_gain
    query_grad, key_grad, value_grad = jnp.split(qkv_reduced, [q_cols, q_cols + k_cols], axis=1)
    return (
        block_output[None],
        input_grad[None],
        first_gain_grad,
        query_grad,
        key_grad,
        value_grad,
        merge_grad,
        side_grad[:, :expert_count],
        side_grad[:, expert_count],
        gate_grad,
        up_grad,
        down_grad,
    )


def solution(mesh):
    both = ("expert", "shard")
    in_specs = (
        P(both, None, None),
        P(both),
        P(both, None, None),
        P(both, None),
        P("shard"),
        P("shard", None),
        P("shard", None),
        P("shard", None),
        P("shard", None),
        P("shard", None),
        P("shard"),
        P("expert", "shard", None),
        P("expert", "shard", None),
        P("expert", "shard", None),
        P(both, None, None),
    )
    out_specs = (
        P(both, None, None),
        P(both, None, None),
        P(both),
        P(both, None),
        P(both, None),
        P(both, None),
        P(both, None),
        P(both, None),
        P(both),
        P("expert", "shard", None),
        P("expert", "shard", None),
        P("expert", "shard", None),
    )
    return jax.shard_map(body, mesh=mesh, in_specs=in_specs, out_specs=out_specs, check_vma=False)
```

```python
import functools

import jax
import jax.numpy as jnp
import numpy as np
from jax import lax
from jax.experimental import pallas as pl
from jax.experimental.pallas import tpu as pltpu
from jax.sharding import PartitionSpec as P

HEADS = 24
KV_HEADS = 8
HD = 64
TOP = 8
EXP_DEV = 5
SHARE = HEADS // KV_HEADS
Q_BLOCK = 256
ROWS = 128
VMEM_BYTES = 63 * 2**20
CHUNKS = 4
COLS = 256

EPS = 1e-05
THETA = 10000.0
NEGATIVE = -1e30
F32 = jnp.float32
BF16 = jnp.bfloat16


def rope_tables(slots):
    frequency = THETA ** (-np.arange(HD // 2, dtype=np.float32) * np.float32(2.0) / HD)
    angles = np.arange(slots, dtype=np.float32)[:, None] * frequency.astype(np.float32)[None, :]
    cosine, sine = np.cos(angles), np.sin(angles)
    return (
        jnp.asarray(np.concatenate([cosine] * 4, axis=1), F32),
        jnp.asarray(np.concatenate([-sine, sine, -sine, sine], axis=1), F32),
    )


def dispatch_matrix(routes, priority, length, expert_ids, capacity):
    slots = routes.shape[0]
    positions = jnp.arange(slots, dtype=jnp.int32)
    live = positions < length
    named = jnp.any(routes[:, :, None] == expert_ids[None, None, :], axis=1) & live[:, None]
    earlier = (priority[None, :] < priority[:, None]).astype(BF16)
    slot = jnp.dot(earlier, named.astype(BF16), preferred_element_type=F32).astype(jnp.int32)
    slot = jnp.where(named, slot, capacity)
    return (
        slot.T[:, None, :] == jnp.arange(capacity, dtype=jnp.int32)[None, :, None]
    ).astype(BF16)


def line_hops(block, first=0, last=None, held=None):
    count = lax.axis_size("expert")
    last = count - 1 if last is None else last
    held_up, held_down = (block, block) if held is None else held
    up, down = [], []
    for step in range(first, last):
        held_up = lax.ppermute(
            held_up, "expert", [(i, i + 1) for i in range(step, count - 1)]
        )
        held_down = lax.ppermute(
            held_down, "expert", [(i + 1, i) for i in range(0, count - 1 - step)]
        )
        up.append(held_up)
        down.append(held_down)
    return up, down


def scatter_hops(parts, first=0, last=None, held=None):
    count = lax.axis_size("expert")
    last = count - 1 if last is None else last
    held_up, held_down = (None, None) if held is None else held
    for step in range(first, last):
        piece_up = parts[step + 1]
        piece_down = parts[count - 1 - step]
        if step:
            piece_up = piece_up.astype(F32) + held_up.astype(F32)
            piece_down = piece_down.astype(F32) + held_down.astype(F32)
        held_up = lax.ppermute(
            piece_up.astype(BF16), "expert", [(i, i + 1) for i in range(step + 1)]
        )
        held_down = lax.ppermute(
            piece_down.astype(BF16),
            "expert",
            [(i + 1, i) for i in range(count - 2 - step, count - 1)],
        )
    return held_up, held_down


def turn(values, cosine, sine):
    first = lax.broadcasted_iota(jnp.int32, (1, 2 * HD), 1) % HD < HD // 2
    out = []
    for start in range(0, values.shape[1], 2 * HD):
        part = values[:, start : start + 2 * HD]
        other = jnp.where(
            first, pltpu.roll(part, 2 * HD - HD // 2, 1), pltpu.roll(part, HD // 2, 1)
        )
        out.append(part * cosine + other * sine)
    return out[0] if len(out) == 1 else jnp.concatenate(out, axis=1)


def last_keys(block, length):
    lane = lax.broadcasted_iota(jnp.int32, (1, SHARE * Q_BLOCK), 1)
    return jnp.minimum(block * Q_BLOCK + lane % Q_BLOCK, length - 1)


def head_block(values, pair_head, block):
    rows = slice(block * Q_BLOCK, (block + 1) * Q_BLOCK)
    heads = range(pair_head * SHARE, (pair_head + 1) * SHARE)
    return jnp.concatenate([values[rows, h * HD : (h + 1) * HD] for h in heads], axis=0)


def rows_of_heads(parts):
    tall = [
        part[:, g * Q_BLOCK : (g + 1) * Q_BLOCK] for part in parts for g in range(SHARE)
    ]
    return jnp.concatenate(tall, axis=0).T


def dot_last(a, b):
    return lax.dot_general(a, b, (((1,), (1,)), ((), ())), preferred_element_type=F32)


def attend_kernel(
    length_ref, q_ref, k_ref, v_ref, cos_ref, sin_ref,
    mixed_ref, q_low_ref, k_low_ref, v_low_ref, lse_ref,
):
    length = length_ref[0]
    slots = q_ref.shape[0]
    cosine, sine = cos_ref[...], sin_ref[...]
    queries = (turn(q_ref[...], cosine, sine) * HD**-0.5).astype(BF16)
    keys = turn(k_ref[...], cosine, sine).astype(BF16)
    values = v_ref[...]
    q_low_ref[...] = queries
    k_low_ref[...] = keys
    v_low_ref[...] = values.astype(BF16)
    values_t = values.T.astype(BF16)
    blocks = slots // Q_BLOCK
    for block in range(blocks):
        span = (block + 1) * Q_BLOCK
        limit = last_keys(block, length)
        key_id = lax.broadcasted_iota(jnp.int32, (span, 1), 0)
        parts = []
        for head in range(2):
            scores = dot_last(
                keys[:span, head * HD : (head + 1) * HD], head_block(queries, head, block)
            )
            scores = jnp.where(key_id <= limit, scores, NEGATIVE)
            peak = jnp.max(scores, axis=0, keepdims=True)
            exp_scores = jnp.exp(scores - peak)
            total = jnp.sum(exp_scores, axis=0, keepdims=True)
            lse_ref[0, pl.ds(head * blocks + block, 1), :] = peak + jnp.log(total)
            part = jnp.dot(
                values_t[head * HD : (head + 1) * HD, :span],
                exp_scores.astype(BF16),
                preferred_element_type=F32,
            )
            parts.append(part / total)
        mixed_ref[block * Q_BLOCK : span, :] = rows_of_heads(parts).astype(BF16)


def attend_back_kernel(
    length_ref, q_ref, k_ref, v_ref, grad_ref, lse_ref, cos_ref, sin_ref, out_ref, dk_ref, dv_ref
):
    length = length_ref[0]
    slots, q_cols = q_ref.shape
    pairs = pl.num_programs(0)
    pair = pl.program_id(0)
    q_at = pl.ds(pl.multiple_of(pair * q_cols, 2 * HD), q_cols)
    k_at = pl.ds(pl.multiple_of(pairs * q_cols + pair * 2 * HD, 2 * HD), 2 * HD)
    v_at = pl.ds(pl.multiple_of(pairs * (q_cols + 2 * HD) + pair * 2 * HD, 2 * HD), 2 * HD)
    cosine, sine = cos_ref[...], -sin_ref[...]
    queries, keys, values = q_ref[...], k_ref[...], v_ref[...]
    grad = grad_ref[...]
    keys_t = keys.astype(F32).T.astype(BF16)
    dk_ref[...] = jnp.zeros_like(dk_ref)
    dv_ref[...] = jnp.zeros_like(dv_ref)
    blocks = slots // Q_BLOCK
    for block in range(blocks):
        rows = slice(block * Q_BLOCK, (block + 1) * Q_BLOCK)
        span = (block + 1) * Q_BLOCK
        limit = last_keys(block, length)
        key_id = lax.broadcasted_iota(jnp.int32, (span, 1), 0)
        parts = []
        for head in range(2):
            cols = slice(head * HD, (head + 1) * HD)
            query = head_block(queries, head, block)
            out_grad = head_block(grad, head, block)
            scores = dot_last(keys[:span, cols], query)
            scores = jnp.where(key_id <= limit, scores, NEGATIVE)
            probs = jnp.exp(scores - lse_ref[0, pl.ds(head * blocks + block, 1), :])
            prob_back = dot_last(values[:span, cols], out_grad)
            mean = jnp.sum(probs * prob_back, axis=0, keepdims=True)
            score_grad = (probs * (prob_back - mean)).astype(BF16)
            dv_ref[head, :span, :] += jnp.dot(
                probs.astype(BF16), out_grad, preferred_element_type=F32
            )
            dk_ref[head, :span, :] += jnp.dot(score_grad, query, preferred_element_type=F32)
            parts.append(
                jnp.dot(keys_t[cols, :span], score_grad, preferred_element_type=F32)
                * HD**-0.5
            )
        out_ref[rows, q_at] = turn(rows_of_heads(parts), cosine[rows], sine[rows]).astype(
            BF16
        )
    key_grad = jnp.concatenate([dk_ref[0], dk_ref[1]], axis=1)
    out_ref[:, k_at] = turn(key_grad, cosine, sine).astype(BF16)
    out_ref[:, v_at] = jnp.concatenate([dv_ref[0], dv_ref[1]], axis=1).astype(BF16)


def column_block(slots, columns, first=0):
    return pl.BlockSpec((slots, columns), lambda p: (0, first + p))


def attention_specs(slots):
    pairs = KV_HEADS // 2
    q_cols, cols = 2 * SHARE * HD, 2 * (SHARE + 2) * HD
    blocks = slots // Q_BLOCK
    whole = pl.BlockSpec((slots, 2 * HD), lambda p: (0, 0))
    lse = pl.BlockSpec((1, 2 * blocks, SHARE * Q_BLOCK), lambda p: (p, 0, 0))
    scalar = pl.BlockSpec(memory_space=pltpu.SMEM)
    return pairs, q_cols, cols, blocks, whole, lse, scalar


def attend(length, qkv, cosine, sine):
    slots = qkv.shape[0]
    pairs, q_cols, cols, blocks, whole, lse, scalar = attention_specs(slots)
    queries, keys = column_block(slots, q_cols), column_block(slots, 2 * HD)
    key_first = pairs * q_cols // (2 * HD)
    low_keys = jax.ShapeDtypeStruct((slots, pairs * 2 * HD), BF16)
    low_queries = jax.ShapeDtypeStruct((slots, pairs * q_cols), BF16)
    return pl.pallas_call(
        attend_kernel,
        grid=(pairs,),
        in_specs=[
            scalar,
            queries,
            column_block(slots, 2 * HD, key_first),
            column_block(slots, 2 * HD, key_first + pairs),
            whole,
            whole,
        ],
        out_specs=[queries, queries, keys, keys, lse],
        out_shape=[
            low_queries,
            low_queries,
            low_keys,
            low_keys,
            jax.ShapeDtypeStruct((pairs, 2 * blocks, SHARE * Q_BLOCK), F32),
        ],
        cost_estimate=pl.CostEstimate(
            flops=24 * HEADS * slots * slots * HD // 4, bytes_accessed=10**7, transcendentals=0
        ),
    )(length, qkv, qkv, qkv, cosine, sine)


def attend_back(length, queries, keys, values, grad, lse_rows, cosine, sine):
    slots = grad.shape[0]
    pairs, q_cols, cols, blocks, whole, lse, scalar = attention_specs(slots)
    wide, narrow = column_block(slots, q_cols), column_block(slots, 2 * HD)
    return pl.pallas_call(
        attend_back_kernel,
        grid=(pairs,),
        in_specs=[scalar, wide, narrow, narrow, wide, lse, whole, whole],
        out_specs=pl.BlockSpec((slots, pairs * cols), lambda p: (0, 0)),
        out_shape=jax.ShapeDtypeStruct((slots, pairs * cols), BF16),
        scratch_shapes=[pltpu.VMEM((2, slots, HD), F32), pltpu.VMEM((2, slots, HD), F32)],
        cost_estimate=pl.CostEstimate(
            flops=60 * HEADS * slots * slots * HD // 4, bytes_accessed=10**7, transcendentals=0
        ),
    )(length, queries, keys, values, grad, lse_rows, cosine, sine)


def stage_out(count, make, stage_ref, targets, sems):
    copies = [
        pltpu.make_async_copy(stage_ref.at[p % 2], targets(p), sems.at[p % 2])
        for p in range(count)
    ]
    for p in range(count):
        if p > 1:
            copies[p - 2].wait()
        stage_ref[p % 2] = make(p)
        copies[p].start()
    for copy in copies[-2:]:
        copy.wait()


def token_sum(spread_ref, rows_ref, place):
    capacity = rows_ref.shape[1] // spread_ref.shape[0]
    pick = spread_ref[place].reshape(EXP_DEV * capacity, -1).T
    rows = rows_ref[:, place * capacity : (place + 1) * capacity, :]
    return jnp.dot(
        pick, rows.reshape(EXP_DEV * capacity, -1), preferred_element_type=F32
    ).astype(BF16)


def expert_kernel(
    rows_ref, ups_ref, gates_ref, gate_ref, up_ref, down_ref, spread_ref,
    gated_ref, gate_grad_ref, lift_grad_ref, parts_ref, slot_ref,
    back_ref, stage_ref, sems,
):
    rows, gates = rows_ref[0], gates_ref[0]
    gate_pre = jnp.dot(rows, gate_ref[0], preferred_element_type=F32)
    lift_pre = jnp.dot(rows, up_ref[0], preferred_element_type=F32)
    act_grad = jnp.dot(ups_ref[0], down_ref[0], preferred_element_type=F32)
    sigmoid_gate = jax.nn.sigmoid(gate_pre)
    silu_gate = gate_pre * sigmoid_gate
    activated = silu_gate * lift_pre
    slot_ref[0] = jnp.sum(act_grad * activated, axis=-1, keepdims=True)
    gated_ref[0] = (activated * gates).astype(BF16)
    act_grad = act_grad * gates
    gate_pre_grad = (
        act_grad * lift_pre * (sigmoid_gate + silu_gate * (1.0 - sigmoid_gate))
    ).astype(BF16)
    lift_pre_grad = (act_grad * silu_gate).astype(BF16)
    gate_grad_ref[0] = gate_pre_grad
    lift_grad_ref[0] = lift_pre_grad
    step = pl.program_id(0)
    back_ref[step] = (
        dot_last(gate_pre_grad, gate_ref[0]) + dot_last(lift_pre_grad, up_ref[0])
    ).astype(BF16)

    @pl.when(step == pl.num_programs(0) - 1)
    def _():
        stage_out(
            spread_ref.shape[0],
            lambda p: token_sum(spread_ref, back_ref, p),
            stage_ref,
            lambda p: parts_ref.at[p],
            sems,
        )


def expert_block(*shape, first=0):
    return pl.BlockSpec((1,) + shape, lambda x: (first + x, 0, 0))


def expert_core(rows, ups, gates, both_full, down_full, spread):
    experts, total, width = ups.shape
    count, _, capacity, slots = spread.shape
    hidden = down_full.shape[-1]
    narrow, wide = expert_block(total, hidden), expert_block(total, width)
    weight, single = expert_block(width, hidden), expert_block(total, 1)
    low = jax.ShapeDtypeStruct((experts, total, hidden), BF16)
    return pl.pallas_call(
        expert_kernel,
        grid=(experts,),
        in_specs=[
            wide, wide, single,
            weight, expert_block(width, hidden, first=experts), weight,
            pl.BlockSpec(spread.shape, lambda x: (0, 0, 0, 0)),
        ],
        out_specs=[narrow, narrow, narrow, pl.BlockSpec(memory_space=pl.ANY), single],
        out_shape=[
            low,
            low,
            low,
            jax.ShapeDtypeStruct((count, slots, width), BF16),
            jax.ShapeDtypeStruct((experts, total, 1), F32),
        ],
        scratch_shapes=[
            pltpu.VMEM((experts, total, width), BF16),
            pltpu.VMEM((2, slots, width), BF16),
            pltpu.SemaphoreType.DMA((2,)),
        ],
        compiler_params=pltpu.CompilerParams(vmem_limit_bytes=VMEM_BYTES),
        cost_estimate=pl.CostEstimate(
            flops=12 * experts * total * width * hidden,
            bytes_accessed=60 * 10**6,
            transcendentals=0,
        ),
    )(rows, ups, gates, both_full, both_full, down_full, spread)


def weight_kernel(rows_ref, ups_ref, gated_ref, gate_grad_ref, lift_grad_ref, grads_ref):
    rows_t = rows_ref[0].T
    grads_ref[0, 0] = jnp.dot(
        rows_t, gate_grad_ref[0], preferred_element_type=F32
    ).astype(BF16)
    grads_ref[1, 0] = jnp.dot(
        rows_t, lift_grad_ref[0], preferred_element_type=F32
    ).astype(BF16)
    grads_ref[2, 0] = jnp.dot(
        ups_ref[0].T, gated_ref[0], preferred_element_type=F32
    ).astype(BF16)


def expert_weights(rows, ups, gated, gate_grad, lift_grad):
    experts, count, width = ups.shape
    hidden = gated.shape[-1]
    narrow, wide = expert_block(count, hidden), expert_block(count, width)
    return pl.pallas_call(
        weight_kernel,
        grid=(experts,),
        in_specs=[wide, wide, narrow, narrow, narrow],
        out_specs=pl.BlockSpec((3, 1, width, hidden), lambda x: (0, x, 0, 0)),
        out_shape=jax.ShapeDtypeStruct((3, experts, width, hidden), BF16),
        compiler_params=pltpu.CompilerParams(vmem_limit_bytes=VMEM_BYTES),
        cost_estimate=pl.CostEstimate(
            flops=6 * experts * count * width * hidden, bytes_accessed=50 * 10**6, transcendentals=0
        ),
    )(rows, ups, gated, gate_grad, lift_grad)


def line_copy(source, target, sems, step, up, chunk):
    send_sems, recv_sems = sems
    side = 0 if up else 1
    me = lax.axis_index("expert")
    return pltpu.make_async_remote_copy(
        src_ref=source,
        dst_ref=target,
        send_sem=send_sems.at[side, step, chunk],
        recv_sem=recv_sems.at[side, step, chunk],
        device_id={"expert": me + 1 if up else me - 1},
        device_id_type=pl.DeviceIdType.MESH,
    )


def greet_line(count):
    me = lax.axis_index("expert")
    barrier = pltpu.get_barrier_semaphore()
    for up in (True, False):
        there = me < count - 1 if up else me > 0

        @pl.when(there)
        def _():
            pl.semaphore_signal(
                barrier,
                inc=1,
                device_id={"expert": me + 1 if up else me - 1},
                device_id_type=pl.DeviceIdType.MESH,
            )

    ends = (me == 0) | (me == count - 1)

    @pl.when(ends)
    def _():
        pl.semaphore_wait(barrier, 1)

    @pl.when(jnp.logical_not(ends))
    def _():
        pl.semaphore_wait(barrier, 2)


def gather_line(count, own, held, chunks, sems, work, short=0):
    me = lax.axis_index("expert")

    def after(step, up):
        return me + step < count if up else me - step >= 0

    def place(step, up):
        return step if up else count - step

    def reach(chunk):
        return count - 1 if chunk < chunks - short else 1

    for chunk in range(chunks):
        for up in (True, False):

            @pl.when(after(1, up))
            def _():
                line_copy(own(chunk), held(place(1, up), chunk), sems, 0, up, chunk).start()

    work(0, True)
    for step in range(1, count):
        for chunk in range(chunks):
            for up in (True, False):
                if step > reach(chunk):
                    continue
                here = held(place(step, up), chunk)

                @pl.when(after(step, not up))
                def _():
                    line_copy(here, here, sems, step - 1, up, chunk).wait_recv()

                if step < reach(chunk):

                    @pl.when(after(step, not up) & after(1, up))
                    def _():
                        there = held(place(step + 1, up), chunk)
                        line_copy(here, there, sems, step, up, chunk).start()

        for up in (True, False):

            @pl.when(after(step, not up))
            def _():
                work(place(step, up), up)

    for step in range(count - 1):
        for chunk in range(chunks):
            for up in (True, False):
                if step >= reach(chunk):
                    continue

                @pl.when(after(step, not up) & after(1, up))
                def _():
                    source = held(place(step, up), chunk) if step else own(chunk)
                    line_copy(
                        source, held(place(step + 1, up), chunk), sems, step, up, chunk
                    ).wait_send()


def early_kernel(
    count, columns, block_ref, tables_ref, gate_ref, up_ref,
    held_ref, tables_out, late_up, late_down, both_ref,
    both_vmem, local_sems, send_sems, recv_sems,
):
    greet_line(count)
    tall = block_ref.shape[0] // CHUNKS
    experts = gate_ref.shape[0]

    def rows(chunk):
        return pl.ds(chunk * tall, tall)

    def own(chunk):
        if chunk == CHUNKS:
            return tables_ref
        if chunk > CHUNKS:
            late = block_ref.shape[1] - columns
            return block_ref.at[rows(chunk - CHUNKS - 1), pl.ds(columns, late)]
        return block_ref.at[rows(chunk), pl.ds(0, columns)]

    def held(place, chunk):
        if chunk == CHUNKS:
            return tables_out.at[place - 1]
        if chunk > CHUNKS:
            late = late_up if place == 1 else late_down
            return late.at[rows(chunk - CHUNKS - 1), :]
        return held_ref.at[place - 1, rows(chunk), :]

    def work(place, up):
        if place:
            return
        loads = [
            pltpu.make_async_copy(gate_ref, both_vmem.at[pl.ds(0, experts)], local_sems.at[0]),
            pltpu.make_async_copy(up_ref, both_vmem.at[pl.ds(experts, experts)], local_sems.at[1]),
        ]
        store = pltpu.make_async_copy(both_vmem, both_ref, local_sems.at[2])
        for copy in loads:
            copy.start()
        for copy in loads:
            copy.wait()
        store.start()
        store.wait()

    gather_line(
        count, own, held, 2 * CHUNKS + 1, (send_sems, recv_sems), work, short=CHUNKS
    )


def early_gather(block, tables, gate_weight, up_weight, columns):
    count = lax.axis_size("expert")
    slots, width = block.shape
    sems = pltpu.SemaphoreType.DMA((2, count - 1, 2 * CHUNKS + 1))
    sent = 2 * (count - 1) * slots * columns
    vmem, anywhere = pl.BlockSpec(memory_space=pltpu.VMEM), pl.BlockSpec(memory_space=pl.ANY)
    both = (2 * gate_weight.shape[0],) + gate_weight.shape[1:]
    return pl.pallas_call(
        functools.partial(early_kernel, count, columns),
        in_specs=[vmem, vmem, anywhere, anywhere],
        out_specs=[anywhere] * 5,
        out_shape=[
            jax.ShapeDtypeStruct((count - 1, slots, columns), BF16),
            jax.ShapeDtypeStruct((count - 1,) + tables.shape, jnp.int32),
            jax.ShapeDtypeStruct((slots, width - columns), BF16),
            jax.ShapeDtypeStruct((slots, width - columns), BF16),
            jax.ShapeDtypeStruct(both, BF16),
        ],
        scratch_shapes=[pltpu.VMEM(both, BF16), pltpu.SemaphoreType.DMA((3,)), sems, sems],
        compiler_params=pltpu.CompilerParams(
            collective_id=1, has_side_effects=True, vmem_limit_bytes=VMEM_BYTES
        ),
        cost_estimate=pl.CostEstimate(flops=0, bytes_accessed=40 * sent, transcendentals=0),
    )(block, tables, gate_weight, up_weight)


def dispatch_kernel(count, normed_ref, gates_ref, *refs):
    sources = refs[: 2 * count + 1]
    rows_out, ups_out, gates_out, rows_ref, ups_ref, held_ref = refs[2 * count + 1 : 2 * count + 7]
    loaded = refs[2 * count + 7 : 4 * count + 8]
    load_sems, store_sems, send_sems, recv_sems = refs[4 * count + 8 :]
    block_ref, early_ref, spread_ref = loaded[:3]
    late_up, late_down = loaded[3 : count + 2], loaded[count + 2 :]
    greet_line(count)
    tall = normed_ref.shape[0] // CHUNKS
    capacity = rows_ref.shape[1] // count
    columns = early_ref.shape[-1]
    loads = [
        pltpu.make_async_copy(source, target, load_sems.at[k])
        for k, (source, target) in enumerate(zip(sources, loaded))
    ]

    def cut(chunk):
        return pl.ds(chunk * tall, tall)

    def own(chunk):
        return gates_ref if chunk == CHUNKS else normed_ref.at[cut(chunk), :]

    def held(place, chunk):
        if chunk == CHUNKS:
            return gates_out.at[place - 1]
        return held_ref.at[place - 1, cut(chunk), :]

    def stores(place):
        at = pl.ds(place * capacity, capacity)
        return [
            pltpu.make_async_copy(
                full.at[:, at, :], target.at[:, at, :], store_sems.at[k, place]
            )
            for k, (full, target) in enumerate([(rows_ref, rows_out), (ups_ref, ups_out)])
        ]

    def dispatch(place, parts, full, store):
        at = slice(place * capacity, (place + 1) * capacity)
        for expert in range(EXP_DEV):
            pick = spread_ref[place, expert]
            start = 0
            for part in parts:
                stop = start + part.shape[1]
                full[expert, at, start:stop] = jnp.dot(
                    pick, part, preferred_element_type=F32
                ).astype(BF16)
                start = stop
        store.start()

    def gradients(place, late):
        dispatch(place, [early_ref[place - 1], late[...]], ups_ref, stores(place)[1])

    def work(place, up):
        if place:
            dispatch(place, [held_ref[place - 1]], rows_ref, stores(place)[0])
            return
        for copy in loads:
            copy.start()
        for copy in loads:
            copy.wait()
        me = lax.axis_index("expert")
        dispatch(0, [normed_ref[...]], rows_ref, stores(0)[0])
        dispatch(0, [block_ref[...]], ups_ref, stores(0)[1])
        for other in range(1, count):

            @pl.when(me >= other)
            def _():
                gradients(other, late_up[other - 1])

            @pl.when(me < other)
            def _():
                gradients(other, late_down[count - other - 1])

    gather_line(count, own, held, CHUNKS + 1, (send_sems, recv_sems), work)
    for place in range(count):
        for copy in stores(place):
            copy.wait()


def gather_dispatch(normed, gates, block, early, late_up, late_down, spread):
    count = lax.axis_size("expert")
    slots, width = normed.shape
    capacity = spread.shape[2]
    vmem, anywhere = pl.BlockSpec(memory_space=pltpu.VMEM), pl.BlockSpec(memory_space=pl.ANY)
    sems = pltpu.SemaphoreType.DMA((2, count - 1, CHUNKS + 1))
    sent = 2 * (count - 1) * slots * width
    full = (EXP_DEV, count * capacity, width)
    sources = [block, early, spread, *late_up, *late_down]
    return pl.pallas_call(
        functools.partial(dispatch_kernel, count),
        in_specs=[vmem] * 2 + [anywhere] * len(sources),
        out_specs=[anywhere] * 3,
        out_shape=[
            jax.ShapeDtypeStruct(full, BF16),
            jax.ShapeDtypeStruct(full, BF16),
            jax.ShapeDtypeStruct((count - 1,) + gates.shape, F32),
        ],
        scratch_shapes=[
            pltpu.VMEM(full, BF16),
            pltpu.VMEM(full, BF16),
            pltpu.VMEM((count - 1, slots, width), BF16),
        ]
        + [pltpu.VMEM(source.shape, BF16) for source in sources]
        + [
            pltpu.SemaphoreType.DMA((len(sources),)),
            pltpu.SemaphoreType.DMA((2, count)),
            sems,
            sems,
        ],
        compiler_params=pltpu.CompilerParams(
            collective_id=0, has_side_effects=True, vmem_limit_bytes=VMEM_BYTES
        ),
        cost_estimate=pl.CostEstimate(flops=0, bytes_accessed=40 * sent, transcendentals=0),
    )(normed, gates, *sources)


def sum_line(count, chunks, first, own, held, out, sems, fill):
    me = lax.axis_index("expert")

    def after(step, up):
        return me + step < count if up else me - step >= 0

    for step in range(count - 1, 0, -1):
        if step == count - 2:
            fill()
        for chunk in range(chunks):
            for up in (True, False):
                there = held(step - 1, up, chunk)

                @pl.when(after(step, up) & jnp.logical_not(after(1, not up)))
                def _():
                    line_copy(first(step, up, chunk), there, sems, step - 1, up, chunk).start()

                if step < count - 1:
                    here = held(step, up, chunk)

                    @pl.when(after(step, up) & after(1, not up))
                    def _():
                        line_copy(here, here, sems, step, up, chunk).wait_recv()
                        here[...] = (
                            here[...].astype(F32) + own(step, up, chunk)[...].astype(F32)
                        ).astype(here.dtype)
                        line_copy(here, there, sems, step - 1, up, chunk).start()

    for chunk in range(chunks):
        result = out(chunk)
        result[...] = own(0, True, chunk)[...].astype(F32)
        for up in (True, False):
            here = held(0, up, chunk)

            @pl.when(after(1, not up))
            def _():
                line_copy(here, here, sems, 0, up, chunk).wait_recv()
                result[...] += here[...].astype(F32)

    for step in range(count - 1, 0, -1):
        for chunk in range(chunks):
            for up in (True, False):

                @pl.when(after(step, up))
                def _():
                    source = first(step, up, chunk)
                    line_copy(
                        source, held(step - 1, up, chunk), sems, step - 1, up, chunk
                    ).wait_send()


def sum_kernel(
    count, slot_ref, parts_ref, gated_ref, down_ref, spread_ref, out_ref, slot_out, *refs
):
    produced_out = refs[:count]
    held_ref, *loaded = refs[count : count + 5]
    slot_held, stage_ref, stage_sems, load_sems, send_sems, recv_sems = refs[count + 5 :]
    parts, gated, down, spread = loaded
    greet_line(count)
    tall = out_ref.shape[0] // CHUNKS
    capacity = gated.shape[1] // count
    loads = [
        pltpu.make_async_copy(source, target, load_sems.at[k])
        for k, (source, target) in enumerate(
            zip([parts_ref, gated_ref, down_ref, spread_ref], loaded)
        )
    ]

    def cut(chunk):
        return pl.ds(chunk * tall, tall)

    def part(ref):
        def pick(step, up, chunk):
            place = (count - step) % count if up else step
            return slot_ref.at[place] if chunk == CHUNKS else ref.at[place, cut(chunk), :]

        return pick

    def held(step, up, chunk):
        side = 0 if up else 1
        if chunk == CHUNKS:
            return slot_held.at[side, step]
        return held_ref.at[side, step, cut(chunk), :]

    def produced(place):
        at = slice(place * capacity, (place + 1) * capacity)
        rows = [dot_last(gated[x, at, :], down[x]).astype(BF16) for x in range(EXP_DEV)]
        pick = spread[place].reshape(EXP_DEV * capacity, -1).T
        return jnp.dot(
            pick, jnp.concatenate(rows, axis=0), preferred_element_type=F32
        ).astype(BF16)

    def fill():
        for copy in loads:
            copy.start()
        for copy in loads:
            copy.wait()
        stage_out(count, produced, stage_ref, lambda p: produced_out[p], stage_sems)

    sum_line(
        count,
        CHUNKS + 1,
        part(parts_ref),
        part(parts),
        held,
        lambda c: slot_out if c == CHUNKS else out_ref.at[cut(c), :],
        (send_sems, recv_sems),
        fill,
    )


def line_sum(slot_parts, parts, gated, down_full, spread):
    count, slots, width = parts.shape
    vmem, anywhere = pl.BlockSpec(memory_space=pltpu.VMEM), pl.BlockSpec(memory_space=pl.ANY)
    sems = pltpu.SemaphoreType.DMA((2, count - 1, CHUNKS + 1))
    sources = [parts, gated, down_full, spread]
    total, slot_total, *produced = pl.pallas_call(
        functools.partial(sum_kernel, count),
        in_specs=[vmem] + [anywhere] * 4,
        out_specs=[vmem] * 2 + [anywhere] * count,
        out_shape=[
            jax.ShapeDtypeStruct((slots, width), F32),
            jax.ShapeDtypeStruct(slot_parts.shape[1:], F32),
        ]
        + [jax.ShapeDtypeStruct((slots, width), BF16)] * count,
        scratch_shapes=[pltpu.VMEM((2, count - 1, slots, width), BF16)]
        + [pltpu.VMEM(source.shape, BF16) for source in sources]
        + [
            pltpu.VMEM((2, count - 1) + slot_parts.shape[1:], F32),
            pltpu.VMEM((2, slots, width), BF16),
            pltpu.SemaphoreType.DMA((2,)),
            pltpu.SemaphoreType.DMA((4,)),
            sems,
            sems,
        ],
        compiler_params=pltpu.CompilerParams(
            collective_id=2, has_side_effects=True, vmem_limit_bytes=VMEM_BYTES
        ),
        cost_estimate=pl.CostEstimate(
            flops=0, bytes_accessed=80 * (count - 1) * slots * width, transcendentals=0
        ),
    )(slot_parts, *sources)
    return total, slot_total, produced


def last_kernel(count, parts_ref, out_ref, held_ref, send_sems, recv_sems):
    greet_line(count)
    me = lax.axis_index("expert")
    planes = out_ref.shape[0]
    edges = [planes * c // CHUNKS for c in range(CHUNKS + 1)]

    def cut(chunk):
        return pl.ds(edges[chunk], edges[chunk + 1] - edges[chunk])

    def own(step, up, chunk):
        return parts_ref.at[cut(chunk), me + step if up else me - step]

    sum_line(
        count,
        CHUNKS,
        own,
        own,
        lambda step, up, c: held_ref.at[0 if up else 1, step, cut(c)],
        lambda c: out_ref.at[cut(c)],
        (send_sems, recv_sems),
        lambda: None,
    )


def last_sum(parts):
    planes, count, rows, columns = parts.shape
    vmem = pl.BlockSpec(memory_space=pltpu.VMEM)
    sems = pltpu.SemaphoreType.DMA((2, count - 1, CHUNKS))
    return pl.pallas_call(
        functools.partial(last_kernel, count),
        in_specs=[vmem],
        out_specs=vmem,
        out_shape=jax.ShapeDtypeStruct((planes, rows, columns), F32),
        scratch_shapes=[pltpu.VMEM((2, count - 1, planes, rows, columns), BF16), sems, sems],
        compiler_params=pltpu.CompilerParams(
            collective_id=3, has_side_effects=True, vmem_limit_bytes=VMEM_BYTES
        ),
        cost_estimate=pl.CostEstimate(
            flops=0, bytes_accessed=80 * parts.size, transcendentals=0
        ),
    )(parts)


def norm_back_kernel(
    length_ref, logit_ref, side_ref, back_ref, hidden_ref, upstream_ref, gain_ref, merge_ref,
    hidden_grad_ref, attended_ref, mixed_ref, gain_grad_ref,
):
    step = pl.program_id(0)
    rows = hidden_ref.shape[0]
    hidden = hidden_ref[...]
    rms = lax.rsqrt(jnp.mean(hidden * hidden, axis=-1, keepdims=True) + EPS)
    unit = hidden * rms
    grad = dot_last(logit_ref[...], side_ref[...]) + back_ref[...]
    gain_part = jnp.sum(grad * unit, axis=0, keepdims=True)

    @pl.when(step == 0)
    def _():
        gain_grad_ref[...] = gain_part

    @pl.when(step > 0)
    def _():
        gain_grad_ref[...] += gain_part

    scaled = grad * gain_ref[...]
    hidden_grad = upstream_ref[...].astype(F32) + rms * (
        scaled - unit * jnp.mean(scaled * unit, axis=-1, keepdims=True)
    )
    hidden_grad_ref[...] = hidden_grad
    position = step * rows + lax.broadcasted_iota(jnp.int32, (rows, 1), 0)
    attended = jnp.where(position < length_ref[0], hidden_grad, 0.0).astype(BF16)
    attended_ref[...] = attended
    mixed_ref[...] = dot_last(attended, merge_ref[...]).astype(BF16)


def norm_back(length, logit_grad, first_set, back_total, hidden, upstream, gain, merge_full):
    slots, width = hidden.shape
    lanes = logit_grad.shape[1]
    side_block = first_set.shape[1] // lanes - 1
    rows = pl.BlockSpec((ROWS, width), lambda j: (j, 0))
    single = pl.BlockSpec((1, width), lambda j: (0, 0))
    low = jax.ShapeDtypeStruct((slots, width), BF16)
    return pl.pallas_call(
        norm_back_kernel,
        grid=(slots // ROWS,),
        in_specs=[
            pl.BlockSpec(memory_space=pltpu.SMEM),
            pl.BlockSpec((ROWS, lanes), lambda j: (j, 0)),
            pl.BlockSpec((width, lanes), lambda j: (0, side_block)),
            rows,
            rows,
            rows,
            single,
            pl.BlockSpec((width, width), lambda j: (0, 0)),
        ],
        out_specs=[rows, rows, rows, single],
        out_shape=[
            jax.ShapeDtypeStruct((slots, width), F32),
            low,
            low,
            jax.ShapeDtypeStruct((1, width), F32),
        ],
        cost_estimate=pl.CostEstimate(
            flops=2 * slots * width * width, bytes_accessed=2 * 10**7, transcendentals=0
        ),
    )(length, logit_grad, first_set, back_total, hidden, upstream, gain, merge_full)


def projection_kernel(
    mixed_ref, normed_ref, merge_ref, qkv_ref, side_ref, out_ref, turned_ref, stage_ref, sems
):
    step = pl.program_id(0)
    steps = pl.num_programs(0)
    merge_steps = mixed_ref.shape[1] // (2 * COLS)
    slot = step % 2

    def store(at):
        return pltpu.make_async_copy(
            stage_ref.at[at % 2], out_ref.at[pl.ds(2 * at, 2)], sems.at[at % 2]
        )

    def fill(rhs_ref):
        for half in range(2):
            stage_ref[slot, half] = jnp.dot(
                turned_ref[...],
                rhs_ref[:, half * COLS : (half + 1) * COLS],
                preferred_element_type=F32,
            ).astype(BF16)

    @pl.when(step == 0)
    def _():
        turned_ref[...] = mixed_ref[...].T

    @pl.when(step == merge_steps)
    def _():
        turned_ref[...] = normed_ref[...].T

    @pl.when(step >= 2)
    def _():
        store(step - 2).wait()

    @pl.when(step < merge_steps)
    def _():
        fill(merge_ref)

    @pl.when(step >= merge_steps)
    def _():
        fill(qkv_ref)

    store(step).start()

    @pl.when(step == steps - 1)
    def _():
        side = pltpu.make_async_copy(side_ref, out_ref.at[2 * steps], sems.at[2])
        side.start()
        store(step - 1).wait()
        store(step).wait()
        side.wait()


def projection_terms(mixed, normed, attended_grad, qkv_grad, side):
    slots, width = mixed.shape
    wide = 2 * COLS
    first, second = attended_grad.shape[1] // wide, qkv_grad.shape[1] // wide
    whole = pl.BlockSpec((slots, width), lambda j: (0, 0))
    return pl.pallas_call(
        projection_kernel,
        grid=(first + second,),
        in_specs=[
            whole,
            whole,
            pl.BlockSpec((slots, wide), lambda j: (0, jnp.minimum(j, first - 1))),
            pl.BlockSpec((slots, wide), lambda j: (0, jnp.maximum(j - first, 0))),
            pl.BlockSpec((width, COLS), lambda j: (0, 0)),
        ],
        out_specs=pl.BlockSpec(memory_space=pl.ANY),
        out_shape=jax.ShapeDtypeStruct((2 * (first + second) + 1, width, COLS), BF16),
        scratch_shapes=[
            pltpu.VMEM((width, slots), BF16),
            pltpu.VMEM((2, 2, width, COLS), BF16),
            pltpu.SemaphoreType.DMA((3,)),
        ],
        cost_estimate=pl.CostEstimate(
            flops=2 * slots * width * (first + second) * wide,
            bytes_accessed=2 * 10**7,
            transcendentals=0,
        ),
    )(mixed, normed, attended_grad, qkv_grad, side)


def body(
    tokens,
    lengths,
    routes,
    priority,
    first_gain,
    query_weight,
    key_weight,
    value_weight,
    merge_weight,
    router_weight,
    second_gain,
    gate_weight,
    up_weight,
    down_weight,
    cotangent,
):
    slots = tokens.shape[1]
    width = tokens.shape[2]
    groups = lax.axis_size("expert")
    expert_count = router_weight.shape[1]
    capacity = 5 * slots * TOP // (8 * expert_count)
    q_cols, k_cols = HEADS * HD, KV_HEADS * HD
    side_cols = 128

    def gather_shard(value, axis=0):
        return lax.all_gather(value, "shard", axis=axis, tiled=True)

    def scatter_all(part, ahead=None):
        planes, _, columns = part.shape
        part = lax.psum_scatter(
            part.reshape(planes * groups, -1, columns), "shard", scatter_dimension=1, tiled=True
        ).reshape(planes, groups, -1, columns)
        part, ahead = lax.optimization_barrier((part, ahead))
        return last_sum(part), ahead

    side = jnp.concatenate(
        [router_weight, first_gain[:, None], second_gain[:, None]], axis=1
    )
    side = jnp.pad(side, ((0, 0), (0, side_cols - expert_count - 2)))
    first_set = gather_shard(
        jnp.concatenate([query_weight, key_weight, value_weight, side], axis=1)
    )
    merge_full = gather_shard(merge_weight)
    tables = jnp.concatenate(
        [routes[0].T, priority, jnp.broadcast_to(lengths[:, None], (1, slots))], axis=0
    )
    early_columns = 5 * width // 12
    early, other_tables, first_up, first_down, both = early_gather(
        cotangent[0], tables, gate_weight, up_weight, early_columns
    )
    tables = jnp.concatenate([tables[None], other_tables], axis=0).transpose(0, 2, 1)
    tokens, first_up, first_down = lax.optimization_barrier((tokens, first_up, first_down))
    next_up, next_down = line_hops(None, 1, 2, (first_up, first_down))
    both_full = gather_shard(both, 1)
    down_full = gather_shard(down_weight, 1)

    group = lax.axis_index("expert")
    own_experts = group * EXP_DEV + jnp.arange(EXP_DEV, dtype=jnp.int32)
    spread = jax.vmap(
        lambda t: dispatch_matrix(t[:, :TOP], t[:, TOP], t[0, TOP + 1], own_experts, capacity)
    )(tables)

    qkv_full = first_set[:, : q_cols + 2 * k_cols]
    side_full = first_set[:, q_cols + 2 * k_cols :]
    router_full = side_full[:, :expert_count]
    gain_first = side_full[:, expert_count].astype(F32)
    gain_second = side_full[:, expert_count + 1].astype(F32)

    inputs = tokens[0].astype(F32)
    length = lengths[0]
    positions = jnp.arange(slots, dtype=jnp.int32)
    live_rows = (positions < length).astype(F32)[:, None]
    cosine, sine_table = rope_tables(slots)
    rms_one = lax.rsqrt(jnp.mean(inputs * inputs, axis=-1, keepdims=True) + EPS)
    unit_one = inputs * rms_one
    normed_one = (unit_one * gain_first).astype(BF16)
    qkv = jnp.dot(normed_one, qkv_full, preferred_element_type=F32)
    qkv, next_up, next_down = lax.optimization_barrier((qkv, next_up, next_down))
    last_up, last_down = line_hops(None, 2, held=(next_up[-1], next_down[-1]))
    mixed, *low_parts, lse = attend(lengths, qkv, cosine, sine_table)
    late_up = [first_up] + next_up + last_up
    late_down = [first_down] + next_down + last_down
    attended = jnp.dot(mixed, merge_full, preferred_element_type=F32)
    hidden = inputs + live_rows * attended
    rms_two = lax.rsqrt(jnp.mean(hidden * hidden, axis=-1, keepdims=True) + EPS)
    unit_two = hidden * rms_two
    normed_two = (unit_two * gain_second).astype(BF16)

    logits = jnp.dot(normed_two, router_full, preferred_element_type=F32)
    chosen = (
        routes[0][:, :, None] == jnp.arange(expert_count, dtype=jnp.int32)[None, None, :]
    ).astype(F32)
    chosen_any = jnp.sum(chosen, axis=1)
    masked = jnp.where(chosen_any > 0, logits, NEGATIVE)
    peak = jnp.max(masked, axis=-1, keepdims=True)
    exp_logits = jnp.exp(masked - peak) * chosen_any
    gate_dense = exp_logits / jnp.sum(exp_logits, axis=-1, keepdims=True)

    gates = gate_dense.T
    rows, ups, other_gates = gather_dispatch(
        normed_two, gates, cotangent[0], early, late_up, late_down, spread
    )
    gates_all = jnp.concatenate([gates[None], other_gates], axis=0)
    gates_own = lax.dynamic_slice_in_dim(gates_all, group * EXP_DEV, EXP_DEV, axis=1)
    slot_gate = jnp.sum(spread.astype(F32) * gates_own[:, :, None, :], axis=-1)
    gates = slot_gate.transpose(1, 0, 2).reshape(EXP_DEV, groups * capacity, 1)

    gated, gate_pre_grad, lift_pre_grad, back_parts, slot_grad = expert_core(
        rows, ups, gates, both_full, down_full, spread
    )

    slot_grad = slot_grad.reshape(EXP_DEV, groups, capacity).transpose(1, 0, 2)
    token_grad = jnp.sum(spread.astype(F32) * slot_grad[:, :, :, None], axis=2)
    token_grad = lax.dynamic_update_slice_in_dim(
        jnp.zeros((groups, expert_count, slots), F32), token_grad, group * EXP_DEV, axis=1
    )
    expert_grads = expert_weights(rows, ups, gated, gate_pre_grad, lift_pre_grad)
    back_parts, expert_grads = lax.optimization_barrier((back_parts, expert_grads))
    back_total, slot_back, produced = line_sum(
        token_grad, back_parts, gated, down_full, spread
    )
    slot_back = slot_back.T
    expert_grads = lax.psum_scatter(
        expert_grads.reshape(3 * EXP_DEV, width, -1), "shard", scatter_dimension=1, tiled=True
    )
    sums = scatter_hops(produced, 0, 1)

    picked_grad = gate_dense * (
        slot_back - jnp.sum(gate_dense * slot_back, axis=-1, keepdims=True)
    )
    logit_grad = jnp.pad(
        picked_grad.astype(BF16), ((0, 0), (0, side_cols - expert_count))
    )
    hidden_grad, attended_grad, mixed_grad, second_gain_part = norm_back(
        lengths, logit_grad, first_set, back_total, hidden, cotangent[0],
        gain_second[None], merge_full,
    )
    side_part = jnp.einsum("ld,le->de", normed_two, logit_grad, preferred_element_type=F32)
    side_part = jnp.where(
        jnp.arange(side_cols) == expert_count, second_gain_part[0][:, None], side_part
    )
    side_part = jnp.pad(side_part, ((0, 0), (0, COLS - side_cols))).astype(BF16)

    qkv_grad = attend_back(lengths, *low_parts, mixed_grad, lse, cosine, sine_table)
    terms = projection_terms(mixed, normed_one, attended_grad, qkv_grad, side_part)
    terms, expert_grads = lax.optimization_barrier((terms, expert_grads))
    sums, qkv_grad, terms = lax.optimization_barrier((sums, qkv_grad, terms))
    sums = scatter_hops(produced, 1, groups - 1, sums)
    normed_one_grad = jnp.einsum("lh,dh->ld", qkv_grad, qkv_full, preferred_element_type=F32)
    scaled_one = normed_one_grad * gain_first
    input_grad = hidden_grad + rms_one * (
        scaled_one - unit_one * jnp.mean(scaled_one * unit_one, axis=-1, keepdims=True)
    )
    block_output = (
        hidden + produced[0].astype(F32) + sums[0].astype(F32) + sums[1].astype(F32)
    )
    gate_grad, up_grad, down_grad = jnp.split(expert_grads.astype(F32), 3)
    reduced, (block_output, input_grad) = scatter_all(terms, (block_output, input_grad))
    own_rows = reduced.shape[1]
    reduced = reduced.transpose(1, 0, 2).reshape(own_rows, -1)
    place = (group * lax.axis_size("shard") + lax.axis_index("shard")) * own_rows
    merge_grad, qkv_reduced, side_grad = jnp.split(
        reduced, [width, width + q_cols + 2 * k_cols], axis=1
    )
    own_weights = lax.dynamic_slice_in_dim(qkv_full, place, own_rows, axis=0).astype(F32)
    own_gain = lax.dynamic_slice_in_dim(gain_first, place, own_rows)
    first_gain_grad = jnp.sum(own_weights * qkv_reduced, axis=1) / own_gain
    query_grad, key_grad, value_grad = jnp.split(qkv_reduced, [q_cols, q_cols + k_cols], axis=1)
    return (
        block_output[None],
        input_grad[None],
        first_gain_grad,
        query_grad,
        key_grad,
        value_grad,
        merge_grad,
        side_grad[:, :expert_count],
        side_grad[:, expert_count],
        gate_grad,
        up_grad,
        down_grad,
    )


def solution(mesh):
    both = ("expert", "shard")
    in_specs = (
        P(both, None, None),
        P(both),
        P(both, None, None),
        P(both, None),
        P("shard"),
        P("shard", None),
        P("shard", None),
        P("shard", None),
        P("shard", None),
        P("shard", None),
        P("shard"),
        P("expert", "shard", None),
        P("expert", "shard", None),
        P("expert", "shard", None),
        P(both, None, None),
    )
    out_specs = (
        P(both, None, None),
        P(both, None, None),
        P(both),
        P(both, None),
        P(both, None),
        P(both, None),
        P(both, None),
        P(both, None),
        P(both),
        P("expert", "shard", None),
        P("expert", "shard", None),
        P("expert", "shard", None),
    )
    return jax.shard_map(body, mesh=mesh, in_specs=in_specs, out_specs=out_specs, check_vma=False)
```
